32 devices in a mesh: clus: 4 (over y, x), dir: 8 (over z, core).
Axes of the slice: x: 2, y: 2, z: 4, core: 2. Of those that a mesh axis runs over, the one named last changes fastest.
Arguments:
- child_patterns: float32 [192, 2, 256, 128], P('clus', None, 'dir'), may hold values from -6 to 6
- trans_table: bfloat16 [316, 2, 73728], P(None, None, 'dir'), may hold values from -0.875 to 0.875
- child_parent: int32 [4, 48], P('clus'), may hold values from 0 to 7, never falling along the last dimension, each value on 1 to 8 neighbouring positions
- child_octant: int32 [192], P('clus'), may hold values from 0 to 7
- partner_src: int32 [32, 31], replicated, may hold values from 0 to 31, as said below
- partner_off: int32 [32, 31], replicated, may hold values from 0 to 315
- partner_count: int32 [32], replicated, may hold values from 8 to 31, as said below
Outputs:
- child_incoming: float32 [192, 2, 256, 128], P('clus', None, 'dir')
The draws below stay inside these ranges and needn't reach their ends.
Inputs may be any that keep to these rules, and one draw needn't show every extreme that they name: `partner_src`: each row lists 31 distinct parent clusters, none equal to the row's own index. `partner_count`: the number of live slots at the head of each row of partner_src and partner_off. On one index of clus, all of its 8 parents have 31 live slots. `child_parent`: Non-decreasing along each row; every one of the 8 parents of the row has 1 to 8 children.
All inputs are finite; a program needn't handle non-finite values.
Results may differ from the reference program's by a relative error of at most 0.0003.
Values sent between devices are 32-bit elements; how exact they have to be, the bound alone decides.
No kernel may reach another device: no remote copies, remote signals or barrier semaphores. Data moves between devices by JAX's collectives and lax.ppermute only.
A program may use at most 128 MiB of HBM per device.

```python
import math
import jax
import jax.numpy as jnp
import numpy as np
from jax import lax

NTHETA_C = 128
NPHI_C = 256
NTHETA_P = 192
NPHI_P = 384
OFFSETS = 316
PAR_DEV = 8
CHILD_DEV = 48
PARENTS = 32
CHILDREN = 192
PARTNERS = 31
N_CLUS = 4


def draw_partner_src(key, part):
    row_keys = jax.random.split(jax.random.fold_in(key, 11), PARENTS)

    def one_row(row_key, target):
        shuffled = jax.random.permutation(row_key, PARENTS - 1).astype(jnp.int32)
        shuffled = shuffled + (shuffled >= target).astype(jnp.int32)
        return shuffled[:PARTNERS]
    return jax.vmap(one_row)(row_keys, jnp.arange(PARENTS, dtype=jnp.int32)).astype(jnp.int32)


def draw_partner_count(key, part):
    count_key, device_key = jax.random.split(jax.random.fold_in(key, 23))
    counts = jax.random.randint(count_key, (PARENTS,), PARTNERS // 4 + 1, PARTNERS + 1)
    full_device = jax.random.randint(device_key, (), 0, PARENTS // PAR_DEV)
    owner_device = jnp.arange(PARENTS, dtype=jnp.int32) // PAR_DEV
    return jnp.where(owner_device == full_device, PARTNERS, counts).astype(jnp.int32)


def set_ends(values, stream_key, smallest, top_value):
    place = [jax.random.randint(jax.random.fold_in(stream_key, axis), (), 0, length) for axis, length in enumerate(values.shape)]
    main_axis = values.shape.index(max(values.shape))
    next_to = place[:main_axis] + [(place[main_axis] + 1) % values.shape[main_axis]] + place[main_axis + 1:]
    return values.at[tuple(place)].set(smallest).at[tuple(next_to)].set(top_value)


def steps_of(rng, shape, cuts, least, largest):
    level, own = 1.0, jax.random.fold_in(rng, 6)
    for position, shards_of in cuts:
        steps = jnp.exp(jax.random.uniform(jax.random.fold_in(own, position), (shards_of,), jnp.float32, least / len(cuts), largest / len(cuts)))
        level = level * jnp.repeat(steps, shape[position] // shards_of).reshape([-1 if axis == position else 1 for axis in range(len(shape))])
    return level


def split_up(number_of, total, reach, slope):
    weights = [(1 << 20) // math.isqrt(rank ** slope) + 1 for rank in range(2, number_of + 1)]
    rest, holding = total - reach - (number_of - 1), [1] * (number_of - 1)
    while rest > 0:
        free = [i for i in range(number_of - 1) if holding[i] < reach]
        pool, left = sum([weights[i] for i in free]), rest
        for i in free:
            more = min(reach - holding[i], max(1, left * weights[i] // pool), rest)
            holding[i] = holding[i] + more
            rest = rest - more
    return np.array([reach] + holding)


def ragged(rng, count, total, limit, skew):
    if count == 2:
        one = jax.random.randint(rng, (), max(1, total - limit), min(limit, total - 1) + 1)
        return jnp.stack([one, total - one])
    lengths = jnp.asarray(split_up(count, total, limit, skew), jnp.int32)
    pairs = (count - 1) // 2
    donor, taker = lengths[1:1 + 2 * pairs:2], lengths[2:2 + 2 * pairs:2]
    room = jnp.minimum(donor - 1, limit - taker)
    passed = jax.random.randint(jax.random.fold_in(rng, 1), (pairs,), 0, 1 << 20) % (room + 1)
    lengths = lengths.at[1:1 + 2 * pairs:2].set(donor - passed).at[2:2 + 2 * pairs:2].set(taker + passed)
    return lengths[jax.random.permutation(jax.random.fold_in(rng, 2), count)]


def bell_draw(key, extent, width, reach, cuts=(), held_as=jnp.bfloat16):
    level = steps_of(key, extent, cuts, -0.22, 0.18) if cuts else 1.0
    values = jax.random.normal(key, extent, jnp.float32) * width * level
    return jnp.minimum(jnp.maximum(values, -reach), reach).astype(held_as)


def setup_inputs(seed: int = 0) -> dict:
    seeds = jax.random.split(jax.random.key(seed), 8)
    child_patterns = bell_draw(seeds[0], (CHILDREN, 2, NPHI_C, NTHETA_C), 1.0, 6.0, ((0, 4), (2, 8)), jnp.float32)
    trans_table = bell_draw(seeds[1], (OFFSETS, 2, NPHI_P * NTHETA_P), 0.15, 0.875, ((2, 8),))
    child_parent = jax.vmap(lambda own: jnp.searchsorted(jnp.cumsum(ragged(own, PAR_DEV, CHILD_DEV, min(8, CHILD_DEV), 1)), jnp.arange(CHILD_DEV), side="right"))(jax.random.split(seeds[2], N_CLUS)).reshape((N_CLUS, CHILD_DEV)).astype(jnp.int32)
    child_octant = set_ends(jax.random.randint(seeds[3], (CHILDREN,), 0, 8), jax.random.fold_in(seeds[3], 1), 0, 7).astype(jnp.int32)
    partner_src = draw_partner_src(jax.random.fold_in(seeds[7], 71), 0)
    partner_off = set_ends(jax.random.randint(seeds[5], (PARENTS, PARTNERS), 0, OFFSETS), jax.random.fold_in(seeds[5], 1), 0, OFFSETS - 1).astype(jnp.int32)
    partner_count = draw_partner_count(jax.random.fold_in(seeds[7], 71), 0)
    return {"child_patterns": child_patterns, "trans_table": trans_table, "child_parent": child_parent, "child_octant": child_octant, "partner_src": partner_src, "partner_off": partner_off, "partner_count": partner_count}


phase_scale = 8.0 * math.pi
highest = lax.Precision.HIGHEST


def lagrange(offset):
    weights = []
    for anchor in range(5):
        factor = jnp.ones_like(offset)
        for neighbour in range(5):
            if neighbour != anchor:
                factor = factor * (offset - neighbour) / (anchor - neighbour)
        weights.append(factor)
    return weights


def polar_matrix_of(rows_out, rows_in):
    target = (jnp.arange(rows_out, dtype=jnp.float32) + 0.5) * rows_in / rows_out - 0.5
    start_row = jnp.clip(jnp.floor(target + 0.5).astype(jnp.int32) - 2, 0, rows_in - 5)
    weights = lagrange(target - start_row.astype(jnp.float32))
    columns = jnp.arange(rows_in, dtype=jnp.int32)
    matrix = jnp.zeros((rows_out, rows_in), jnp.float32)
    for anchor in range(5):
        matrix = matrix + jnp.where(columns[None, :] == (start_row + anchor)[:, None], weights[anchor][:, None], 0.0)
    return matrix


def azimuth_matrix_of(out_index, in_index, total_out, total_in, period):
    target = (out_index * total_in).astype(jnp.float32) / total_out
    nearest = jnp.floor(target + 0.5).astype(jnp.int32)
    weights = lagrange(target - nearest.astype(jnp.float32) + 2.0)
    matrix = jnp.zeros((out_index.shape[0], in_index.shape[0]), jnp.float32)
    for anchor in range(5):
        columns = nearest + anchor - 2
        if period > 0:
            columns = jnp.mod(columns, period)
        matrix = matrix + jnp.where(in_index[None, :] == columns[:, None], weights[anchor][:, None], 0.0)
    return matrix


def shift_phases(octant, azimuth_index, azimuth_total, polar_total):
    azimuth = 2.0 * math.pi * azimuth_index.astype(jnp.float32) / azimuth_total
    polar = math.pi * (jnp.arange(polar_total, dtype=jnp.float32) + 0.5) / polar_total
    first_axis = jnp.sin(polar)[None, :] * jnp.cos(azimuth)[:, None]
    second_axis = jnp.sin(polar)[None, :] * jnp.sin(azimuth)[:, None]
    third_axis = jnp.cos(polar)[None, :] * jnp.ones_like(azimuth)[:, None]
    first_sign = (1 - 2 * (octant % 2)).astype(jnp.float32)
    second_sign = (1 - 2 * ((octant // 2) % 2)).astype(jnp.float32)
    third_sign = (1 - 2 * (octant // 4)).astype(jnp.float32)
    phase_angle = phase_scale * (first_sign[:, None, None] * first_axis[None] + second_sign[:, None, None] * second_axis[None] + third_sign[:, None, None] * third_axis[None])
    return jnp.cos(phase_angle), jnp.sin(phase_angle)


def reference(child_patterns, trans_table, child_parent, child_octant, partner_src, partner_off, partner_count):
    azimuth_matrix = azimuth_matrix_of(jnp.arange(NPHI_P, dtype=jnp.int32), jnp.arange(NPHI_C, dtype=jnp.int32), NPHI_P, NPHI_C, NPHI_C)
    polar_matrix = polar_matrix_of(NTHETA_P, NTHETA_C)
    azimuth_rows = jnp.arange(NPHI_P, dtype=jnp.int32)
    device_blocks = child_patterns.reshape(N_CLUS, CHILD_DEV, 2, NPHI_C, NTHETA_C)
    octant_blocks = child_octant.reshape(N_CLUS, CHILD_DEV)
    parent_ids = jnp.arange(PAR_DEV, dtype=jnp.int32)

    def aggregate(inputs):
        patterns, parents, octant = inputs
        along_azimuth = jnp.einsum("pc,kacz->kapz", azimuth_matrix, patterns, precision=highest)
        refined = jnp.einsum("kapz,tz->kapt", along_azimuth, polar_matrix, precision=highest)
        cosine, sine_part = shift_phases(octant, azimuth_rows, NPHI_P, NTHETA_P)
        real_part = refined[:, 0] * cosine - refined[:, 1] * sine_part
        imaginary = refined[:, 0] * sine_part + refined[:, 1] * cosine
        shifted = jnp.stack([real_part, imaginary], axis=1)
        onehot = (parents[None, :] == parent_ids[:, None]).astype(jnp.float32)
        return jnp.einsum("gk,kapt->gapt", onehot, shifted, precision=highest)

    radiation = lax.map(aggregate, (device_blocks, child_parent, octant_blocks)).reshape(PARENTS, 2, NPHI_P, NTHETA_P)

    def translate_one(inputs):
        sources, offsets, live_count = inputs
        live_mask = (jnp.arange(PARTNERS, dtype=jnp.int32) < live_count).astype(jnp.float32)
        picked = radiation[sources]
        operator = trans_table[offsets].astype(jnp.float32).reshape(PARTNERS, 2, NPHI_P, NTHETA_P) * live_mask[:, None, None, None]
        real_part = jnp.sum(operator[:, 0] * picked[:, 0] - operator[:, 1] * picked[:, 1], axis=0)
        imaginary = jnp.sum(operator[:, 0] * picked[:, 1] + operator[:, 1] * picked[:, 0], axis=0)
        return jnp.stack([real_part, imaginary], axis=0)

    incoming = lax.map(translate_one, (partner_src, partner_off, partner_count))
    incoming_blocks = incoming.reshape(N_CLUS, PAR_DEV, 2, NPHI_P, NTHETA_P)

    def disaggregate(inputs):
        parent_patterns, parents, octant = inputs
        onehot = (parents[None, :] == parent_ids[:, None]).astype(jnp.float32)
        per_child = jnp.einsum("gk,gapt->kapt", onehot, parent_patterns, precision=highest)
        cosine, sine_part = shift_phases(octant, azimuth_rows, NPHI_P, NTHETA_P)
        real_part = per_child[:, 0] * cosine + per_child[:, 1] * sine_part
        imaginary = per_child[:, 1] * cosine - per_child[:, 0] * sine_part
        returned = jnp.stack([real_part, imaginary], axis=1)
        coarse = jnp.einsum("kapt,tz->kapz", returned, polar_matrix, precision=highest)
        return jnp.einsum("pc,kapz->kacz", azimuth_matrix, coarse, precision=highest)

    result = lax.map(disaggregate, (incoming_blocks, child_parent, octant_blocks))
    return result.reshape(CHILDREN, 2, NPHI_C, NTHETA_C)
```

```python
import functools
import math

import jax
import jax.numpy as jnp
import numpy as np
from jax import lax
from jax.experimental import pallas as pl
from jax.experimental.pallas import tpu as pltpu
from jax.sharding import PartitionSpec as P

NTHETA_C = 128
NPHI_C = 256
NTHETA_P = 192
NPHI_P = 384

LANES = 128
PERIOD_P = 6
PERIOD_C = 4
ROWS_PER_PERIOD = PERIOD_P * NTHETA_P // LANES
GROUP = 8
UNROLL = 4

phase_scale = 8.0 * math.pi
highest = lax.Precision.HIGHEST
f32 = jnp.float32
bf16 = jnp.bfloat16


def lagrange(offset):
    weights = []
    for anchor in range(5):
        factor = 1.0
        for neighbour in range(5):
            if neighbour != anchor:
                factor = factor * (offset - neighbour) / (anchor - neighbour)
        weights.append(factor)
    return weights


TAPS_A = [float(w) for w in lagrange(5.0 / 3.0)]
TAPS_B = [float(w) for w in lagrange(7.0 / 3.0)]


def polar_matrix_np():
    target = (np.arange(NTHETA_P, dtype=np.float32) + np.float32(0.5)) * NTHETA_C / NTHETA_P - np.float32(0.5)
    start = np.clip(np.floor(target + 0.5).astype(np.int32) - 2, 0, NTHETA_C - 5)
    weights = lagrange((target - start).astype(np.float64))
    matrix = np.zeros((NTHETA_P, NTHETA_C), np.float64)
    for anchor in range(5):
        matrix[np.arange(NTHETA_P), start + anchor] += weights[anchor]
    return matrix.astype(np.float32)


def polar_blocks():
    matrix = polar_matrix_np().T
    even = np.zeros((NTHETA_C, 2 * LANES), np.float32)
    odd = np.zeros((NTHETA_C, 2 * LANES), np.float32)
    half = NTHETA_P - LANES
    even[:, :NTHETA_P] = matrix
    odd[:, :LANES] = matrix[:, half:]
    odd[:, 2 * LANES - half :] = matrix[:, :half]
    return even, odd


def split_np(matrix):
    high = jnp.asarray(matrix, f32).astype(bf16)
    low = (jnp.asarray(matrix, f32) - high.astype(f32)).astype(bf16)
    return high, low


def split(values):
    high = values.astype(bf16)
    low = (values - high.astype(f32)).astype(bf16)
    return high, low


def dot3(values, high_matrix, low_matrix):
    high, low = split(values)
    dot = functools.partial(jnp.dot, preferred_element_type=f32)
    return dot(high, high_matrix) + dot(low, high_matrix) + dot(high, low_matrix)


SIN_COEFFS = [(-1) ** k * math.pi ** (2 * k + 1) / math.factorial(2 * k + 1) for k in range(7)]
COS_COEFFS = [(-1) ** k * math.pi ** (2 * k) / math.factorial(2 * k) for k in range(7)]


def sincos_turns(turns):
    rest = turns - jnp.round(turns)
    square = rest * rest
    sine = jnp.full_like(square, SIN_COEFFS[-1])
    for coeff in SIN_COEFFS[-2::-1]:
        sine = sine * square + coeff
    sine = sine * rest
    cosine = jnp.full_like(square, COS_COEFFS[-1])
    for coeff in COS_COEFFS[-2::-1]:
        cosine = cosine * square + coeff
    return 2.0 * sine * cosine, 1.0 - 2.0 * sine * sine


def phase_kernel(where_ref, out_ref):
    periods = out_ref.shape[3]
    lane = lax.broadcasted_iota(jnp.int32, (periods, LANES), 1)
    period = lax.broadcasted_iota(jnp.int32, (periods, LANES), 0)
    first = where_ref[1] * (PERIOD_P * periods)
    for w in range(ROWS_PER_PERIOD):
        position = lane + w * LANES
        row = w * LANES // NTHETA_P
        row = jnp.where(position >= (row + 1) * NTHETA_P, row + 1, row)
        polar_index = position - row * NTHETA_P
        azimuth_index = first + period * PERIOD_P + row
        sin_polar, cos_polar = sincos_turns((polar_index.astype(f32) + 0.5) / (2 * NTHETA_P))
        sin_azimuth, cos_azimuth = sincos_turns(azimuth_index.astype(f32) / NPHI_P)
        along_x = 4.0 * sin_polar * cos_azimuth
        along_y = 4.0 * sin_polar * sin_azimuth
        along_z = 4.0 * cos_polar
        for octant in (0, 2, 4, 6):
            turns = along_x + along_y if octant % 4 == 0 else along_x - along_y
            turns = turns + along_z if octant < 4 else turns - along_z
            sine, cosine = sincos_turns(turns)
            out_ref[octant, 0, w] = cosine
            out_ref[octant, 1, w] = sine
            out_ref[7 - octant, 0, w] = cosine
            out_ref[7 - octant, 1, w] = -sine


def aggregate_kernel(
    peers, parents_ref, octants_ref, where_ref, x_ref, before_ref, after_ref, phase_ref, eh_ref, el_ref, oh_ref, ol_ref, *rest
):
    outs, (az_e, az_o, res_e, res_o, acc, flat) = rest[:peers], rest[peers:]
    periods = x_ref.shape[2] // PERIOD_C
    step = pl.program_id(0)
    sublane = lax.broadcasted_iota(jnp.int32, (periods, LANES), 0)

    @pl.when(step == 0)
    def _():
        acc[...] = jnp.zeros_like(acc)

    for kp in range(2 * GROUP):
        k, part = divmod(kp, 2)
        x = [x_ref[k, part, pl.ds(u, periods, stride=PERIOD_C), :] for u in range(PERIOD_C)]
        left = jnp.where(sublane == 0, before_ref[kp : kp + 1, :], pltpu.roll(x[3], 1, 0))
        right = [
            jnp.where(sublane == periods - 1, after_ref[i, kp : kp + 1, :], pltpu.roll(x[i], periods - 1, 0))
            for i in range(2)
        ]
        lower = [left, x[0], x[1], x[2], x[3]]
        upper = [x[1], x[2], x[3], right[0], right[1]]

        def taps(weights, rows):
            total = weights[0] * rows[0]
            for weight, row in zip(weights[1:], rows[1:]):
                total = total + weight * row
            return total

        rows = [x[0], taps(TAPS_A, lower), taps(TAPS_B, lower), x[2], taps(TAPS_A, upper), taps(TAPS_B, upper)]
        for r in range(3):
            base = (kp * 3 + r) * periods
            az_e[base : base + periods, :] = rows[2 * r]
            az_o[base : base + periods, :] = rows[2 * r + 1]

    res_e[...] = dot3(az_e[...], eh_ref[...], el_ref[...])
    res_o[...] = dot3(az_o[...], oh_ref[...], ol_ref[...])

    for k in range(GROUP):
        octant = octants_ref[step * GROUP + k]
        parent = parents_ref[step * GROUP + k]
        for r in range(3):
            parts = []
            for part in range(2):
                rows = pl.ds(((2 * k + part) * 3 + r) * periods, periods)
                middle = res_e[rows, LANES:] + res_o[rows, LANES:]
                parts.append((res_e[rows, :LANES], middle, res_o[rows, :LANES]))
            for i in range(3):
                w = 3 * r + i
                real, imaginary = parts[0][i], parts[1][i]
                cosine, sine = phase_ref[octant, 0, w], phase_ref[octant, 1, w]
                acc[parent, 0, w] += real * cosine - imaginary * sine
                acc[parent, 1, w] += real * sine + imaginary * cosine

    @pl.when(step == pl.num_programs(0) - 1)
    def _():
        me = where_ref[0]
        share = ROWS_PER_PERIOD * periods // peers
        for gp in range(flat.shape[0]):
            for w in range(ROWS_PER_PERIOD):
                flat[gp, pl.ds(w, periods, stride=ROWS_PER_PERIOD), :] = acc[gp // 2, gp % 2, w]
            for d in range(peers):
                outs[d][gp * share : (gp + 1) * share, :] = flat[gp, pl.ds((me ^ d) * share, share), :]


def translate_kernel(peers, source_ref, offset_ref, groups_ref, where_ref, *rest):
    chunks, table_ref = rest[:peers], rest[peers]
    outs = rest[peers + 1 : 2 * peers + 1]
    table, real_twice, imag_twice, sum_real, sum_imag, sem = rest[2 * peers + 1 :]
    me = where_ref[0]
    slots = real_twice.shape[0] - 1
    own = slots // peers
    share = chunks[0].shape[0] // (2 * own)
    stride = source_ref.shape[0] // slots
    frame = table.shape[1]
    first_tile = me * (2 * share) // 8
    skip = me * (2 * share) - first_tile * 8
    copy = pltpu.make_async_copy(table_ref.at[:, pl.ds(pl.multiple_of(first_tile * 8, 8), frame), :], table, sem)
    copy.start()
    real_twice[slots] = jnp.zeros(real_twice.shape[1:], f32)
    imag_twice[slots] = jnp.zeros(imag_twice.shape[1:], f32)
    for d in range(peers):
        base = (me ^ d) * own
        for g in range(own):
            for part, twice in enumerate((real_twice, imag_twice)):
                rows = chunks[d][(2 * g + part) * share : (2 * g + part + 1) * share, :]
                twice[base + g, pl.ds(skip, share, stride=2), :] = rows
                twice[base + g, pl.ds(skip + 1, share, stride=2), :] = rows
    copy.wait()
    for d in range(peers):
        first = (me ^ d) * own

        def one_target(g, carry):
            target = first + g

            def some_slots(i, sums):
                by_real, by_imag = sums
                for j in range(UNROLL):
                    slot = target * stride + i * UNROLL + j
                    source = source_ref[slot]
                    operator = table[offset_ref[slot]].astype(f32)
                    by_real = by_real + operator * real_twice[source]
                    by_imag = by_imag + operator * imag_twice[source]
                return by_real, by_imag

            zero = jnp.zeros((frame, LANES), f32)
            by_real, by_imag = lax.fori_loop(0, groups_ref[target], some_slots, (zero, zero))
            sum_real[...] = by_real
            sum_imag[...] = by_imag
            even, odd = pl.ds(skip, share, stride=2), pl.ds(skip + 1, share, stride=2)
            row = g * (2 * share)
            outs[d][pl.ds(row, share), :] = sum_real[even, :] - sum_imag[odd, :]
            outs[d][pl.ds(row + share, share), :] = sum_real[odd, :] + sum_imag[even, :]
            return carry

        lax.fori_loop(0, own, one_target, 0)


def disaggregate_kernel(peers, parents_ref, octants_ref, where_ref, *rest):
    chunks = rest[:peers]
    phase_ref, eh_ref, el_ref, oh_ref, ol_ref, out_ref, next_ref, prev_ref = rest[peers : peers + 8]
    flat, lhs_e, lhs_o, coarse_e, coarse_o = rest[peers + 8 :]
    periods = out_ref.shape[2] // PERIOD_C
    step = pl.program_id(0)
    sublane = lax.broadcasted_iota(jnp.int32, (periods, LANES), 0)

    @pl.when(step == 0)
    def _():
        me = where_ref[0]
        share = ROWS_PER_PERIOD * periods // peers
        for gp in range(flat.shape[0]):
            for d in range(peers):
                flat[gp, pl.ds((me ^ d) * share, share), :] = chunks[d][gp * share : (gp + 1) * share, :]

    for k in range(GROUP):
        octant = octants_ref[step * GROUP + k]
        parent = parents_ref[step * GROUP + k]
        for r in range(3):
            parts = ([], [])
            for i in range(3):
                w = 3 * r + i
                rows = pl.ds(w, periods, stride=ROWS_PER_PERIOD)
                real, imaginary = flat[2 * parent, rows, :], flat[2 * parent + 1, rows, :]
                cosine, sine = phase_ref[octant, 0, w], phase_ref[octant, 1, w]
                parts[0].append(real * cosine + imaginary * sine)
                parts[1].append(imaginary * cosine - real * sine)
            for part in range(2):
                base = ((2 * k + part) * 3 + r) * periods
                low, middle, high = parts[part]
                lhs_e[base : base + periods, :LANES] = low
                lhs_e[base : base + periods, LANES:] = middle
                lhs_o[base : base + periods, :LANES] = high
                lhs_o[base : base + periods, LANES:] = middle

    coarse_e[...] = dot3(lhs_e[...], eh_ref[...], el_ref[...])
    coarse_o[...] = dot3(lhs_o[...], oh_ref[...], ol_ref[...])

    for kp in range(2 * GROUP):
        k, part = divmod(kp, 2)
        c = []
        for r in range(3):
            base = (kp * 3 + r) * periods
            c.append(coarse_e[base : base + periods, :])
            c.append(coarse_o[base : base + periods, :])
        a, b = TAPS_A, TAPS_B
        to_left = a[0] * c[1] + b[0] * c[2]
        to_right = [a[3] * c[4] + b[3] * c[5], a[4] * c[4] + b[4] * c[5]]
        down = [jnp.where(sublane == 0, 0.0, pltpu.roll(v, 1, 0)) for v in to_right]
        up = jnp.where(sublane == periods - 1, 0.0, pltpu.roll(to_left, periods - 1, 0))
        rows = [
            c[0] + a[1] * c[1] + b[1] * c[2] + down[0],
            a[2] * c[1] + b[2] * c[2] + a[0] * c[4] + b[0] * c[5] + down[1],
            c[3] + a[3] * c[1] + b[3] * c[2] + a[1] * c[4] + b[1] * c[5],
            a[4] * c[1] + b[4] * c[2] + a[2] * c[4] + b[2] * c[5] + up,
        ]
        for u in range(PERIOD_C):
            out_ref[k, part, pl.ds(u, periods, stride=PERIOD_C), :] = rows[u]
        for i in range(2):
            next_ref[i, kp : kp + 1, :] = to_right[i][periods - 1 :, :]
        prev_ref[kp : kp + 1, :] = to_left[:1, :]


def finish_kernel(part_ref, before_ref, after_ref, out_ref):
    rows = part_ref.shape[2]
    for kp in range(2 * GROUP):
        k, part = divmod(kp, 2)
        out_ref[k, part] = part_ref[k, part]
        for i in range(2):
            out_ref[k, part, i : i + 1, :] = part_ref[k, part, i : i + 1, :] + before_ref[i, kp : kp + 1, :]
        out_ref[k, part, rows - 1 :, :] = part_ref[k, part, rows - 1 :, :] + after_ref[kp : kp + 1, :]


def shifted(values, axis, by):
    size = lax.axis_size(axis)
    return lax.ppermute(values, axis, [(i, (i + by) % size) for i in range(size)])


def exchanged(values, axis, mask):
    size = lax.axis_size(axis)
    return lax.ppermute(values, axis, [(i, i ^ mask) for i in range(size)])


def whole(shape, *_):
    return pl.BlockSpec(shape, lambda *_: (0,) * len(shape))


def cost(flops, bytes_accessed):
    return pl.CostEstimate(flops=flops, bytes_accessed=bytes_accessed, transcendentals=0)


def on_device_exchange(
    child_patterns, trans_table, child_parent, child_octant, partner_src, partner_off, partner_count
):
    children, _, azimuth_in, polar_in = child_patterns.shape
    peers = lax.axis_size("clus")
    parent_total, partners = partner_src.shape
    own = parent_total // peers
    periods = azimuth_in // PERIOD_C
    flat_rows = ROWS_PER_PERIOD * periods
    share = flat_rows // peers
    offsets = trans_table.shape[0]
    smem = pl.BlockSpec(memory_space=pltpu.SMEM)
    vmem = pl.BlockSpec(memory_space=pltpu.VMEM)
    where = jnp.stack([lax.axis_index("clus"), lax.axis_index("dir")]).astype(jnp.int32)
    parents = child_parent[0]

    before = shifted(child_patterns[:, :, azimuth_in - 1, :].reshape(2 * children, polar_in), "dir", 1)
    after = shifted(
        jnp.stack([child_patterns[:, :, i, :].reshape(2 * children, polar_in) for i in range(2)]), "dir", -1
    )

    even, odd = polar_blocks()
    eh, el = split_np(even)
    oh, ol = split_np(odd)
    eth, etl = split_np(even.T)
    oth, otl = split_np(odd.T)

    phases = pl.pallas_call(
        phase_kernel,
        out_shape=jax.ShapeDtypeStruct((8, 2, ROWS_PER_PERIOD, periods, LANES), f32),
        in_specs=[smem],
        out_specs=vmem,
        cost_estimate=cost(2_000_000, 1_000_000),
        name="phases",
    )(where)

    slots = -(-partners // UNROLL) * UNROLL
    live = jnp.arange(partners, dtype=jnp.int32)[None, :] < partner_count[:, None]
    fill = ((0, 0), (0, slots - partners))
    source = jnp.pad(jnp.where(live, partner_src, parent_total), fill, constant_values=parent_total).reshape(-1)
    offset = jnp.pad(partner_off, fill).reshape(-1)
    groups = (partner_count + (UNROLL - 1)) // UNROLL

    steps = children // GROUP
    rows = 2 * GROUP * 3 * periods
    phase_spec = whole(phases.shape)
    chunk = jax.ShapeDtypeStruct((2 * own * share, LANES), f32)
    sent = pl.pallas_call(
        functools.partial(aggregate_kernel, peers),
        out_shape=[chunk] * peers,
        grid=(steps,),
        in_specs=[
            smem,
            smem,
            smem,
            pl.BlockSpec((GROUP, 2, azimuth_in, polar_in), lambda i: (i, 0, 0, 0)),
            pl.BlockSpec((2 * GROUP, polar_in), lambda i: (i, 0)),
            pl.BlockSpec((2, 2 * GROUP, polar_in), lambda i: (0, i, 0)),
            phase_spec,
        ]
        + [whole(eh.shape)] * 4,
        out_specs=[whole(chunk.shape)] * peers,
        scratch_shapes=[
            pltpu.VMEM((rows, LANES), f32),
            pltpu.VMEM((rows, LANES), f32),
            pltpu.VMEM((rows, 2 * LANES), f32),
            pltpu.VMEM((rows, 2 * LANES), f32),
            pltpu.VMEM((own, 2, ROWS_PER_PERIOD, periods, LANES), f32),
            pltpu.VMEM((2 * own, flat_rows, LANES), f32),
        ],
        cost_estimate=cost(2_000_000_000, 4_000_000),
        name="aggregate",
    )(parents, child_octant, where, child_patterns, before, after, phases, eh, el, oh, ol)

    received = [sent[0]] + [exchanged(sent[d], "clus", d) for d in range(1, peers)]

    view = trans_table.reshape(offsets, 2, flat_rows, LANES).transpose(0, 2, 1, 3).reshape(offsets, 2 * flat_rows, LANES)
    frame = -(-(2 * share) // 8) * 8
    frame = frame + 8 if any((q * 2 * share) % 8 + 2 * share > frame for q in range(peers)) else frame
    back = pl.pallas_call(
        functools.partial(translate_kernel, peers),
        out_shape=[chunk] * peers,
        in_specs=[smem] * 4 + [vmem] * peers + [pl.BlockSpec(memory_space=pl.ANY)],
        out_specs=[vmem] * peers,
        scratch_shapes=[
            pltpu.VMEM((offsets, frame, LANES), bf16),
            pltpu.VMEM((parent_total + 1, frame, LANES), f32),
            pltpu.VMEM((parent_total + 1, frame, LANES), f32),
            pltpu.VMEM((frame, LANES), f32),
            pltpu.VMEM((frame, LANES), f32),
            pltpu.SemaphoreType.DMA,
        ],
        cost_estimate=cost(40_000_000, 4_000_000),
        name="translate",
    )(source, offset, groups, where, *received, view)

    incoming = [back[0]] + [exchanged(back[d], "clus", d) for d in range(1, peers)]

    partial_out, to_next, to_prev = pl.pallas_call(
        functools.partial(disaggregate_kernel, peers),
        out_shape=[
            jax.ShapeDtypeStruct(child_patterns.shape, f32),
            jax.ShapeDtypeStruct((2, 2 * children, polar_in), f32),
            jax.ShapeDtypeStruct((2 * children, polar_in), f32),
        ],
        grid=(steps,),
        in_specs=[smem] * 3 + [whole(chunk.shape)] * peers + [phase_spec] + [whole(eth.shape)] * 4,
        out_specs=[
            pl.BlockSpec((GROUP, 2, azimuth_in, polar_in), lambda i: (i, 0, 0, 0)),
            pl.BlockSpec((2, 2 * GROUP, polar_in), lambda i: (0, i, 0)),
            pl.BlockSpec((2 * GROUP, polar_in), lambda i: (i, 0)),
        ],
        scratch_shapes=[
            pltpu.VMEM((2 * own, flat_rows, LANES), f32),
            pltpu.VMEM((rows, 2 * LANES), f32),
            pltpu.VMEM((rows, 2 * LANES), f32),
            pltpu.VMEM((rows, LANES), f32),
            pltpu.VMEM((rows, LANES), f32),
        ],
        cost_estimate=cost(2_000_000_000, 4_000_000),
        name="disaggregate",
    )(parents, child_octant, where, *incoming, phases, eth, etl, oth, otl)

    from_before = shifted(to_next, "dir", 1)
    from_after = shifted(to_prev, "dir", -1)
    return pl.pallas_call(
        finish_kernel,
        out_shape=jax.ShapeDtypeStruct(child_patterns.shape, f32),
        grid=(steps,),
        in_specs=[
            pl.BlockSpec((GROUP, 2, azimuth_in, polar_in), lambda i: (i, 0, 0, 0)),
            pl.BlockSpec((2, 2 * GROUP, polar_in), lambda i: (0, i, 0)),
            pl.BlockSpec((2 * GROUP, polar_in), lambda i: (i, 0)),
        ],
        out_specs=pl.BlockSpec((GROUP, 2, azimuth_in, polar_in), lambda i: (i, 0, 0, 0)),
        cost_estimate=cost(1_000_000, 3_000_000),
        name="finish",
    )(partial_out, from_before, from_after)


def with_halo(shard, sides, width):
    for axis, dim in sides:
        size, length = (lax.axis_size(axis), shard.shape[dim])
        up = [(i, (i + 1) % size) for i in range(size)]
        down = [(j, i) for i, j in up]
        last = lax.slice_in_dim(shard, length - width, length, axis=dim)
        initial = lax.slice_in_dim(shard, 0, width, axis=dim)
        before = lax.ppermute(last, axis, up)
        after = lax.ppermute(initial, axis, down)
        shard = jnp.concatenate([before, shard, after], axis=dim)
    return shard


def lagrange_rows(offset):
    weights = []
    for anchor in range(5):
        factor = jnp.ones_like(offset)
        for neighbour in range(5):
            if neighbour != anchor:
                factor = factor * (offset - neighbour) / (anchor - neighbour)
        weights.append(factor)
    return weights


def polar_matrix_of(rows_out, rows_in):
    target = (jnp.arange(rows_out, dtype=jnp.float32) + 0.5) * rows_in / rows_out - 0.5
    start_row = jnp.clip(jnp.floor(target + 0.5).astype(jnp.int32) - 2, 0, rows_in - 5)
    weights = lagrange_rows(target - start_row.astype(jnp.float32))
    columns = jnp.arange(rows_in, dtype=jnp.int32)
    matrix = jnp.zeros((rows_out, rows_in), jnp.float32)
    for anchor in range(5):
        matrix = matrix + jnp.where(
            columns[None, :] == (start_row + anchor)[:, None], weights[anchor][:, None], 0.0
        )
    return matrix


def azimuth_matrix_of(out_index, in_index, total_out, total_in):
    target = (out_index * total_in).astype(jnp.float32) / total_out
    nearest = jnp.floor(target + 0.5).astype(jnp.int32)
    weights = lagrange_rows(target - nearest.astype(jnp.float32) + 2.0)
    matrix = jnp.zeros((out_index.shape[0], in_index.shape[0]), jnp.float32)
    for anchor in range(5):
        columns = nearest + anchor - 2
        matrix = matrix + jnp.where(
            in_index[None, :] == columns[:, None], weights[anchor][:, None], 0.0
        )
    return matrix


def shift_phases(octant, azimuth_index, azimuth_total, polar_total):
    azimuth = 2.0 * math.pi * azimuth_index.astype(jnp.float32) / azimuth_total
    polar = math.pi * (jnp.arange(polar_total, dtype=jnp.float32) + 0.5) / polar_total
    first_axis = jnp.sin(polar)[None, :] * jnp.cos(azimuth)[:, None]
    second_axis = jnp.sin(polar)[None, :] * jnp.sin(azimuth)[:, None]
    third_axis = jnp.cos(polar)[None, :] * jnp.ones_like(azimuth)[:, None]
    first_sign = (1 - 2 * (octant % 2)).astype(jnp.float32)
    second_sign = (1 - 2 * (octant // 2 % 2)).astype(jnp.float32)
    third_sign = (1 - 2 * (octant // 4)).astype(jnp.float32)
    phase_angle = phase_scale * (
        first_sign[:, None, None] * first_axis[None]
        + second_sign[:, None, None] * second_axis[None]
        + third_sign[:, None, None] * third_axis[None]
    )
    return (jnp.cos(phase_angle), jnp.sin(phase_angle))


def translate(sources, table, partner_src, partner_off, partner_count):
    live_mask = (
        jnp.arange(partner_src.shape[1], dtype=jnp.int32)[None, :] < partner_count[:, None]
    ).astype(jnp.float32)
    picked = sources[partner_src]
    operator = table[partner_off].astype(jnp.float32) * live_mask[:, :, None, None]
    real_part = jnp.sum(
        operator[:, :, 0] * picked[:, :, 0] - operator[:, :, 1] * picked[:, :, 1], axis=1
    )
    imaginary = jnp.sum(
        operator[:, :, 0] * picked[:, :, 1] + operator[:, :, 1] * picked[:, :, 0], axis=1
    )
    return jnp.stack([real_part, imaginary], axis=1)


def forward_shift(patterns, cosine, sine_part):
    real_part = patterns[:, 0] * cosine - patterns[:, 1] * sine_part
    imaginary = patterns[:, 0] * sine_part + patterns[:, 1] * cosine
    return jnp.stack([real_part, imaginary], axis=1)


def conjugate_shift(patterns, cosine, sine_part):
    real_part = patterns[:, 0] * cosine + patterns[:, 1] * sine_part
    imaginary = patterns[:, 1] * cosine - patterns[:, 0] * sine_part
    return jnp.stack([real_part, imaginary], axis=1)


def on_device_gather(
    child_patterns, trans_table, child_parent, child_octant, partner_src, partner_off, partner_count
):
    child_slots, _, azimuth_in, polar_in = child_patterns.shape
    polar_out = NTHETA_P
    azimuth_out = trans_table.shape[2] // polar_out
    parent_slots = partner_src.shape[0] // lax.axis_size("clus")
    cluster_index = lax.axis_index("clus")
    direction_index = lax.axis_index("dir")
    parents = child_parent[0]
    polar_matrix = polar_matrix_of(NTHETA_P, NTHETA_C)
    onehot = (parents[None, :] == jnp.arange(parent_slots, dtype=jnp.int32)[:, None]).astype(
        jnp.float32
    )
    own_rows = jnp.mod(
        direction_index * azimuth_out + jnp.arange(azimuth_out, dtype=jnp.int32), NPHI_P
    )
    cosine, sine_part = shift_phases(child_octant, own_rows, NPHI_P, polar_out)
    extended = with_halo(child_patterns, (("dir", 2),), 2)
    gather_matrix = azimuth_matrix_of(
        jnp.arange(azimuth_out, dtype=jnp.int32),
        jnp.arange(azimuth_in + 4, dtype=jnp.int32) - 2,
        NPHI_P,
        NPHI_C,
    )
    along_azimuth = jnp.einsum("pc,kacz->kapz", gather_matrix, extended, precision=highest)
    refined = jnp.einsum("kapz,tz->kapt", along_azimuth, polar_matrix, precision=highest)
    shifted = forward_shift(refined, cosine, sine_part)
    radiation = jnp.einsum("gk,kapt->gapt", onehot, shifted, precision=highest)
    flattened = radiation.reshape(parent_slots, 2, azimuth_out * polar_out)
    sources = lax.all_gather(flattened, "clus", axis=0, tiled=True)
    first_row = cluster_index * parent_slots
    own_src = lax.dynamic_slice_in_dim(partner_src, first_row, parent_slots, 0)
    own_off = lax.dynamic_slice_in_dim(partner_off, first_row, parent_slots, 0)
    own_count = lax.dynamic_slice_in_dim(partner_count, first_row, parent_slots, 0)
    incoming = translate(sources, trans_table, own_src, own_off, own_count)
    incoming = incoming.reshape(parent_slots, 2, azimuth_out, polar_out)
    return_matrix = azimuth_matrix_of(
        jnp.arange(azimuth_out + 6, dtype=jnp.int32) - 3,
        jnp.arange(azimuth_in, dtype=jnp.int32),
        NPHI_P,
        NPHI_C,
    )
    per_child = jnp.einsum("gk,gapt->kapt", onehot, incoming, precision=highest)
    returned = conjugate_shift(per_child, cosine, sine_part)
    coarse_own = jnp.einsum("kapt,tz->kapz", returned, polar_matrix, precision=highest)
    coarse = with_halo(coarse_own, (("dir", 2),), 3)
    return jnp.einsum("pc,kapz->kacz", return_matrix, coarse, precision=highest)


def solution(mesh):
    def on_device(child_patterns, trans_table, *rest):
        peers = lax.axis_size("clus")
        children, _, azimuth_in, polar_in = child_patterns.shape
        flat_rows = trans_table.shape[2] // LANES
        fits = (
            azimuth_in % (8 * PERIOD_C) == 0
            and polar_in == LANES
            and flat_rows * PERIOD_C == ROWS_PER_PERIOD * azimuth_in
            and flat_rows % peers == 0
            and peers & (peers - 1) == 0
            and children % GROUP == 0
        )
        plan = on_device_exchange if fits else on_device_gather
        return plan(child_patterns, trans_table, *rest)

    return jax.shard_map(
        on_device,
        mesh=mesh,
        in_specs=(
            P("clus", None, "dir", None),
            P(None, None, "dir"),
            P("clus", None),
            P("clus"),
            P(),
            P(),
            P(),
        ),
        out_specs=P("clus", None, "dir", None),
        check_vma=False,
    )
```

```python
import functools
import math

import jax
import jax.numpy as jnp
import numpy as np
from jax import lax
from jax.experimental import pallas as pl
from jax.experimental.pallas import tpu as pltpu
from jax.sharding import PartitionSpec as P

NTHETA_C = 128
NPHI_C = 256
NTHETA_P = 192
NPHI_P = 384

LANES = 128
PERIOD_P = 6
PERIOD_C = 4
ROWS_PER_PERIOD = PERIOD_P * NTHETA_P // LANES
GROUP = 8
UNROLL = 4

phase_scale = 8.0 * math.pi
highest = lax.Precision.HIGHEST
f32 = jnp.float32
bf16 = jnp.bfloat16


def lagrange(offset):
    weights = []
    for anchor in range(5):
        factor = 1.0
        for neighbour in range(5):
            if neighbour != anchor:
                factor = factor * (offset - neighbour) / (anchor - neighbour)
        weights.append(factor)
    return weights


TAPS_A = [float(w) for w in lagrange(5.0 / 3.0)]
TAPS_B = [float(w) for w in lagrange(7.0 / 3.0)]


def polar_matrix_np():
    target = (np.arange(NTHETA_P, dtype=np.float32) + np.float32(0.5)) * NTHETA_C / NTHETA_P - np.float32(0.5)
    start = np.clip(np.floor(target + 0.5).astype(np.int32) - 2, 0, NTHETA_C - 5)
    weights = lagrange((target - start).astype(np.float64))
    matrix = np.zeros((NTHETA_P, NTHETA_C), np.float64)
    for anchor in range(5):
        matrix[np.arange(NTHETA_P), start + anchor] += weights[anchor]
    return matrix.astype(np.float32)


def polar_blocks():
    matrix = polar_matrix_np().T
    even = np.zeros((NTHETA_C, 2 * LANES), np.float32)
    odd = np.zeros((NTHETA_C, 2 * LANES), np.float32)
    half = NTHETA_P - LANES
    even[:, :NTHETA_P] = matrix
    odd[:, :LANES] = matrix[:, half:]
    odd[:, 2 * LANES - half :] = matrix[:, :half]
    return even, odd


def split_np(matrix):
    high = matrix.astype(bf16)
    low = (matrix - high.astype(np.float32)).astype(bf16)
    return high, low


def split(values):
    high = values.astype(bf16)
    low = (values - high.astype(f32)).astype(bf16)
    return high, low


def dot3(values, high_matrix, low_matrix):
    high, low = split(values)
    dot = functools.partial(jnp.dot, preferred_element_type=f32)
    return dot(high, high_matrix) + dot(low, high_matrix) + dot(high, low_matrix)


SIN_COEFFS = [(-1) ** k * math.pi ** (2 * k + 1) / math.factorial(2 * k + 1) for k in range(7)]
COS_COEFFS = [(-1) ** k * math.pi ** (2 * k) / math.factorial(2 * k) for k in range(7)]


def sincos_turns(turns):
    rest = turns - jnp.round(turns)
    square = rest * rest
    sine = jnp.full_like(square, SIN_COEFFS[-1])
    for coeff in SIN_COEFFS[-2::-1]:
        sine = sine * square + coeff
    sine = sine * rest
    cosine = jnp.full_like(square, COS_COEFFS[-1])
    for coeff in COS_COEFFS[-2::-1]:
        cosine = cosine * square + coeff
    return 2.0 * sine * cosine, 1.0 - 2.0 * sine * sine


def fill_phases(direction, out_ref):
    periods = out_ref.shape[3]
    lane = lax.broadcasted_iota(jnp.int32, (periods, LANES), 1)
    period = lax.broadcasted_iota(jnp.int32, (periods, LANES), 0)
    first = direction * (PERIOD_P * periods)
    for w in range(ROWS_PER_PERIOD):
        position = lane + w * LANES
        row = w * LANES // NTHETA_P
        row = jnp.where(position >= (row + 1) * NTHETA_P, row + 1, row)
        polar_index = position - row * NTHETA_P
        azimuth_index = first + period * PERIOD_P + row
        sin_polar, cos_polar = sincos_turns((polar_index.astype(f32) + 0.5) / (2 * NTHETA_P))
        sin_azimuth, cos_azimuth = sincos_turns(azimuth_index.astype(f32) / NPHI_P)
        along_x = 4.0 * sin_polar * cos_azimuth
        along_y = 4.0 * sin_polar * sin_azimuth
        along_z = 4.0 * cos_polar
        for octant in (0, 2, 4, 6):
            turns = along_x + along_y if octant % 4 == 0 else along_x - along_y
            turns = turns + along_z if octant < 4 else turns - along_z
            sine, cosine = sincos_turns(turns)
            out_ref[octant, 0, w] = cosine
            out_ref[octant, 1, w] = sine
            out_ref[7 - octant, 0, w] = cosine
            out_ref[7 - octant, 1, w] = -sine


def edge_rows(periods):
    return [(w, 0) for w in (1, 2, 3, 4)] + [(w, periods - 1) for w in (6, 7, 8)]


def rows_kernel(x_ref, held_ref, last_ref, first_ref, sem):
    pairs, azimuth_in, _ = x_ref.shape
    copy = pltpu.make_async_copy(x_ref, held_ref, sem)
    copy.start()
    copy.wait()
    for part in range(2):
        source = pl.ds(part, pairs // 2, stride=2)
        target = slice(part * (pairs // 2), (part + 1) * (pairs // 2))
        last_ref[target] = held_ref[source, azimuth_in - 1, :]
        for i in range(2):
            first_ref[i, target] = held_ref[source, i, :]


def main_kernel(
    peers, parents_ref, octants_ref, x_ref, table_ref, spread_ref, *rest
):
    flat_ref, phase_ref, edge_phase_ref, slice_ref = rest[:4]
    az_e, az_o, res_e, res_o, acc, flat, table_sem = rest[4:]
    children = octants_ref.shape[0]
    periods = phase_ref.shape[3]
    azimuth_in = periods * PERIOD_C
    own = acc.shape[0]
    me = lax.axis_index("clus")
    share = ROWS_PER_PERIOD * periods // peers
    first_tile = me * (2 * share) // 8
    table_rows = pl.ds(pl.multiple_of(first_tile * 8, 8), slice_ref.shape[1])
    table_copy = pltpu.make_async_copy(table_ref.at[:, table_rows, :], slice_ref, table_sem)
    table_copy.start()

    fill_phases(lax.axis_index("dir"), phase_ref)

    def edge_of(k, carry):
        octant = octants_ref[k]
        for e, (w, m) in enumerate(edge_rows(periods)):
            for i in range(2):
                edge_phase_ref[e, i, pl.ds(k, 1), :] = phase_ref[octant, i, w, m : m + 1, :]
        return carry

    lax.fori_loop(0, children, edge_of, 0)
    acc[...] = jnp.zeros_like(acc)
    sublane = lax.broadcasted_iota(jnp.int32, (periods, LANES), 0)

    def one_group(step, carry):
        for kp in range(2 * GROUP):
            start = pl.multiple_of((step * (2 * GROUP) + kp) * azimuth_in, 8)
            x = [x_ref[pl.ds(start + u, periods, stride=PERIOD_C), :] for u in range(PERIOD_C)]
            left = jnp.where(sublane == 0, 0.0, pltpu.roll(x[3], 1, 0))
            right = [jnp.where(sublane == periods - 1, 0.0, pltpu.roll(x[i], periods - 1, 0)) for i in range(2)]
            lower = [left, x[0], x[1], x[2], x[3]]
            upper = [x[1], x[2], x[3], right[0], right[1]]

            def taps(weights, rows):
                total = weights[0] * rows[0]
                for weight, row in zip(weights[1:], rows[1:]):
                    total = total + weight * row
                return total

            rows = [x[0], taps(TAPS_A, lower), taps(TAPS_B, lower), x[2], taps(TAPS_A, upper), taps(TAPS_B, upper)]
            for r in range(3):
                base = (kp * 3 + r) * periods
                az_e[base : base + periods, :] = rows[2 * r]
                az_o[base : base + periods, :] = rows[2 * r + 1]

        res_e[...] = dot3(az_e[...], spread_ref[0], spread_ref[1])
        res_o[...] = dot3(az_o[...], spread_ref[2], spread_ref[3])

        for k in range(GROUP):
            octant = octants_ref[step * GROUP + k]
            parent = parents_ref[step * GROUP + k]
            for r in range(3):
                parts = []
                for part in range(2):
                    rows = pl.ds(((2 * k + part) * 3 + r) * periods, periods)
                    middle = res_e[rows, LANES:] + res_o[rows, LANES:]
                    parts.append((res_e[rows, :LANES], middle, res_o[rows, :LANES]))
                for i in range(3):
                    w = 3 * r + i
                    real, imaginary = parts[0][i], parts[1][i]
                    cosine, sine = phase_ref[octant, 0, w], phase_ref[octant, 1, w]
                    acc[parent, 0, w] += real * cosine - imaginary * sine
                    acc[parent, 1, w] += real * sine + imaginary * cosine
        return carry

    lax.fori_loop(0, children // GROUP, one_group, 0)
    for gp in range(2 * own):
        for w in range(ROWS_PER_PERIOD):
            flat[pl.ds(gp * ROWS_PER_PERIOD * periods + w, periods, stride=ROWS_PER_PERIOD), :] = acc[gp // 2, gp % 2, w]
        for q in range(peers):
            source = gp * ROWS_PER_PERIOD * periods + q * share
            target = (q * 2 * own + gp) * share
            flat_ref[target : target + share, :] = flat[source : source + share, :]
    table_copy.wait()


def one_hot(parents, own):
    index = lax.broadcasted_iota(jnp.int32, (own, parents.shape[1]), 0)
    return (index == parents).astype(f32)


def dot2(exact, values):
    exact = exact.astype(bf16)
    high, low = split(values)
    dot = functools.partial(jnp.dot, preferred_element_type=f32)
    return dot(exact, high) + dot(exact, low)


def fix_kernel(
    peers, own, parents_ref, before_ref, after_ref, flat_ref, edge_phase_ref, spread_ref, *rest
):
    outs, (fixed,) = rest[:peers], rest[peers:]
    pairs = before_ref.shape[0]
    children = pairs // 2
    chunk_rows = outs[0].shape[0]
    share = chunk_rows // (2 * own)
    periods = share * peers // ROWS_PER_PERIOD
    fixed[...] = flat_ref[...]
    left, right = before_ref[...], [after_ref[0], after_ref[1]]
    a, b = TAPS_A, TAPS_B
    even = jnp.concatenate([b[0] * left, a[3] * right[0] + a[4] * right[1]], axis=0)
    odd = jnp.concatenate([a[0] * left, b[3] * right[0] + b[4] * right[1]], axis=0)
    even = dot3(even, spread_ref[0], spread_ref[1])
    odd = dot3(odd, spread_ref[2], spread_ref[3])
    first, last = slice(0, pairs), slice(pairs, 2 * pairs)
    low, high = slice(0, LANES), slice(LANES, 2 * LANES)
    refined = [
        odd[first, high],
        odd[first, low],
        even[first, low],
        even[first, high],
        even[last, low],
        even[last, high] + odd[last, high],
        odd[last, low],
    ]
    shifted_rows = []
    for e, rows in enumerate(refined):
        real, imaginary = rows[:children], rows[children:]
        cosine, sine = edge_phase_ref[e, 0], edge_phase_ref[e, 1]
        shifted_rows.append(real * cosine - imaginary * sine)
        shifted_rows.append(real * sine + imaginary * cosine)
    summed = dot2(one_hot(parents_ref[...], own), jnp.concatenate(shifted_rows, axis=1))
    for e, (w, m) in enumerate(edge_rows(periods)):
        q, row = divmod(ROWS_PER_PERIOD * m + w, share)
        for part in range(2):
            rows = pl.ds(q * chunk_rows + part * share + row, own, stride=2 * share)
            column = (2 * e + part) * LANES
            fixed[rows, :] = fixed[rows, :] + summed[:, column : column + LANES]
    me = lax.axis_index("clus")
    for d in range(peers):
        start = pl.multiple_of((me ^ d) * chunk_rows, 8)
        outs[d][...] = fixed[pl.ds(start, chunk_rows), :]


def translate_kernel(peers, targets, prepare, source_ref, offset_ref, count_ref, *rest):
    table = rest[0]
    if prepare:
        chunks, real_twice, imag_twice = rest[1 : peers + 1], rest[peers + 1], rest[peers + 2]
        outs, (sum_real, sum_imag) = rest[peers + 3 : -2], rest[-2:]
    else:
        real_twice, imag_twice = rest[1:3]
        outs, (sum_real, sum_imag) = rest[3:-2], rest[-2:]
    me = lax.axis_index("clus")
    slots = real_twice.shape[0] - 1
    own = slots // peers
    share = outs[0].shape[0] // (2 * own)
    partners = source_ref.shape[1]
    frame = table.shape[1]
    skip = lax.rem(me * (2 * share), 8)
    if prepare:
        real_twice[slots] = jnp.zeros(real_twice.shape[1:], f32)
        imag_twice[slots] = jnp.zeros(imag_twice.shape[1:], f32)
        for d in range(peers):
            base = (me ^ d) * own
            for g in range(own):
                for part, twice in enumerate((real_twice, imag_twice)):
                    rows = chunks[d][(2 * g + part) * share : (2 * g + part + 1) * share, :]
                    twice[base + g, pl.ds(skip, share, stride=2), :] = rows
                    twice[base + g, pl.ds(skip + 1, share, stride=2), :] = rows
    for out, d in zip(outs, targets):
        first = (me ^ d) * own

        def one_target(g, carry):
            target = first + g
            count = count_ref[target]

            def some_slots(i, sums):
                by_real, by_imag = sums
                for j in range(UNROLL):
                    slot = i * UNROLL + j
                    index = jnp.minimum(slot, partners - 1)
                    source = jnp.where(slot < count, source_ref[target, index], slots)
                    operator = table[offset_ref[target, index]].astype(f32)
                    by_real = by_real + operator * real_twice[source]
                    by_imag = by_imag + operator * imag_twice[source]
                return by_real, by_imag

            zero = jnp.zeros((frame, LANES), f32)
            by_real, by_imag = lax.fori_loop(0, (count + (UNROLL - 1)) // UNROLL, some_slots, (zero, zero))
            sum_real[...] = by_real
            sum_imag[...] = by_imag
            even, odd = pl.ds(skip, share, stride=2), pl.ds(skip + 1, share, stride=2)
            row = g * (2 * share)
            out[pl.ds(row, share), :] = sum_real[even, :] - sum_imag[odd, :]
            out[pl.ds(row + share, share), :] = sum_real[odd, :] + sum_imag[even, :]
            return carry

        lax.fori_loop(0, own, one_target, 0)


def edge_kernel(peers, parents_ref, edge_phase_ref, gather_ref, *rest):
    chunks = rest[:peers]
    incoming_ref, next_ref, prev_ref, flat = rest[peers:]
    own2, _, periods, _ = incoming_ref.shape
    own = own2 // 2
    pairs = prev_ref.shape[0]
    children = pairs // 2
    flat_rows = ROWS_PER_PERIOD * periods
    share = flat_rows // peers
    me = lax.axis_index("clus")
    for gp in range(own2):
        for d in range(peers):
            flat[pl.ds(gp * flat_rows + (me ^ d) * share, share), :] = chunks[d][gp * share : (gp + 1) * share, :]
    edges = []
    for w, m in edge_rows(periods):
        for part in range(2):
            edges.append(flat[pl.ds(part * flat_rows + ROWS_PER_PERIOD * m + w, own, stride=2 * flat_rows), :])
    per_child = dot2(one_hot(parents_ref[...], own).T, jnp.concatenate(edges, axis=1))
    returned = []
    for e in range(len(edges) // 2):
        real = per_child[:, 2 * e * LANES : (2 * e + 1) * LANES]
        imaginary = per_child[:, (2 * e + 1) * LANES : (2 * e + 2) * LANES]
        cosine, sine = edge_phase_ref[e, 0], edge_phase_ref[e, 1]
        returned.append(
            jnp.concatenate([real * cosine + imaginary * sine, imaginary * cosine - real * sine], axis=0)
        )
    join = functools.partial(jnp.concatenate, axis=1)
    even = jnp.concatenate([join([returned[2], returned[3]]), join([returned[4], returned[5]])], axis=0)
    odd = jnp.concatenate([join([returned[1], returned[0]]), join([returned[6], returned[5]])], axis=0)
    even = dot3(even, gather_ref[0], gather_ref[1])
    odd = dot3(odd, gather_ref[2], gather_ref[3])
    a, b = TAPS_A, TAPS_B
    prev_ref[...] = a[0] * odd[:pairs] + b[0] * even[:pairs]
    next_ref[0] = a[3] * even[pairs:] + b[3] * odd[pairs:]
    next_ref[1] = a[4] * even[pairs:] + b[4] * odd[pairs:]
    for gp in range(own2):
        for w in range(ROWS_PER_PERIOD):
            incoming_ref[gp, w] = flat[pl.ds(gp * flat_rows + w, periods, stride=ROWS_PER_PERIOD), :]


def disaggregate_kernel(
    parents_ref, octants_ref, incoming_ref, phase_ref, gather_ref, out_ref, lhs_e, lhs_o, coarse_e, coarse_o
):
    children = octants_ref.shape[0]
    periods = incoming_ref.shape[2]
    azimuth_in = periods * PERIOD_C
    sublane = lax.broadcasted_iota(jnp.int32, (periods, LANES), 0)

    def one_group(step, carry):
        for k in range(GROUP):
            octant = octants_ref[step * GROUP + k]
            parent = parents_ref[step * GROUP + k]
            for r in range(3):
                parts = ([], [])
                for i in range(3):
                    w = 3 * r + i
                    real, imaginary = incoming_ref[2 * parent, w], incoming_ref[2 * parent + 1, w]
                    cosine, sine = phase_ref[octant, 0, w], phase_ref[octant, 1, w]
                    parts[0].append(real * cosine + imaginary * sine)
                    parts[1].append(imaginary * cosine - real * sine)
                for part in range(2):
                    base = ((2 * k + part) * 3 + r) * periods
                    low, middle, high = parts[part]
                    lhs_e[base : base + periods, :LANES] = low
                    lhs_e[base : base + periods, LANES:] = middle
                    lhs_o[base : base + periods, :LANES] = high
                    lhs_o[base : base + periods, LANES:] = middle

        coarse_e[...] = dot3(lhs_e[...], gather_ref[0], gather_ref[1])
        coarse_o[...] = dot3(lhs_o[...], gather_ref[2], gather_ref[3])

        for kp in range(2 * GROUP):
            c = []
            for r in range(3):
                base = (kp * 3 + r) * periods
                c.append(coarse_e[base : base + periods, :])
                c.append(coarse_o[base : base + periods, :])
            a, b = TAPS_A, TAPS_B
            to_left = a[0] * c[1] + b[0] * c[2]
            to_right = [a[3] * c[4] + b[3] * c[5], a[4] * c[4] + b[4] * c[5]]
            down = [jnp.where(sublane == 0, 0.0, pltpu.roll(v, 1, 0)) for v in to_right]
            up = jnp.where(sublane == periods - 1, 0.0, pltpu.roll(to_left, periods - 1, 0))
            rows = [
                c[0] + a[1] * c[1] + b[1] * c[2] + down[0],
                a[2] * c[1] + b[2] * c[2] + a[0] * c[4] + b[0] * c[5] + down[1],
                c[3] + a[3] * c[1] + b[3] * c[2] + a[1] * c[4] + b[1] * c[5],
                a[4] * c[1] + b[4] * c[2] + a[2] * c[4] + b[2] * c[5] + up,
            ]
            start = pl.multiple_of((step * (2 * GROUP) + kp) * azimuth_in, 8)
            for u in range(PERIOD_C):
                out_ref[pl.ds(start + u, periods, stride=PERIOD_C), :] = rows[u]
        return carry

    lax.fori_loop(0, children // GROUP, one_group, 0)


def finish_kernel(part_ref, before_ref, after_ref, out_ref):
    rows, pairs = part_ref.shape[0], after_ref.shape[0]
    azimuth_in = rows // pairs
    out_ref[...] = part_ref[...]
    for part in range(2):
        for k in range(0, pairs // 2, 8):
            source = slice(part * (pairs // 2) + k, part * (pairs // 2) + k + 8)
            for row, values in ((0, before_ref[0, source]), (1, before_ref[1, source]), (azimuth_in - 1, after_ref[source])):
                target = pl.ds((2 * k + part) * azimuth_in + row, 8, stride=2 * azimuth_in)
                out_ref[target, :] = part_ref[target, :] + values


def shifted(values, axis, by):
    size = lax.axis_size(axis)
    return lax.ppermute(values, axis, [(i, (i + by) % size) for i in range(size)])


def exchanged(values, axis, mask):
    size = lax.axis_size(axis)
    return lax.ppermute(values, axis, [(i, i ^ mask) for i in range(size)])


SMEM = pl.BlockSpec(memory_space=pltpu.SMEM)
VMEM = pl.BlockSpec(memory_space=pltpu.VMEM)
HBM = pl.BlockSpec(memory_space=pltpu.HBM)


def local_call(kernel, name, out_shape, in_specs, scratch, grant, flops=1_000_000, bytes_accessed=1_000_000):
    return pl.pallas_call(
        kernel,
        out_shape=out_shape,
        in_specs=in_specs,
        out_specs=jax.tree.map(lambda _: VMEM, out_shape),
        scratch_shapes=scratch,
        compiler_params=pltpu.CompilerParams(vmem_limit_bytes=grant << 20),
        cost_estimate=pl.CostEstimate(flops=flops, bytes_accessed=bytes_accessed, transcendentals=0),
        name=name,
    )


def on_device_exchange(
    child_patterns, trans_table, child_parent, child_octant, partner_src, partner_off, partner_count
):
    children, _, azimuth_in, polar_in = child_patterns.shape
    pairs = 2 * children
    peers = lax.axis_size("clus")
    parent_total, _ = partner_src.shape
    own = parent_total // peers
    periods = azimuth_in // PERIOD_C
    flat_rows = ROWS_PER_PERIOD * periods
    share = flat_rows // peers
    offsets = trans_table.shape[0]
    array = lambda *shape: jax.ShapeDtypeStruct(shape, f32)
    buffer = lambda *shape: pltpu.VMEM(shape, f32)
    parents = child_parent[0]

    held, last, first = local_call(
        rows_kernel,
        "rows",
        [array(pairs, azimuth_in, polar_in), array(pairs, polar_in), array(2, pairs, polar_in)],
        [HBM],
        [pltpu.SemaphoreType.DMA],
        51,
    )(child_patterns.reshape(pairs, azimuth_in, polar_in))
    before = shifted(last, "dir", 1)
    after = shifted(first, "dir", -1)

    even, odd = polar_blocks()
    spread = np.stack([*split_np(even), *split_np(odd)])
    gather = np.stack([*split_np(even.T), *split_np(odd.T)])

    frame = max(-(-((q * 2 * share) % 8 + 2 * share) // 8) * 8 for q in range(peers))
    view = trans_table.reshape(offsets, 2, flat_rows, LANES).transpose(0, 2, 1, 3).reshape(offsets, 2 * flat_rows, LANES)
    rows = 2 * GROUP * 3 * periods
    edges = len(edge_rows(periods))
    flat, phases, edge_phases, table = local_call(
        functools.partial(main_kernel, peers),
        "aggregate",
        [
            array(2 * own * flat_rows, LANES),
            array(8, 2, ROWS_PER_PERIOD, periods, LANES),
            array(edges, 2, children, LANES),
            jax.ShapeDtypeStruct((offsets, frame, LANES), bf16),
        ],
        [SMEM] * 2 + [VMEM, HBM, VMEM],
        [
            buffer(rows, LANES),
            buffer(rows, LANES),
            buffer(rows, 2 * LANES),
            buffer(rows, 2 * LANES),
            buffer(own, 2, ROWS_PER_PERIOD, periods, LANES),
            buffer(2 * own * flat_rows, LANES),
            pltpu.SemaphoreType.DMA,
        ],
        46,
        flops=4_000_000_000,
        bytes_accessed=12_000_000,
    )(parents, child_octant, held.reshape(pairs * azimuth_in, polar_in), view, spread)

    chunk = array(2 * own * share, LANES)
    sent = local_call(
        functools.partial(fix_kernel, peers, own),
        "fix_edges",
        [chunk] * peers,
        [VMEM] * 6,
        [buffer(2 * own * flat_rows, LANES)],
        8,
    )(child_parent, before, after, flat, edge_phases, spread)

    masks = sorted(range(1, peers), key=lambda d: -bin(d).count("1"))
    received = {0: sent[0]}
    for d in masks:
        received[d] = exchanged(sent[d], "clus", d)

    twice = array(parent_total + 1, frame, LANES)
    sums = [buffer(frame, LANES)] * 2
    lists = (partner_src, partner_off, partner_count)
    back = {}
    real_twice = imag_twice = None
    for targets in (masks[:1], masks[1:], [0]):
        prepare = real_twice is None
        call = local_call(
            functools.partial(translate_kernel, peers, tuple(targets), prepare),
            "translate",
            ([twice] * 2 if prepare else []) + [chunk] * len(targets),
            [SMEM] * 3 + [VMEM] * (1 + peers if prepare else 3),
            sums,
            12,
            flops=20_000_000 * len(targets),
            bytes_accessed=4_000_000 * len(targets),
        )
        if prepare:
            real_twice, imag_twice, *results = call(*lists, table, *[received[d] for d in range(peers)])
        else:
            results = call(*lists, table, real_twice, imag_twice)
        for d, result in zip(targets, results):
            back[d] = exchanged(result, "clus", d) if d else result

    incoming, to_next, to_prev = local_call(
        functools.partial(edge_kernel, peers),
        "edges",
        [array(2 * own, ROWS_PER_PERIOD, periods, LANES), array(2, pairs, polar_in), array(pairs, polar_in)],
        [VMEM] * (3 + peers),
        [buffer(2 * own * flat_rows, LANES)],
        8,
    )(child_parent, edge_phases, gather, *[back[d] for d in range(peers)])

    from_before = shifted(to_next, "dir", 1)
    from_after = shifted(to_prev, "dir", -1)

    partial_out = local_call(
        disaggregate_kernel,
        "disaggregate",
        array(pairs * azimuth_in, polar_in),
        [SMEM] * 2 + [VMEM] * 3,
        [buffer(rows, 2 * LANES), buffer(rows, 2 * LANES), buffer(rows, LANES), buffer(rows, LANES)],
        12,
        flops=4_000_000_000,
        bytes_accessed=12_000_000,
    )(parents, child_octant, incoming, phases, gather)

    out = local_call(finish_kernel, "finish", array(pairs * azimuth_in, polar_in), [VMEM] * 3, [], 8)(
        partial_out, from_before, from_after
    )
    return out.reshape(child_patterns.shape)


def with_halo(shard, sides, width):
    for axis, dim in sides:
        size, length = (lax.axis_size(axis), shard.shape[dim])
        up = [(i, (i + 1) % size) for i in range(size)]
        down = [(j, i) for i, j in up]
        last = lax.slice_in_dim(shard, length - width, length, axis=dim)
        initial = lax.slice_in_dim(shard, 0, width, axis=dim)
        before = lax.ppermute(last, axis, up)
        after = lax.ppermute(initial, axis, down)
        shard = jnp.concatenate([before, shard, after], axis=dim)
    return shard


def lagrange_rows(offset):
    weights = []
    for anchor in range(5):
        factor = jnp.ones_like(offset)
        for neighbour in range(5):
            if neighbour != anchor:
                factor = factor * (offset - neighbour) / (anchor - neighbour)
        weights.append(factor)
    return weights


def polar_matrix_of(rows_out, rows_in):
    target = (jnp.arange(rows_out, dtype=jnp.float32) + 0.5) * rows_in / rows_out - 0.5
    start_row = jnp.clip(jnp.floor(target + 0.5).astype(jnp.int32) - 2, 0, rows_in - 5)
    weights = lagrange_rows(target - start_row.astype(jnp.float32))
    columns = jnp.arange(rows_in, dtype=jnp.int32)
    matrix = jnp.zeros((rows_out, rows_in), jnp.float32)
    for anchor in range(5):
        matrix = matrix + jnp.where(
            columns[None, :] == (start_row + anchor)[:, None], weights[anchor][:, None], 0.0
        )
    return matrix


def azimuth_matrix_of(out_index, in_index, total_out, total_in):
    target = (out_index * total_in).astype(jnp.float32) / total_out
    nearest = jnp.floor(target + 0.5).astype(jnp.int32)
    weights = lagrange_rows(target - nearest.astype(jnp.float32) + 2.0)
    matrix = jnp.zeros((out_index.shape[0], in_index.shape[0]), jnp.float32)
    for anchor in range(5):
        columns = nearest + anchor - 2
        matrix = matrix + jnp.where(
            in_index[None, :] == columns[:, None], weights[anchor][:, None], 0.0
        )
    return matrix


def shift_phases(octant, azimuth_index, azimuth_total, polar_total):
    azimuth = 2.0 * math.pi * azimuth_index.astype(jnp.float32) / azimuth_total
    polar = math.pi * (jnp.arange(polar_total, dtype=jnp.float32) + 0.5) / polar_total
    first_axis = jnp.sin(polar)[None, :] * jnp.cos(azimuth)[:, None]
    second_axis = jnp.sin(polar)[None, :] * jnp.sin(azimuth)[:, None]
    third_axis = jnp.cos(polar)[None, :] * jnp.ones_like(azimuth)[:, None]
    first_sign = (1 - 2 * (octant % 2)).astype(jnp.float32)
    second_sign = (1 - 2 * (octant // 2 % 2)).astype(jnp.float32)
    third_sign = (1 - 2 * (octant // 4)).astype(jnp.float32)
    phase_angle = phase_scale * (
        first_sign[:, None, None] * first_axis[None]
        + second_sign[:, None, None] * second_axis[None]
        + third_sign[:, None, None] * third_axis[None]
    )
    return (jnp.cos(phase_angle), jnp.sin(phase_angle))


def translate(sources, table, partner_src, partner_off, partner_count):
    live_mask = (
        jnp.arange(partner_src.shape[1], dtype=jnp.int32)[None, :] < partner_count[:, None]
    ).astype(jnp.float32)
    picked = sources[partner_src]
    operator = table[partner_off].astype(jnp.float32) * live_mask[:, :, None, None]
    real_part = jnp.sum(
        operator[:, :, 0] * picked[:, :, 0] - operator[:, :, 1] * picked[:, :, 1], axis=1
    )
    imaginary = jnp.sum(
        operator[:, :, 0] * picked[:, :, 1] + operator[:, :, 1] * picked[:, :, 0], axis=1
    )
    return jnp.stack([real_part, imaginary], axis=1)


def forward_shift(patterns, cosine, sine_part):
    real_part = patterns[:, 0] * cosine - patterns[:, 1] * sine_part
    imaginary = patterns[:, 0] * sine_part + patterns[:, 1] * cosine
    return jnp.stack([real_part, imaginary], axis=1)


def conjugate_shift(patterns, cosine, sine_part):
    real_part = patterns[:, 0] * cosine + patterns[:, 1] * sine_part
    imaginary = patterns[:, 1] * cosine - patterns[:, 0] * sine_part
    return jnp.stack([real_part, imaginary], axis=1)


def on_device_gather(
    child_patterns, trans_table, child_parent, child_octant, partner_src, partner_off, partner_count
):
    child_slots, _, azimuth_in, polar_in = child_patterns.shape
    polar_out = NTHETA_P
    azimuth_out = trans_table.shape[2] // polar_out
    parent_slots = partner_src.shape[0] // lax.axis_size("clus")
    cluster_index = lax.axis_index("clus")
    direction_index = lax.axis_index("dir")
    parents = child_parent[0]
    polar_matrix = polar_matrix_of(NTHETA_P, NTHETA_C)
    onehot = (parents[None, :] == jnp.arange(parent_slots, dtype=jnp.int32)[:, None]).astype(
        jnp.float32
    )
    own_rows = jnp.mod(
        direction_index * azimuth_out + jnp.arange(azimuth_out, dtype=jnp.int32), NPHI_P
    )
    cosine, sine_part = shift_phases(child_octant, own_rows, NPHI_P, polar_out)
    extended = with_halo(child_patterns, (("dir", 2),), 2)
    gather_matrix = azimuth_matrix_of(
        jnp.arange(azimuth_out, dtype=jnp.int32),
        jnp.arange(azimuth_in + 4, dtype=jnp.int32) - 2,
        NPHI_P,
        NPHI_C,
    )
    along_azimuth = jnp.einsum("pc,kacz->kapz", gather_matrix, extended, precision=highest)
    refined = jnp.einsum("kapz,tz->kapt", along_azimuth, polar_matrix, precision=highest)
    shifted = forward_shift(refined, cosine, sine_part)
    radiation = jnp.einsum("gk,kapt->gapt", onehot, shifted, precision=highest)
    flattened = radiation.reshape(parent_slots, 2, azimuth_out * polar_out)
    sources = lax.all_gather(flattened, "clus", axis=0, tiled=True)
    first_row = cluster_index * parent_slots
    own_src = lax.dynamic_slice_in_dim(partner_src, first_row, parent_slots, 0)
    own_off = lax.dynamic_slice_in_dim(partner_off, first_row, parent_slots, 0)
    own_count = lax.dynamic_slice_in_dim(partner_count, first_row, parent_slots, 0)
    incoming = translate(sources, trans_table, own_src, own_off, own_count)
    incoming = incoming.reshape(parent_slots, 2, azimuth_out, polar_out)
    return_matrix = azimuth_matrix_of(
        jnp.arange(azimuth_out + 6, dtype=jnp.int32) - 3,
        jnp.arange(azimuth_in, dtype=jnp.int32),
        NPHI_P,
        NPHI_C,
    )
    per_child = jnp.einsum("gk,gapt->kapt", onehot, incoming, precision=highest)
    returned = conjugate_shift(per_child, cosine, sine_part)
    coarse_own = jnp.einsum("kapt,tz->kapz", returned, polar_matrix, precision=highest)
    coarse = with_halo(coarse_own, (("dir", 2),), 3)
    return jnp.einsum("pc,kapz->kacz", return_matrix, coarse, precision=highest)


def solution(mesh):
    def on_device(child_patterns, trans_table, *rest):
        peers = lax.axis_size("clus")
        children, _, azimuth_in, polar_in = child_patterns.shape
        flat_rows = trans_table.shape[2] // LANES
        fits = (
            azimuth_in % (8 * PERIOD_C) == 0
            and polar_in == LANES
            and flat_rows * PERIOD_C == ROWS_PER_PERIOD * azimuth_in
            and flat_rows % peers == 0
            and peers & (peers - 1) == 0
            and children % GROUP == 0
        )
        plan = on_device_exchange if fits else on_device_gather
        return plan(child_patterns, trans_table, *rest)

    return jax.shard_map(
        on_device,
        mesh=mesh,
        in_specs=(
            P("clus", None, "dir", None),
            P(None, None, "dir"),
            P("clus", None),
            P("clus"),
            P(),
            P(),
            P(),
        ),
        out_specs=P("clus", None, "dir", None),
        check_vma=False,
    )
```

```python
import functools
import math

import jax
import jax.numpy as jnp
import numpy as np
from jax import lax
from jax.experimental import pallas as pl
from jax.experimental.pallas import tpu as pltpu
from jax.sharding import PartitionSpec as P


NTHETA_C = 128
NPHI_C = 256
NTHETA_P = 192
NPHI_P = 384

LANES = 128
PERIOD_P = 6
PERIOD_C = 4
ROWS_PER_PERIOD = PERIOD_P * NTHETA_P // LANES
GROUP = 8
UNROLL = 8
PAIR = 2

phase_scale = 8.0 * math.pi
highest = lax.Precision.HIGHEST
f32 = jnp.float32
bf16 = jnp.bfloat16


def lagrange(offset):
    weights = []
    for anchor in range(5):
        factor = 1.0
        for neighbour in range(5):
            if neighbour != anchor:
                factor = factor * (offset - neighbour) / (anchor - neighbour)
        weights.append(factor)
    return weights


TAPS_A = [float(w) for w in lagrange(5.0 / 3.0)]
TAPS_B = [float(w) for w in lagrange(7.0 / 3.0)]


def polar_matrix_np():
    target = (np.arange(NTHETA_P, dtype=np.float32) + np.float32(0.5)) * NTHETA_C / NTHETA_P - np.float32(0.5)
    start = np.clip(np.floor(target + 0.5).astype(np.int32) - 2, 0, NTHETA_C - 5)
    weights = lagrange((target - start).astype(np.float64))
    matrix = np.zeros((NTHETA_P, NTHETA_C), np.float64)
    for anchor in range(5):
        matrix[np.arange(NTHETA_P), start + anchor] += weights[anchor]
    return matrix.astype(np.float32)


def polar_blocks():
    matrix = polar_matrix_np().T
    even = np.zeros((NTHETA_C, 2 * LANES), np.float32)
    odd = np.zeros((NTHETA_C, 2 * LANES), np.float32)
    half = NTHETA_P - LANES
    even[:, :NTHETA_P] = matrix
    odd[:, :LANES] = matrix[:, half:]
    odd[:, 2 * LANES - half :] = matrix[:, :half]
    return even, odd


def split_np(matrix):
    high = matrix.astype(bf16)
    low = (matrix - high.astype(np.float32)).astype(bf16)
    return high, low


def split(values):
    high = values.astype(bf16)
    low = (values - high.astype(f32)).astype(bf16)
    return high, low


def dot3(values, high_matrix, low_matrix):
    high, low = split(values)
    dot = functools.partial(jnp.dot, preferred_element_type=f32)
    return dot(high, high_matrix) + dot(low, high_matrix) + dot(high, low_matrix)


SIN_COEFFS = [(-1) ** k * math.pi ** (2 * k + 1) / math.factorial(2 * k + 1) for k in range(7)]
COS_COEFFS = [(-1) ** k * math.pi ** (2 * k) / math.factorial(2 * k) for k in range(7)]


def sincos_turns(turns):
    rest = turns - jnp.round(turns)
    square = rest * rest
    sine = jnp.full_like(square, SIN_COEFFS[-1])
    for coeff in SIN_COEFFS[-2::-1]:
        sine = sine * square + coeff
    sine = sine * rest
    cosine = jnp.full_like(square, COS_COEFFS[-1])
    for coeff in COS_COEFFS[-2::-1]:
        cosine = cosine * square + coeff
    return 2.0 * sine * cosine, 1.0 - 2.0 * sine * sine


def fill_phases(direction, out_ref):
    periods = out_ref.shape[3]
    lane = lax.broadcasted_iota(jnp.int32, (periods, LANES), 1)
    period = lax.broadcasted_iota(jnp.int32, (periods, LANES), 0)
    first = direction * (PERIOD_P * periods)
    for w in range(ROWS_PER_PERIOD):
        position = lane + w * LANES
        row = w * LANES // NTHETA_P
        row = jnp.where(position >= (row + 1) * NTHETA_P, row + 1, row)
        polar_index = position - row * NTHETA_P
        azimuth_index = first + period * PERIOD_P + row
        sin_polar, cos_polar = sincos_turns((polar_index.astype(f32) + 0.5) / (2 * NTHETA_P))
        sin_azimuth, cos_azimuth = sincos_turns(azimuth_index.astype(f32) / NPHI_P)
        along_x = 4.0 * sin_polar * cos_azimuth
        along_y = 4.0 * sin_polar * sin_azimuth
        along_z = 4.0 * cos_polar
        for octant in (0, 2, 4, 6):
            turns = along_x + along_y if octant % 4 == 0 else along_x - along_y
            turns = turns + along_z if octant < 4 else turns - along_z
            sine, cosine = sincos_turns(turns)
            out_ref[octant, 0, w] = cosine
            out_ref[octant, 1, w] = sine
            out_ref[7 - octant, 0, w] = cosine
            out_ref[7 - octant, 1, w] = -sine


def edge_rows(periods):
    return [(w, 0) for w in (1, 2, 3, 4)] + [(w, periods - 1) for w in (6, 7, 8)]


def rows_kernel(octants_ref, x_ref, held_ref, last_ref, first_ref, phase_ref, edge_phase_ref, sem):
    pairs, azimuth_in, _ = x_ref.shape
    periods = phase_ref.shape[3]
    copy = pltpu.make_async_copy(x_ref, held_ref, sem)
    copy.start()
    fill_phases(lax.axis_index("dir"), phase_ref)

    def edges_of(step, carry):
        for j in range(GROUP):
            k = step * GROUP + j
            octant = octants_ref[k]
            for e, (w, m) in enumerate(edge_rows(periods)):
                for i in range(2):
                    edge_phase_ref[e, i, pl.ds(k, 1), :] = phase_ref[octant, i, w, m : m + 1, :]
        return carry

    lax.fori_loop(0, pairs // 2 // GROUP, edges_of, 0)
    copy.wait()
    for part in range(2):
        source = pl.ds(part, pairs // 2, stride=2)
        target = slice(part * (pairs // 2), (part + 1) * (pairs // 2))
        last_ref[target] = held_ref[source, azimuth_in - 1, :]
        for i in range(2):
            first_ref[i, target] = held_ref[source, i, :]


def taps(weights, rows):
    total = weights[0] * rows[0]
    for weight, row in zip(weights[1:], rows[1:]):
        total = total + weight * row
    return total


def main_kernel(peers, parents_ref, octants_ref, x_ref, table_ref, phase_ref, spread_ref, *rest):
    flat_ref, slice_ref, az_e, az_o, res_e, res_o, acc, flat, table_sem = rest
    children = octants_ref.shape[0]
    periods = phase_ref.shape[3]
    azimuth_in = periods * PERIOD_C
    own = acc.shape[0]
    me = lax.axis_index("clus")
    share = ROWS_PER_PERIOD * periods // peers
    first_tile = me * (2 * share) // 8
    table_rows = pl.ds(pl.multiple_of(first_tile * 8, 8), slice_ref.shape[1])
    table_copy = pltpu.make_async_copy(table_ref.at[:, table_rows, :], slice_ref, table_sem)
    table_copy.start()
    acc[...] = jnp.zeros_like(acc)
    sublane = lax.broadcasted_iota(jnp.int32, (periods, LANES), 0)

    def azimuth(step, h):
        for kp in range(2 * GROUP):
            start = pl.multiple_of((step * (2 * GROUP) + kp) * azimuth_in, 8)
            x = [x_ref[pl.ds(start + u, periods, stride=PERIOD_C), :] for u in range(PERIOD_C)]
            left = jnp.where(sublane == 0, 0.0, pltpu.roll(x[3], 1, 0))
            right = [jnp.where(sublane == periods - 1, 0.0, pltpu.roll(x[i], periods - 1, 0)) for i in range(2)]
            lower = [left, x[0], x[1], x[2], x[3]]
            upper = [x[1], x[2], x[3], right[0], right[1]]
            rows = [x[0], taps(TAPS_A, lower), taps(TAPS_B, lower), x[2], taps(TAPS_A, upper), taps(TAPS_B, upper)]
            for r in range(3):
                base = (kp * 3 + r) * periods
                az_e[h, base : base + periods, :] = rows[2 * r]
                az_o[h, base : base + periods, :] = rows[2 * r + 1]

    def polar(h):
        res_e[h] = dot3(az_e[h], spread_ref[0], spread_ref[1])
        res_o[h] = dot3(az_o[h], spread_ref[2], spread_ref[3])

    def shift(step, h):
        for k in range(GROUP):
            octant = octants_ref[step * GROUP + k]
            parent = parents_ref[step * GROUP + k]
            for r in range(3):
                parts = []
                for part in range(2):
                    rows = pl.ds(((2 * k + part) * 3 + r) * periods, periods)
                    middle = res_e[h, rows, LANES:] + res_o[h, rows, LANES:]
                    parts.append((res_e[h, rows, :LANES], middle, res_o[h, rows, :LANES]))
                for i in range(3):
                    w = 3 * r + i
                    real, imaginary = parts[0][i], parts[1][i]
                    cosine, sine = phase_ref[octant, 0, w], phase_ref[octant, 1, w]
                    acc[parent, 0, w] += real * cosine - imaginary * sine
                    acc[parent, 1, w] += real * sine + imaginary * cosine

    def some_groups(i, carry):
        for h in range(PAIR):
            azimuth(i * PAIR + h, h)
            polar(h)
        for h in range(PAIR):
            shift(i * PAIR + h, h)
        return carry

    lax.fori_loop(0, children // (PAIR * GROUP), some_groups, 0)
    for gp in range(2 * own):
        for w in range(ROWS_PER_PERIOD):
            flat[pl.ds(gp * ROWS_PER_PERIOD * periods + w, periods, stride=ROWS_PER_PERIOD), :] = acc[gp // 2, gp % 2, w]
        for q in range(peers):
            source = gp * ROWS_PER_PERIOD * periods + q * share
            target = (q * 2 * own + gp) * share
            flat_ref[target : target + share, :] = flat[source : source + share, :]
    table_copy.wait()


def one_hot(parents, own):
    index = lax.broadcasted_iota(jnp.int32, (own, parents.shape[1]), 0)
    return (index == parents).astype(f32)


def dot2(exact, values):
    exact = exact.astype(bf16)
    high, low = split(values)
    dot = functools.partial(jnp.dot, preferred_element_type=f32)
    return dot(exact, high) + dot(exact, low)


def fix_kernel(
    peers, own, parents_ref, before_ref, after_ref, flat_ref, edge_phase_ref, spread_ref, *rest
):
    outs, (fixed,) = rest[:peers], rest[peers:]
    pairs = before_ref.shape[0]
    children = pairs // 2
    chunk_rows = outs[0].shape[0]
    share = chunk_rows // (2 * own)
    periods = share * peers // ROWS_PER_PERIOD
    fixed[...] = flat_ref[...]
    left, right = before_ref[...], [after_ref[0], after_ref[1]]
    a, b = TAPS_A, TAPS_B
    even = jnp.concatenate([b[0] * left, a[3] * right[0] + a[4] * right[1]], axis=0)
    odd = jnp.concatenate([a[0] * left, b[3] * right[0] + b[4] * right[1]], axis=0)
    even = dot3(even, spread_ref[0], spread_ref[1])
    odd = dot3(odd, spread_ref[2], spread_ref[3])
    first, last = slice(0, pairs), slice(pairs, 2 * pairs)
    low, high = slice(0, LANES), slice(LANES, 2 * LANES)
    refined = [
        odd[first, high],
        odd[first, low],
        even[first, low],
        even[first, high],
        even[last, low],
        even[last, high] + odd[last, high],
        odd[last, low],
    ]
    shifted_rows = []
    for e, rows in enumerate(refined):
        real, imaginary = rows[:children], rows[children:]
        cosine, sine = edge_phase_ref[e, 0], edge_phase_ref[e, 1]
        shifted_rows.append(real * cosine - imaginary * sine)
        shifted_rows.append(real * sine + imaginary * cosine)
    summed = dot2(one_hot(parents_ref[...], own), jnp.concatenate(shifted_rows, axis=1))
    for e, (w, m) in enumerate(edge_rows(periods)):
        q, row = divmod(ROWS_PER_PERIOD * m + w, share)
        for part in range(2):
            rows = pl.ds(q * chunk_rows + part * share + row, own, stride=2 * share)
            column = (2 * e + part) * LANES
            fixed[rows, :] = fixed[rows, :] + summed[:, column : column + LANES]
    me = lax.axis_index("clus")
    for d in range(peers):
        start = pl.multiple_of((me ^ d) * chunk_rows, 8)
        outs[d][...] = fixed[pl.ds(start, chunk_rows), :]


def widen_kernel(source_ref, offset_ref, count_ref, table_ref, wide_ref, sources_ref, offsets_ref):
    targets, partners = source_ref.shape
    frame = table_ref.shape[1]
    slots = sources_ref.shape[0] // targets

    def some_offsets(i, carry):
        for j in range(4):
            wide_ref[pl.ds(pl.multiple_of((i * 4 + j) * frame, 8), frame), :] = table_ref[i * 4 + j].astype(f32)
        return carry

    whole_steps = table_ref.shape[0] // 4
    lax.fori_loop(0, whole_steps, some_offsets, 0)
    for offset in range(whole_steps * 4, table_ref.shape[0]):
        wide_ref[offset * frame : (offset + 1) * frame, :] = table_ref[offset].astype(f32)

    def one_target(t, carry):
        count = count_ref[t]
        for p in range(slots):
            index = min(p, partners - 1)
            source = jnp.where(p < count, source_ref[t, index], targets)
            sources_ref[t * slots + p] = source * frame
            offsets_ref[t * slots + p] = offset_ref[t, index] * frame
        return carry

    lax.fori_loop(0, targets, one_target, 0)


def translate_kernel(peers, targets, prepare, frame, sources_ref, offsets_ref, count_ref, *rest):
    table = rest[0]
    if prepare:
        chunks, real_twice, imag_twice = rest[1 : peers + 1], rest[peers + 1], rest[peers + 2]
        outs, (sum_real, sum_imag) = rest[peers + 3 : -2], rest[-2:]
    else:
        real_twice, imag_twice = rest[1:3]
        outs, (sum_real, sum_imag) = rest[3:-2], rest[-2:]
    me = lax.axis_index("clus")
    parents = count_ref.shape[0]
    slots = sources_ref.shape[0] // parents
    own = parents // peers
    share = outs[0].shape[0] // (2 * own)
    skip = lax.rem(me * (2 * share), 8)
    if prepare:
        zeros = jnp.zeros((frame, LANES), f32)
        real_twice[parents * frame :, :] = zeros
        imag_twice[parents * frame :, :] = zeros
        for d in range(peers):
            base = (me ^ d) * (own * frame) + skip
            for g in range(own):
                for part, twice in enumerate((real_twice, imag_twice)):
                    rows = chunks[d][(2 * g + part) * share : (2 * g + part + 1) * share, :]
                    twice[pl.ds(base + g * frame, share, stride=2), :] = rows
                    twice[pl.ds(base + g * frame + 1, share, stride=2), :] = rows
    for out, d in zip(outs, targets):
        first = (me ^ d) * own

        def one_target(g, carry):
            target = first + g

            def some_slots(i, sums):
                by_real, by_imag = sums
                for j in range(UNROLL):
                    slot = target * slots + i * UNROLL + j
                    source = pl.ds(pl.multiple_of(sources_ref[slot], 8), frame)
                    operator = table[pl.ds(pl.multiple_of(offsets_ref[slot], 8), frame), :]
                    by_real = by_real + operator * real_twice[source, :]
                    by_imag = by_imag + operator * imag_twice[source, :]
                return by_real, by_imag

            zero = jnp.zeros((frame, LANES), f32)
            steps = (count_ref[target] + (UNROLL - 1)) // UNROLL
            by_real, by_imag = lax.fori_loop(0, steps, some_slots, (zero, zero))
            sum_real[...] = by_real
            sum_imag[...] = by_imag
            even, odd = pl.ds(skip, share, stride=2), pl.ds(skip + 1, share, stride=2)
            row = g * (2 * share)
            out[pl.ds(row, share), :] = sum_real[even, :] - sum_imag[odd, :]
            out[pl.ds(row + share, share), :] = sum_real[odd, :] + sum_imag[even, :]
            return carry

        lax.fori_loop(0, own, one_target, 0)


def edge_kernel(peers, parents_ref, edge_phase_ref, gather_ref, *rest):
    chunks = rest[:peers]
    incoming_ref, next_ref, prev_ref, flat = rest[peers:]
    own2, _, periods, _ = incoming_ref.shape
    own = own2 // 2
    pairs = prev_ref.shape[0]
    flat_rows = ROWS_PER_PERIOD * periods
    share = flat_rows // peers
    me = lax.axis_index("clus")
    for gp in range(own2):
        for d in range(peers):
            flat[pl.ds(gp * flat_rows + (me ^ d) * share, share), :] = chunks[d][gp * share : (gp + 1) * share, :]
    edges = []
    for w, m in edge_rows(periods):
        for part in range(2):
            edges.append(flat[pl.ds(part * flat_rows + ROWS_PER_PERIOD * m + w, own, stride=2 * flat_rows), :])
    per_child = dot2(one_hot(parents_ref[...], own).T, jnp.concatenate(edges, axis=1))
    returned = []
    for e in range(len(edges) // 2):
        real = per_child[:, 2 * e * LANES : (2 * e + 1) * LANES]
        imaginary = per_child[:, (2 * e + 1) * LANES : (2 * e + 2) * LANES]
        cosine, sine = edge_phase_ref[e, 0], edge_phase_ref[e, 1]
        returned.append(
            jnp.concatenate([real * cosine + imaginary * sine, imaginary * cosine - real * sine], axis=0)
        )
    join = functools.partial(jnp.concatenate, axis=1)
    even = jnp.concatenate([join([returned[2], returned[3]]), join([returned[4], returned[5]])], axis=0)
    odd = jnp.concatenate([join([returned[1], returned[0]]), join([returned[6], returned[5]])], axis=0)
    even = dot3(even, gather_ref[0], gather_ref[1])
    odd = dot3(odd, gather_ref[2], gather_ref[3])
    a, b = TAPS_A, TAPS_B
    prev_ref[...] = a[0] * odd[:pairs] + b[0] * even[:pairs]
    next_ref[0] = a[3] * even[pairs:] + b[3] * odd[pairs:]
    next_ref[1] = a[4] * even[pairs:] + b[4] * odd[pairs:]
    for gp in range(own2):
        for w in range(ROWS_PER_PERIOD):
            incoming_ref[gp, w] = flat[pl.ds(gp * flat_rows + w, periods, stride=ROWS_PER_PERIOD), :]


def disaggregate(groups, parents_ref, octants_ref, incoming_ref, phase_ref, gather_ref, out_ref, lhs_e, lhs_o, coarse_e, coarse_o):
    periods = incoming_ref.shape[2]
    azimuth_in = periods * PERIOD_C
    sublane = lax.broadcasted_iota(jnp.int32, (periods, LANES), 0)

    def shift(step, h):
        for k in range(GROUP):
            octant = octants_ref[step * GROUP + k]
            parent = parents_ref[step * GROUP + k]
            for r in range(3):
                parts = ([], [])
                for i in range(3):
                    w = 3 * r + i
                    real, imaginary = incoming_ref[2 * parent, w], incoming_ref[2 * parent + 1, w]
                    cosine, sine = phase_ref[octant, 0, w], phase_ref[octant, 1, w]
                    parts[0].append(real * cosine + imaginary * sine)
                    parts[1].append(imaginary * cosine - real * sine)
                for part in range(2):
                    base = ((2 * k + part) * 3 + r) * periods
                    low, middle, high = parts[part]
                    lhs_e[h, base : base + periods, :LANES] = low
                    lhs_e[h, base : base + periods, LANES:] = middle
                    lhs_o[h, base : base + periods, :LANES] = high
                    lhs_o[h, base : base + periods, LANES:] = middle

    def polar(h):
        coarse_e[h] = dot3(lhs_e[h], gather_ref[0], gather_ref[1])
        coarse_o[h] = dot3(lhs_o[h], gather_ref[2], gather_ref[3])

    def azimuth(step, h):
        for kp in range(2 * GROUP):
            c = []
            for r in range(3):
                base = (kp * 3 + r) * periods
                c.append(coarse_e[h, base : base + periods, :])
                c.append(coarse_o[h, base : base + periods, :])
            a, b = TAPS_A, TAPS_B
            to_left = a[0] * c[1] + b[0] * c[2]
            to_right = [a[3] * c[4] + b[3] * c[5], a[4] * c[4] + b[4] * c[5]]
            down = [jnp.where(sublane == 0, 0.0, pltpu.roll(v, 1, 0)) for v in to_right]
            up = jnp.where(sublane == periods - 1, 0.0, pltpu.roll(to_left, periods - 1, 0))
            rows = [
                c[0] + a[1] * c[1] + b[1] * c[2] + down[0],
                a[2] * c[1] + b[2] * c[2] + a[0] * c[4] + b[0] * c[5] + down[1],
                c[3] + a[3] * c[1] + b[3] * c[2] + a[1] * c[4] + b[1] * c[5],
                a[4] * c[1] + b[4] * c[2] + a[2] * c[4] + b[2] * c[5] + up,
            ]
            start = pl.multiple_of((step * (2 * GROUP) + kp) * azimuth_in, 8)
            for u in range(PERIOD_C):
                out_ref[pl.ds(start + u, periods, stride=PERIOD_C), :] = rows[u]

    def some_groups(i, carry):
        for h in range(PAIR):
            shift(i * PAIR + h, h)
            polar(h)
        for h in range(PAIR):
            azimuth(i * PAIR + h, h)
        return carry

    lax.fori_loop(groups[0] // PAIR, groups[1] // PAIR, some_groups, 0)


def add_edges(children, pairs, azimuth_in, before_ref, after_ref, out_ref):
    for part in range(2):
        for k in range(*children, 8):
            source = slice(part * (pairs // 2) + k, part * (pairs // 2) + k + 8)
            for row, values in ((0, before_ref[0, source]), (1, before_ref[1, source]), (azimuth_in - 1, after_ref[source])):
                target = pl.ds((2 * k + part) * azimuth_in + row, 8, stride=2 * azimuth_in)
                out_ref[target, :] = out_ref[target, :] + values


def finish_kernel(groups, parents_ref, octants_ref, incoming_ref, phase_ref, gather_ref, *rest):
    part_ref, before_ref, after_ref, out_ref, whole_out, lhs_e, lhs_o, coarse_e, coarse_o, sems = rest
    pairs = after_ref.shape[0]
    azimuth_in = out_ref.shape[0] // pairs
    done = part_ref.shape[0]
    whole_out[:done, :] = part_ref[...]
    add_edges((0, groups[0] * GROUP), pairs, azimuth_in, before_ref, after_ref, whole_out)
    first = pltpu.make_async_copy(whole_out.at[pl.ds(0, done)], out_ref.at[pl.ds(0, done)], sems.at[0])
    first.start()
    disaggregate(
        groups, parents_ref, octants_ref, incoming_ref, phase_ref, gather_ref, whole_out, lhs_e, lhs_o, coarse_e, coarse_o
    )
    add_edges((groups[0] * GROUP, pairs // 2), pairs, azimuth_in, before_ref, after_ref, whole_out)
    rest_rows = pl.ds(done, out_ref.shape[0] - done)
    second = pltpu.make_async_copy(whole_out.at[rest_rows], out_ref.at[rest_rows], sems.at[1])
    second.start()
    first.wait()
    second.wait()


def shifted(values, axis, by):
    size = lax.axis_size(axis)
    return lax.ppermute(values, axis, [(i, (i + by) % size) for i in range(size)])


def exchanged(values, axis, mask):
    size = lax.axis_size(axis)
    return lax.ppermute(values, axis, [(i, i ^ mask) for i in range(size)])


ROWS_GRANT = 50
MAIN_GRANT = 46

SMEM = pl.BlockSpec(memory_space=pltpu.SMEM)
VMEM = pl.BlockSpec(memory_space=pltpu.VMEM)
HBM = pl.BlockSpec(memory_space=pltpu.HBM)


def local_call(kernel, out_shape, in_specs, scratch, grant, flops=1_000_000, bytes_accessed=1_000_000, out_specs=None):
    return pl.pallas_call(
        kernel,
        out_shape=out_shape,
        in_specs=in_specs,
        out_specs=jax.tree.map(lambda _: VMEM, out_shape) if out_specs is None else out_specs,
        scratch_shapes=scratch,
        compiler_params=pltpu.CompilerParams(vmem_limit_bytes=grant << 20),
        cost_estimate=pl.CostEstimate(flops=flops, bytes_accessed=bytes_accessed, transcendentals=0),
    )


def on_device_exchange(
    child_patterns, trans_table, child_parent, child_octant, partner_src, partner_off, partner_count
):
    children, _, azimuth_in, polar_in = child_patterns.shape
    pairs = 2 * children
    peers = lax.axis_size("clus")
    parent_total, _ = partner_src.shape
    own = parent_total // peers
    periods = azimuth_in // PERIOD_C
    flat_rows = ROWS_PER_PERIOD * periods
    share = flat_rows // peers
    offsets = trans_table.shape[0]
    array = lambda *shape: jax.ShapeDtypeStruct(shape, f32)
    buffer = lambda *shape: pltpu.VMEM(shape, f32)
    parents = child_parent[0]

    edges = len(edge_rows(periods))
    held, last, first, phases, edge_phases = local_call(
        rows_kernel,
        [
            array(pairs, azimuth_in, polar_in),
            array(pairs, polar_in),
            array(2, pairs, polar_in),
            array(8, 2, ROWS_PER_PERIOD, periods, LANES),
            array(edges, 2, children, LANES),
        ],
        [SMEM, HBM],
        [pltpu.SemaphoreType.DMA],
        ROWS_GRANT,
    )(child_octant, child_patterns.reshape(pairs, azimuth_in, polar_in))
    before = shifted(last, "dir", 1)
    after = shifted(first, "dir", -1)

    even, odd = polar_blocks()
    spread = np.stack([*split_np(even), *split_np(odd)])
    gather = np.stack([*split_np(even.T), *split_np(odd.T)])

    frame = max(-(-((q * 2 * share) % 8 + 2 * share) // 8) * 8 for q in range(peers))
    view = trans_table.reshape(offsets, 2, flat_rows, LANES).transpose(0, 2, 1, 3).reshape(offsets, 2 * flat_rows, LANES)
    rows = 2 * GROUP * 3 * periods
    flat, table = local_call(
        functools.partial(main_kernel, peers),
        [array(2 * own * flat_rows, LANES), jax.ShapeDtypeStruct((offsets, frame, LANES), bf16)],
        [SMEM] * 2 + [VMEM, HBM, VMEM, VMEM],
        [
            buffer(PAIR, rows, LANES),
            buffer(PAIR, rows, LANES),
            buffer(PAIR, rows, 2 * LANES),
            buffer(PAIR, rows, 2 * LANES),
            buffer(own, 2, ROWS_PER_PERIOD, periods, LANES),
            buffer(2 * own * flat_rows, LANES),
            pltpu.SemaphoreType.DMA,
        ],
        MAIN_GRANT,
        flops=4_000_000_000,
        bytes_accessed=12_000_000,
    )(parents, child_octant, held.reshape(pairs * azimuth_in, polar_in), view, phases, spread)

    chunk = array(2 * own * share, LANES)
    sent = local_call(
        functools.partial(fix_kernel, peers, own), [chunk] * peers, [VMEM] * 6, [buffer(2 * own * flat_rows, LANES)], 8
    )(child_parent, before, after, flat, edge_phases, spread)

    masks = sorted(range(1, peers), key=lambda d: -bin(d).count("1"))
    received = {0: sent[0]}
    for d in masks:
        received[d] = exchanged(sent[d], "clus", d)

    slots = -(-partner_src.shape[1] // UNROLL) * UNROLL
    listed = jax.ShapeDtypeStruct((parent_total * slots,), jnp.int32)
    wide, sources, slot_offsets = local_call(
        widen_kernel,
        [array(offsets * frame, LANES), listed, listed],
        [SMEM] * 3 + [VMEM],
        [],
        20,
        flops=50_000_000,
        bytes_accessed=8_000_000,
        out_specs=[VMEM, SMEM, SMEM],
    )(partner_src, partner_off, partner_count, table)

    twice = array((parent_total + 1) * frame, LANES)
    sums = [buffer(frame, LANES)] * 2
    lists = (sources, slot_offsets, partner_count)
    back = {}
    real_twice = imag_twice = None
    for targets in (masks[:1], masks[1:], [0]):
        prepare = real_twice is None
        call = local_call(
            functools.partial(translate_kernel, peers, tuple(targets), prepare, frame),
            ([twice] * 2 if prepare else []) + [chunk] * len(targets),
            [SMEM] * 3 + [VMEM] * (1 + peers if prepare else 3),
            sums,
            20,
            flops=20_000_000 * len(targets),
            bytes_accessed=4_000_000 * len(targets),
        )
        if prepare:
            real_twice, imag_twice, *results = call(*lists, wide, *[received[d] for d in range(peers)])
        else:
            results = call(*lists, wide, real_twice, imag_twice)
        for d, result in zip(targets, results):
            back[d] = exchanged(result, "clus", d) if d else result

    incoming, to_next, to_prev = local_call(
        functools.partial(edge_kernel, peers),
        [array(2 * own, ROWS_PER_PERIOD, periods, LANES), array(2, pairs, polar_in), array(pairs, polar_in)],
        [VMEM] * (3 + peers),
        [buffer(2 * own * flat_rows, LANES)],
        8,
    )(child_parent, edge_phases, gather, *[back[d] for d in range(peers)])

    from_before = shifted(to_next, "dir", 1)
    from_after = shifted(to_prev, "dir", -1)

    split_at = children // GROUP - PAIR
    work = [
        buffer(PAIR, rows, 2 * LANES),
        buffer(PAIR, rows, 2 * LANES),
        buffer(PAIR, rows, LANES),
        buffer(PAIR, rows, LANES),
    ]
    operands = (parents, child_octant, incoming, phases, gather)
    partial_out = local_call(
        functools.partial(disaggregate, (0, split_at)),
        array(split_at * 2 * GROUP * azimuth_in, polar_in),
        [SMEM] * 2 + [VMEM] * 3,
        work,
        12,
        flops=4_000_000_000,
        bytes_accessed=12_000_000,
    )(*operands)

    out = local_call(
        functools.partial(finish_kernel, (split_at, children // GROUP)),
        array(pairs * azimuth_in, polar_in),
        [SMEM] * 2 + [VMEM] * 6,
        [buffer(pairs * azimuth_in, polar_in)] + work + [pltpu.SemaphoreType.DMA((2,))],
        16,
        out_specs=HBM,
    )(*operands, partial_out, from_before, from_after)
    return out.reshape(child_patterns.shape)


def with_halo(shard, sides, width):
    for axis, dim in sides:
        size, length = (lax.axis_size(axis), shard.shape[dim])
        up = [(i, (i + 1) % size) for i in range(size)]
        down = [(j, i) for i, j in up]
        last = lax.slice_in_dim(shard, length - width, length, axis=dim)
        initial = lax.slice_in_dim(shard, 0, width, axis=dim)
        before = lax.ppermute(last, axis, up)
        after = lax.ppermute(initial, axis, down)
        shard = jnp.concatenate([before, shard, after], axis=dim)
    return shard


def lagrange_rows(offset):
    weights = []
    for anchor in range(5):
        factor = jnp.ones_like(offset)
        for neighbour in range(5):
            if neighbour != anchor:
                factor = factor * (offset - neighbour) / (anchor - neighbour)
        weights.append(factor)
    return weights


def polar_matrix_of(rows_out, rows_in):
    target = (jnp.arange(rows_out, dtype=jnp.float32) + 0.5) * rows_in / rows_out - 0.5
    start_row = jnp.clip(jnp.floor(target + 0.5).astype(jnp.int32) - 2, 0, rows_in - 5)
    weights = lagrange_rows(target - start_row.astype(jnp.float32))
    columns = jnp.arange(rows_in, dtype=jnp.int32)
    matrix = jnp.zeros((rows_out, rows_in), jnp.float32)
    for anchor in range(5):
        matrix = matrix + jnp.where(
            columns[None, :] == (start_row + anchor)[:, None], weights[anchor][:, None], 0.0
        )
    return matrix


def azimuth_matrix_of(out_index, in_index, total_out, total_in):
    target = (out_index * total_in).astype(jnp.float32) / total_out
    nearest = jnp.floor(target + 0.5).astype(jnp.int32)
    weights = lagrange_rows(target - nearest.astype(jnp.float32) + 2.0)
    matrix = jnp.zeros((out_index.shape[0], in_index.shape[0]), jnp.float32)
    for anchor in range(5):
        columns = nearest + anchor - 2
        matrix = matrix + jnp.where(
            in_index[None, :] == columns[:, None], weights[anchor][:, None], 0.0
        )
    return matrix


def shift_phases(octant, azimuth_index, azimuth_total, polar_total):
    azimuth = 2.0 * math.pi * azimuth_index.astype(jnp.float32) / azimuth_total
    polar = math.pi * (jnp.arange(polar_total, dtype=jnp.float32) + 0.5) / polar_total
    first_axis = jnp.sin(polar)[None, :] * jnp.cos(azimuth)[:, None]
    second_axis = jnp.sin(polar)[None, :] * jnp.sin(azimuth)[:, None]
    third_axis = jnp.cos(polar)[None, :] * jnp.ones_like(azimuth)[:, None]
    first_sign = (1 - 2 * (octant % 2)).astype(jnp.float32)
    second_sign = (1 - 2 * (octant // 2 % 2)).astype(jnp.float32)
    third_sign = (1 - 2 * (octant // 4)).astype(jnp.float32)
    phase_angle = phase_scale * (
        first_sign[:, None, None] * first_axis[None]
        + second_sign[:, None, None] * second_axis[None]
        + third_sign[:, None, None] * third_axis[None]
    )
    return (jnp.cos(phase_angle), jnp.sin(phase_angle))


def translate(sources, table, partner_src, partner_off, partner_count):
    live_mask = (
        jnp.arange(partner_src.shape[1], dtype=jnp.int32)[None, :] < partner_count[:, None]
    ).astype(jnp.float32)
    picked = sources[partner_src]
    operator = table[partner_off].astype(jnp.float32) * live_mask[:, :, None, None]
    real_part = jnp.sum(
        operator[:, :, 0] * picked[:, :, 0] - operator[:, :, 1] * picked[:, :, 1], axis=1
    )
    imaginary = jnp.sum(
        operator[:, :, 0] * picked[:, :, 1] + operator[:, :, 1] * picked[:, :, 0], axis=1
    )
    return jnp.stack([real_part, imaginary], axis=1)


def forward_shift(patterns, cosine, sine_part):
    real_part = patterns[:, 0] * cosine - patterns[:, 1] * sine_part
    imaginary = patterns[:, 0] * sine_part + patterns[:, 1] * cosine
    return jnp.stack([real_part, imaginary], axis=1)


def conjugate_shift(patterns, cosine, sine_part):
    real_part = patterns[:, 0] * cosine + patterns[:, 1] * sine_part
    imaginary = patterns[:, 1] * cosine - patterns[:, 0] * sine_part
    return jnp.stack([real_part, imaginary], axis=1)


def on_device_gather(
    child_patterns, trans_table, child_parent, child_octant, partner_src, partner_off, partner_count
):
    _, _, azimuth_in, _ = child_patterns.shape
    polar_out = NTHETA_P
    azimuth_out = trans_table.shape[2] // polar_out
    parent_slots = partner_src.shape[0] // lax.axis_size("clus")
    cluster_index = lax.axis_index("clus")
    direction_index = lax.axis_index("dir")
    parents = child_parent[0]
    polar_matrix = polar_matrix_of(NTHETA_P, NTHETA_C)
    onehot = (parents[None, :] == jnp.arange(parent_slots, dtype=jnp.int32)[:, None]).astype(
        jnp.float32
    )
    own_rows = jnp.mod(
        direction_index * azimuth_out + jnp.arange(azimuth_out, dtype=jnp.int32), NPHI_P
    )
    cosine, sine_part = shift_phases(child_octant, own_rows, NPHI_P, polar_out)
    extended = with_halo(child_patterns, (("dir", 2),), 2)
    gather_matrix = azimuth_matrix_of(
        jnp.arange(azimuth_out, dtype=jnp.int32),
        jnp.arange(azimuth_in + 4, dtype=jnp.int32) - 2,
        NPHI_P,
        NPHI_C,
    )
    along_azimuth = jnp.einsum("pc,kacz->kapz", gather_matrix, extended, precision=highest)
    refined = jnp.einsum("kapz,tz->kapt", along_azimuth, polar_matrix, precision=highest)
    shifted = forward_shift(refined, cosine, sine_part)
    radiation = jnp.einsum("gk,kapt->gapt", onehot, shifted, precision=highest)
    flattened = radiation.reshape(parent_slots, 2, azimuth_out * polar_out)
    sources = lax.all_gather(flattened, "clus", axis=0, tiled=True)
    first_row = cluster_index * parent_slots
    own_src = lax.dynamic_slice_in_dim(partner_src, first_row, parent_slots, 0)
    own_off = lax.dynamic_slice_in_dim(partner_off, first_row, parent_slots, 0)
    own_count = lax.dynamic_slice_in_dim(partner_count, first_row, parent_slots, 0)
    incoming = translate(sources, trans_table, own_src, own_off, own_count)
    incoming = incoming.reshape(parent_slots, 2, azimuth_out, polar_out)
    return_matrix = azimuth_matrix_of(
        jnp.arange(azimuth_out + 6, dtype=jnp.int32) - 3,
        jnp.arange(azimuth_in, dtype=jnp.int32),
        NPHI_P,
        NPHI_C,
    )
    per_child = jnp.einsum("gk,gapt->kapt", onehot, incoming, precision=highest)
    returned = conjugate_shift(per_child, cosine, sine_part)
    coarse_own = jnp.einsum("kapt,tz->kapz", returned, polar_matrix, precision=highest)
    coarse = with_halo(coarse_own, (("dir", 2),), 3)
    return jnp.einsum("pc,kapz->kacz", return_matrix, coarse, precision=highest)


def solution(mesh):
    def on_device(child_patterns, trans_table, *rest):
        peers = lax.axis_size("clus")
        children, _, azimuth_in, polar_in = child_patterns.shape
        flat_rows = trans_table.shape[2] // LANES
        fits = (
            azimuth_in % (8 * PERIOD_C) == 0
            and polar_in == LANES
            and flat_rows * PERIOD_C == ROWS_PER_PERIOD * azimuth_in
            and flat_rows % peers == 0
            and peers & (peers - 1) == 0
            and children % (PAIR * GROUP) == 0
            and children > PAIR * GROUP
        )
        plan = on_device_exchange if fits else on_device_gather
        return plan(child_patterns, trans_table, *rest)

    return jax.shard_map(
        on_device,
        mesh=mesh,
        in_specs=(
            P("clus", None, "dir", None),
            P(None, None, "dir"),
            P("clus", None),
            P("clus"),
            P(),
            P(),
            P(),
        ),
        out_specs=P("clus", None, "dir", None),
        check_vma=False,
    )
```

```python
import functools
import math

import jax
import jax.numpy as jnp
import numpy as np
from jax import lax
from jax.experimental import pallas as pl
from jax.experimental.pallas import tpu as pltpu
from jax.sharding import PartitionSpec as P


NTHETA_C = 128
NPHI_C = 256
NTHETA_P = 192
NPHI_P = 384

LANES = 128
PERIOD_P = 6
PERIOD_C = 4
ROWS_PER_PERIOD = PERIOD_P * NTHETA_P // LANES
GROUP = 8
TILE = 8
UNROLL = 8
BLOCK = 2 * GROUP

phase_scale = 8.0 * math.pi
highest = lax.Precision.HIGHEST
f32 = jnp.float32
bf16 = jnp.bfloat16


def lagrange(offset):
    weights = []
    for anchor in range(5):
        factor = 1.0
        for neighbour in range(5):
            if neighbour != anchor:
                factor = factor * (offset - neighbour) / (anchor - neighbour)
        weights.append(factor)
    return weights


TAPS_A = [float(w) for w in lagrange(5.0 / 3.0)]
TAPS_B = [float(w) for w in lagrange(7.0 / 3.0)]


SUMS = [(TAPS_A[i] + TAPS_A[4 - i]) / 2 for i in range(2)]
DIFFS = [(TAPS_A[i] - TAPS_A[4 - i]) / 2 for i in range(2)]
CENTRE = TAPS_A[2]


def polar_matrix_np():
    target = (np.arange(NTHETA_P, dtype=np.float32) + np.float32(0.5)) * NTHETA_C / NTHETA_P - np.float32(0.5)
    start = np.clip(np.floor(target + 0.5).astype(np.int32) - 2, 0, NTHETA_C - 5)
    weights = lagrange((target - start).astype(np.float64))
    matrix = np.zeros((NTHETA_P, NTHETA_C), np.float64)
    for anchor in range(5):
        matrix[np.arange(NTHETA_P), start + anchor] += weights[anchor]
    return matrix.astype(np.float32)


def polar_blocks():
    matrix = polar_matrix_np().T
    even = np.zeros((NTHETA_C, 2 * LANES), np.float32)
    odd = np.zeros((NTHETA_C, 2 * LANES), np.float32)
    half = NTHETA_P - LANES
    even[:, :NTHETA_P] = matrix
    odd[:, :LANES] = matrix[:, half:]
    odd[:, 2 * LANES - half :] = matrix[:, :half]
    return even, odd


def split_np(matrix):
    high = matrix.astype(bf16)
    low = (matrix - high.astype(np.float32)).astype(bf16)
    return high, low


def split(values):
    high = values.astype(bf16)
    low = (values - high.astype(f32)).astype(bf16)
    return high, low


def dot3(values, high_matrix, low_matrix):
    high, low = split(values)
    dot = functools.partial(jnp.dot, preferred_element_type=f32)
    return dot(high, high_matrix) + dot(low, high_matrix) + dot(high, low_matrix)


SIN_COEFFS = [(-1) ** k * math.pi ** (2 * k + 1) / math.factorial(2 * k + 1) for k in range(7)]
COS_COEFFS = [(-1) ** k * math.pi ** (2 * k) / math.factorial(2 * k) for k in range(7)]


def sincos_turns(turns):
    rest = turns - jnp.round(turns)
    square = rest * rest
    sine = jnp.full_like(square, SIN_COEFFS[-1])
    for coeff in SIN_COEFFS[-2::-1]:
        sine = sine * square + coeff
    sine = sine * rest
    cosine = jnp.full_like(square, COS_COEFFS[-1])
    for coeff in COS_COEFFS[-2::-1]:
        cosine = cosine * square + coeff
    return 2.0 * sine * cosine, 1.0 - 2.0 * sine * sine


def fill_phases(direction, out_ref):
    periods = out_ref.shape[3]
    lane = lax.broadcasted_iota(jnp.int32, (periods, LANES), 1)
    period = lax.broadcasted_iota(jnp.int32, (periods, LANES), 0)
    first = direction * (PERIOD_P * periods)
    for w in range(ROWS_PER_PERIOD):
        position = lane + w * LANES
        row = w * LANES // NTHETA_P
        row = jnp.where(position >= (row + 1) * NTHETA_P, row + 1, row)
        polar_index = position - row * NTHETA_P
        azimuth_index = first + period * PERIOD_P + row
        sin_polar, cos_polar = sincos_turns((polar_index.astype(f32) + 0.5) / (2 * NTHETA_P))
        sin_azimuth, cos_azimuth = sincos_turns(azimuth_index.astype(f32) / NPHI_P)
        along_x = 4.0 * sin_polar * cos_azimuth
        along_y = 4.0 * sin_polar * sin_azimuth
        along_z = 4.0 * cos_polar
        for octant in (0, 2, 4, 6):
            turns = along_x + along_y if octant % 4 == 0 else along_x - along_y
            turns = turns + along_z if octant < 4 else turns - along_z
            sine, cosine = sincos_turns(turns)
            out_ref[octant, 0, w] = cosine
            out_ref[octant, 1, w] = sine
            out_ref[7 - octant, 0, w] = cosine
            out_ref[7 - octant, 1, w] = -sine


def edge_rows(periods):
    return [(w, 0) for w in (1, 2, 3, 4)] + [(w, periods - 1) for w in (6, 7, 8)]


def rows_kernel(octants_ref, x_ref, blocks_ref, held_ref, last_ref, first_ref, phase_ref, edge_phase_ref, blocks_out, sem, blocks_sem):
    pairs, azimuth_in, _ = x_ref.shape
    periods = phase_ref.shape[3]
    copy = pltpu.make_async_copy(x_ref, held_ref, sem)
    copy.start()
    blocks_copy = pltpu.make_async_copy(blocks_ref, blocks_out, blocks_sem)
    blocks_copy.start()
    fill_phases(lax.axis_index("dir"), phase_ref)

    def edges_of(step, carry):
        for j in range(GROUP):
            k = step * GROUP + j
            octant = octants_ref[k]
            for e, (w, m) in enumerate(edge_rows(periods)):
                for i in range(2):
                    edge_phase_ref[e, i, pl.ds(k, 1), :] = phase_ref[octant, i, w, m : m + 1, :]
        return carry

    lax.fori_loop(0, pairs // 2 // GROUP, edges_of, 0)
    copy.wait()
    for part in range(2):
        source = pl.ds(part, pairs // 2, stride=2)
        target = slice(part * (pairs // 2), (part + 1) * (pairs // 2))
        last_ref[target] = held_ref[source, azimuth_in - 1, :]
        for i in range(2):
            first_ref[i, target] = held_ref[source, i, :]
    blocks_copy.wait()


def both_taps(rows):
    even = SUMS[0] * (rows[0] + rows[4]) + SUMS[1] * (rows[1] + rows[3]) + CENTRE * rows[2]
    odd = DIFFS[0] * (rows[0] - rows[4]) + DIFFS[1] * (rows[1] - rows[3])
    return even + odd, even - odd


def both_taps_transposed(first, second):
    total, difference = first + second, first - second
    outer = [SUMS[i] * total for i in range(2)]
    inner = [DIFFS[i] * difference for i in range(2)]
    return [outer[0] + inner[0], outer[1] + inner[1], CENTRE * total, outer[1] - inner[1], outer[0] - inner[0]]


def in_stages(blocks, before, product, after):
    for i in range(blocks + 1):
        if i < blocks:
            before(i)
            product(i)
        if i > 0:
            after(i - 1)


def main_kernel(peers, parents_ref, octants_ref, x_ref, table_ref, phase_ref, spread_ref, *rest):
    flat_ref, slice_ref, az_e, az_o, res_e, res_o, acc, flat, table_sem = rest
    periods = phase_ref.shape[3]
    azimuth_in = periods * PERIOD_C
    own = acc.shape[0]
    me = lax.axis_index("clus")
    share = ROWS_PER_PERIOD * periods // peers
    first_tile = me * (2 * share) // 8
    table_rows = pl.ds(pl.multiple_of(first_tile * 8, 8), slice_ref.shape[1])
    table_copy = pltpu.make_async_copy(table_ref.at[:, table_rows, :], slice_ref, table_sem)
    table_copy.start()
    acc[...] = jnp.zeros_like(acc)
    sublane = lax.broadcasted_iota(jnp.int32, (periods, LANES), 0)

    def azimuth(block):
        for kp in range(2 * BLOCK):
            start = (block * (2 * BLOCK) + kp) * azimuth_in
            x = [x_ref[pl.ds(start + u, periods, stride=PERIOD_C), :] for u in range(PERIOD_C)]
            left = jnp.where(sublane == 0, 0.0, pltpu.roll(x[3], 1, 0))
            right = [jnp.where(sublane == periods - 1, 0.0, pltpu.roll(x[i], periods - 1, 0)) for i in range(2)]
            lower = [left, x[0], x[1], x[2], x[3]]
            upper = [x[1], x[2], x[3], right[0], right[1]]
            rows = [x[0], *both_taps(lower), x[2], *both_taps(upper)]
            for r in range(3):
                base = (kp * 3 + r) * periods
                az_e[block, base : base + periods, :] = rows[2 * r]
                az_o[block, base : base + periods, :] = rows[2 * r + 1]

    def polar(block):
        res_e[block] = dot3(az_e[block], spread_ref[0], spread_ref[1])
        res_o[block] = dot3(az_o[block], spread_ref[2], spread_ref[3])

    def shift(block):
        for k in range(BLOCK):
            octant = octants_ref[block * BLOCK + k]
            parent = parents_ref[block * BLOCK + k]
            for r in range(3):
                parts = []
                for part in range(2):
                    rows = pl.ds(((2 * k + part) * 3 + r) * periods, periods)
                    middle = res_e[block, rows, LANES:] + res_o[block, rows, LANES:]
                    parts.append((res_e[block, rows, :LANES], middle, res_o[block, rows, :LANES]))
                for i in range(3):
                    w = 3 * r + i
                    real, imaginary = parts[0][i], parts[1][i]
                    cosine, sine = phase_ref[octant, 0, w], phase_ref[octant, 1, w]
                    acc[parent, 0, w] += real * cosine - imaginary * sine
                    acc[parent, 1, w] += real * sine + imaginary * cosine

    in_stages(az_e.shape[0], azimuth, polar, shift)
    for gp in range(2 * own):
        for w in range(ROWS_PER_PERIOD):
            flat[pl.ds(gp * ROWS_PER_PERIOD * periods + w, periods, stride=ROWS_PER_PERIOD), :] = acc[gp // 2, gp % 2, w]
        for q in range(peers):
            source = gp * ROWS_PER_PERIOD * periods + q * share
            target = (q * 2 * own + gp) * share
            flat_ref[target : target + share, :] = flat[source : source + share, :]
    table_copy.wait()


def one_hot(parents, own):
    index = lax.broadcasted_iota(jnp.int32, (own, parents.shape[1]), 0)
    return (index == parents).astype(f32)


def dot2(exact, values):
    exact = exact.astype(bf16)
    high, low = split(values)
    dot = functools.partial(jnp.dot, preferred_element_type=f32)
    return dot(exact, high) + dot(exact, low)


def fix_kernel(
    peers, own, parents_ref, before_ref, after_ref, flat_ref, edge_phase_ref, spread_ref, *rest
):
    outs, (fixed,) = rest[:peers], rest[peers:]
    pairs = before_ref.shape[0]
    children = pairs // 2
    chunk_rows = outs[0].shape[0]
    share = chunk_rows // (2 * own)
    periods = share * peers // ROWS_PER_PERIOD
    fixed[...] = flat_ref[...]
    left, right = before_ref[...], [after_ref[0], after_ref[1]]
    a, b = TAPS_A, TAPS_B
    even = jnp.concatenate([b[0] * left, a[3] * right[0] + a[4] * right[1]], axis=0)
    odd = jnp.concatenate([a[0] * left, b[3] * right[0] + b[4] * right[1]], axis=0)
    even = dot3(even, spread_ref[0], spread_ref[1])
    odd = dot3(odd, spread_ref[2], spread_ref[3])
    first, last = slice(0, pairs), slice(pairs, 2 * pairs)
    low, high = slice(0, LANES), slice(LANES, 2 * LANES)
    refined = [
        odd[first, high],
        odd[first, low],
        even[first, low],
        even[first, high],
        even[last, low],
        even[last, high] + odd[last, high],
        odd[last, low],
    ]
    shifted_rows = []
    for e, rows in enumerate(refined):
        real, imaginary = rows[:children], rows[children:]
        cosine, sine = edge_phase_ref[e, 0], edge_phase_ref[e, 1]
        shifted_rows.append(real * cosine - imaginary * sine)
        shifted_rows.append(real * sine + imaginary * cosine)
    summed = dot2(one_hot(parents_ref[...], own), jnp.concatenate(shifted_rows, axis=1))
    for e, (w, m) in enumerate(edge_rows(periods)):
        q, row = divmod(ROWS_PER_PERIOD * m + w, share)
        for part in range(2):
            rows = pl.ds(q * chunk_rows + part * share + row, own, stride=2 * share)
            column = (2 * e + part) * LANES
            fixed[rows, :] = fixed[rows, :] + summed[:, column : column + LANES]
    me = lax.axis_index("clus")
    for d in range(peers):
        start = pl.multiple_of((me ^ d) * chunk_rows, 8)
        outs[d][...] = fixed[pl.ds(start, chunk_rows), :]


def widen_kernel(source_ref, offset_ref, count_ref, table_ref, wide_ref, sources_ref, offsets_ref):
    targets, partners = source_ref.shape
    frame = table_ref.shape[1]
    slots = sources_ref.shape[0] // targets

    def some_offsets(i, carry):
        for j in range(4):
            wide_ref[pl.ds(pl.multiple_of((i * 4 + j) * frame, 8), frame), :] = table_ref[i * 4 + j].astype(f32)
        return carry

    whole_steps = table_ref.shape[0] // 4
    lax.fori_loop(0, whole_steps, some_offsets, 0)
    for offset in range(whole_steps * 4, table_ref.shape[0]):
        wide_ref[offset * frame : (offset + 1) * frame, :] = table_ref[offset].astype(f32)

    def one_target(t, carry):
        count = count_ref[t]
        for p in range(slots):
            index = min(p, partners - 1)
            source = jnp.where(p < count, source_ref[t, index], targets)
            sources_ref[t * slots + p] = source * frame
            offsets_ref[t * slots + p] = offset_ref[t, index] * frame
        return carry

    lax.fori_loop(0, targets, one_target, 0)


def translate_kernel(peers, targets, prepare, frame, sources_ref, offsets_ref, count_ref, *rest):
    table = rest[0]
    if prepare:
        chunks, real_twice, imag_twice = rest[1 : peers + 1], rest[peers + 1], rest[peers + 2]
        outs, (sum_real, sum_imag) = rest[peers + 3 : -2], rest[-2:]
    else:
        real_twice, imag_twice = rest[1:3]
        outs, (sum_real, sum_imag) = rest[3:-2], rest[-2:]
    me = lax.axis_index("clus")
    parents = count_ref.shape[0]
    slots = sources_ref.shape[0] // parents
    own = parents // peers
    share = outs[0].shape[0] // (2 * own)
    skip = lax.rem(me * (2 * share), 8)
    if prepare:
        zeros = jnp.zeros((frame, LANES), f32)
        real_twice[parents * frame :, :] = zeros
        imag_twice[parents * frame :, :] = zeros
        for d in range(peers):
            base = (me ^ d) * (own * frame) + skip
            for g in range(own):
                for part, twice in enumerate((real_twice, imag_twice)):
                    rows = chunks[d][(2 * g + part) * share : (2 * g + part + 1) * share, :]
                    twice[pl.ds(base + g * frame, share, stride=2), :] = rows
                    twice[pl.ds(base + g * frame + 1, share, stride=2), :] = rows
    for out, d in zip(outs, targets):
        first = (me ^ d) * own

        def one_target(g, carry):
            target = first + g

            def some_slots(i, sums):
                by_real, by_imag = sums
                for j in range(UNROLL):
                    slot = target * slots + i * UNROLL + j
                    source = pl.ds(pl.multiple_of(sources_ref[slot], 8), frame)
                    operator = table[pl.ds(pl.multiple_of(offsets_ref[slot], 8), frame), :]
                    by_real = by_real + operator * real_twice[source, :]
                    by_imag = by_imag + operator * imag_twice[source, :]
                return by_real, by_imag

            zero = jnp.zeros((frame, LANES), f32)
            steps = (count_ref[target] + (UNROLL - 1)) // UNROLL
            by_real, by_imag = lax.fori_loop(0, steps, some_slots, (zero, zero))
            sum_real[...] = by_real
            sum_imag[...] = by_imag
            even, odd = pl.ds(skip, share, stride=2), pl.ds(skip + 1, share, stride=2)
            row = g * (2 * share)
            out[pl.ds(row, share), :] = sum_real[even, :] - sum_imag[odd, :]
            out[pl.ds(row + share, share), :] = sum_real[odd, :] + sum_imag[even, :]
            return carry

        lax.fori_loop(0, own, one_target, 0)


def edge_kernel(peers, parents_ref, edge_phase_ref, gather_ref, *rest):
    chunks = rest[:peers]
    incoming_ref, next_ref, prev_ref, flat = rest[peers:]
    own2, _, periods, _ = incoming_ref.shape
    own = own2 // 2
    pairs = prev_ref.shape[0]
    flat_rows = ROWS_PER_PERIOD * periods
    share = flat_rows // peers
    me = lax.axis_index("clus")
    for gp in range(own2):
        for d in range(peers):
            flat[pl.ds(gp * flat_rows + (me ^ d) * share, share), :] = chunks[d][gp * share : (gp + 1) * share, :]
    edges = []
    for w, m in edge_rows(periods):
        for part in range(2):
            edges.append(flat[pl.ds(part * flat_rows + ROWS_PER_PERIOD * m + w, own, stride=2 * flat_rows), :])
    per_child = dot2(one_hot(parents_ref[...], own).T, jnp.concatenate(edges, axis=1))
    returned = []
    for e in range(len(edges) // 2):
        real = per_child[:, 2 * e * LANES : (2 * e + 1) * LANES]
        imaginary = per_child[:, (2 * e + 1) * LANES : (2 * e + 2) * LANES]
        cosine, sine = edge_phase_ref[e, 0], edge_phase_ref[e, 1]
        returned.append(
            jnp.concatenate([real * cosine + imaginary * sine, imaginary * cosine - real * sine], axis=0)
        )
    join = functools.partial(jnp.concatenate, axis=1)
    even = jnp.concatenate([join([returned[2], returned[3]]), join([returned[4], returned[5]])], axis=0)
    odd = jnp.concatenate([join([returned[0], returned[1]]), join([returned[5], returned[6]])], axis=0)
    even = dot3(even, gather_ref[0], gather_ref[1])
    odd = dot3(odd, gather_ref[2], gather_ref[3])
    a, b = TAPS_A, TAPS_B
    prev_ref[...] = a[0] * odd[:pairs] + b[0] * even[:pairs]
    next_ref[0] = a[3] * even[pairs:] + b[3] * odd[pairs:]
    next_ref[1] = a[4] * even[pairs:] + b[4] * odd[pairs:]
    for gp in range(own2):
        for w in range(ROWS_PER_PERIOD):
            incoming_ref[gp, w] = flat[pl.ds(gp * flat_rows + w, periods, stride=ROWS_PER_PERIOD), :]


def disaggregate_kernel(parents_ref, octants_ref, incoming_ref, phase_ref, gather_ref, out_ref, edge_ref, lhs, coarse_e, coarse_o, whole_out, sems):
    periods = incoming_ref.shape[2]
    azimuth_in = periods * PERIOD_C
    sublane = lax.broadcasted_iota(jnp.int32, (periods, LANES), 0)
    inner = pl.ds(TILE, azimuth_in - 2 * TILE)
    copies = []

    def shift(block):
        for k in range(BLOCK):
            octant = octants_ref[block * BLOCK + k]
            parent = parents_ref[block * BLOCK + k]
            for r in range(3):
                for i in range(3):
                    w = 3 * r + i
                    real, imaginary = incoming_ref[2 * parent, w], incoming_ref[2 * parent + 1, w]
                    cosine, sine = phase_ref[octant, 0, w], phase_ref[octant, 1, w]
                    returned = (real * cosine + imaginary * sine, imaginary * cosine - real * sine)
                    for part in range(2):
                        base = ((2 * k + part) * 3 + r) * periods
                        lhs[block, base : base + periods, i * LANES : (i + 1) * LANES] = returned[part]

    def polar(block):
        high, low = split(lhs[block])
        dot = functools.partial(jnp.dot, preferred_element_type=f32)
        for coarse, columns, i in ((coarse_e, slice(0, 2 * LANES), 0), (coarse_o, slice(LANES, 3 * LANES), 2)):
            coarse[block] = (
                dot(high[:, columns], gather_ref[i])
                + dot(low[:, columns], gather_ref[i])
                + dot(high[:, columns], gather_ref[i + 1])
            )

    def azimuth(block):
        for j in range(2 * BLOCK):
            c = []
            for r in range(3):
                base = (j * 3 + r) * periods
                c.append(coarse_e[block, base : base + periods, :])
                c.append(coarse_o[block, base : base + periods, :])
            lower = both_taps_transposed(c[1], c[2])
            upper = both_taps_transposed(c[4], c[5])
            down = [jnp.where(sublane == 0, 0.0, pltpu.roll(upper[i], 1, 0)) for i in (3, 4)]
            up = jnp.where(sublane == periods - 1, 0.0, pltpu.roll(lower[0], periods - 1, 0))
            rows = [c[0] + lower[1] + down[0], lower[2] + upper[0] + down[1], c[3] + lower[3] + upper[1], lower[4] + upper[2] + up]
            kp = block * (2 * BLOCK) + j
            for u in range(PERIOD_C):
                whole_out[kp, pl.ds(u, periods, stride=PERIOD_C), :] = rows[u]
            edge_ref[0, kp] = whole_out[kp, :TILE, :]
            edge_ref[1, kp] = whole_out[kp, azimuth_in - TILE :, :]
        some = pl.ds(block * (2 * BLOCK), 2 * BLOCK)
        copy = pltpu.make_async_copy(whole_out.at[some, inner, :], out_ref.at[some, inner, :], sems.at[block])
        copy.start()
        copies.append(copy)

    in_stages(lhs.shape[0], shift, polar, azimuth)
    for copy in copies:
        copy.wait()


def finish_kernel(edge_ref, before_ref, after_ref, part_ref, out_ref, tiles, sems):
    pairs, azimuth_in, _ = out_ref.shape
    tiles[...] = edge_ref[...]
    flat = tiles.reshape(2 * pairs * TILE, LANES)
    ends = ((0, 0, before_ref.at[0]), (0, 1, before_ref.at[1]), (1, TILE - 1, after_ref))
    copies = []
    for i, start in enumerate((0, azimuth_in - TILE)):
        for end, row, values_ref in ends:
            if end == i:
                for part in range(2):
                    for k in range(0, pairs // 2, 8):
                        source = slice(part * (pairs // 2) + k, part * (pairs // 2) + k + 8)
                        rows = pl.ds((i * pairs + 2 * k + part) * TILE + row, 8, stride=2 * TILE)
                        flat[rows, :] = flat[rows, :] + values_ref[source, :]
        copy = pltpu.make_async_copy(tiles.at[i], out_ref.at[:, pl.ds(start, TILE), :], sems.at[i])
        copy.start()
        copies.append(copy)
    for copy in copies:
        copy.wait()


def shifted(values, axis, by):
    size = lax.axis_size(axis)
    return lax.ppermute(values, axis, [(i, (i + by) % size) for i in range(size)])


def exchanged(values, axis, mask):
    size = lax.axis_size(axis)
    return lax.ppermute(values, axis, [(i, i ^ mask) for i in range(size)])


SMEM = pl.BlockSpec(memory_space=pltpu.SMEM)
VMEM = pl.BlockSpec(memory_space=pltpu.VMEM)
HBM = pl.BlockSpec(memory_space=pltpu.HBM)


def in_hbm(values):
    return pltpu.with_memory_space_constraint(values, pltpu.HBM)


def local_call(kernel, out_shape, in_specs, scratch, grant, flops=1_000_000, bytes_accessed=1_000_000, out_specs=None, aliases={}):
    return pl.pallas_call(
        kernel,
        out_shape=out_shape,
        in_specs=in_specs,
        out_specs=jax.tree.map(lambda _: VMEM, out_shape) if out_specs is None else out_specs,
        scratch_shapes=scratch,
        input_output_aliases=aliases,
        compiler_params=pltpu.CompilerParams(vmem_limit_bytes=grant << 20),
        cost_estimate=pl.CostEstimate(flops=flops, bytes_accessed=bytes_accessed, transcendentals=0),
    )


def on_device_exchange(
    child_patterns, trans_table, child_parent, child_octant, partner_src, partner_off, partner_count
):
    children, _, azimuth_in, polar_in = child_patterns.shape
    pairs = 2 * children
    peers = lax.axis_size("clus")
    parent_total, _ = partner_src.shape
    own = parent_total // peers
    periods = azimuth_in // PERIOD_C
    flat_rows = ROWS_PER_PERIOD * periods
    share = flat_rows // peers
    offsets = trans_table.shape[0]
    array = lambda *shape: jax.ShapeDtypeStruct(shape, f32)
    buffer = lambda *shape: pltpu.VMEM(shape, f32)
    parents = in_hbm(child_parent[0])

    edges = len(edge_rows(periods))
    even, odd = polar_blocks()
    blocks_np = np.stack([*split_np(even), *split_np(odd)])
    octants = in_hbm(child_octant)
    held, last, first, phases, edge_phases, spread = local_call(
        rows_kernel,
        [
            array(pairs, azimuth_in, polar_in),
            array(pairs, polar_in),
            array(2, pairs, polar_in),
            array(8, 2, ROWS_PER_PERIOD, periods, LANES),
            array(edges, 2, children, LANES),
            jax.ShapeDtypeStruct(blocks_np.shape, bf16),
        ],
        [SMEM, HBM, HBM],
        [pltpu.SemaphoreType.DMA] * 2,
        12,
    )(octants, in_hbm(child_patterns.reshape(pairs, azimuth_in, polar_in)), in_hbm(jnp.asarray(blocks_np)))
    before = shifted(last, "dir", 1)
    after = shifted(first, "dir", -1)

    odd_gather = np.concatenate([odd.T[LANES:], odd.T[:LANES]])
    gather = np.stack([*split_np(even.T), *split_np(odd_gather)])

    frame = max(-(-((q * 2 * share) % 8 + 2 * share) // 8) * 8 for q in range(peers))
    view = trans_table.reshape(offsets, 2, flat_rows, LANES).transpose(0, 2, 1, 3).reshape(offsets, 2 * flat_rows, LANES)
    blocks = children // BLOCK
    rows = 2 * BLOCK * 3 * periods
    flat, table = local_call(
        functools.partial(main_kernel, peers),
        [array(2 * own * flat_rows, LANES), jax.ShapeDtypeStruct((offsets, frame, LANES), bf16)],
        [SMEM] * 2 + [VMEM, HBM, VMEM, VMEM],
        [
            buffer(blocks, rows, LANES),
            buffer(blocks, rows, LANES),
            buffer(blocks, rows, 2 * LANES),
            buffer(blocks, rows, 2 * LANES),
            buffer(own, 2, ROWS_PER_PERIOD, periods, LANES),
            buffer(2 * own * flat_rows, LANES),
            pltpu.SemaphoreType.DMA,
        ],
        24,
        flops=4_000_000_000,
        bytes_accessed=12_000_000,
    )(parents, octants, held.reshape(pairs * azimuth_in, polar_in), in_hbm(view), phases, spread)

    chunk = array(2 * own * share, LANES)
    sent = local_call(
        functools.partial(fix_kernel, peers, own), [chunk] * peers, [VMEM] * 6, [buffer(2 * own * flat_rows, LANES)], 8
    )(child_parent, before, after, flat, edge_phases, spread)

    masks = sorted(range(1, peers), key=lambda d: -bin(d).count("1"))
    received = {0: sent[0]}
    for d in masks:
        received[d] = exchanged(sent[d], "clus", d)

    slots = -(-partner_src.shape[1] // UNROLL) * UNROLL
    listed = jax.ShapeDtypeStruct((parent_total * slots,), jnp.int32)
    wide, sources, slot_offsets = local_call(
        widen_kernel,
        [array(offsets * frame, LANES), listed, listed],
        [SMEM] * 3 + [VMEM],
        [],
        20,
        flops=50_000_000,
        bytes_accessed=8_000_000,
        out_specs=[VMEM, SMEM, SMEM],
    )(partner_src, partner_off, partner_count, table)

    twice = array((parent_total + 1) * frame, LANES)
    sums = [buffer(frame, LANES)] * 2
    lists = (sources, slot_offsets, partner_count)
    back = {}
    real_twice = imag_twice = None
    for targets in (masks[:1], masks[1:], [0]):
        prepare = real_twice is None
        call = local_call(
            functools.partial(translate_kernel, peers, tuple(targets), prepare, frame),
            ([twice] * 2 if prepare else []) + [chunk] * len(targets),
            [SMEM] * 3 + [VMEM] * (1 + peers if prepare else 3),
            sums,
            20,
            flops=20_000_000 * len(targets),
            bytes_accessed=4_000_000 * len(targets),
        )
        if prepare:
            real_twice, imag_twice, *results = call(*lists, wide, *[received[d] for d in range(peers)])
        else:
            results = call(*lists, wide, real_twice, imag_twice)
        for d, result in zip(targets, results):
            back[d] = exchanged(result, "clus", d) if d else result

    incoming, to_next, to_prev = local_call(
        functools.partial(edge_kernel, peers),
        [array(2 * own, ROWS_PER_PERIOD, periods, LANES), array(2, pairs, polar_in), array(pairs, polar_in)],
        [VMEM] * (3 + peers),
        [buffer(2 * own * flat_rows, LANES)],
        8,
    )(child_parent, edge_phases, gather, *[back[d] for d in range(peers)])

    from_before = shifted(to_next, "dir", 1)
    from_after = shifted(to_prev, "dir", -1)

    inner, edge_tiles = local_call(
        disaggregate_kernel,
        [array(pairs, azimuth_in, polar_in), array(2, pairs, TILE, polar_in)],
        [SMEM] * 2 + [VMEM] * 3,
        [
            buffer(blocks, rows, 3 * LANES),
            buffer(blocks, rows, LANES),
            buffer(blocks, rows, LANES),
            buffer(pairs, azimuth_in, polar_in),
            pltpu.SemaphoreType.DMA((blocks,)),
        ],
        24,
        flops=4_000_000_000,
        bytes_accessed=12_000_000,
        out_specs=[HBM, VMEM],
    )(parents, child_octant, incoming, phases, gather)

    out = local_call(
        finish_kernel,
        array(pairs, azimuth_in, polar_in),
        [VMEM] * 3 + [HBM],
        [buffer(2, pairs, TILE, polar_in), pltpu.SemaphoreType.DMA((2,))],
        8,
        out_specs=HBM,
        aliases={3: 0},
    )(edge_tiles, from_before, from_after, in_hbm(inner))
    return out.reshape(child_patterns.shape)


def with_halo(shard, sides, width):
    for axis, dim in sides:
        size, length = (lax.axis_size(axis), shard.shape[dim])
        up = [(i, (i + 1) % size) for i in range(size)]
        down = [(j, i) for i, j in up]
        last = lax.slice_in_dim(shard, length - width, length, axis=dim)
        initial = lax.slice_in_dim(shard, 0, width, axis=dim)
        before = lax.ppermute(last, axis, up)
        after = lax.ppermute(initial, axis, down)
        shard = jnp.concatenate([before, shard, after], axis=dim)
    return shard


def lagrange_rows(offset):
    weights = []
    for anchor in range(5):
        factor = jnp.ones_like(offset)
        for neighbour in range(5):
            if neighbour != anchor:
                factor = factor * (offset - neighbour) / (anchor - neighbour)
        weights.append(factor)
    return weights


def polar_matrix_of(rows_out, rows_in):
    target = (jnp.arange(rows_out, dtype=jnp.float32) + 0.5) * rows_in / rows_out - 0.5
    start_row = jnp.clip(jnp.floor(target + 0.5).astype(jnp.int32) - 2, 0, rows_in - 5)
    weights = lagrange_rows(target - start_row.astype(jnp.float32))
    columns = jnp.arange(rows_in, dtype=jnp.int32)
    matrix = jnp.zeros((rows_out, rows_in), jnp.float32)
    for anchor in range(5):
        matrix = matrix + jnp.where(
            columns[None, :] == (start_row + anchor)[:, None], weights[anchor][:, None], 0.0
        )
    return matrix


def azimuth_matrix_of(out_index, in_index, total_out, total_in):
    target = (out_index * total_in).astype(jnp.float32) / total_out
    nearest = jnp.floor(target + 0.5).astype(jnp.int32)
    weights = lagrange_rows(target - nearest.astype(jnp.float32) + 2.0)
    matrix = jnp.zeros((out_index.shape[0], in_index.shape[0]), jnp.float32)
    for anchor in range(5):
        columns = nearest + anchor - 2
        matrix = matrix + jnp.where(
            in_index[None, :] == columns[:, None], weights[anchor][:, None], 0.0
        )
    return matrix


def shift_phases(octant, azimuth_index, azimuth_total, polar_total):
    azimuth = 2.0 * math.pi * azimuth_index.astype(jnp.float32) / azimuth_total
    polar = math.pi * (jnp.arange(polar_total, dtype=jnp.float32) + 0.5) / polar_total
    first_axis = jnp.sin(polar)[None, :] * jnp.cos(azimuth)[:, None]
    second_axis = jnp.sin(polar)[None, :] * jnp.sin(azimuth)[:, None]
    third_axis = jnp.cos(polar)[None, :] * jnp.ones_like(azimuth)[:, None]
    first_sign = (1 - 2 * (octant % 2)).astype(jnp.float32)
    second_sign = (1 - 2 * (octant // 2 % 2)).astype(jnp.float32)
    third_sign = (1 - 2 * (octant // 4)).astype(jnp.float32)
    phase_angle = phase_scale * (
        first_sign[:, None, None] * first_axis[None]
        + second_sign[:, None, None] * second_axis[None]
        + third_sign[:, None, None] * third_axis[None]
    )
    return (jnp.cos(phase_angle), jnp.sin(phase_angle))


def translate(sources, table, partner_src, partner_off, partner_count):
    live_mask = (
        jnp.arange(partner_src.shape[1], dtype=jnp.int32)[None, :] < partner_count[:, None]
    ).astype(jnp.float32)
    picked = sources[partner_src]
    operator = table[partner_off].astype(jnp.float32) * live_mask[:, :, None, None]
    real_part = jnp.sum(
        operator[:, :, 0] * picked[:, :, 0] - operator[:, :, 1] * picked[:, :, 1], axis=1
    )
    imaginary = jnp.sum(
        operator[:, :, 0] * picked[:, :, 1] + operator[:, :, 1] * picked[:, :, 0], axis=1
    )
    return jnp.stack([real_part, imaginary], axis=1)


def forward_shift(patterns, cosine, sine_part):
    real_part = patterns[:, 0] * cosine - patterns[:, 1] * sine_part
    imaginary = patterns[:, 0] * sine_part + patterns[:, 1] * cosine
    return jnp.stack([real_part, imaginary], axis=1)


def conjugate_shift(patterns, cosine, sine_part):
    real_part = patterns[:, 0] * cosine + patterns[:, 1] * sine_part
    imaginary = patterns[:, 1] * cosine - patterns[:, 0] * sine_part
    return jnp.stack([real_part, imaginary], axis=1)


def on_device_gather(
    child_patterns, trans_table, child_parent, child_octant, partner_src, partner_off, partner_count
):
    _, _, azimuth_in, _ = child_patterns.shape
    polar_out = NTHETA_P
    azimuth_out = trans_table.shape[2] // polar_out
    parent_slots = partner_src.shape[0] // lax.axis_size("clus")
    cluster_index = lax.axis_index("clus")
    direction_index = lax.axis_index("dir")
    parents = child_parent[0]
    polar_matrix = polar_matrix_of(NTHETA_P, NTHETA_C)
    onehot = (parents[None, :] == jnp.arange(parent_slots, dtype=jnp.int32)[:, None]).astype(
        jnp.float32
    )
    own_rows = jnp.mod(
        direction_index * azimuth_out + jnp.arange(azimuth_out, dtype=jnp.int32), NPHI_P
    )
    cosine, sine_part = shift_phases(child_octant, own_rows, NPHI_P, polar_out)
    extended = with_halo(child_patterns, (("dir", 2),), 2)
    gather_matrix = azimuth_matrix_of(
        jnp.arange(azimuth_out, dtype=jnp.int32),
        jnp.arange(azimuth_in + 4, dtype=jnp.int32) - 2,
        NPHI_P,
        NPHI_C,
    )
    along_azimuth = jnp.einsum("pc,kacz->kapz", gather_matrix, extended, precision=highest)
    refined = jnp.einsum("kapz,tz->kapt", along_azimuth, polar_matrix, precision=highest)
    shifted = forward_shift(refined, cosine, sine_part)
    radiation = jnp.einsum("gk,kapt->gapt", onehot, shifted, precision=highest)
    flattened = radiation.reshape(parent_slots, 2, azimuth_out * polar_out)
    sources = lax.all_gather(flattened, "clus", axis=0, tiled=True)
    first_row = cluster_index * parent_slots
    own_src = lax.dynamic_slice_in_dim(partner_src, first_row, parent_slots, 0)
    own_off = lax.dynamic_slice_in_dim(partner_off, first_row, parent_slots, 0)
    own_count = lax.dynamic_slice_in_dim(partner_count, first_row, parent_slots, 0)
    incoming = translate(sources, trans_table, own_src, own_off, own_count)
    incoming = incoming.reshape(parent_slots, 2, azimuth_out, polar_out)
    return_matrix = azimuth_matrix_of(
        jnp.arange(azimuth_out + 6, dtype=jnp.int32) - 3,
        jnp.arange(azimuth_in, dtype=jnp.int32),
        NPHI_P,
        NPHI_C,
    )
    per_child = jnp.einsum("gk,gapt->kapt", onehot, incoming, precision=highest)
    returned = conjugate_shift(per_child, cosine, sine_part)
    coarse_own = jnp.einsum("kapt,tz->kapz", returned, polar_matrix, precision=highest)
    coarse = with_halo(coarse_own, (("dir", 2),), 3)
    return jnp.einsum("pc,kapz->kacz", return_matrix, coarse, precision=highest)


def solution(mesh):
    def on_device(child_patterns, trans_table, *rest):
        peers = lax.axis_size("clus")
        children, _, azimuth_in, polar_in = child_patterns.shape
        flat_rows = trans_table.shape[2] // LANES
        fits = (
            azimuth_in % (8 * PERIOD_C) == 0
            and polar_in == LANES
            and flat_rows * PERIOD_C == ROWS_PER_PERIOD * azimuth_in
            and flat_rows % peers == 0
            and peers & (peers - 1) == 0
            and children % BLOCK == 0
        )
        plan = on_device_exchange if fits else on_device_gather
        return plan(child_patterns, trans_table, *rest)

    return jax.shard_map(
        on_device,
        mesh=mesh,
        in_specs=(
            P("clus", None, "dir", None),
            P(None, None, "dir"),
            P("clus", None),
            P("clus"),
            P(),
            P(),
            P(),
        ),
        out_specs=P("clus", None, "dir", None),
        check_vma=False,
    )
```

```python
import functools
import math

import jax
import jax.numpy as jnp
import numpy as np
from jax import lax
from jax.experimental import pallas as pl
from jax.experimental.pallas import tpu as pltpu
from jax.sharding import PartitionSpec as P


NTHETA_C = 128
NPHI_C = 256
NTHETA_P = 192
NPHI_P = 384

LANES = 128
PERIOD_P = 6
PERIOD_C = 4
ROWS_PER_PERIOD = PERIOD_P * NTHETA_P // LANES
GROUP = 8
TILE = 8
TOGETHER = 2
BLOCK = 2 * GROUP

phase_scale = 8.0 * math.pi
highest = lax.Precision.HIGHEST
f32 = jnp.float32
bf16 = jnp.bfloat16


def lagrange(offset):
    weights = []
    for anchor in range(5):
        factor = 1.0
        for neighbour in range(5):
            if neighbour != anchor:
                factor = factor * (offset - neighbour) / (anchor - neighbour)
        weights.append(factor)
    return weights


TAPS_A = [float(w) for w in lagrange(5.0 / 3.0)]
TAPS_B = [float(w) for w in lagrange(7.0 / 3.0)]


SUMS = [(TAPS_A[i] + TAPS_A[4 - i]) / 2 for i in range(2)]
DIFFS = [(TAPS_A[i] - TAPS_A[4 - i]) / 2 for i in range(2)]
CENTRE = TAPS_A[2]


def polar_matrix_np():
    target = (np.arange(NTHETA_P, dtype=np.float32) + np.float32(0.5)) * NTHETA_C / NTHETA_P - np.float32(0.5)
    start = np.clip(np.floor(target + 0.5).astype(np.int32) - 2, 0, NTHETA_C - 5)
    weights = lagrange((target - start).astype(np.float64))
    matrix = np.zeros((NTHETA_P, NTHETA_C), np.float64)
    for anchor in range(5):
        matrix[np.arange(NTHETA_P), start + anchor] += weights[anchor]
    return matrix.astype(np.float32)


def polar_blocks():
    matrix = polar_matrix_np().T
    even = np.zeros((NTHETA_C, 2 * LANES), np.float32)
    odd = np.zeros((NTHETA_C, 2 * LANES), np.float32)
    half = NTHETA_P - LANES
    even[:, :NTHETA_P] = matrix
    odd[:, :LANES] = matrix[:, half:]
    odd[:, 2 * LANES - half :] = matrix[:, :half]
    return even, odd


def split_np(matrix):
    high = matrix.astype(bf16)
    low = (matrix - high.astype(np.float32)).astype(bf16)
    return high, low


def split(values):
    high = values.astype(bf16)
    low = (values - high.astype(f32)).astype(bf16)
    return high, low


def dot3(values, high_matrix, low_matrix):
    high, low = split(values)
    dot = functools.partial(jnp.dot, preferred_element_type=f32)
    return dot(high, high_matrix) + dot(low, high_matrix) + dot(high, low_matrix)


SIN_COEFFS = [(-1) ** k * math.pi ** (2 * k + 1) / math.factorial(2 * k + 1) for k in range(7)]
COS_COEFFS = [(-1) ** k * math.pi ** (2 * k) / math.factorial(2 * k) for k in range(7)]


def sincos_turns(turns):
    rest = turns - jnp.round(turns)
    square = rest * rest
    sine = jnp.full_like(square, SIN_COEFFS[-1])
    for coeff in SIN_COEFFS[-2::-1]:
        sine = sine * square + coeff
    sine = sine * rest
    cosine = jnp.full_like(square, COS_COEFFS[-1])
    for coeff in COS_COEFFS[-2::-1]:
        cosine = cosine * square + coeff
    return 2.0 * sine * cosine, 1.0 - 2.0 * sine * sine


def fill_phases(direction, out_ref):
    periods = out_ref.shape[3]
    lane = lax.broadcasted_iota(jnp.int32, (periods, LANES), 1)
    period = lax.broadcasted_iota(jnp.int32, (periods, LANES), 0)
    first = direction * (PERIOD_P * periods)

    def two_rows(r, carry):
        for i in range(3):
            position = lane + i * LANES
            second = (position >= NTHETA_P).astype(jnp.int32)
            polar_index = position - second * NTHETA_P
            azimuth_index = first + period * PERIOD_P + 2 * r + second
            sin_polar, cos_polar = sincos_turns((polar_index.astype(f32) + 0.5) / (2 * NTHETA_P))
            sin_azimuth, cos_azimuth = sincos_turns(azimuth_index.astype(f32) / NPHI_P)
            along_x = 4.0 * sin_polar * cos_azimuth
            along_y = 4.0 * sin_polar * sin_azimuth
            along_z = 4.0 * cos_polar
            w = 3 * r + i
            for octant in (0, 2, 4, 6):
                turns = along_x + along_y if octant % 4 == 0 else along_x - along_y
                turns = turns + along_z if octant < 4 else turns - along_z
                sine, cosine = sincos_turns(turns)
                out_ref[octant, 0, w] = cosine
                out_ref[octant, 1, w] = sine
                out_ref[7 - octant, 0, w] = cosine
                out_ref[7 - octant, 1, w] = -sine
        return carry

    lax.fori_loop(0, PERIOD_P // 2, two_rows, 0)


def edge_rows(periods):
    return [(w, 0) for w in (1, 2, 3, 4)] + [(w, periods - 1) for w in (6, 7, 8)]


def rows_kernel(
    octants_hbm, x_ref, blocks_ref, held_ref, last_ref, first_ref, phase_ref, edge_phase_ref, blocks_out, octants_ref, sem, blocks_sem, octants_sem
):
    pairs, azimuth_in, _ = x_ref.shape
    periods = phase_ref.shape[3]
    copy = pltpu.make_async_copy(x_ref, held_ref, sem)
    copy.start()
    blocks_copy = pltpu.make_async_copy(blocks_ref, blocks_out, blocks_sem)
    blocks_copy.start()
    octants_copy = pltpu.make_async_copy(octants_hbm, octants_ref, octants_sem)
    octants_copy.start()
    fill_phases(lax.axis_index("dir"), phase_ref)

    octants_copy.wait()

    def edges_of(step, carry):
        for j in range(GROUP):
            k = step * GROUP + j
            octant = octants_ref[k]
            for e, (w, m) in enumerate(edge_rows(periods)):
                for i in range(2):
                    edge_phase_ref[e, i, pl.ds(k, 1), :] = phase_ref[octant, i, w, m : m + 1, :]
        return carry

    lax.fori_loop(0, pairs // 2 // GROUP, edges_of, 0)
    copy.wait()
    for part in range(2):
        source = pl.ds(part, pairs // 2, stride=2)
        target = slice(part * (pairs // 2), (part + 1) * (pairs // 2))
        last_ref[target] = held_ref[source, azimuth_in - 1, :]
        for i in range(2):
            first_ref[i, target] = held_ref[source, i, :]
    blocks_copy.wait()


def both_taps(rows):
    even = SUMS[0] * (rows[0] + rows[4]) + SUMS[1] * (rows[1] + rows[3]) + CENTRE * rows[2]
    odd = DIFFS[0] * (rows[0] - rows[4]) + DIFFS[1] * (rows[1] - rows[3])
    return even + odd, even - odd


def both_taps_transposed(first, second):
    total, difference = first + second, first - second
    outer = [SUMS[i] * total for i in range(2)]
    inner = [DIFFS[i] * difference for i in range(2)]
    return [outer[0] + inner[0], outer[1] + inner[1], CENTRE * total, outer[1] - inner[1], outer[0] - inner[0]]


def main_kernel(peers, parents_ref, octants_ref, x_ref, table_ref, phase_ref, spread_ref, *rest):
    flat_ref, slice_ref, az_e, az_o, res_e, res_o, acc, flat, table_sem = rest
    children = octants_ref.shape[0]
    periods = phase_ref.shape[3]
    azimuth_in = periods * PERIOD_C
    own = acc.shape[0]
    me = lax.axis_index("clus")
    share = ROWS_PER_PERIOD * periods // peers
    first_tile = me * (2 * share) // 8
    table_rows = pl.ds(pl.multiple_of(first_tile * 8, 8), slice_ref.shape[1])
    table_copy = pltpu.make_async_copy(table_ref.at[:, table_rows, :], slice_ref, table_sem)
    table_copy.start()
    acc[...] = jnp.zeros_like(acc)
    sublane = lax.broadcasted_iota(jnp.int32, (periods, LANES), 0)

    def azimuth(block):
        for kp in range(2 * BLOCK):
            start = pl.multiple_of((block * (2 * BLOCK) + kp) * azimuth_in, 8)
            x = [x_ref[pl.ds(start + u, periods, stride=PERIOD_C), :] for u in range(PERIOD_C)]
            left = jnp.where(sublane == 0, 0.0, pltpu.roll(x[3], 1, 0))
            right = [jnp.where(sublane == periods - 1, 0.0, pltpu.roll(x[i], periods - 1, 0)) for i in range(2)]
            lower = [left, x[0], x[1], x[2], x[3]]
            upper = [x[1], x[2], x[3], right[0], right[1]]
            rows = [x[0], *both_taps(lower), x[2], *both_taps(upper)]
            for r in range(3):
                base = (kp * 3 + r) * periods
                az_e[base : base + periods, :] = rows[2 * r]
                az_o[base : base + periods, :] = rows[2 * r + 1]

    def polar():
        res_e[...] = dot3(az_e[...], spread_ref[0], spread_ref[1])
        res_o[...] = dot3(az_o[...], spread_ref[2], spread_ref[3])

    def shift(block):
        for k in range(BLOCK):
            octant = octants_ref[block * BLOCK + k]
            parent = parents_ref[block * BLOCK + k]
            for r in range(3):
                parts = []
                for part in range(2):
                    rows = pl.ds(((2 * k + part) * 3 + r) * periods, periods)
                    middle = res_e[rows, LANES:] + res_o[rows, LANES:]
                    parts.append((res_e[rows, :LANES], middle, res_o[rows, :LANES]))
                for i in range(3):
                    w = 3 * r + i
                    real, imaginary = parts[0][i], parts[1][i]
                    cosine, sine = phase_ref[octant, 0, w], phase_ref[octant, 1, w]
                    acc[parent, 0, w] += real * cosine - imaginary * sine
                    acc[parent, 1, w] += real * sine + imaginary * cosine

    def one_block(block, carry):
        azimuth(block)
        polar()
        shift(block)
        return carry

    lax.fori_loop(0, children // BLOCK, one_block, 0)
    for gp in range(2 * own):
        for w in range(ROWS_PER_PERIOD):
            flat[pl.ds(gp * ROWS_PER_PERIOD * periods + w, periods, stride=ROWS_PER_PERIOD), :] = acc[gp // 2, gp % 2, w]
        for q in range(peers):
            source = gp * ROWS_PER_PERIOD * periods + q * share
            target = (q * 2 * own + gp) * share
            flat_ref[target : target + share, :] = flat[source : source + share, :]
    table_copy.wait()


def one_hot(parents, own):
    index = lax.broadcasted_iota(jnp.int32, (own, parents.shape[1]), 0)
    return (index == parents).astype(f32)


def dot2(exact, values):
    exact = exact.astype(bf16)
    high, low = split(values)
    dot = functools.partial(jnp.dot, preferred_element_type=f32)
    return dot(exact, high) + dot(exact, low)


def fix_kernel(
    peers, own, parents_ref, before_ref, after_ref, flat_ref, edge_phase_ref, spread_ref, *rest
):
    outs, (fixed,) = rest[:peers], rest[peers:]
    pairs = before_ref.shape[0]
    children = pairs // 2
    chunk_rows = outs[0].shape[0]
    share = chunk_rows // (2 * own)
    periods = share * peers // ROWS_PER_PERIOD
    fixed[...] = flat_ref[...]
    left, right = before_ref[...], [after_ref[0], after_ref[1]]
    a, b = TAPS_A, TAPS_B
    even = jnp.concatenate([b[0] * left, a[3] * right[0] + a[4] * right[1]], axis=0)
    odd = jnp.concatenate([a[0] * left, b[3] * right[0] + b[4] * right[1]], axis=0)
    even = dot3(even, spread_ref[0], spread_ref[1])
    odd = dot3(odd, spread_ref[2], spread_ref[3])
    first, last = slice(0, pairs), slice(pairs, 2 * pairs)
    low, high = slice(0, LANES), slice(LANES, 2 * LANES)
    refined = [
        odd[first, high],
        odd[first, low],
        even[first, low],
        even[first, high],
        even[last, low],
        even[last, high] + odd[last, high],
        odd[last, low],
    ]
    shifted_rows = []
    for e, rows in enumerate(refined):
        real, imaginary = rows[:children], rows[children:]
        cosine, sine = edge_phase_ref[e, 0], edge_phase_ref[e, 1]
        shifted_rows.append(real * cosine - imaginary * sine)
        shifted_rows.append(real * sine + imaginary * cosine)
    summed = dot2(one_hot(parents_ref[...], own), jnp.concatenate(shifted_rows, axis=1))
    for e, (w, m) in enumerate(edge_rows(periods)):
        q, row = divmod(ROWS_PER_PERIOD * m + w, share)
        for part in range(2):
            rows = pl.ds(q * chunk_rows + part * share + row, own, stride=2 * share)
            column = (2 * e + part) * LANES
            fixed[rows, :] = fixed[rows, :] + summed[:, column : column + LANES]
    me = lax.axis_index("clus")
    for d in range(peers):
        start = pl.multiple_of((me ^ d) * chunk_rows, 8)
        outs[d][...] = fixed[pl.ds(start, chunk_rows), :]


def widen_kernel(source_ref, offset_ref, count_ref, table_ref, wide_ref, operator_ref):
    targets, partners = source_ref.shape
    offsets, frame, _ = table_ref.shape

    def some_offsets(i, carry):
        for j in range(4):
            wide_ref[pl.ds(pl.multiple_of((i * 4 + j) * frame, 8), frame), :] = table_ref[i * 4 + j].astype(f32)
        return carry

    whole_steps = offsets // 4
    lax.fori_loop(0, whole_steps, some_offsets, 0)
    for offset in range(whole_steps * 4, offsets):
        wide_ref[offset * frame : (offset + 1) * frame, :] = table_ref[offset].astype(f32)
    wide_ref[offsets * frame :, :] = jnp.zeros((frame, LANES), f32)

    shape = (targets, targets)
    row, lane = (lax.broadcasted_iota(jnp.int32, shape, d) for d in range(2))
    count = jnp.sum(jnp.where(row == lane, count_ref[...], 0), axis=1, keepdims=True)
    operator = jnp.full(shape, offsets, jnp.int32)
    for p in range(partners):
        here = (lane == source_ref[:, p : p + 1]) & (p < count)
        operator = jnp.where(here, offset_ref[:, p : p + 1], operator)
    operator_ref[...] = operator * frame


def doubled(chunk, real_twice, imag_twice, first, own, share, frame, skip):
    for g in range(own):
        for part, twice in enumerate((real_twice, imag_twice)):
            rows = chunk[(2 * g + part) * share : (2 * g + part + 1) * share, :]
            base = (first + g) * frame + skip
            twice[pl.ds(base, share, stride=2), :] = rows
            twice[pl.ds(base + 1, share, stride=2), :] = rows


def add_sources(sums, targets, devices, own, frame, operator_ref, wide_ref, real_twice, imag_twice):
    for number, device in enumerate(devices):
        for g in range(own):
            source = slice((number * own + g) * frame, (number * own + g + 1) * frame)
            real, imaginary = real_twice[source, :], imag_twice[source, :]
            for i, target in enumerate(targets):
                first = pl.multiple_of(operator_ref[target, device * own + g], 8)
                operator = wide_ref[pl.ds(first, frame), :]
                sums[i] = (sums[i][0] + operator * real, sums[i][1] + operator * imaginary)
    return sums


def gather_kernel(peers, frame, masks, operator_ref, wide_ref, *rest):
    chunks, rest = rest[: len(masks)], rest[len(masks) :]
    before, (real_sum, imag_sum, real_twice, imag_twice) = rest[:-4], rest[-4:]
    me = lax.axis_index("clus")
    targets = operator_ref.shape[0]
    own = targets // peers
    share = chunks[0].shape[0] // (2 * own)
    skip = lax.rem(me * (2 * share), 8)
    for number, chunk in enumerate(chunks):
        doubled(chunk, real_twice, imag_twice, number * own, own, share, frame, skip)

    def some_targets(i, carry):
        some = [i * TOGETHER + j for j in range(TOGETHER)]
        places = [pl.ds(pl.multiple_of(target * frame, 8), frame) for target in some]
        if before:
            sums = [tuple(ref[place, :] for ref in before) for place in places]
        else:
            sums = [(jnp.zeros((frame, LANES), f32),) * 2 for _ in some]
        sums = add_sources(sums, some, [me ^ d for d in masks], own, frame, operator_ref, wide_ref, real_twice, imag_twice)
        for place, (by_real, by_imag) in zip(places, sums):
            real_sum[place, :] = by_real
            imag_sum[place, :] = by_imag
        return carry

    lax.fori_loop(0, targets // TOGETHER, some_targets, 0)


def translate_kernel(peers, frame, mask, targets, operator_ref, wide_ref, real_sum, imag_sum, *rest):
    if len(rest) == 5 + len(targets):
        chunk, real_twice, imag_twice = rest[:3]
        prepare = True
    else:
        real_twice, imag_twice = rest[:2]
        prepare = False
    outs, (total_real, total_imag) = rest[-2 - len(targets) : -2], rest[-2:]
    me = lax.axis_index("clus")
    own = operator_ref.shape[0] // peers
    share = outs[0].shape[0] // (2 * own)
    skip = lax.rem(me * (2 * share), 8)
    if prepare:
        doubled(chunk, real_twice, imag_twice, 0, own, share, frame, skip)
    even, odd = pl.ds(skip, share, stride=2), pl.ds(skip + 1, share, stride=2)
    for out, d in zip(outs, targets):
        first = (me ^ d) * own

        def some_targets(i, carry):
            places = [i * TOGETHER + j for j in range(TOGETHER)]
            some = [first + g for g in places]
            rows = [pl.ds(pl.multiple_of(target * frame, 8), frame) for target in some]
            sums = [(real_sum[r, :], imag_sum[r, :]) for r in rows]
            sums = add_sources(sums, some, [me ^ mask], own, frame, operator_ref, wide_ref, real_twice, imag_twice)
            for j, (g, (by_real, by_imag)) in enumerate(zip(places, sums)):
                total_real[j] = by_real
                total_imag[j] = by_imag
                row = g * (2 * share)
                out[pl.ds(row, share), :] = total_real[j, even, :] - total_imag[j, odd, :]
                out[pl.ds(row + share, share), :] = total_real[j, odd, :] + total_imag[j, even, :]
            return carry

        lax.fori_loop(0, own // TOGETHER, some_targets, 0)


def edge_kernel(peers, parents_ref, edge_phase_ref, gather_ref, *rest):
    chunks = rest[:peers]
    incoming_ref, next_ref, prev_ref, flat = rest[peers:]
    own2, _, periods, _ = incoming_ref.shape
    own = own2 // 2
    pairs = prev_ref.shape[0]
    flat_rows = ROWS_PER_PERIOD * periods
    share = flat_rows // peers
    me = lax.axis_index("clus")
    for gp in range(own2):
        for d in range(peers):
            flat[pl.ds(gp * flat_rows + (me ^ d) * share, share), :] = chunks[d][gp * share : (gp + 1) * share, :]
    edges = []
    for w, m in edge_rows(periods):
        for part in range(2):
            edges.append(flat[pl.ds(part * flat_rows + ROWS_PER_PERIOD * m + w, own, stride=2 * flat_rows), :])
    per_child = dot2(one_hot(parents_ref[...], own).T, jnp.concatenate(edges, axis=1))
    returned = []
    for e in range(len(edges) // 2):
        real = per_child[:, 2 * e * LANES : (2 * e + 1) * LANES]
        imaginary = per_child[:, (2 * e + 1) * LANES : (2 * e + 2) * LANES]
        cosine, sine = edge_phase_ref[e, 0], edge_phase_ref[e, 1]
        returned.append(
            jnp.concatenate([real * cosine + imaginary * sine, imaginary * cosine - real * sine], axis=0)
        )
    join = functools.partial(jnp.concatenate, axis=1)
    even = jnp.concatenate([join([returned[2], returned[3]]), join([returned[4], returned[5]])], axis=0)
    odd = jnp.concatenate([join([returned[0], returned[1]]), join([returned[5], returned[6]])], axis=0)
    even = dot3(even, gather_ref[0], gather_ref[1])
    odd = dot3(odd, gather_ref[2], gather_ref[3])
    a, b = TAPS_A, TAPS_B
    prev_ref[...] = a[0] * odd[:pairs] + b[0] * even[:pairs]
    next_ref[0] = a[3] * even[pairs:] + b[3] * odd[pairs:]
    next_ref[1] = a[4] * even[pairs:] + b[4] * odd[pairs:]
    for gp in range(own2):
        for w in range(ROWS_PER_PERIOD):
            incoming_ref[gp, w] = flat[pl.ds(gp * flat_rows + w, periods, stride=ROWS_PER_PERIOD), :]


def disaggregate_kernel(parents_ref, octants_ref, incoming_ref, phase_ref, gather_ref, out_ref, edge_ref, lhs, coarse_e, coarse_o, whole_out, sems):
    periods = incoming_ref.shape[2]
    azimuth_in = periods * PERIOD_C
    sublane = lax.broadcasted_iota(jnp.int32, (periods, LANES), 0)
    inner = pl.ds(TILE, azimuth_in - 2 * TILE)

    def shift(block):
        for k in range(BLOCK):
            octant = octants_ref[block * BLOCK + k]
            parent = parents_ref[block * BLOCK + k]
            for r in range(3):
                for i in range(3):
                    w = 3 * r + i
                    real, imaginary = incoming_ref[2 * parent, w], incoming_ref[2 * parent + 1, w]
                    cosine, sine = phase_ref[octant, 0, w], phase_ref[octant, 1, w]
                    returned = (real * cosine + imaginary * sine, imaginary * cosine - real * sine)
                    for part in range(2):
                        base = ((2 * k + part) * 3 + r) * periods
                        lhs[base : base + periods, i * LANES : (i + 1) * LANES] = returned[part]

    def polar():
        high, low = split(lhs[...])
        dot = functools.partial(jnp.dot, preferred_element_type=f32)
        for coarse, columns, i in ((coarse_e, slice(0, 2 * LANES), 0), (coarse_o, slice(LANES, 3 * LANES), 2)):
            coarse[...] = (
                dot(high[:, columns], gather_ref[i])
                + dot(low[:, columns], gather_ref[i])
                + dot(high[:, columns], gather_ref[i + 1])
            )

    def azimuth(block):
        for j in range(2 * BLOCK):
            c = []
            for r in range(3):
                base = (j * 3 + r) * periods
                c.append(coarse_e[base : base + periods, :])
                c.append(coarse_o[base : base + periods, :])
            lower = both_taps_transposed(c[1], c[2])
            upper = both_taps_transposed(c[4], c[5])
            down = [jnp.where(sublane == 0, 0.0, pltpu.roll(upper[i], 1, 0)) for i in (3, 4)]
            up = jnp.where(sublane == periods - 1, 0.0, pltpu.roll(lower[0], periods - 1, 0))
            rows = [c[0] + lower[1] + down[0], lower[2] + upper[0] + down[1], c[3] + lower[3] + upper[1], lower[4] + upper[2] + up]
            kp = block * (2 * BLOCK) + j
            for u in range(PERIOD_C):
                whole_out[kp, pl.ds(u, periods, stride=PERIOD_C), :] = rows[u]
            edge_ref[0, kp] = whole_out[kp, :TILE, :]
            edge_ref[1, kp] = whole_out[kp, azimuth_in - TILE :, :]

    def written(block):
        some = pl.ds(block * (2 * BLOCK), 2 * BLOCK)
        return pltpu.make_async_copy(whole_out.at[some, inner, :], out_ref.at[some, inner, :], sems.at[block])

    def one_block(block, carry):
        shift(block)
        polar()
        azimuth(block)
        written(block).start()
        return carry

    blocks = octants_ref.shape[0] // BLOCK
    lax.fori_loop(0, blocks, one_block, 0)
    for block in range(blocks):
        written(block).wait()


def finish_kernel(edge_ref, before_ref, after_ref, part_ref, out_ref, tiles, sems):
    pairs, azimuth_in, _ = out_ref.shape
    tiles[...] = edge_ref[...]
    flat = tiles.reshape(2 * pairs * TILE, LANES)
    ends = ((0, 0, before_ref.at[0]), (0, 1, before_ref.at[1]), (1, TILE - 1, after_ref))
    copies = []
    for i, start in enumerate((0, azimuth_in - TILE)):
        for end, row, values_ref in ends:
            if end == i:
                for part in range(2):
                    for k in range(0, pairs // 2, 8):
                        source = slice(part * (pairs // 2) + k, part * (pairs // 2) + k + 8)
                        rows = pl.ds((i * pairs + 2 * k + part) * TILE + row, 8, stride=2 * TILE)
                        flat[rows, :] = flat[rows, :] + values_ref[source, :]
        copy = pltpu.make_async_copy(tiles.at[i], out_ref.at[:, pl.ds(start, TILE), :], sems.at[i])
        copy.start()
        copies.append(copy)
    for copy in copies:
        copy.wait()


def shifted(values, axis, by):
    size = lax.axis_size(axis)
    return lax.ppermute(values, axis, [(i, (i + by) % size) for i in range(size)])


def exchanged(values, axis, mask):
    size = lax.axis_size(axis)
    return lax.ppermute(values, axis, [(i, i ^ mask) for i in range(size)])


SMEM = pl.BlockSpec(memory_space=pltpu.SMEM)
VMEM = pl.BlockSpec(memory_space=pltpu.VMEM)
HBM = pl.BlockSpec(memory_space=pltpu.HBM)


def in_hbm(values):
    return pltpu.with_memory_space_constraint(values, pltpu.HBM)


def local_call(kernel, out_shape, in_specs, scratch, grant, flops=1_000_000, bytes_accessed=1_000_000, out_specs=None, aliases={}):
    return pl.pallas_call(
        kernel,
        out_shape=out_shape,
        in_specs=in_specs,
        out_specs=jax.tree.map(lambda _: VMEM, out_shape) if out_specs is None else out_specs,
        scratch_shapes=scratch,
        input_output_aliases=aliases,
        compiler_params=pltpu.CompilerParams(vmem_limit_bytes=grant << 20),
        cost_estimate=pl.CostEstimate(flops=flops, bytes_accessed=bytes_accessed, transcendentals=0),
    )


def on_device_exchange(
    child_patterns, trans_table, child_parent, child_octant, partner_src, partner_off, partner_count
):
    children, _, azimuth_in, polar_in = child_patterns.shape
    pairs = 2 * children
    peers = lax.axis_size("clus")
    parent_total, _ = partner_src.shape
    own = parent_total // peers
    periods = azimuth_in // PERIOD_C
    flat_rows = ROWS_PER_PERIOD * periods
    share = flat_rows // peers
    offsets = trans_table.shape[0]
    array = lambda *shape: jax.ShapeDtypeStruct(shape, f32)
    buffer = lambda *shape: pltpu.VMEM(shape, f32)
    parents = child_parent[0]

    edges = len(edge_rows(periods))
    even, odd = polar_blocks()
    blocks_np = np.stack([*split_np(even), *split_np(odd)])
    held, last, first, phases, edge_phases, spread = local_call(
        rows_kernel,
        [
            array(pairs, azimuth_in, polar_in),
            array(pairs, polar_in),
            array(2, pairs, polar_in),
            array(8, 2, ROWS_PER_PERIOD, periods, LANES),
            array(edges, 2, children, LANES),
            jax.ShapeDtypeStruct(blocks_np.shape, bf16),
        ],
        [HBM, HBM, HBM],
        [pltpu.SMEM((children,), jnp.int32)] + [pltpu.SemaphoreType.DMA] * 3,
        12,
    )(in_hbm(child_octant), in_hbm(child_patterns.reshape(pairs, azimuth_in, polar_in)), in_hbm(jnp.asarray(blocks_np)))
    before = shifted(last, "dir", 1)
    after = shifted(first, "dir", -1)

    odd_gather = np.concatenate([odd.T[LANES:], odd.T[:LANES]])
    gather = np.stack([*split_np(even.T), *split_np(odd_gather)])

    frame = max(-(-((q * 2 * share) % 8 + 2 * share) // 8) * 8 for q in range(peers))
    view = trans_table.reshape(offsets, 2, flat_rows, LANES).transpose(0, 2, 1, 3).reshape(offsets, 2 * flat_rows, LANES)
    blocks = children // BLOCK
    rows = 2 * BLOCK * 3 * periods
    flat, table = local_call(
        functools.partial(main_kernel, peers),
        [array(2 * own * flat_rows, LANES), jax.ShapeDtypeStruct((offsets, frame, LANES), bf16)],
        [SMEM] * 2 + [VMEM, HBM, VMEM, VMEM],
        [
            buffer(rows, LANES),
            buffer(rows, LANES),
            buffer(rows, 2 * LANES),
            buffer(rows, 2 * LANES),
            buffer(own, 2, ROWS_PER_PERIOD, periods, LANES),
            buffer(2 * own * flat_rows, LANES),
            pltpu.SemaphoreType.DMA,
        ],
        24,
        flops=4_000_000_000,
        bytes_accessed=12_000_000,
    )(parents, child_octant, held.reshape(pairs * azimuth_in, polar_in), in_hbm(view), phases, spread)

    chunk = array(2 * own * share, LANES)
    sent = local_call(
        functools.partial(fix_kernel, peers, own), [chunk] * peers, [VMEM] * 6, [buffer(2 * own * flat_rows, LANES)], 8
    )(child_parent, before, after, flat, edge_phases, spread)

    masks = sorted(range(1, peers), key=lambda d: bin(d).count("1"))
    middle, late = masks[:-1], masks[-1]
    received = {0: sent[0]}
    for d in middle:
        received[d] = exchanged(sent[d], "clus", d)
    received[late] = exchanged(sent[late], "clus", late)

    wide, operator = local_call(
        widen_kernel,
        [array((offsets + 1) * frame, LANES), jax.ShapeDtypeStruct((parent_total, parent_total), jnp.int32)],
        [VMEM] * 4,
        [],
        20,
        flops=50_000_000,
        bytes_accessed=8_000_000,
    )(partner_src, partner_off, partner_count.reshape(1, parent_total), table)

    sums = []
    for group in ([0], middle):
        sums = local_call(
            functools.partial(gather_kernel, peers, frame, tuple(group)),
            [array(parent_total * frame, LANES)] * 2,
            [SMEM] + [VMEM] * (1 + len(group) + len(sums)),
            [buffer(len(group) * own * frame, LANES)] * 2,
            20,
            flops=40_000_000 * len(group),
            bytes_accessed=4_000_000 * len(group),
        )(operator, wide, *[received[d] for d in group], *sums)

    back = {}
    last_sources = [received[late]]
    for targets in ([late], middle, [0]):
        prepare = len(last_sources) == 1
        results = local_call(
            functools.partial(translate_kernel, peers, frame, late, tuple(targets)),
            ([array(own * frame, LANES)] * 2 if prepare else []) + [chunk] * len(targets),
            [SMEM] + [VMEM] * (3 + len(last_sources)),
            [buffer(TOGETHER, frame, LANES)] * 2,
            20,
            flops=10_000_000 * len(targets),
            bytes_accessed=2_000_000 * len(targets),
        )(operator, wide, *sums, *last_sources)
        if prepare:
            last_sources, results = results[:2], results[2:]
        for d, result in zip(targets, results):
            back[d] = exchanged(result, "clus", d) if d else result

    incoming, to_next, to_prev = local_call(
        functools.partial(edge_kernel, peers),
        [array(2 * own, ROWS_PER_PERIOD, periods, LANES), array(2, pairs, polar_in), array(pairs, polar_in)],
        [VMEM] * (3 + peers),
        [buffer(2 * own * flat_rows, LANES)],
        8,
    )(child_parent, edge_phases, gather, *[back[d] for d in range(peers)])

    from_before = shifted(to_next, "dir", 1)
    from_after = shifted(to_prev, "dir", -1)

    inner, edge_tiles = local_call(
        disaggregate_kernel,
        [array(pairs, azimuth_in, polar_in), array(2, pairs, TILE, polar_in)],
        [SMEM] * 2 + [VMEM] * 3,
        [
            buffer(rows, 3 * LANES),
            buffer(rows, LANES),
            buffer(rows, LANES),
            buffer(pairs, azimuth_in, polar_in),
            pltpu.SemaphoreType.DMA((blocks,)),
        ],
        24,
        flops=4_000_000_000,
        bytes_accessed=12_000_000,
        out_specs=[HBM, VMEM],
    )(parents, child_octant, incoming, phases, gather)

    out = local_call(
        finish_kernel,
        array(pairs, azimuth_in, polar_in),
        [VMEM] * 3 + [HBM],
        [buffer(2, pairs, TILE, polar_in), pltpu.SemaphoreType.DMA((2,))],
        8,
        out_specs=HBM,
        aliases={3: 0},
    )(edge_tiles, from_before, from_after, in_hbm(inner))
    return out.reshape(child_patterns.shape)


def with_halo(shard, sides, width):
    for axis, dim in sides:
        size, length = (lax.axis_size(axis), shard.shape[dim])
        up = [(i, (i + 1) % size) for i in range(size)]
        down = [(j, i) for i, j in up]
        last = lax.slice_in_dim(shard, length - width, length, axis=dim)
        initial = lax.slice_in_dim(shard, 0, width, axis=dim)
        before = lax.ppermute(last, axis, up)
        after = lax.ppermute(initial, axis, down)
        shard = jnp.concatenate([before, shard, after], axis=dim)
    return shard


def lagrange_rows(offset):
    weights = []
    for anchor in range(5):
        factor = jnp.ones_like(offset)
        for neighbour in range(5):
            if neighbour != anchor:
                factor = factor * (offset - neighbour) / (anchor - neighbour)
        weights.append(factor)
    return weights


def polar_matrix_of(rows_out, rows_in):
    target = (jnp.arange(rows_out, dtype=jnp.float32) + 0.5) * rows_in / rows_out - 0.5
    start_row = jnp.clip(jnp.floor(target + 0.5).astype(jnp.int32) - 2, 0, rows_in - 5)
    weights = lagrange_rows(target - start_row.astype(jnp.float32))
    columns = jnp.arange(rows_in, dtype=jnp.int32)
    matrix = jnp.zeros((rows_out, rows_in), jnp.float32)
    for anchor in range(5):
        matrix = matrix + jnp.where(
            columns[None, :] == (start_row + anchor)[:, None], weights[anchor][:, None], 0.0
        )
    return matrix


def azimuth_matrix_of(out_index, in_index, total_out, total_in):
    target = (out_index * total_in).astype(jnp.float32) / total_out
    nearest = jnp.floor(target + 0.5).astype(jnp.int32)
    weights = lagrange_rows(target - nearest.astype(jnp.float32) + 2.0)
    matrix = jnp.zeros((out_index.shape[0], in_index.shape[0]), jnp.float32)
    for anchor in range(5):
        columns = nearest + anchor - 2
        matrix = matrix + jnp.where(
            in_index[None, :] == columns[:, None], weights[anchor][:, None], 0.0
        )
    return matrix


def shift_phases(octant, azimuth_index, azimuth_total, polar_total):
    azimuth = 2.0 * math.pi * azimuth_index.astype(jnp.float32) / azimuth_total
    polar = math.pi * (jnp.arange(polar_total, dtype=jnp.float32) + 0.5) / polar_total
    first_axis = jnp.sin(polar)[None, :] * jnp.cos(azimuth)[:, None]
    second_axis = jnp.sin(polar)[None, :] * jnp.sin(azimuth)[:, None]
    third_axis = jnp.cos(polar)[None, :] * jnp.ones_like(azimuth)[:, None]
    first_sign = (1 - 2 * (octant % 2)).astype(jnp.float32)
    second_sign = (1 - 2 * (octant // 2 % 2)).astype(jnp.float32)
    third_sign = (1 - 2 * (octant // 4)).astype(jnp.float32)
    phase_angle = phase_scale * (
        first_sign[:, None, None] * first_axis[None]
        + second_sign[:, None, None] * second_axis[None]
        + third_sign[:, None, None] * third_axis[None]
    )
    return (jnp.cos(phase_angle), jnp.sin(phase_angle))


def translate(sources, table, partner_src, partner_off, partner_count):
    live_mask = (
        jnp.arange(partner_src.shape[1], dtype=jnp.int32)[None, :] < partner_count[:, None]
    ).astype(jnp.float32)
    picked = sources[partner_src]
    operator = table[partner_off].astype(jnp.float32) * live_mask[:, :, None, None]
    real_part = jnp.sum(
        operator[:, :, 0] * picked[:, :, 0] - operator[:, :, 1] * picked[:, :, 1], axis=1
    )
    imaginary = jnp.sum(
        operator[:, :, 0] * picked[:, :, 1] + operator[:, :, 1] * picked[:, :, 0], axis=1
    )
    return jnp.stack([real_part, imaginary], axis=1)


def forward_shift(patterns, cosine, sine_part):
    real_part = patterns[:, 0] * cosine - patterns[:, 1] * sine_part
    imaginary = patterns[:, 0] * sine_part + patterns[:, 1] * cosine
    return jnp.stack([real_part, imaginary], axis=1)


def conjugate_shift(patterns, cosine, sine_part):
    real_part = patterns[:, 0] * cosine + patterns[:, 1] * sine_part
    imaginary = patterns[:, 1] * cosine - patterns[:, 0] * sine_part
    return jnp.stack([real_part, imaginary], axis=1)


def on_device_gather(
    child_patterns, trans_table, child_parent, child_octant, partner_src, partner_off, partner_count
):
    _, _, azimuth_in, _ = child_patterns.shape
    polar_out = NTHETA_P
    azimuth_out = trans_table.shape[2] // polar_out
    parent_slots = partner_src.shape[0] // lax.axis_size("clus")
    cluster_index = lax.axis_index("clus")
    direction_index = lax.axis_index("dir")
    parents = child_parent[0]
    polar_matrix = polar_matrix_of(NTHETA_P, NTHETA_C)
    onehot = (parents[None, :] == jnp.arange(parent_slots, dtype=jnp.int32)[:, None]).astype(
        jnp.float32
    )
    own_rows = jnp.mod(
        direction_index * azimuth_out + jnp.arange(azimuth_out, dtype=jnp.int32), NPHI_P
    )
    cosine, sine_part = shift_phases(child_octant, own_rows, NPHI_P, polar_out)
    extended = with_halo(child_patterns, (("dir", 2),), 2)
    gather_matrix = azimuth_matrix_of(
        jnp.arange(azimuth_out, dtype=jnp.int32),
        jnp.arange(azimuth_in + 4, dtype=jnp.int32) - 2,
        NPHI_P,
        NPHI_C,
    )
    along_azimuth = jnp.einsum("pc,kacz->kapz", gather_matrix, extended, precision=highest)
    refined = jnp.einsum("kapz,tz->kapt", along_azimuth, polar_matrix, precision=highest)
    shifted = forward_shift(refined, cosine, sine_part)
    radiation = jnp.einsum("gk,kapt->gapt", onehot, shifted, precision=highest)
    flattened = radiation.reshape(parent_slots, 2, azimuth_out * polar_out)
    sources = lax.all_gather(flattened, "clus", axis=0, tiled=True)
    first_row = cluster_index * parent_slots
    own_src = lax.dynamic_slice_in_dim(partner_src, first_row, parent_slots, 0)
    own_off = lax.dynamic_slice_in_dim(partner_off, first_row, parent_slots, 0)
    own_count = lax.dynamic_slice_in_dim(partner_count, first_row, parent_slots, 0)
    incoming = translate(sources, trans_table, own_src, own_off, own_count)
    incoming = incoming.reshape(parent_slots, 2, azimuth_out, polar_out)
    return_matrix = azimuth_matrix_of(
        jnp.arange(azimuth_out + 6, dtype=jnp.int32) - 3,
        jnp.arange(azimuth_in, dtype=jnp.int32),
        NPHI_P,
        NPHI_C,
    )
    per_child = jnp.einsum("gk,gapt->kapt", onehot, incoming, precision=highest)
    returned = conjugate_shift(per_child, cosine, sine_part)
    coarse_own = jnp.einsum("kapt,tz->kapz", returned, polar_matrix, precision=highest)
    coarse = with_halo(coarse_own, (("dir", 2),), 3)
    return jnp.einsum("pc,kapz->kacz", return_matrix, coarse, precision=highest)


def solution(mesh):
    def on_device(child_patterns, trans_table, *rest):
        peers = lax.axis_size("clus")
        children, _, azimuth_in, polar_in = child_patterns.shape
        flat_rows = trans_table.shape[2] // LANES
        fits = (
            azimuth_in % (8 * PERIOD_C) == 0
            and polar_in == LANES
            and flat_rows * PERIOD_C == ROWS_PER_PERIOD * azimuth_in
            and flat_rows % peers == 0
            and peers & (peers - 1) == 0
            and peers > 2
            and children % BLOCK == 0
        )
        plan = on_device_exchange if fits else on_device_gather
        return plan(child_patterns, trans_table, *rest)

    return jax.shard_map(
        on_device,
        mesh=mesh,
        in_specs=(
            P("clus", None, "dir", None),
            P(None, None, "dir"),
            P("clus", None),
            P("clus"),
            P(),
            P(),
            P(),
        ),
        out_specs=P("clus", None, "dir", None),
        check_vma=False,
    )
```

```python
import functools
import math

import jax
import jax.numpy as jnp
import numpy as np
from jax import lax
from jax.experimental import pallas as pl
from jax.experimental.pallas import tpu as pltpu
from jax.sharding import PartitionSpec as P


NTHETA_C = 128
NPHI_C = 256
NTHETA_P = 192
NPHI_P = 384

LANES = 128
PERIOD_P = 6
PERIOD_C = 4
ROWS_PER_PERIOD = PERIOD_P * NTHETA_P // LANES
GROUP = 8
TILE = 8
TOGETHER = 2
BLOCK = 2 * GROUP

phase_scale = 8.0 * math.pi
highest = lax.Precision.HIGHEST
f32 = jnp.float32
bf16 = jnp.bfloat16


def lagrange(offset):
    weights = []
    for anchor in range(5):
        factor = 1.0
        for neighbour in range(5):
            if neighbour != anchor:
                factor = factor * (offset - neighbour) / (anchor - neighbour)
        weights.append(factor)
    return weights


TAPS_A = [float(w) for w in lagrange(5.0 / 3.0)]
TAPS_B = [float(w) for w in lagrange(7.0 / 3.0)]


SUMS = [(TAPS_A[i] + TAPS_A[4 - i]) / 2 for i in range(2)]
DIFFS = [(TAPS_A[i] - TAPS_A[4 - i]) / 2 for i in range(2)]
CENTRE = TAPS_A[2]


def polar_matrix_np():
    target = (np.arange(NTHETA_P, dtype=np.float32) + np.float32(0.5)) * NTHETA_C / NTHETA_P - np.float32(0.5)
    start = np.clip(np.floor(target + 0.5).astype(np.int32) - 2, 0, NTHETA_C - 5)
    weights = lagrange((target - start).astype(np.float64))
    matrix = np.zeros((NTHETA_P, NTHETA_C), np.float64)
    for anchor in range(5):
        matrix[np.arange(NTHETA_P), start + anchor] += weights[anchor]
    return matrix.astype(np.float32)


def polar_blocks():
    matrix = polar_matrix_np().T
    even = np.zeros((NTHETA_C, 2 * LANES), np.float32)
    odd = np.zeros((NTHETA_C, 2 * LANES), np.float32)
    half = NTHETA_P - LANES
    even[:, :NTHETA_P] = matrix
    odd[:, :LANES] = matrix[:, half:]
    odd[:, 2 * LANES - half :] = matrix[:, :half]
    return even, odd


def split_np(matrix):
    high = matrix.astype(bf16)
    low = (matrix - high.astype(np.float32)).astype(bf16)
    return high, low


def split(values):
    high = values.astype(bf16)
    low = (values - high.astype(f32)).astype(bf16)
    return high, low


def dot(left, right):
    return jnp.dot(left, right, preferred_element_type=f32)


def spread_dot(values, matrix_ref, i):
    high, low = split(values)
    depth = values.shape[1]
    return dot(jnp.concatenate([high, low], axis=1), matrix_ref[i, : 2 * depth]) + dot(high, matrix_ref[i, 2 * depth :])


def gather_dot(high, low, matrix_ref, i):
    width = matrix_ref.shape[2] // 2
    both = dot(high, matrix_ref[i])
    return both[:, :width] + (both[:, width:] + dot(low, matrix_ref[i, :, :width]))


SIN_COEFFS = [(-1) ** k * math.pi ** (2 * k + 1) / math.factorial(2 * k + 1) for k in range(7)]
COS_COEFFS = [(-1) ** k * math.pi ** (2 * k) / math.factorial(2 * k) for k in range(7)]


def sincos_turns(turns):
    rest = turns - jnp.round(turns)
    square = rest * rest
    sine = jnp.full_like(square, SIN_COEFFS[-1])
    for coeff in SIN_COEFFS[-2::-1]:
        sine = sine * square + coeff
    sine = sine * rest
    cosine = jnp.full_like(square, COS_COEFFS[-1])
    for coeff in COS_COEFFS[-2::-1]:
        cosine = cosine * square + coeff
    return 2.0 * sine * cosine, 1.0 - 2.0 * sine * sine


def fill_phases(direction, out_ref):
    periods = out_ref.shape[3]
    lane = lax.broadcasted_iota(jnp.int32, (periods, LANES), 1)
    period = lax.broadcasted_iota(jnp.int32, (periods, LANES), 0)
    first = direction * (PERIOD_P * periods)

    def two_rows(r, carry):
        for i in range(3):
            position = lane + i * LANES
            second = (position >= NTHETA_P).astype(jnp.int32)
            polar_index = position - second * NTHETA_P
            azimuth_index = first + period * PERIOD_P + 2 * r + second
            sin_polar, cos_polar = sincos_turns((polar_index.astype(f32) + 0.5) / (2 * NTHETA_P))
            sin_azimuth, cos_azimuth = sincos_turns(azimuth_index.astype(f32) / NPHI_P)
            along_x = 4.0 * sin_polar * cos_azimuth
            along_y = 4.0 * sin_polar * sin_azimuth
            along_z = 4.0 * cos_polar
            w = 3 * r + i
            for octant in (0, 2, 4, 6):
                turns = along_x + along_y if octant % 4 == 0 else along_x - along_y
                turns = turns + along_z if octant < 4 else turns - along_z
                sine, cosine = sincos_turns(turns)
                out_ref[octant, 0, w] = cosine
                out_ref[octant, 1, w] = sine
                out_ref[7 - octant, 0, w] = cosine
                out_ref[7 - octant, 1, w] = -sine
        return carry

    lax.fori_loop(0, PERIOD_P // 2, two_rows, 0)


def edge_rows(periods):
    return [(w, 0) for w in (1, 2, 3, 4)] + [(w, periods - 1) for w in (6, 7, 8)]


def rows_kernel(
    octants_hbm, x_ref, blocks_ref, held_ref, last_ref, first_ref, phase_ref, edge_phase_ref, blocks_out, octants_ref, sem, blocks_sem, octants_sem
):
    pairs, azimuth_in, _ = x_ref.shape
    periods = phase_ref.shape[3]
    copy = pltpu.make_async_copy(x_ref, held_ref, sem)
    copy.start()
    blocks_copy = pltpu.make_async_copy(blocks_ref, blocks_out, blocks_sem)
    blocks_copy.start()
    octants_copy = pltpu.make_async_copy(octants_hbm, octants_ref, octants_sem)
    octants_copy.start()
    fill_phases(lax.axis_index("dir"), phase_ref)

    octants_copy.wait()

    def edges_of(step, carry):
        for j in range(GROUP):
            k = step * GROUP + j
            octant = octants_ref[k]
            for e, (w, m) in enumerate(edge_rows(periods)):
                for i in range(2):
                    edge_phase_ref[e, i, pl.ds(k, 1), :] = phase_ref[octant, i, w, m : m + 1, :]
        return carry

    lax.fori_loop(0, pairs // 2 // GROUP, edges_of, 0)
    copy.wait()
    for part in range(2):
        source = pl.ds(part, pairs // 2, stride=2)
        target = slice(part * (pairs // 2), (part + 1) * (pairs // 2))
        last_ref[target] = held_ref[source, azimuth_in - 1, :]
        for i in range(2):
            first_ref[i, target] = held_ref[source, i, :]
    blocks_copy.wait()


def both_taps(rows):
    even = SUMS[0] * (rows[0] + rows[4]) + SUMS[1] * (rows[1] + rows[3]) + CENTRE * rows[2]
    odd = DIFFS[0] * (rows[0] - rows[4]) + DIFFS[1] * (rows[1] - rows[3])
    return even + odd, even - odd


def both_taps_transposed(first, second):
    total, difference = first + second, first - second
    outer = [SUMS[i] * total for i in range(2)]
    inner = [DIFFS[i] * difference for i in range(2)]
    return [outer[0] + inner[0], outer[1] + inner[1], CENTRE * total, outer[1] - inner[1], outer[0] - inner[0]]


def main_kernel(peers, parents_ref, octants_ref, x_ref, table_ref, phase_ref, spread_ref, *rest):
    flat_ref, slice_ref, az_e, az_o, res_e, res_o, acc, flat, table_sem = rest
    children = octants_ref.shape[0]
    periods = phase_ref.shape[3]
    azimuth_in = periods * PERIOD_C
    own = acc.shape[0]
    me = lax.axis_index("clus")
    share = ROWS_PER_PERIOD * periods // peers
    first_tile = me * (2 * share) // 8
    table_rows = pl.ds(pl.multiple_of(first_tile * 8, 8), slice_ref.shape[1])
    table_copy = pltpu.make_async_copy(table_ref.at[:, table_rows, :], slice_ref, table_sem)
    table_copy.start()
    acc[...] = jnp.zeros_like(acc)
    sublane = lax.broadcasted_iota(jnp.int32, (periods, LANES), 0)

    def azimuth(block):
        for kp in range(2 * BLOCK):
            start = pl.multiple_of((block * (2 * BLOCK) + kp) * azimuth_in, 8)
            x = [x_ref[pl.ds(start + u, periods, stride=PERIOD_C), :] for u in range(PERIOD_C)]
            left = jnp.where(sublane == 0, 0.0, pltpu.roll(x[3], 1, 0))
            right = [jnp.where(sublane == periods - 1, 0.0, pltpu.roll(x[i], periods - 1, 0)) for i in range(2)]
            lower = [left, x[0], x[1], x[2], x[3]]
            upper = [x[1], x[2], x[3], right[0], right[1]]
            rows = [x[0], *both_taps(lower), x[2], *both_taps(upper)]
            for r in range(3):
                base = (kp * 3 + r) * periods
                az_e[base : base + periods, :] = rows[2 * r]
                az_o[base : base + periods, :] = rows[2 * r + 1]

    def polar():
        res_e[...] = spread_dot(az_e[...], spread_ref, 0)
        res_o[...] = spread_dot(az_o[...], spread_ref, 1)

    def shift(block):
        for k in range(BLOCK):
            octant = octants_ref[block * BLOCK + k]
            parent = parents_ref[block * BLOCK + k]
            for r in range(3):
                parts = []
                for part in range(2):
                    rows = pl.ds(((2 * k + part) * 3 + r) * periods, periods)
                    middle = res_e[rows, LANES:] + res_o[rows, LANES:]
                    parts.append((res_e[rows, :LANES], middle, res_o[rows, :LANES]))
                for i in range(3):
                    w = 3 * r + i
                    real, imaginary = parts[0][i], parts[1][i]
                    cosine, sine = phase_ref[octant, 0, w], phase_ref[octant, 1, w]
                    acc[parent, 0, w] += real * cosine - imaginary * sine
                    acc[parent, 1, w] += real * sine + imaginary * cosine

    def one_block(block, carry):
        azimuth(block)
        polar()
        shift(block)
        return carry

    lax.fori_loop(0, children // BLOCK, one_block, 0)
    for gp in range(2 * own):
        for w in range(ROWS_PER_PERIOD):
            flat[pl.ds(gp * ROWS_PER_PERIOD * periods + w, periods, stride=ROWS_PER_PERIOD), :] = acc[gp // 2, gp % 2, w]
        for q in range(peers):
            source = gp * ROWS_PER_PERIOD * periods + q * share
            target = (q * 2 * own + gp) * share
            flat_ref[target : target + share, :] = flat[source : source + share, :]
    table_copy.wait()


def one_hot(parents, own):
    index = lax.broadcasted_iota(jnp.int32, (own, parents.shape[1]), 0)
    return (index == parents).astype(f32)


def dot2(exact, values):
    exact = exact.astype(bf16)
    high, low = split(values)
    return dot(exact, high) + dot(exact, low)


def fix_kernel(
    peers, own, parents_ref, before_ref, after_ref, flat_ref, edge_phase_ref, spread_ref, *rest
):
    outs, (fixed,) = rest[:peers], rest[peers:]
    pairs = before_ref.shape[0]
    children = pairs // 2
    chunk_rows = outs[0].shape[0]
    share = chunk_rows // (2 * own)
    periods = share * peers // ROWS_PER_PERIOD
    fixed[...] = flat_ref[...]
    left, right = before_ref[...], [after_ref[0], after_ref[1]]
    a, b = TAPS_A, TAPS_B
    even = jnp.concatenate([b[0] * left, a[3] * right[0] + a[4] * right[1]], axis=0)
    odd = jnp.concatenate([a[0] * left, b[3] * right[0] + b[4] * right[1]], axis=0)
    even = spread_dot(even, spread_ref, 0)
    odd = spread_dot(odd, spread_ref, 1)
    first, last = slice(0, pairs), slice(pairs, 2 * pairs)
    low, high = slice(0, LANES), slice(LANES, 2 * LANES)
    refined = [
        odd[first, high],
        odd[first, low],
        even[first, low],
        even[first, high],
        even[last, low],
        even[last, high] + odd[last, high],
        odd[last, low],
    ]
    shifted_rows = []
    for e, rows in enumerate(refined):
        real, imaginary = rows[:children], rows[children:]
        cosine, sine = edge_phase_ref[e, 0], edge_phase_ref[e, 1]
        shifted_rows.append(real * cosine - imaginary * sine)
        shifted_rows.append(real * sine + imaginary * cosine)
    summed = dot2(one_hot(parents_ref[...], own), jnp.concatenate(shifted_rows, axis=1))
    for e, (w, m) in enumerate(edge_rows(periods)):
        q, row = divmod(ROWS_PER_PERIOD * m + w, share)
        for part in range(2):
            rows = pl.ds(q * chunk_rows + part * share + row, own, stride=2 * share)
            column = (2 * e + part) * LANES
            fixed[rows, :] = fixed[rows, :] + summed[:, column : column + LANES]
    me = lax.axis_index("clus")
    for d in range(peers):
        start = pl.multiple_of((me ^ d) * chunk_rows, 8)
        outs[d][...] = fixed[pl.ds(start, chunk_rows), :]


def widen_kernel(source_ref, offset_ref, count_ref, table_ref, wide_ref, operator_ref):
    targets, partners = source_ref.shape
    offsets, frame, _ = table_ref.shape

    def some_offsets(i, carry):
        for j in range(4):
            wide_ref[pl.ds(pl.multiple_of((i * 4 + j) * frame, 8), frame), :] = table_ref[i * 4 + j].astype(f32)
        return carry

    whole_steps = offsets // 4
    lax.fori_loop(0, whole_steps, some_offsets, 0)
    for offset in range(whole_steps * 4, offsets):
        wide_ref[offset * frame : (offset + 1) * frame, :] = table_ref[offset].astype(f32)
    wide_ref[offsets * frame :, :] = jnp.zeros((frame, LANES), f32)

    shape = (targets, targets)
    row, lane = (lax.broadcasted_iota(jnp.int32, shape, d) for d in range(2))
    count = jnp.sum(jnp.where(row == lane, count_ref[...], 0), axis=1, keepdims=True)
    operator = jnp.full(shape, offsets, jnp.int32)
    for p in range(partners):
        here = (lane == source_ref[:, p : p + 1]) & (p < count)
        operator = jnp.where(here, offset_ref[:, p : p + 1], operator)
    operator_ref[...] = operator * frame


def doubled(chunk, real_twice, imag_twice, first, own, share, frame, skip):
    for g in range(own):
        for part, twice in enumerate((real_twice, imag_twice)):
            rows = chunk[(2 * g + part) * share : (2 * g + part + 1) * share, :]
            base = (first + g) * frame + skip
            twice[pl.ds(base, share, stride=2), :] = rows
            twice[pl.ds(base + 1, share, stride=2), :] = rows


def add_sources(sums, targets, devices, own, frame, operator_ref, wide_ref, real_twice, imag_twice):
    for number, device in enumerate(devices):
        for g in range(own):
            source = slice((number * own + g) * frame, (number * own + g + 1) * frame)
            real, imaginary = real_twice[source, :], imag_twice[source, :]
            for i, target in enumerate(targets):
                first = pl.multiple_of(operator_ref[target, device * own + g], 8)
                operator = wide_ref[pl.ds(first, frame), :]
                sums[i] = (sums[i][0] + operator * real, sums[i][1] + operator * imaginary)
    return sums


def gather_kernel(peers, frame, masks, operator_ref, wide_ref, *rest):
    chunks, rest = rest[: len(masks)], rest[len(masks) :]
    before, (real_sum, imag_sum, real_twice, imag_twice) = rest[:-4], rest[-4:]
    me = lax.axis_index("clus")
    targets = operator_ref.shape[0]
    own = targets // peers
    share = chunks[0].shape[0] // (2 * own)
    skip = lax.rem(me * (2 * share), 8)
    for number, chunk in enumerate(chunks):
        doubled(chunk, real_twice, imag_twice, number * own, own, share, frame, skip)

    def some_targets(i, carry):
        some = [i * TOGETHER + j for j in range(TOGETHER)]
        places = [pl.ds(pl.multiple_of(target * frame, 8), frame) for target in some]
        if before:
            sums = [tuple(ref[place, :] for ref in before) for place in places]
        else:
            sums = [(jnp.zeros((frame, LANES), f32),) * 2 for _ in some]
        sums = add_sources(sums, some, [me ^ d for d in masks], own, frame, operator_ref, wide_ref, real_twice, imag_twice)
        for place, (by_real, by_imag) in zip(places, sums):
            real_sum[place, :] = by_real
            imag_sum[place, :] = by_imag
        return carry

    lax.fori_loop(0, targets // TOGETHER, some_targets, 0)


def translate_kernel(peers, frame, mask, targets, operator_ref, wide_ref, real_sum, imag_sum, *rest):
    if len(rest) == 5 + len(targets):
        chunk, real_twice, imag_twice = rest[:3]
        prepare = True
    else:
        real_twice, imag_twice = rest[:2]
        prepare = False
    outs, (total_real, total_imag) = rest[-2 - len(targets) : -2], rest[-2:]
    me = lax.axis_index("clus")
    own = operator_ref.shape[0] // peers
    share = outs[0].shape[0] // (2 * own)
    skip = lax.rem(me * (2 * share), 8)
    if prepare:
        doubled(chunk, real_twice, imag_twice, 0, own, share, frame, skip)
    even, odd = pl.ds(skip, share, stride=2), pl.ds(skip + 1, share, stride=2)
    for out, d in zip(outs, targets):
        first = (me ^ d) * own

        def some_targets(i, carry):
            places = [i * TOGETHER + j for j in range(TOGETHER)]
            some = [first + g for g in places]
            rows = [pl.ds(pl.multiple_of(target * frame, 8), frame) for target in some]
            sums = [(real_sum[r, :], imag_sum[r, :]) for r in rows]
            sums = add_sources(sums, some, [me ^ mask], own, frame, operator_ref, wide_ref, real_twice, imag_twice)
            for j, (g, (by_real, by_imag)) in enumerate(zip(places, sums)):
                total_real[j] = by_real
                total_imag[j] = by_imag
                row = g * (2 * share)
                out[pl.ds(row, share), :] = total_real[j, even, :] - total_imag[j, odd, :]
                out[pl.ds(row + share, share), :] = total_real[j, odd, :] + total_imag[j, even, :]
            return carry

        lax.fori_loop(0, own // TOGETHER, some_targets, 0)


def edge_kernel(peers, parents_ref, edge_phase_ref, gather_ref, *rest):
    chunks = rest[:peers]
    incoming_ref, next_ref, prev_ref, flat = rest[peers:]
    own2, _, periods, _ = incoming_ref.shape
    own = own2 // 2
    pairs = prev_ref.shape[0]
    flat_rows = ROWS_PER_PERIOD * periods
    share = flat_rows // peers
    me = lax.axis_index("clus")
    for gp in range(own2):
        for d in range(peers):
            flat[pl.ds(gp * flat_rows + (me ^ d) * share, share), :] = chunks[d][gp * share : (gp + 1) * share, :]
    edges = []
    for w, m in edge_rows(periods):
        for part in range(2):
            edges.append(flat[pl.ds(part * flat_rows + ROWS_PER_PERIOD * m + w, own, stride=2 * flat_rows), :])
    per_child = dot2(one_hot(parents_ref[...], own).T, jnp.concatenate(edges, axis=1))
    returned = []
    for e in range(len(edges) // 2):
        real = per_child[:, 2 * e * LANES : (2 * e + 1) * LANES]
        imaginary = per_child[:, (2 * e + 1) * LANES : (2 * e + 2) * LANES]
        cosine, sine = edge_phase_ref[e, 0], edge_phase_ref[e, 1]
        returned.append(
            jnp.concatenate([real * cosine + imaginary * sine, imaginary * cosine - real * sine], axis=0)
        )
    join = functools.partial(jnp.concatenate, axis=1)
    even = jnp.concatenate([join([returned[2], returned[3]]), join([returned[4], returned[5]])], axis=0)
    odd = jnp.concatenate([join([returned[0], returned[1]]), join([returned[5], returned[6]])], axis=0)
    even = gather_dot(*split(even), gather_ref, 0)
    odd = gather_dot(*split(odd), gather_ref, 1)
    a, b = TAPS_A, TAPS_B
    prev_ref[...] = a[0] * odd[:pairs] + b[0] * even[:pairs]
    next_ref[0] = a[3] * even[pairs:] + b[3] * odd[pairs:]
    next_ref[1] = a[4] * even[pairs:] + b[4] * odd[pairs:]
    for gp in range(own2):
        for w in range(ROWS_PER_PERIOD):
            incoming_ref[gp, w] = flat[pl.ds(gp * flat_rows + w, periods, stride=ROWS_PER_PERIOD), :]


def disaggregate_kernel(parents_ref, octants_ref, incoming_ref, phase_ref, gather_ref, out_ref, edge_ref, lhs, coarse_e, coarse_o, whole_out, sems):
    periods = incoming_ref.shape[2]
    azimuth_in = periods * PERIOD_C
    sublane = lax.broadcasted_iota(jnp.int32, (periods, LANES), 0)
    inner = pl.ds(TILE, azimuth_in - 2 * TILE)

    def shift(block):
        for k in range(BLOCK):
            octant = octants_ref[block * BLOCK + k]
            parent = parents_ref[block * BLOCK + k]
            for r in range(3):
                for i in range(3):
                    w = 3 * r + i
                    real, imaginary = incoming_ref[2 * parent, w], incoming_ref[2 * parent + 1, w]
                    cosine, sine = phase_ref[octant, 0, w], phase_ref[octant, 1, w]
                    returned = (real * cosine + imaginary * sine, imaginary * cosine - real * sine)
                    for part in range(2):
                        base = ((2 * k + part) * 3 + r) * periods
                        lhs[base : base + periods, i * LANES : (i + 1) * LANES] = returned[part]

    def polar():
        high, low = split(lhs[...])
        coarse_e[...] = gather_dot(high[:, : 2 * LANES], low[:, : 2 * LANES], gather_ref, 0)
        coarse_o[...] = gather_dot(high[:, LANES:], low[:, LANES:], gather_ref, 1)

    def azimuth(block):
        for j in range(2 * BLOCK):
            c = []
            for r in range(3):
                base = (j * 3 + r) * periods
                c.append(coarse_e[base : base + periods, :])
                c.append(coarse_o[base : base + periods, :])
            lower = both_taps_transposed(c[1], c[2])
            upper = both_taps_transposed(c[4], c[5])
            down = [jnp.where(sublane == 0, 0.0, pltpu.roll(upper[i], 1, 0)) for i in (3, 4)]
            up = jnp.where(sublane == periods - 1, 0.0, pltpu.roll(lower[0], periods - 1, 0))
            rows = [c[0] + lower[1] + down[0], lower[2] + upper[0] + down[1], c[3] + lower[3] + upper[1], lower[4] + upper[2] + up]
            kp = block * (2 * BLOCK) + j
            for u in range(PERIOD_C):
                whole_out[kp, pl.ds(u, periods, stride=PERIOD_C), :] = rows[u]
            edge_ref[0, kp] = whole_out[kp, :TILE, :]
            edge_ref[1, kp] = whole_out[kp, azimuth_in - TILE :, :]

    def written(block):
        some = pl.ds(block * (2 * BLOCK), 2 * BLOCK)
        return pltpu.make_async_copy(whole_out.at[some, inner, :], out_ref.at[some, inner, :], sems.at[block])

    def one_block(block, carry):
        shift(block)
        polar()
        azimuth(block)
        written(block).start()
        return carry

    blocks = octants_ref.shape[0] // BLOCK
    lax.fori_loop(0, blocks, one_block, 0)
    for block in range(blocks):
        written(block).wait()


def finish_kernel(edge_ref, before_ref, after_ref, part_ref, out_ref, tiles, sems):
    pairs, azimuth_in, _ = out_ref.shape
    tiles[...] = edge_ref[...]
    flat = tiles.reshape(2 * pairs * TILE, LANES)
    ends = ((0, 0, before_ref.at[0]), (0, 1, before_ref.at[1]), (1, TILE - 1, after_ref))
    copies = []
    for i, start in enumerate((0, azimuth_in - TILE)):
        for end, row, values_ref in ends:
            if end == i:
                for part in range(2):
                    for k in range(0, pairs // 2, 8):
                        source = slice(part * (pairs // 2) + k, part * (pairs // 2) + k + 8)
                        rows = pl.ds((i * pairs + 2 * k + part) * TILE + row, 8, stride=2 * TILE)
                        flat[rows, :] = flat[rows, :] + values_ref[source, :]
        copy = pltpu.make_async_copy(tiles.at[i], out_ref.at[:, pl.ds(start, TILE), :], sems.at[i])
        copy.start()
        copies.append(copy)
    for copy in copies:
        copy.wait()


def shifted(values, axis, by):
    size = lax.axis_size(axis)
    return lax.ppermute(values, axis, [(i, (i + by) % size) for i in range(size)])


def exchanged(values, axis, mask):
    size = lax.axis_size(axis)
    return lax.ppermute(values, axis, [(i, i ^ mask) for i in range(size)])


SMEM = pl.BlockSpec(memory_space=pltpu.SMEM)
VMEM = pl.BlockSpec(memory_space=pltpu.VMEM)
HBM = pl.BlockSpec(memory_space=pltpu.HBM)


def in_hbm(values):
    return pltpu.with_memory_space_constraint(values, pltpu.HBM)


def local_call(kernel, out_shape, in_specs, scratch, grant, flops=1_000_000, bytes_accessed=1_000_000, out_specs=None, aliases={}):
    return pl.pallas_call(
        kernel,
        out_shape=out_shape,
        in_specs=in_specs,
        out_specs=jax.tree.map(lambda _: VMEM, out_shape) if out_specs is None else out_specs,
        scratch_shapes=scratch,
        input_output_aliases=aliases,
        compiler_params=pltpu.CompilerParams(vmem_limit_bytes=grant << 20),
        cost_estimate=pl.CostEstimate(flops=flops, bytes_accessed=bytes_accessed, transcendentals=0),
    )


def on_device_exchange(
    child_patterns, trans_table, child_parent, child_octant, partner_src, partner_off, partner_count
):
    children, _, azimuth_in, polar_in = child_patterns.shape
    pairs = 2 * children
    peers = lax.axis_size("clus")
    parent_total, _ = partner_src.shape
    own = parent_total // peers
    periods = azimuth_in // PERIOD_C
    flat_rows = ROWS_PER_PERIOD * periods
    share = flat_rows // peers
    offsets = trans_table.shape[0]
    array = lambda *shape: jax.ShapeDtypeStruct(shape, f32)
    buffer = lambda *shape: pltpu.VMEM(shape, f32)
    parents = child_parent[0]

    edges = len(edge_rows(periods))
    even, odd = polar_blocks()
    blocks_np = np.stack([np.concatenate([h, h, l]) for h, l in (split_np(even), split_np(odd))])
    held, last, first, phases, edge_phases, spread = local_call(
        rows_kernel,
        [
            array(pairs, azimuth_in, polar_in),
            array(pairs, polar_in),
            array(2, pairs, polar_in),
            array(8, 2, ROWS_PER_PERIOD, periods, LANES),
            array(edges, 2, children, LANES),
            jax.ShapeDtypeStruct(blocks_np.shape, bf16),
        ],
        [HBM, HBM, HBM],
        [pltpu.SMEM((children,), jnp.int32)] + [pltpu.SemaphoreType.DMA] * 3,
        12,
    )(in_hbm(child_octant), in_hbm(child_patterns.reshape(pairs, azimuth_in, polar_in)), in_hbm(jnp.asarray(blocks_np)))
    before = shifted(last, "dir", 1)
    after = shifted(first, "dir", -1)

    odd_gather = np.concatenate([odd.T[LANES:], odd.T[:LANES]])
    gather = np.stack([np.concatenate(split_np(m), axis=1) for m in (even.T, odd_gather)])

    frame = max(-(-((q * 2 * share) % 8 + 2 * share) // 8) * 8 for q in range(peers))
    view = trans_table.reshape(offsets, 2, flat_rows, LANES).transpose(0, 2, 1, 3).reshape(offsets, 2 * flat_rows, LANES)
    blocks = children // BLOCK
    rows = 2 * BLOCK * 3 * periods
    flat, table = local_call(
        functools.partial(main_kernel, peers),
        [array(2 * own * flat_rows, LANES), jax.ShapeDtypeStruct((offsets, frame, LANES), bf16)],
        [SMEM] * 2 + [VMEM, HBM, VMEM, VMEM],
        [
            buffer(rows, LANES),
            buffer(rows, LANES),
            buffer(rows, 2 * LANES),
            buffer(rows, 2 * LANES),
            buffer(own, 2, ROWS_PER_PERIOD, periods, LANES),
            buffer(2 * own * flat_rows, LANES),
            pltpu.SemaphoreType.DMA,
        ],
        24,
        flops=4_000_000_000,
        bytes_accessed=12_000_000,
    )(parents, child_octant, held.reshape(pairs * azimuth_in, polar_in), in_hbm(view), phases, spread)

    chunk = array(2 * own * share, LANES)
    sent = local_call(
        functools.partial(fix_kernel, peers, own), [chunk] * peers, [VMEM] * 6, [buffer(2 * own * flat_rows, LANES)], 8
    )(child_parent, before, after, flat, edge_phases, spread)

    masks = sorted(range(1, peers), key=lambda d: bin(d).count("1"))
    middle, late = masks[:-1], masks[-1]
    received = {0: sent[0]}
    for d in middle:
        received[d] = exchanged(sent[d], "clus", d)
    received[late] = exchanged(sent[late], "clus", late)

    wide, operator = local_call(
        widen_kernel,
        [array((offsets + 1) * frame, LANES), jax.ShapeDtypeStruct((parent_total, parent_total), jnp.int32)],
        [VMEM] * 4,
        [],
        20,
        flops=50_000_000,
        bytes_accessed=8_000_000,
    )(partner_src, partner_off, partner_count.reshape(1, parent_total), table)

    sums = []
    for group in ([0], middle):
        sums = local_call(
            functools.partial(gather_kernel, peers, frame, tuple(group)),
            [array(parent_total * frame, LANES)] * 2,
            [SMEM] + [VMEM] * (1 + len(group) + len(sums)),
            [buffer(len(group) * own * frame, LANES)] * 2,
            20,
            flops=40_000_000 * len(group),
            bytes_accessed=4_000_000 * len(group),
        )(operator, wide, *[received[d] for d in group], *sums)

    back = {}
    last_sources = [received[late]]
    for targets in ([late], middle, [0]):
        prepare = len(last_sources) == 1
        results = local_call(
            functools.partial(translate_kernel, peers, frame, late, tuple(targets)),
            ([array(own * frame, LANES)] * 2 if prepare else []) + [chunk] * len(targets),
            [SMEM] + [VMEM] * (3 + len(last_sources)),
            [buffer(TOGETHER, frame, LANES)] * 2,
            20,
            flops=10_000_000 * len(targets),
            bytes_accessed=2_000_000 * len(targets),
        )(operator, wide, *sums, *last_sources)
        if prepare:
            last_sources, results = results[:2], results[2:]
        for d, result in zip(targets, results):
            back[d] = exchanged(result, "clus", d) if d else result

    incoming, to_next, to_prev = local_call(
        functools.partial(edge_kernel, peers),
        [array(2 * own, ROWS_PER_PERIOD, periods, LANES), array(2, pairs, polar_in), array(pairs, polar_in)],
        [VMEM] * (3 + peers),
        [buffer(2 * own * flat_rows, LANES)],
        8,
    )(child_parent, edge_phases, gather, *[back[d] for d in range(peers)])

    from_before = shifted(to_next, "dir", 1)
    from_after = shifted(to_prev, "dir", -1)

    inner, edge_tiles = local_call(
        disaggregate_kernel,
        [array(pairs, azimuth_in, polar_in), array(2, pairs, TILE, polar_in)],
        [SMEM] * 2 + [VMEM] * 3,
        [
            buffer(rows, 3 * LANES),
            buffer(rows, LANES),
            buffer(rows, LANES),
            buffer(pairs, azimuth_in, polar_in),
            pltpu.SemaphoreType.DMA((blocks,)),
        ],
        24,
        flops=4_000_000_000,
        bytes_accessed=12_000_000,
        out_specs=[HBM, VMEM],
    )(parents, child_octant, incoming, phases, gather)

    out = local_call(
        finish_kernel,
        array(pairs, azimuth_in, polar_in),
        [VMEM] * 3 + [HBM],
        [buffer(2, pairs, TILE, polar_in), pltpu.SemaphoreType.DMA((2,))],
        8,
        out_specs=HBM,
        aliases={3: 0},
    )(edge_tiles, from_before, from_after, in_hbm(inner))
    return out.reshape(child_patterns.shape)


def with_halo(shard, sides, width):
    for axis, dim in sides:
        size, length = (lax.axis_size(axis), shard.shape[dim])
        up = [(i, (i + 1) % size) for i in range(size)]
        down = [(j, i) for i, j in up]
        last = lax.slice_in_dim(shard, length - width, length, axis=dim)
        initial = lax.slice_in_dim(shard, 0, width, axis=dim)
        before = lax.ppermute(last, axis, up)
        after = lax.ppermute(initial, axis, down)
        shard = jnp.concatenate([before, shard, after], axis=dim)
    return shard


def lagrange_rows(offset):
    weights = []
    for anchor in range(5):
        factor = jnp.ones_like(offset)
        for neighbour in range(5):
            if neighbour != anchor:
                factor = factor * (offset - neighbour) / (anchor - neighbour)
        weights.append(factor)
    return weights


def polar_matrix_of(rows_out, rows_in):
    target = (jnp.arange(rows_out, dtype=jnp.float32) + 0.5) * rows_in / rows_out - 0.5
    start_row = jnp.clip(jnp.floor(target + 0.5).astype(jnp.int32) - 2, 0, rows_in - 5)
    weights = lagrange_rows(target - start_row.astype(jnp.float32))
    columns = jnp.arange(rows_in, dtype=jnp.int32)
    matrix = jnp.zeros((rows_out, rows_in), jnp.float32)
    for anchor in range(5):
        matrix = matrix + jnp.where(
            columns[None, :] == (start_row + anchor)[:, None], weights[anchor][:, None], 0.0
        )
    return matrix


def azimuth_matrix_of(out_index, in_index, total_out, total_in):
    target = (out_index * total_in).astype(jnp.float32) / total_out
    nearest = jnp.floor(target + 0.5).astype(jnp.int32)
    weights = lagrange_rows(target - nearest.astype(jnp.float32) + 2.0)
    matrix = jnp.zeros((out_index.shape[0], in_index.shape[0]), jnp.float32)
    for anchor in range(5):
        columns = nearest + anchor - 2
        matrix = matrix + jnp.where(
            in_index[None, :] == columns[:, None], weights[anchor][:, None], 0.0
        )
    return matrix


def shift_phases(octant, azimuth_index, azimuth_total, polar_total):
    azimuth = 2.0 * math.pi * azimuth_index.astype(jnp.float32) / azimuth_total
    polar = math.pi * (jnp.arange(polar_total, dtype=jnp.float32) + 0.5) / polar_total
    first_axis = jnp.sin(polar)[None, :] * jnp.cos(azimuth)[:, None]
    second_axis = jnp.sin(polar)[None, :] * jnp.sin(azimuth)[:, None]
    third_axis = jnp.cos(polar)[None, :] * jnp.ones_like(azimuth)[:, None]
    first_sign = (1 - 2 * (octant % 2)).astype(jnp.float32)
    second_sign = (1 - 2 * (octant // 2 % 2)).astype(jnp.float32)
    third_sign = (1 - 2 * (octant // 4)).astype(jnp.float32)
    phase_angle = phase_scale * (
        first_sign[:, None, None] * first_axis[None]
        + second_sign[:, None, None] * second_axis[None]
        + third_sign[:, None, None] * third_axis[None]
    )
    return (jnp.cos(phase_angle), jnp.sin(phase_angle))


def translate(sources, table, partner_src, partner_off, partner_count):
    live_mask = (
        jnp.arange(partner_src.shape[1], dtype=jnp.int32)[None, :] < partner_count[:, None]
    ).astype(jnp.float32)
    picked = sources[partner_src]
    operator = table[partner_off].astype(jnp.float32) * live_mask[:, :, None, None]
    real_part = jnp.sum(
        operator[:, :, 0] * picked[:, :, 0] - operator[:, :, 1] * picked[:, :, 1], axis=1
    )
    imaginary = jnp.sum(
        operator[:, :, 0] * picked[:, :, 1] + operator[:, :, 1] * picked[:, :, 0], axis=1
    )
    return jnp.stack([real_part, imaginary], axis=1)


def forward_shift(patterns, cosine, sine_part):
    real_part = patterns[:, 0] * cosine - patterns[:, 1] * sine_part
    imaginary = patterns[:, 0] * sine_part + patterns[:, 1] * cosine
    return jnp.stack([real_part, imaginary], axis=1)


def conjugate_shift(patterns, cosine, sine_part):
    real_part = patterns[:, 0] * cosine + patterns[:, 1] * sine_part
    imaginary = patterns[:, 1] * cosine - patterns[:, 0] * sine_part
    return jnp.stack([real_part, imaginary], axis=1)


def on_device_gather(
    child_patterns, trans_table, child_parent, child_octant, partner_src, partner_off, partner_count
):
    _, _, azimuth_in, _ = child_patterns.shape
    polar_out = NTHETA_P
    azimuth_out = trans_table.shape[2] // polar_out
    parent_slots = partner_src.shape[0] // lax.axis_size("clus")
    cluster_index = lax.axis_index("clus")
    direction_index = lax.axis_index("dir")
    parents = child_parent[0]
    polar_matrix = polar_matrix_of(NTHETA_P, NTHETA_C)
    onehot = (parents[None, :] == jnp.arange(parent_slots, dtype=jnp.int32)[:, None]).astype(
        jnp.float32
    )
    own_rows = jnp.mod(
        direction_index * azimuth_out + jnp.arange(azimuth_out, dtype=jnp.int32), NPHI_P
    )
    cosine, sine_part = shift_phases(child_octant, own_rows, NPHI_P, polar_out)
    extended = with_halo(child_patterns, (("dir", 2),), 2)
    gather_matrix = azimuth_matrix_of(
        jnp.arange(azimuth_out, dtype=jnp.int32),
        jnp.arange(azimuth_in + 4, dtype=jnp.int32) - 2,
        NPHI_P,
        NPHI_C,
    )
    along_azimuth = jnp.einsum("pc,kacz->kapz", gather_matrix, extended, precision=highest)
    refined = jnp.einsum("kapz,tz->kapt", along_azimuth, polar_matrix, precision=highest)
    shifted = forward_shift(refined, cosine, sine_part)
    radiation = jnp.einsum("gk,kapt->gapt", onehot, shifted, precision=highest)
    flattened = radiation.reshape(parent_slots, 2, azimuth_out * polar_out)
    sources = lax.all_gather(flattened, "clus", axis=0, tiled=True)
    first_row = cluster_index * parent_slots
    own_src = lax.dynamic_slice_in_dim(partner_src, first_row, parent_slots, 0)
    own_off = lax.dynamic_slice_in_dim(partner_off, first_row, parent_slots, 0)
    own_count = lax.dynamic_slice_in_dim(partner_count, first_row, parent_slots, 0)
    incoming = translate(sources, trans_table, own_src, own_off, own_count)
    incoming = incoming.reshape(parent_slots, 2, azimuth_out, polar_out)
    return_matrix = azimuth_matrix_of(
        jnp.arange(azimuth_out + 6, dtype=jnp.int32) - 3,
        jnp.arange(azimuth_in, dtype=jnp.int32),
        NPHI_P,
        NPHI_C,
    )
    per_child = jnp.einsum("gk,gapt->kapt", onehot, incoming, precision=highest)
    returned = conjugate_shift(per_child, cosine, sine_part)
    coarse_own = jnp.einsum("kapt,tz->kapz", returned, polar_matrix, precision=highest)
    coarse = with_halo(coarse_own, (("dir", 2),), 3)
    return jnp.einsum("pc,kapz->kacz", return_matrix, coarse, precision=highest)


def solution(mesh):
    def on_device(child_patterns, trans_table, *rest):
        peers = lax.axis_size("clus")
        children, _, azimuth_in, polar_in = child_patterns.shape
        flat_rows = trans_table.shape[2] // LANES
        fits = (
            azimuth_in % (8 * PERIOD_C) == 0
            and polar_in == LANES
            and flat_rows * PERIOD_C == ROWS_PER_PERIOD * azimuth_in
            and flat_rows % peers == 0
            and peers & (peers - 1) == 0
            and peers > 2
            and children % BLOCK == 0
        )
        plan = on_device_exchange if fits else on_device_gather
        return plan(child_patterns, trans_table, *rest)

    return jax.shard_map(
        on_device,
        mesh=mesh,
        in_specs=(
            P("clus", None, "dir", None),
            P(None, None, "dir"),
            P("clus", None),
            P("clus"),
            P(),
            P(),
            P(),
        ),
        out_specs=P("clus", None, "dir", None),
        check_vma=False,
    )
```

```python
import functools
import math

import jax
import jax.numpy as jnp
import numpy as np
from jax import lax
from jax.experimental import pallas as pl
from jax.experimental.pallas import tpu as pltpu
from jax.sharding import PartitionSpec as P


NTHETA_C = 128
NPHI_C = 256
NTHETA_P = 192
NPHI_P = 384

LANES = 128
PERIOD_P = 6
PERIOD_C = 4
ROWS_PER_PERIOD = PERIOD_P * NTHETA_P // LANES
GROUP = 8
TILE = 8
TOGETHER = 2
BLOCK = 2 * GROUP

phase_scale = 8.0 * math.pi
highest = lax.Precision.HIGHEST
f32 = jnp.float32
bf16 = jnp.bfloat16


def lagrange(offset):
    weights = []
    for anchor in range(5):
        factor = 1.0
        for neighbour in range(5):
            if neighbour != anchor:
                factor = factor * (offset - neighbour) / (anchor - neighbour)
        weights.append(factor)
    return weights


TAPS_A = [float(w) for w in lagrange(5.0 / 3.0)]
TAPS_B = [float(w) for w in lagrange(7.0 / 3.0)]


SUMS = [(TAPS_A[i] + TAPS_A[4 - i]) / 2 for i in range(2)]
DIFFS = [(TAPS_A[i] - TAPS_A[4 - i]) / 2 for i in range(2)]
CENTRE = TAPS_A[2]


def polar_matrix_np():
    target = (np.arange(NTHETA_P, dtype=np.float32) + np.float32(0.5)) * NTHETA_C / NTHETA_P - np.float32(0.5)
    start = np.clip(np.floor(target + 0.5).astype(np.int32) - 2, 0, NTHETA_C - 5)
    weights = lagrange((target - start).astype(np.float64))
    matrix = np.zeros((NTHETA_P, NTHETA_C), np.float64)
    for anchor in range(5):
        matrix[np.arange(NTHETA_P), start + anchor] += weights[anchor]
    return matrix.astype(np.float32)


def polar_blocks():
    matrix = polar_matrix_np().T
    even = np.zeros((NTHETA_C, 2 * LANES), np.float32)
    odd = np.zeros((NTHETA_C, 2 * LANES), np.float32)
    half = NTHETA_P - LANES
    even[:, :NTHETA_P] = matrix
    odd[:, :LANES] = matrix[:, half:]
    odd[:, 2 * LANES - half :] = matrix[:, :half]
    return even, odd


def split_np(matrix):
    high = matrix.astype(bf16)
    low = (matrix - high.astype(np.float32)).astype(bf16)
    return high, low


def split(values):
    high = values.astype(bf16)
    low = (values - high.astype(f32)).astype(bf16)
    return high, low


def dot(left, right):
    return jnp.dot(left, right, preferred_element_type=f32)


def spread_dot(values, matrix_ref, i):
    high, low = split(values)
    depth = values.shape[1]
    return dot(jnp.concatenate([high, low], axis=1), matrix_ref[i, : 2 * depth]) + dot(high, matrix_ref[i, 2 * depth :])


def gather_dot(high, low, matrix_ref, i):
    width = matrix_ref.shape[2] // 2
    both = dot(high, matrix_ref[i])
    return both[:, :width] + (both[:, width:] + dot(low, matrix_ref[i, :, :width]))


SIN_COEFFS = [(-1) ** k * math.pi ** (2 * k + 1) / math.factorial(2 * k + 1) for k in range(7)]
COS_COEFFS = [(-1) ** k * math.pi ** (2 * k) / math.factorial(2 * k) for k in range(7)]


def sincos_turns(turns):
    rest = turns - jnp.round(turns)
    square = rest * rest
    sine = jnp.full_like(square, SIN_COEFFS[-1])
    for coeff in SIN_COEFFS[-2::-1]:
        sine = sine * square + coeff
    sine = sine * rest
    cosine = jnp.full_like(square, COS_COEFFS[-1])
    for coeff in COS_COEFFS[-2::-1]:
        cosine = cosine * square + coeff
    return 2.0 * sine * cosine, 1.0 - 2.0 * sine * sine


def fill_phases(direction, out_ref):
    periods = out_ref.shape[3]
    lane = lax.broadcasted_iota(jnp.int32, (periods, LANES), 1)
    period = lax.broadcasted_iota(jnp.int32, (periods, LANES), 0)
    first = direction * (PERIOD_P * periods)

    def two_rows(r, carry):
        for i in range(3):
            position = lane + i * LANES
            second = (position >= NTHETA_P).astype(jnp.int32)
            polar_index = position - second * NTHETA_P
            azimuth_index = first + period * PERIOD_P + 2 * r + second
            sin_polar, cos_polar = sincos_turns((polar_index.astype(f32) + 0.5) / (2 * NTHETA_P))
            sin_azimuth, cos_azimuth = sincos_turns(azimuth_index.astype(f32) / NPHI_P)
            along_x = 4.0 * sin_polar * cos_azimuth
            along_y = 4.0 * sin_polar * sin_azimuth
            along_z = 4.0 * cos_polar
            w = 3 * r + i
            for octant in (0, 2, 4, 6):
                turns = along_x + along_y if octant % 4 == 0 else along_x - along_y
                turns = turns + along_z if octant < 4 else turns - along_z
                sine, cosine = sincos_turns(turns)
                out_ref[octant, 0, w] = cosine
                out_ref[octant, 1, w] = sine
                out_ref[7 - octant, 0, w] = cosine
                out_ref[7 - octant, 1, w] = -sine
        return carry

    lax.fori_loop(0, PERIOD_P // 2, two_rows, 0)


def edge_rows(periods):
    return [(w, 0) for w in (1, 2, 3, 4)] + [(w, periods - 1) for w in (6, 7, 8)]


def rows_kernel(x_ref, last_ref, first_ref, low, high, sems):
    pairs, azimuth_in, _ = x_ref.shape
    low_copy = pltpu.make_async_copy(x_ref.at[:, pl.ds(0, TILE), :], low, sems.at[0])
    high_copy = pltpu.make_async_copy(x_ref.at[:, pl.ds(azimuth_in - TILE, TILE), :], high, sems.at[1])
    low_copy.start()
    high_copy.start()
    low_copy.wait()
    high_copy.wait()
    low_rows, high_rows = (ref.reshape(pairs * TILE, LANES) for ref in (low, high))
    for part in range(2):
        for k in range(0, pairs // 2, 8):
            target = slice(part * (pairs // 2) + k, part * (pairs // 2) + k + 8)
            base = (2 * k + part) * TILE
            for i in range(2):
                first_ref[i, target] = low_rows[pl.ds(base + i, 8, stride=2 * TILE), :]
            last_ref[target] = high_rows[pl.ds(base + TILE - 1, 8, stride=2 * TILE), :]


def phase_kernel(*refs):
    octants_hbm, sources = refs[0], refs[1:5]
    (phase_ref, edge_phase_ref), targets = refs[5:7], refs[7:11]
    octants_ref, octants_sem, sems = refs[11:]
    periods = phase_ref.shape[3]
    octants_copy = pltpu.make_async_copy(octants_hbm, octants_ref, octants_sem)
    octants_copy.start()
    copies = [pltpu.make_async_copy(a, b, sems.at[i]) for i, (a, b) in enumerate(zip(sources, targets))]
    for copy in copies:
        copy.start()
    fill_phases(lax.axis_index("dir"), phase_ref)
    octants_copy.wait()

    def edges_of(step, carry):
        for j in range(GROUP):
            k = step * GROUP + j
            octant = octants_ref[k]
            for e, (w, m) in enumerate(edge_rows(periods)):
                for i in range(2):
                    edge_phase_ref[e, i, pl.ds(k, 1), :] = phase_ref[octant, i, w, m : m + 1, :]
        return carry

    lax.fori_loop(0, octants_ref.shape[0] // GROUP, edges_of, 0)
    for copy in copies:
        copy.wait()


def both_taps(rows):
    even = SUMS[0] * (rows[0] + rows[4]) + SUMS[1] * (rows[1] + rows[3]) + CENTRE * rows[2]
    odd = DIFFS[0] * (rows[0] - rows[4]) + DIFFS[1] * (rows[1] - rows[3])
    return even + odd, even - odd


def both_taps_transposed(first, second):
    total, difference = first + second, first - second
    outer = [SUMS[i] * total for i in range(2)]
    inner = [DIFFS[i] * difference for i in range(2)]
    return [outer[0] + inner[0], outer[1] + inner[1], CENTRE * total, outer[1] - inner[1], outer[0] - inner[0]]


def main_kernel(peers, parents_ref, octants_ref, x_ref, table_ref, phase_ref, spread_ref, *rest):
    flat_ref, slice_ref, az_e, az_o, res_e, res_o, acc, flat, table_sem = rest
    children = octants_ref.shape[0]
    periods = phase_ref.shape[3]
    azimuth_in = periods * PERIOD_C
    own = acc.shape[0]
    me = lax.axis_index("clus")
    share = ROWS_PER_PERIOD * periods // peers
    first_tile = me * (2 * share) // 8
    table_rows = pl.ds(pl.multiple_of(first_tile * 8, 8), slice_ref.shape[1])
    table_copy = pltpu.make_async_copy(table_ref.at[:, table_rows, :], slice_ref, table_sem)
    table_copy.start()
    acc[...] = jnp.zeros_like(acc)
    sublane = lax.broadcasted_iota(jnp.int32, (periods, LANES), 0)

    def azimuth(block):
        for kp in range(2 * BLOCK):
            start = pl.multiple_of((block * (2 * BLOCK) + kp) * azimuth_in, 8)
            x = [x_ref[pl.ds(start + u, periods, stride=PERIOD_C), :] for u in range(PERIOD_C)]
            left = jnp.where(sublane == 0, 0.0, pltpu.roll(x[3], 1, 0))
            right = [jnp.where(sublane == periods - 1, 0.0, pltpu.roll(x[i], periods - 1, 0)) for i in range(2)]
            lower = [left, x[0], x[1], x[2], x[3]]
            upper = [x[1], x[2], x[3], right[0], right[1]]
            rows = [x[0], *both_taps(lower), x[2], *both_taps(upper)]
            for r in range(3):
                base = (kp * 3 + r) * periods
                az_e[base : base + periods, :] = rows[2 * r]
                az_o[base : base + periods, :] = rows[2 * r + 1]

    def polar():
        res_e[...] = spread_dot(az_e[...], spread_ref, 0)
        res_o[...] = spread_dot(az_o[...], spread_ref, 1)

    def shift(block):
        for k in range(BLOCK):
            octant = octants_ref[block * BLOCK + k]
            parent = parents_ref[block * BLOCK + k]
            for r in range(3):
                parts = []
                for part in range(2):
                    rows = pl.ds(((2 * k + part) * 3 + r) * periods, periods)
                    middle = res_e[rows, LANES:] + res_o[rows, LANES:]
                    parts.append((res_e[rows, :LANES], middle, res_o[rows, :LANES]))
                for i in range(3):
                    w = 3 * r + i
                    real, imaginary = parts[0][i], parts[1][i]
                    cosine, sine = phase_ref[octant, 0, w], phase_ref[octant, 1, w]
                    acc[parent, 0, w] += real * cosine - imaginary * sine
                    acc[parent, 1, w] += real * sine + imaginary * cosine

    def one_block(block, carry):
        azimuth(block)
        polar()
        shift(block)
        return carry

    lax.fori_loop(0, children // BLOCK, one_block, 0)
    for gp in range(2 * own):
        for w in range(ROWS_PER_PERIOD):
            flat[pl.ds(gp * ROWS_PER_PERIOD * periods + w, periods, stride=ROWS_PER_PERIOD), :] = acc[gp // 2, gp % 2, w]
        for q in range(peers):
            source = gp * ROWS_PER_PERIOD * periods + q * share
            target = (q * 2 * own + gp) * share
            flat_ref[target : target + share, :] = flat[source : source + share, :]
    table_copy.wait()


def one_hot(parents, own):
    index = lax.broadcasted_iota(jnp.int32, (own, parents.shape[1]), 0)
    return (index == parents).astype(f32)


def dot2(exact, values):
    exact = exact.astype(bf16)
    high, low = split(values)
    return dot(exact, high) + dot(exact, low)


def fix_kernel(
    peers, own, parents_ref, before_ref, after_ref, flat_ref, edge_phase_ref, spread_ref, *rest
):
    outs, (fixed,) = rest[:peers], rest[peers:]
    pairs = before_ref.shape[0]
    children = pairs // 2
    chunk_rows = outs[0].shape[0]
    share = chunk_rows // (2 * own)
    periods = share * peers // ROWS_PER_PERIOD
    fixed[...] = flat_ref[...]
    left, right = before_ref[...], [after_ref[0], after_ref[1]]
    a, b = TAPS_A, TAPS_B
    even = jnp.concatenate([b[0] * left, a[3] * right[0] + a[4] * right[1]], axis=0)
    odd = jnp.concatenate([a[0] * left, b[3] * right[0] + b[4] * right[1]], axis=0)
    even = spread_dot(even, spread_ref, 0)
    odd = spread_dot(odd, spread_ref, 1)
    first, last = slice(0, pairs), slice(pairs, 2 * pairs)
    low, high = slice(0, LANES), slice(LANES, 2 * LANES)
    refined = [
        odd[first, high],
        odd[first, low],
        even[first, low],
        even[first, high],
        even[last, low],
        even[last, high] + odd[last, high],
        odd[last, low],
    ]
    shifted_rows = []
    for e, rows in enumerate(refined):
        real, imaginary = rows[:children], rows[children:]
        cosine, sine = edge_phase_ref[e, 0], edge_phase_ref[e, 1]
        shifted_rows.append(real * cosine - imaginary * sine)
        shifted_rows.append(real * sine + imaginary * cosine)
    summed = dot2(one_hot(parents_ref[...], own), jnp.concatenate(shifted_rows, axis=1))
    for e, (w, m) in enumerate(edge_rows(periods)):
        q, row = divmod(ROWS_PER_PERIOD * m + w, share)
        for part in range(2):
            rows = pl.ds(q * chunk_rows + part * share + row, own, stride=2 * share)
            column = (2 * e + part) * LANES
            fixed[rows, :] = fixed[rows, :] + summed[:, column : column + LANES]
    me = lax.axis_index("clus")
    for d in range(peers):
        start = pl.multiple_of((me ^ d) * chunk_rows, 8)
        outs[d][...] = fixed[pl.ds(start, chunk_rows), :]


def widen_kernel(source_ref, offset_ref, count_ref, table_ref, wide_ref, operator_ref):
    targets, partners = source_ref.shape
    offsets, frame, _ = table_ref.shape

    def some_offsets(i, carry):
        for j in range(4):
            wide_ref[pl.ds(pl.multiple_of((i * 4 + j) * frame, 8), frame), :] = table_ref[i * 4 + j].astype(f32)
        return carry

    whole_steps = offsets // 4
    lax.fori_loop(0, whole_steps, some_offsets, 0)
    for offset in range(whole_steps * 4, offsets):
        wide_ref[offset * frame : (offset + 1) * frame, :] = table_ref[offset].astype(f32)
    wide_ref[offsets * frame :, :] = jnp.zeros((frame, LANES), f32)

    shape = (targets, targets)
    row, lane = (lax.broadcasted_iota(jnp.int32, shape, d) for d in range(2))
    count = jnp.sum(jnp.where(row == lane, count_ref[...], 0), axis=1, keepdims=True)
    operator = jnp.full(shape, offsets, jnp.int32)
    for p in range(partners):
        here = (lane == source_ref[:, p : p + 1]) & (p < count)
        operator = jnp.where(here, offset_ref[:, p : p + 1], operator)
    operator_ref[...] = operator * frame


def doubled(chunk, real_twice, imag_twice, first, own, share, frame, skip):
    for g in range(own):
        for part, twice in enumerate((real_twice, imag_twice)):
            rows = chunk[(2 * g + part) * share : (2 * g + part + 1) * share, :]
            base = (first + g) * frame + skip
            twice[pl.ds(base, share, stride=2), :] = rows
            twice[pl.ds(base + 1, share, stride=2), :] = rows


def add_sources(sums, targets, devices, own, frame, operator_ref, wide_ref, real_twice, imag_twice):
    for number, device in enumerate(devices):
        for g in range(own):
            source = slice((number * own + g) * frame, (number * own + g + 1) * frame)
            real, imaginary = real_twice[source, :], imag_twice[source, :]
            for i, target in enumerate(targets):
                first = pl.multiple_of(operator_ref[target, device * own + g], 8)
                operator = wide_ref[pl.ds(first, frame), :]
                sums[i] = (sums[i][0] + operator * real, sums[i][1] + operator * imaginary)
    return sums


def gather_kernel(peers, frame, masks, operator_ref, wide_ref, *rest):
    chunks, rest = rest[: len(masks)], rest[len(masks) :]
    before, (real_sum, imag_sum, real_twice, imag_twice) = rest[:-4], rest[-4:]
    me = lax.axis_index("clus")
    targets = operator_ref.shape[0]
    own = targets // peers
    share = chunks[0].shape[0] // (2 * own)
    skip = lax.rem(me * (2 * share), 8)
    for number, chunk in enumerate(chunks):
        doubled(chunk, real_twice, imag_twice, number * own, own, share, frame, skip)

    def some_targets(i, carry):
        some = [i * TOGETHER + j for j in range(TOGETHER)]
        places = [pl.ds(pl.multiple_of(target * frame, 8), frame) for target in some]
        if before:
            sums = [tuple(ref[place, :] for ref in before) for place in places]
        else:
            sums = [(jnp.zeros((frame, LANES), f32),) * 2 for _ in some]
        sums = add_sources(sums, some, [me ^ d for d in masks], own, frame, operator_ref, wide_ref, real_twice, imag_twice)
        for place, (by_real, by_imag) in zip(places, sums):
            real_sum[place, :] = by_real
            imag_sum[place, :] = by_imag
        return carry

    lax.fori_loop(0, targets // TOGETHER, some_targets, 0)


def translate_kernel(peers, frame, masks, targets, operator_ref, wide_ref, real_sum, imag_sum, *rest):
    prepare = len(rest) == len(masks) + len(targets) + 4
    chunks, rest = (rest[: len(masks)], rest[len(masks) :]) if prepare else ((), rest)
    real_twice, imag_twice = rest[:2]
    outs, (total_real, total_imag) = rest[-2 - len(targets) : -2], rest[-2:]
    me = lax.axis_index("clus")
    own = operator_ref.shape[0] // peers
    share = outs[0].shape[0] // (2 * own)
    skip = lax.rem(me * (2 * share), 8)
    for number, chunk in enumerate(chunks):
        doubled(chunk, real_twice, imag_twice, number * own, own, share, frame, skip)
    even, odd = pl.ds(skip, share, stride=2), pl.ds(skip + 1, share, stride=2)
    for out, d in zip(outs, targets):
        first = (me ^ d) * own

        def some_targets(i, carry):
            places = [i * TOGETHER + j for j in range(TOGETHER)]
            some = [first + g for g in places]
            rows = [pl.ds(pl.multiple_of(target * frame, 8), frame) for target in some]
            sums = [(real_sum[r, :], imag_sum[r, :]) for r in rows]
            sums = add_sources(sums, some, [me ^ d for d in masks], own, frame, operator_ref, wide_ref, real_twice, imag_twice)
            for j, (g, (by_real, by_imag)) in enumerate(zip(places, sums)):
                total_real[j] = by_real
                total_imag[j] = by_imag
                row = g * (2 * share)
                out[pl.ds(row, share), :] = total_real[j, even, :] - total_imag[j, odd, :]
                out[pl.ds(row + share, share), :] = total_real[j, odd, :] + total_imag[j, even, :]
            return carry

        lax.fori_loop(0, own // TOGETHER, some_targets, 0)


def edge_kernel(peers, parents_ref, edge_phase_ref, gather_ref, *rest):
    chunks = rest[:peers]
    incoming_ref, next_ref, prev_ref, flat = rest[peers:]
    own2, _, periods, _ = incoming_ref.shape
    own = own2 // 2
    pairs = prev_ref.shape[0]
    flat_rows = ROWS_PER_PERIOD * periods
    share = flat_rows // peers
    me = lax.axis_index("clus")
    for gp in range(own2):
        for d in range(peers):
            flat[pl.ds(gp * flat_rows + (me ^ d) * share, share), :] = chunks[d][gp * share : (gp + 1) * share, :]
    edges = []
    for w, m in edge_rows(periods):
        for part in range(2):
            edges.append(flat[pl.ds(part * flat_rows + ROWS_PER_PERIOD * m + w, own, stride=2 * flat_rows), :])
    per_child = dot2(one_hot(parents_ref[...], own).T, jnp.concatenate(edges, axis=1))
    returned = []
    for e in range(len(edges) // 2):
        real = per_child[:, 2 * e * LANES : (2 * e + 1) * LANES]
        imaginary = per_child[:, (2 * e + 1) * LANES : (2 * e + 2) * LANES]
        cosine, sine = edge_phase_ref[e, 0], edge_phase_ref[e, 1]
        returned.append(
            jnp.concatenate([real * cosine + imaginary * sine, imaginary * cosine - real * sine], axis=0)
        )
    join = functools.partial(jnp.concatenate, axis=1)
    even = jnp.concatenate([join([returned[2], returned[3]]), join([returned[4], returned[5]])], axis=0)
    odd = jnp.concatenate([join([returned[0], returned[1]]), join([returned[5], returned[6]])], axis=0)
    even = gather_dot(*split(even), gather_ref, 0)
    odd = gather_dot(*split(odd), gather_ref, 1)
    a, b = TAPS_A, TAPS_B
    prev_ref[...] = a[0] * odd[:pairs] + b[0] * even[:pairs]
    next_ref[0] = a[3] * even[pairs:] + b[3] * odd[pairs:]
    next_ref[1] = a[4] * even[pairs:] + b[4] * odd[pairs:]
    for gp in range(own2):
        for w in range(ROWS_PER_PERIOD):
            incoming_ref[gp, w] = flat[pl.ds(gp * flat_rows + w, periods, stride=ROWS_PER_PERIOD), :]


def disaggregate_kernel(parents_ref, octants_ref, incoming_ref, phase_ref, gather_ref, out_ref, edge_ref, lhs, coarse_e, coarse_o, whole_out, sems):
    periods = incoming_ref.shape[2]
    azimuth_in = periods * PERIOD_C
    sublane = lax.broadcasted_iota(jnp.int32, (periods, LANES), 0)
    inner = pl.ds(TILE, azimuth_in - 2 * TILE)

    def shift(block):
        for k in range(BLOCK):
            octant = octants_ref[block * BLOCK + k]
            parent = parents_ref[block * BLOCK + k]
            for r in range(3):
                for i in range(3):
                    w = 3 * r + i
                    real, imaginary = incoming_ref[2 * parent, w], incoming_ref[2 * parent + 1, w]
                    cosine, sine = phase_ref[octant, 0, w], phase_ref[octant, 1, w]
                    returned = (real * cosine + imaginary * sine, imaginary * cosine - real * sine)
                    for part in range(2):
                        base = ((2 * k + part) * 3 + r) * periods
                        lhs[base : base + periods, i * LANES : (i + 1) * LANES] = returned[part]

    def polar():
        high, low = split(lhs[...])
        coarse_e[...] = gather_dot(high[:, : 2 * LANES], low[:, : 2 * LANES], gather_ref, 0)
        coarse_o[...] = gather_dot(high[:, LANES:], low[:, LANES:], gather_ref, 1)

    def azimuth(block):
        for j in range(2 * BLOCK):
            c = []
            for r in range(3):
                base = (j * 3 + r) * periods
                c.append(coarse_e[base : base + periods, :])
                c.append(coarse_o[base : base + periods, :])
            lower = both_taps_transposed(c[1], c[2])
            upper = both_taps_transposed(c[4], c[5])
            down = [jnp.where(sublane == 0, 0.0, pltpu.roll(upper[i], 1, 0)) for i in (3, 4)]
            up = jnp.where(sublane == periods - 1, 0.0, pltpu.roll(lower[0], periods - 1, 0))
            rows = [c[0] + lower[1] + down[0], lower[2] + upper[0] + down[1], c[3] + lower[3] + upper[1], lower[4] + upper[2] + up]
            kp = block * (2 * BLOCK) + j
            for u in range(PERIOD_C):
                whole_out[kp, pl.ds(u, periods, stride=PERIOD_C), :] = rows[u]
            edge_ref[0, kp] = whole_out[kp, :TILE, :]
            edge_ref[1, kp] = whole_out[kp, azimuth_in - TILE :, :]

    def written(block):
        some = pl.ds(block * (2 * BLOCK), 2 * BLOCK)
        return pltpu.make_async_copy(whole_out.at[some, inner, :], out_ref.at[some, inner, :], sems.at[block])

    def one_block(block, carry):
        shift(block)
        polar()
        azimuth(block)
        written(block).start()
        return carry

    blocks = octants_ref.shape[0] // BLOCK
    lax.fori_loop(0, blocks, one_block, 0)
    for block in range(blocks):
        written(block).wait()


def finish_kernel(edge_ref, before_ref, after_ref, part_ref, out_ref, tiles, sems):
    pairs, azimuth_in, _ = out_ref.shape
    tiles[...] = edge_ref[...]
    flat = tiles.reshape(2 * pairs * TILE, LANES)
    ends = ((0, 0, before_ref.at[0]), (0, 1, before_ref.at[1]), (1, TILE - 1, after_ref))
    copies = []
    for i, start in enumerate((0, azimuth_in - TILE)):
        for end, row, values_ref in ends:
            if end == i:
                for part in range(2):
                    for k in range(0, pairs // 2, 8):
                        source = slice(part * (pairs // 2) + k, part * (pairs // 2) + k + 8)
                        rows = pl.ds((i * pairs + 2 * k + part) * TILE + row, 8, stride=2 * TILE)
                        flat[rows, :] = flat[rows, :] + values_ref[source, :]
        copy = pltpu.make_async_copy(tiles.at[i], out_ref.at[:, pl.ds(start, TILE), :], sems.at[i])
        copy.start()
        copies.append(copy)
    for copy in copies:
        copy.wait()


def shifted(values, axis, by):
    size = lax.axis_size(axis)
    return lax.ppermute(values, axis, [(i, (i + by) % size) for i in range(size)])


def exchanged(values, axis, mask):
    size = lax.axis_size(axis)
    return lax.ppermute(values, axis, [(i, i ^ mask) for i in range(size)])


SMEM = pl.BlockSpec(memory_space=pltpu.SMEM)
VMEM = pl.BlockSpec(memory_space=pltpu.VMEM)
HBM = pl.BlockSpec(memory_space=pltpu.HBM)


def in_hbm(values):
    return pltpu.with_memory_space_constraint(values, pltpu.HBM)


def local_call(kernel, out_shape, in_specs, scratch, grant, flops=1_000_000, bytes_accessed=1_000_000, out_specs=None, aliases={}):
    return pl.pallas_call(
        kernel,
        out_shape=out_shape,
        in_specs=in_specs,
        out_specs=jax.tree.map(lambda _: VMEM, out_shape) if out_specs is None else out_specs,
        scratch_shapes=scratch,
        input_output_aliases=aliases,
        compiler_params=pltpu.CompilerParams(vmem_limit_bytes=grant << 20),
        cost_estimate=pl.CostEstimate(flops=flops, bytes_accessed=bytes_accessed, transcendentals=0),
    )


def on_device_exchange(
    child_patterns, trans_table, child_parent, child_octant, partner_src, partner_off, partner_count
):
    children, _, azimuth_in, polar_in = child_patterns.shape
    pairs = 2 * children
    peers = lax.axis_size("clus")
    parent_total, _ = partner_src.shape
    own = parent_total // peers
    periods = azimuth_in // PERIOD_C
    flat_rows = ROWS_PER_PERIOD * periods
    share = flat_rows // peers
    offsets = trans_table.shape[0]
    array = lambda *shape: jax.ShapeDtypeStruct(shape, f32)
    buffer = lambda *shape: pltpu.VMEM(shape, f32)
    edges = len(edge_rows(periods))
    even, odd = polar_blocks()
    spread = jnp.asarray(np.stack([np.concatenate([h, h, l]) for h, l in (split_np(even), split_np(odd))]))
    last, first = local_call(
        rows_kernel,
        [array(pairs, polar_in), array(2, pairs, polar_in)],
        [HBM],
        [buffer(pairs, TILE, polar_in)] * 2 + [pltpu.SemaphoreType.DMA((2,))],
        8,
    )(in_hbm(child_patterns.reshape(pairs, azimuth_in, polar_in)))
    after = shifted(first, "dir", -1)
    before = shifted(last, "dir", 1)
    copied = (child_patterns.reshape(pairs * azimuth_in, polar_in), spread, child_parent, child_octant.reshape(1, children))
    phases, edge_phases, held, spread, parents, octants = local_call(
        phase_kernel,
        [array(8, 2, ROWS_PER_PERIOD, periods, LANES), array(edges, 2, children, LANES)]
        + [jax.ShapeDtypeStruct(a.shape, a.dtype) for a in copied],
        [HBM] * 5,
        [pltpu.SMEM((children,), jnp.int32), pltpu.SemaphoreType.DMA, pltpu.SemaphoreType.DMA((len(copied),))],
        12,
        flops=50_000_000,
    )(in_hbm(child_octant), *[in_hbm(a) for a in copied])
    parents, octants = parents[0], octants[0]

    odd_gather = np.concatenate([odd.T[LANES:], odd.T[:LANES]])
    gather = np.stack([np.concatenate(split_np(m), axis=1) for m in (even.T, odd_gather)])

    frame = max(-(-((q * 2 * share) % 8 + 2 * share) // 8) * 8 for q in range(peers))
    view = trans_table.reshape(offsets, 2, flat_rows, LANES).transpose(0, 2, 1, 3).reshape(offsets, 2 * flat_rows, LANES)
    blocks = children // BLOCK
    rows = 2 * BLOCK * 3 * periods
    flat, table = local_call(
        functools.partial(main_kernel, peers),
        [array(2 * own * flat_rows, LANES), jax.ShapeDtypeStruct((offsets, frame, LANES), bf16)],
        [SMEM] * 2 + [VMEM, HBM, VMEM, VMEM],
        [
            buffer(rows, LANES),
            buffer(rows, LANES),
            buffer(rows, 2 * LANES),
            buffer(rows, 2 * LANES),
            buffer(own, 2, ROWS_PER_PERIOD, periods, LANES),
            buffer(2 * own * flat_rows, LANES),
            pltpu.SemaphoreType.DMA,
        ],
        24,
        flops=4_000_000_000,
        bytes_accessed=12_000_000,
    )(parents, octants, held, in_hbm(view), phases, spread)

    chunk = array(2 * own * share, LANES)
    sent = local_call(
        functools.partial(fix_kernel, peers, own), [chunk] * peers, [VMEM] * 6, [buffer(2 * own * flat_rows, LANES)], 8
    )(child_parent, before, after, flat, edge_phases, spread)

    masks = sorted(range(1, peers), key=lambda d: bin(d).count("1"))
    early, late = masks[:1], masks[1:]
    received = {0: sent[0]}
    for d in early:
        received[d] = exchanged(sent[d], "clus", d)
    for d in late:
        received[d] = exchanged(sent[d], "clus", d)

    wide, operator = local_call(
        widen_kernel,
        [array((offsets + 1) * frame, LANES), jax.ShapeDtypeStruct((parent_total, parent_total), jnp.int32)],
        [VMEM] * 4,
        [],
        20,
        flops=50_000_000,
        bytes_accessed=8_000_000,
    )(partner_src, partner_off, partner_count.reshape(1, parent_total), table)

    sums = []
    for group in ([0], early):
        sums = local_call(
            functools.partial(gather_kernel, peers, frame, tuple(group)),
            [array(parent_total * frame, LANES)] * 2,
            [SMEM] + [VMEM] * (1 + len(group) + len(sums)),
            [buffer(len(group) * own * frame, LANES)] * 2,
            20,
            flops=40_000_000 * len(group),
            bytes_accessed=4_000_000 * len(group),
        )(operator, wide, *[received[d] for d in group], *sums)

    back = {}
    last_sources = [received[d] for d in late]
    for number, targets in enumerate((masks[-1:], masks[:-1], [0])):
        prepare = number == 0
        results = local_call(
            functools.partial(translate_kernel, peers, frame, tuple(late), tuple(targets)),
            ([array(len(late) * own * frame, LANES)] * 2 if prepare else []) + [chunk] * len(targets),
            [SMEM] + [VMEM] * (3 + len(last_sources)),
            [buffer(TOGETHER, frame, LANES)] * 2,
            20,
            flops=10_000_000 * len(targets),
            bytes_accessed=2_000_000 * len(targets),
        )(operator, wide, *sums, *last_sources)
        if prepare:
            last_sources, results = results[:2], results[2:]
        for d, result in zip(targets, results):
            back[d] = exchanged(result, "clus", d) if d else result

    incoming, to_next, to_prev = local_call(
        functools.partial(edge_kernel, peers),
        [array(2 * own, ROWS_PER_PERIOD, periods, LANES), array(2, pairs, polar_in), array(pairs, polar_in)],
        [VMEM] * (3 + peers),
        [buffer(2 * own * flat_rows, LANES)],
        8,
    )(child_parent, edge_phases, gather, *[back[d] for d in range(peers)])

    from_before = shifted(to_next, "dir", 1)
    from_after = shifted(to_prev, "dir", -1)

    inner, edge_tiles = local_call(
        disaggregate_kernel,
        [array(pairs, azimuth_in, polar_in), array(2, pairs, TILE, polar_in)],
        [SMEM] * 2 + [VMEM] * 3,
        [
            buffer(rows, 3 * LANES),
            buffer(rows, LANES),
            buffer(rows, LANES),
            buffer(pairs, azimuth_in, polar_in),
            pltpu.SemaphoreType.DMA((blocks,)),
        ],
        24,
        flops=4_000_000_000,
        bytes_accessed=12_000_000,
        out_specs=[HBM, VMEM],
    )(parents, octants, incoming, phases, gather)

    out = local_call(
        finish_kernel,
        array(pairs, azimuth_in, polar_in),
        [VMEM] * 3 + [HBM],
        [buffer(2, pairs, TILE, polar_in), pltpu.SemaphoreType.DMA((2,))],
        8,
        out_specs=HBM,
        aliases={3: 0},
    )(edge_tiles, from_before, from_after, in_hbm(inner))
    return out.reshape(child_patterns.shape)


def with_halo(shard, sides, width):
    for axis, dim in sides:
        size, length = (lax.axis_size(axis), shard.shape[dim])
        up = [(i, (i + 1) % size) for i in range(size)]
        down = [(j, i) for i, j in up]
        last = lax.slice_in_dim(shard, length - width, length, axis=dim)
        initial = lax.slice_in_dim(shard, 0, width, axis=dim)
        before = lax.ppermute(last, axis, up)
        after = lax.ppermute(initial, axis, down)
        shard = jnp.concatenate([before, shard, after], axis=dim)
    return shard


def lagrange_rows(offset):
    weights = []
    for anchor in range(5):
        factor = jnp.ones_like(offset)
        for neighbour in range(5):
            if neighbour != anchor:
                factor = factor * (offset - neighbour) / (anchor - neighbour)
        weights.append(factor)
    return weights


def polar_matrix_of(rows_out, rows_in):
    target = (jnp.arange(rows_out, dtype=jnp.float32) + 0.5) * rows_in / rows_out - 0.5
    start_row = jnp.clip(jnp.floor(target + 0.5).astype(jnp.int32) - 2, 0, rows_in - 5)
    weights = lagrange_rows(target - start_row.astype(jnp.float32))
    columns = jnp.arange(rows_in, dtype=jnp.int32)
    matrix = jnp.zeros((rows_out, rows_in), jnp.float32)
    for anchor in range(5):
        matrix = matrix + jnp.where(
            columns[None, :] == (start_row + anchor)[:, None], weights[anchor][:, None], 0.0
        )
    return matrix


def azimuth_matrix_of(out_index, in_index, total_out, total_in):
    target = (out_index * total_in).astype(jnp.float32) / total_out
    nearest = jnp.floor(target + 0.5).astype(jnp.int32)
    weights = lagrange_rows(target - nearest.astype(jnp.float32) + 2.0)
    matrix = jnp.zeros((out_index.shape[0], in_index.shape[0]), jnp.float32)
    for anchor in range(5):
        columns = nearest + anchor - 2
        matrix = matrix + jnp.where(
            in_index[None, :] == columns[:, None], weights[anchor][:, None], 0.0
        )
    return matrix


def shift_phases(octant, azimuth_index, azimuth_total, polar_total):
    azimuth = 2.0 * math.pi * azimuth_index.astype(jnp.float32) / azimuth_total
    polar = math.pi * (jnp.arange(polar_total, dtype=jnp.float32) + 0.5) / polar_total
    first_axis = jnp.sin(polar)[None, :] * jnp.cos(azimuth)[:, None]
    second_axis = jnp.sin(polar)[None, :] * jnp.sin(azimuth)[:, None]
    third_axis = jnp.cos(polar)[None, :] * jnp.ones_like(azimuth)[:, None]
    first_sign = (1 - 2 * (octant % 2)).astype(jnp.float32)
    second_sign = (1 - 2 * (octant // 2 % 2)).astype(jnp.float32)
    third_sign = (1 - 2 * (octant // 4)).astype(jnp.float32)
    phase_angle = phase_scale * (
        first_sign[:, None, None] * first_axis[None]
        + second_sign[:, None, None] * second_axis[None]
        + third_sign[:, None, None] * third_axis[None]
    )
    return (jnp.cos(phase_angle), jnp.sin(phase_angle))


def translate(sources, table, partner_src, partner_off, partner_count):
    live_mask = (
        jnp.arange(partner_src.shape[1], dtype=jnp.int32)[None, :] < partner_count[:, None]
    ).astype(jnp.float32)
    picked = sources[partner_src]
    operator = table[partner_off].astype(jnp.float32) * live_mask[:, :, None, None]
    real_part = jnp.sum(
        operator[:, :, 0] * picked[:, :, 0] - operator[:, :, 1] * picked[:, :, 1], axis=1
    )
    imaginary = jnp.sum(
        operator[:, :, 0] * picked[:, :, 1] + operator[:, :, 1] * picked[:, :, 0], axis=1
    )
    return jnp.stack([real_part, imaginary], axis=1)


def forward_shift(patterns, cosine, sine_part):
    real_part = patterns[:, 0] * cosine - patterns[:, 1] * sine_part
    imaginary = patterns[:, 0] * sine_part + patterns[:, 1] * cosine
    return jnp.stack([real_part, imaginary], axis=1)


def conjugate_shift(patterns, cosine, sine_part):
    real_part = patterns[:, 0] * cosine + patterns[:, 1] * sine_part
    imaginary = patterns[:, 1] * cosine - patterns[:, 0] * sine_part
    return jnp.stack([real_part, imaginary], axis=1)


def on_device_gather(
    child_patterns, trans_table, child_parent, child_octant, partner_src, partner_off, partner_count
):
    _, _, azimuth_in, _ = child_patterns.shape
    polar_out = NTHETA_P
    azimuth_out = trans_table.shape[2] // polar_out
    parent_slots = partner_src.shape[0] // lax.axis_size("clus")
    cluster_index = lax.axis_index("clus")
    direction_index = lax.axis_index("dir")
    parents = child_parent[0]
    polar_matrix = polar_matrix_of(NTHETA_P, NTHETA_C)
    onehot = (parents[None, :] == jnp.arange(parent_slots, dtype=jnp.int32)[:, None]).astype(
        jnp.float32
    )
    own_rows = jnp.mod(
        direction_index * azimuth_out + jnp.arange(azimuth_out, dtype=jnp.int32), NPHI_P
    )
    cosine, sine_part = shift_phases(child_octant, own_rows, NPHI_P, polar_out)
    extended = with_halo(child_patterns, (("dir", 2),), 2)
    gather_matrix = azimuth_matrix_of(
        jnp.arange(azimuth_out, dtype=jnp.int32),
        jnp.arange(azimuth_in + 4, dtype=jnp.int32) - 2,
        NPHI_P,
        NPHI_C,
    )
    along_azimuth = jnp.einsum("pc,kacz->kapz", gather_matrix, extended, precision=highest)
    refined = jnp.einsum("kapz,tz->kapt", along_azimuth, polar_matrix, precision=highest)
    shifted = forward_shift(refined, cosine, sine_part)
    radiation = jnp.einsum("gk,kapt->gapt", onehot, shifted, precision=highest)
    flattened = radiation.reshape(parent_slots, 2, azimuth_out * polar_out)
    sources = lax.all_gather(flattened, "clus", axis=0, tiled=True)
    first_row = cluster_index * parent_slots
    own_src = lax.dynamic_slice_in_dim(partner_src, first_row, parent_slots, 0)
    own_off = lax.dynamic_slice_in_dim(partner_off, first_row, parent_slots, 0)
    own_count = lax.dynamic_slice_in_dim(partner_count, first_row, parent_slots, 0)
    incoming = translate(sources, trans_table, own_src, own_off, own_count)
    incoming = incoming.reshape(parent_slots, 2, azimuth_out, polar_out)
    return_matrix = azimuth_matrix_of(
        jnp.arange(azimuth_out + 6, dtype=jnp.int32) - 3,
        jnp.arange(azimuth_in, dtype=jnp.int32),
        NPHI_P,
        NPHI_C,
    )
    per_child = jnp.einsum("gk,gapt->kapt", onehot, incoming, precision=highest)
    returned = conjugate_shift(per_child, cosine, sine_part)
    coarse_own = jnp.einsum("kapt,tz->kapz", returned, polar_matrix, precision=highest)
    coarse = with_halo(coarse_own, (("dir", 2),), 3)
    return jnp.einsum("pc,kapz->kacz", return_matrix, coarse, precision=highest)


def solution(mesh):
    def on_device(child_patterns, trans_table, *rest):
        peers = lax.axis_size("clus")
        children, _, azimuth_in, polar_in = child_patterns.shape
        flat_rows = trans_table.shape[2] // LANES
        fits = (
            azimuth_in % (8 * PERIOD_C) == 0
            and polar_in == LANES
            and flat_rows * PERIOD_C == ROWS_PER_PERIOD * azimuth_in
            and flat_rows % peers == 0
            and peers & (peers - 1) == 0
            and peers > 2
            and children % BLOCK == 0
        )
        plan = on_device_exchange if fits else on_device_gather
        return plan(child_patterns, trans_table, *rest)

    return jax.shard_map(
        on_device,
        mesh=mesh,
        in_specs=(
            P("clus", None, "dir", None),
            P(None, None, "dir"),
            P("clus", None),
            P("clus"),
            P(),
            P(),
            P(),
        ),
        out_specs=P("clus", None, "dir", None),
        check_vma=False,
    )
```

```python
import functools
import math

import jax
import jax.numpy as jnp
import numpy as np
from jax import lax
from jax.experimental import pallas as pl
from jax.experimental.pallas import tpu as pltpu
from jax.sharding import PartitionSpec as P


NTHETA_C = 128
NPHI_C = 256
NTHETA_P = 192
NPHI_P = 384

LANES = 128
PERIOD_P = 6
PERIOD_C = 4
ROWS_PER_PERIOD = PERIOD_P * NTHETA_P // LANES
GROUP = 8
TILE = 8
TOGETHER = 2
BLOCK = 2 * GROUP

phase_scale = 8.0 * math.pi
highest = lax.Precision.HIGHEST
f32 = jnp.float32
bf16 = jnp.bfloat16


def lagrange(offset):
    weights = []
    for anchor in range(5):
        factor = 1.0
        for neighbour in range(5):
            if neighbour != anchor:
                factor = factor * (offset - neighbour) / (anchor - neighbour)
        weights.append(factor)
    return weights


TAPS_A = [float(w) for w in lagrange(5.0 / 3.0)]
TAPS_B = [float(w) for w in lagrange(7.0 / 3.0)]


SUMS = [(TAPS_A[i] + TAPS_A[4 - i]) / 2 for i in range(2)]
DIFFS = [(TAPS_A[i] - TAPS_A[4 - i]) / 2 for i in range(2)]
CENTRE = TAPS_A[2]


def polar_matrix_np():
    target = (np.arange(NTHETA_P, dtype=np.float32) + np.float32(0.5)) * NTHETA_C / NTHETA_P - np.float32(0.5)
    start = np.clip(np.floor(target + 0.5).astype(np.int32) - 2, 0, NTHETA_C - 5)
    weights = lagrange((target - start).astype(np.float64))
    matrix = np.zeros((NTHETA_P, NTHETA_C), np.float64)
    for anchor in range(5):
        matrix[np.arange(NTHETA_P), start + anchor] += weights[anchor]
    return matrix.astype(np.float32)


def polar_blocks():
    matrix = polar_matrix_np().T
    even = np.zeros((NTHETA_C, 2 * LANES), np.float32)
    odd = np.zeros((NTHETA_C, 2 * LANES), np.float32)
    half = NTHETA_P - LANES
    even[:, :NTHETA_P] = matrix
    odd[:, :LANES] = matrix[:, half:]
    odd[:, 2 * LANES - half :] = matrix[:, :half]
    return even, odd


def split_np(matrix):
    high = matrix.astype(bf16)
    low = (matrix - high.astype(np.float32)).astype(bf16)
    return high, low


def split(values):
    high = values.astype(bf16)
    low = (values - high.astype(f32)).astype(bf16)
    return high, low


def dot(left, right):
    return jnp.dot(left, right, preferred_element_type=f32)


def spread_dot(values, matrix_ref, i):
    high, low = split(values)
    depth = values.shape[1]
    return dot(jnp.concatenate([high, low], axis=1), matrix_ref[i, : 2 * depth]) + dot(high, matrix_ref[i, 2 * depth :])


def gather_dot(high, low, matrix_ref, i):
    width = matrix_ref.shape[2] // 2
    both = dot(high, matrix_ref[i])
    return both[:, :width] + (both[:, width:] + dot(low, matrix_ref[i, :, :width]))


SIN_COEFFS = [(-1) ** k * math.pi ** (2 * k + 1) / math.factorial(2 * k + 1) for k in range(7)]
COS_COEFFS = [(-1) ** k * math.pi ** (2 * k) / math.factorial(2 * k) for k in range(7)]


def sincos_turns(turns):
    rest = turns - jnp.round(turns)
    square = rest * rest
    sine = jnp.full_like(square, SIN_COEFFS[-1])
    for coeff in SIN_COEFFS[-2::-1]:
        sine = sine * square + coeff
    sine = sine * rest
    cosine = jnp.full_like(square, COS_COEFFS[-1])
    for coeff in COS_COEFFS[-2::-1]:
        cosine = cosine * square + coeff
    return 2.0 * sine * cosine, 1.0 - 2.0 * sine * sine


def fill_phases(direction, out_ref):
    periods = out_ref.shape[3]
    lane = lax.broadcasted_iota(jnp.int32, (periods, LANES), 1)
    period = lax.broadcasted_iota(jnp.int32, (periods, LANES), 0)
    first = direction * (PERIOD_P * periods)

    def two_rows(r, carry):
        for i in range(3):
            position = lane + i * LANES
            second = (position >= NTHETA_P).astype(jnp.int32)
            polar_index = position - second * NTHETA_P
            azimuth_index = first + period * PERIOD_P + 2 * r + second
            sin_polar, cos_polar = sincos_turns((polar_index.astype(f32) + 0.5) / (2 * NTHETA_P))
            sin_azimuth, cos_azimuth = sincos_turns(azimuth_index.astype(f32) / NPHI_P)
            along_x = 4.0 * sin_polar * cos_azimuth
            along_y = 4.0 * sin_polar * sin_azimuth
            along_z = 4.0 * cos_polar
            w = 3 * r + i
            for octant in (0, 2, 4, 6):
                turns = along_x + along_y if octant % 4 == 0 else along_x - along_y
                turns = turns + along_z if octant < 4 else turns - along_z
                sine, cosine = sincos_turns(turns)
                out_ref[octant, 0, w] = cosine
                out_ref[octant, 1, w] = sine
                out_ref[7 - octant, 0, w] = cosine
                out_ref[7 - octant, 1, w] = -sine
        return carry

    lax.fori_loop(0, PERIOD_P // 2, two_rows, 0)


def edge_rows(periods):
    return [(w, 0) for w in (1, 2, 3, 4)] + [(w, periods - 1) for w in (6, 7, 8)]


def by_parity(even, odd):
    parity = lax.rem(lax.axis_index("dir"), 2)
    pl.when(parity == 0)(even)
    pl.when(parity == 1)(odd)


def from_sides(far_ref, near_ref):
    is_even = lax.rem(lax.axis_index("dir"), 2) == 0
    far, near = far_ref[...], near_ref[...]
    return jnp.where(is_even, far, near), jnp.where(is_even, near, far)


def rows_kernel(x_ref, far_ref, near_ref, low, high, sems):
    pairs, azimuth_in, _ = x_ref.shape
    low_copy = pltpu.make_async_copy(x_ref.at[:, pl.ds(0, TILE), :], low, sems.at[0])
    high_copy = pltpu.make_async_copy(x_ref.at[:, pl.ds(azimuth_in - TILE, TILE), :], high, sems.at[1])
    low_copy.start()
    high_copy.start()
    low_copy.wait()
    high_copy.wait()
    low_rows, high_rows = (ref.reshape(pairs * TILE, LANES) for ref in (low, high))

    def fill(first_ref, last_ref):
        for part in range(2):
            for k in range(0, pairs // 2, 8):
                target = slice(part * (pairs // 2) + k, part * (pairs // 2) + k + 8)
                base = (2 * k + part) * TILE
                for i in range(2):
                    first_ref[i, target] = low_rows[pl.ds(base + i, 8, stride=2 * TILE), :]
                last = high_rows[pl.ds(base + TILE - 1, 8, stride=2 * TILE), :]
                for i in range(2):
                    last_ref[i, target] = last

    by_parity(lambda: fill(far_ref, near_ref), lambda: fill(near_ref, far_ref))


def phase_kernel(*refs):
    octants_hbm, sources = refs[0], refs[1:5]
    (phase_ref, edge_phase_ref), targets = refs[5:7], refs[7:11]
    octants_ref, octants_sem, sems = refs[11:]
    periods = phase_ref.shape[3]
    octants_copy = pltpu.make_async_copy(octants_hbm, octants_ref, octants_sem)
    octants_copy.start()
    copies = [pltpu.make_async_copy(a, b, sems.at[i]) for i, (a, b) in enumerate(zip(sources, targets))]
    for copy in copies:
        copy.start()
    fill_phases(lax.axis_index("dir"), phase_ref)
    octants_copy.wait()

    def edges_of(step, carry):
        for j in range(GROUP):
            k = step * GROUP + j
            octant = octants_ref[k]
            for e, (w, m) in enumerate(edge_rows(periods)):
                for i in range(2):
                    edge_phase_ref[e, i, pl.ds(k, 1), :] = phase_ref[octant, i, w, m : m + 1, :]
        return carry

    lax.fori_loop(0, octants_ref.shape[0] // GROUP, edges_of, 0)
    for copy in copies:
        copy.wait()


def both_taps(rows):
    even = SUMS[0] * (rows[0] + rows[4]) + SUMS[1] * (rows[1] + rows[3]) + CENTRE * rows[2]
    odd = DIFFS[0] * (rows[0] - rows[4]) + DIFFS[1] * (rows[1] - rows[3])
    return even + odd, even - odd


def both_taps_transposed(first, second):
    total, difference = first + second, first - second
    outer = [SUMS[i] * total for i in range(2)]
    inner = [DIFFS[i] * difference for i in range(2)]
    return [outer[0] + inner[0], outer[1] + inner[1], CENTRE * total, outer[1] - inner[1], outer[0] - inner[0]]


def main_kernel(peers, parents_ref, octants_ref, x_ref, table_ref, phase_ref, spread_ref, *rest):
    flat_ref, slice_ref, az_e, az_o, res_e, res_o, acc, flat, table_sem = rest
    children = octants_ref.shape[0]
    periods = phase_ref.shape[3]
    azimuth_in = periods * PERIOD_C
    own = acc.shape[0]
    me = lax.axis_index("clus")
    share = ROWS_PER_PERIOD * periods // peers
    first_tile = me * (2 * share) // 8
    table_rows = pl.ds(pl.multiple_of(first_tile * 8, 8), slice_ref.shape[1])
    table_copy = pltpu.make_async_copy(table_ref.at[:, table_rows, :], slice_ref, table_sem)
    table_copy.start()
    acc[...] = jnp.zeros_like(acc)
    sublane = lax.broadcasted_iota(jnp.int32, (periods, LANES), 0)

    def azimuth(block):
        for kp in range(2 * BLOCK):
            start = pl.multiple_of((block * (2 * BLOCK) + kp) * azimuth_in, 8)
            x = [x_ref[pl.ds(start + u, periods, stride=PERIOD_C), :] for u in range(PERIOD_C)]
            left = jnp.where(sublane == 0, 0.0, pltpu.roll(x[3], 1, 0))
            right = [jnp.where(sublane == periods - 1, 0.0, pltpu.roll(x[i], periods - 1, 0)) for i in range(2)]
            lower = [left, x[0], x[1], x[2], x[3]]
            upper = [x[1], x[2], x[3], right[0], right[1]]
            rows = [x[0], *both_taps(lower), x[2], *both_taps(upper)]
            for r in range(3):
                base = (kp * 3 + r) * periods
                az_e[base : base + periods, :] = rows[2 * r]
                az_o[base : base + periods, :] = rows[2 * r + 1]

    def polar():
        res_e[...] = spread_dot(az_e[...], spread_ref, 0)
        res_o[...] = spread_dot(az_o[...], spread_ref, 1)

    def shift(block):
        for k in range(BLOCK):
            octant = octants_ref[block * BLOCK + k]
            parent = parents_ref[block * BLOCK + k]
            for r in range(3):
                parts = []
                for part in range(2):
                    rows = pl.ds(((2 * k + part) * 3 + r) * periods, periods)
                    middle = res_e[rows, LANES:] + res_o[rows, LANES:]
                    parts.append((res_e[rows, :LANES], middle, res_o[rows, :LANES]))
                for i in range(3):
                    w = 3 * r + i
                    real, imaginary = parts[0][i], parts[1][i]
                    cosine, sine = phase_ref[octant, 0, w], phase_ref[octant, 1, w]
                    acc[parent, 0, w] += real * cosine - imaginary * sine
                    acc[parent, 1, w] += real * sine + imaginary * cosine

    def one_block(block, carry):
        azimuth(block)
        polar()
        shift(block)
        return carry

    lax.fori_loop(0, children // BLOCK, one_block, 0)
    for gp in range(2 * own):
        for w in range(ROWS_PER_PERIOD):
            flat[pl.ds(gp * ROWS_PER_PERIOD * periods + w, periods, stride=ROWS_PER_PERIOD), :] = acc[gp // 2, gp % 2, w]
        for q in range(peers):
            source = gp * ROWS_PER_PERIOD * periods + q * share
            target = (q * 2 * own + gp) * share
            flat_ref[target : target + share, :] = flat[source : source + share, :]
    table_copy.wait()


def one_hot(parents, own):
    index = lax.broadcasted_iota(jnp.int32, (own, parents.shape[1]), 0)
    return (index == parents).astype(f32)


def dot2(exact, values):
    exact = exact.astype(bf16)
    high, low = split(values)
    return dot(exact, high) + dot(exact, low)


def fix_kernel(
    peers, own, parents_ref, far_ref, near_ref, flat_ref, edge_phase_ref, spread_ref, *rest
):
    outs, (fixed,) = rest[:peers], rest[peers:]
    pairs = far_ref.shape[1]
    children = pairs // 2
    chunk_rows = outs[0].shape[0]
    share = chunk_rows // (2 * own)
    periods = share * peers // ROWS_PER_PERIOD
    fixed[...] = flat_ref[...]
    before, right = from_sides(far_ref, near_ref)
    left = before[0]
    a, b = TAPS_A, TAPS_B
    even = jnp.concatenate([b[0] * left, a[3] * right[0] + a[4] * right[1]], axis=0)
    odd = jnp.concatenate([a[0] * left, b[3] * right[0] + b[4] * right[1]], axis=0)
    even = spread_dot(even, spread_ref, 0)
    odd = spread_dot(odd, spread_ref, 1)
    first, last = slice(0, pairs), slice(pairs, 2 * pairs)
    low, high = slice(0, LANES), slice(LANES, 2 * LANES)
    refined = [
        odd[first, high],
        odd[first, low],
        even[first, low],
        even[first, high],
        even[last, low],
        even[last, high] + odd[last, high],
        odd[last, low],
    ]
    shifted_rows = []
    for e, rows in enumerate(refined):
        real, imaginary = rows[:children], rows[children:]
        cosine, sine = edge_phase_ref[e, 0], edge_phase_ref[e, 1]
        shifted_rows.append(real * cosine - imaginary * sine)
        shifted_rows.append(real * sine + imaginary * cosine)
    summed = dot2(one_hot(parents_ref[...], own), jnp.concatenate(shifted_rows, axis=1))
    for e, (w, m) in enumerate(edge_rows(periods)):
        q, row = divmod(ROWS_PER_PERIOD * m + w, share)
        for part in range(2):
            rows = pl.ds(q * chunk_rows + part * share + row, own, stride=2 * share)
            column = (2 * e + part) * LANES
            fixed[rows, :] = fixed[rows, :] + summed[:, column : column + LANES]
    me = lax.axis_index("clus")
    for d in range(peers):
        start = pl.multiple_of((me ^ d) * chunk_rows, 8)
        outs[d][...] = fixed[pl.ds(start, chunk_rows), :]


def widen_kernel(source_ref, offset_ref, count_ref, table_ref, wide_ref, operator_ref):
    targets, partners = source_ref.shape
    offsets, frame, _ = table_ref.shape

    def some_offsets(i, carry):
        for j in range(4):
            wide_ref[pl.ds(pl.multiple_of((i * 4 + j) * frame, 8), frame), :] = table_ref[i * 4 + j].astype(f32)
        return carry

    whole_steps = offsets // 4
    lax.fori_loop(0, whole_steps, some_offsets, 0)
    for offset in range(whole_steps * 4, offsets):
        wide_ref[offset * frame : (offset + 1) * frame, :] = table_ref[offset].astype(f32)
    wide_ref[offsets * frame :, :] = jnp.zeros((frame, LANES), f32)

    shape = (targets, targets)
    row, lane = (lax.broadcasted_iota(jnp.int32, shape, d) for d in range(2))
    count = jnp.sum(jnp.where(row == lane, count_ref[...], 0), axis=1, keepdims=True)
    operator = jnp.full(shape, offsets, jnp.int32)
    for p in range(partners):
        here = (lane == source_ref[:, p : p + 1]) & (p < count)
        operator = jnp.where(here, offset_ref[:, p : p + 1], operator)
    operator_ref[...] = operator * frame


def doubled(chunk, real_twice, imag_twice, first, own, share, frame, skip):
    for g in range(own):
        for part, twice in enumerate((real_twice, imag_twice)):
            rows = chunk[(2 * g + part) * share : (2 * g + part + 1) * share, :]
            base = (first + g) * frame + skip
            twice[pl.ds(base, share, stride=2), :] = rows
            twice[pl.ds(base + 1, share, stride=2), :] = rows


def add_sources(sums, targets, devices, own, frame, operator_ref, wide_ref, real_twice, imag_twice):
    for number, device in enumerate(devices):
        for g in range(own):
            source = slice((number * own + g) * frame, (number * own + g + 1) * frame)
            real, imaginary = real_twice[source, :], imag_twice[source, :]
            for i, target in enumerate(targets):
                first = pl.multiple_of(operator_ref[target, device * own + g], 8)
                operator = wide_ref[pl.ds(first, frame), :]
                sums[i] = (sums[i][0] + operator * real, sums[i][1] + operator * imaginary)
    return sums


def gather_kernel(peers, frame, masks, operator_ref, wide_ref, *rest):
    chunks, rest = rest[: len(masks)], rest[len(masks) :]
    before, (real_sum, imag_sum, real_twice, imag_twice) = rest[:-4], rest[-4:]
    me = lax.axis_index("clus")
    targets = operator_ref.shape[0]
    own = targets // peers
    share = chunks[0].shape[0] // (2 * own)
    skip = lax.rem(me * (2 * share), 8)
    for number, chunk in enumerate(chunks):
        doubled(chunk, real_twice, imag_twice, number * own, own, share, frame, skip)

    def some_targets(i, carry):
        some = [i * TOGETHER + j for j in range(TOGETHER)]
        places = [pl.ds(pl.multiple_of(target * frame, 8), frame) for target in some]
        if before:
            sums = [tuple(ref[place, :] for ref in before) for place in places]
        else:
            sums = [(jnp.zeros((frame, LANES), f32),) * 2 for _ in some]
        sums = add_sources(sums, some, [me ^ d for d in masks], own, frame, operator_ref, wide_ref, real_twice, imag_twice)
        for place, (by_real, by_imag) in zip(places, sums):
            real_sum[place, :] = by_real
            imag_sum[place, :] = by_imag
        return carry

    lax.fori_loop(0, targets // TOGETHER, some_targets, 0)


def translate_kernel(peers, frame, masks, targets, operator_ref, wide_ref, real_sum, imag_sum, *rest):
    prepare = len(rest) == len(masks) + len(targets) + 4
    chunks, rest = (rest[: len(masks)], rest[len(masks) :]) if prepare else ((), rest)
    real_twice, imag_twice = rest[:2]
    outs, (total_real, total_imag) = rest[-2 - len(targets) : -2], rest[-2:]
    me = lax.axis_index("clus")
    own = operator_ref.shape[0] // peers
    share = outs[0].shape[0] // (2 * own)
    skip = lax.rem(me * (2 * share), 8)
    for number, chunk in enumerate(chunks):
        doubled(chunk, real_twice, imag_twice, number * own, own, share, frame, skip)
    even, odd = pl.ds(skip, share, stride=2), pl.ds(skip + 1, share, stride=2)
    for out, d in zip(outs, targets):
        first = (me ^ d) * own

        def some_targets(i, carry):
            places = [i * TOGETHER + j for j in range(TOGETHER)]
            some = [first + g for g in places]
            rows = [pl.ds(pl.multiple_of(target * frame, 8), frame) for target in some]
            sums = [(real_sum[r, :], imag_sum[r, :]) for r in rows]
            sums = add_sources(sums, some, [me ^ d for d in masks], own, frame, operator_ref, wide_ref, real_twice, imag_twice)
            for j, (g, (by_real, by_imag)) in enumerate(zip(places, sums)):
                total_real[j] = by_real
                total_imag[j] = by_imag
                row = g * (2 * share)
                out[pl.ds(row, share), :] = total_real[j, even, :] - total_imag[j, odd, :]
                out[pl.ds(row + share, share), :] = total_real[j, odd, :] + total_imag[j, even, :]
            return carry

        lax.fori_loop(0, own // TOGETHER, some_targets, 0)


def edge_kernel(peers, parents_ref, edge_phase_ref, gather_ref, *rest):
    chunks = rest[:peers]
    incoming_ref, far_ref, near_ref, flat = rest[peers:]
    own2, _, periods, _ = incoming_ref.shape
    own = own2 // 2
    pairs = far_ref.shape[1]
    flat_rows = ROWS_PER_PERIOD * periods
    share = flat_rows // peers
    me = lax.axis_index("clus")
    for gp in range(own2):
        for d in range(peers):
            flat[pl.ds(gp * flat_rows + (me ^ d) * share, share), :] = chunks[d][gp * share : (gp + 1) * share, :]
    edges = []
    for w, m in edge_rows(periods):
        for part in range(2):
            edges.append(flat[pl.ds(part * flat_rows + ROWS_PER_PERIOD * m + w, own, stride=2 * flat_rows), :])
    per_child = dot2(one_hot(parents_ref[...], own).T, jnp.concatenate(edges, axis=1))
    returned = []
    for e in range(len(edges) // 2):
        real = per_child[:, 2 * e * LANES : (2 * e + 1) * LANES]
        imaginary = per_child[:, (2 * e + 1) * LANES : (2 * e + 2) * LANES]
        cosine, sine = edge_phase_ref[e, 0], edge_phase_ref[e, 1]
        returned.append(
            jnp.concatenate([real * cosine + imaginary * sine, imaginary * cosine - real * sine], axis=0)
        )
    join = functools.partial(jnp.concatenate, axis=1)
    even = jnp.concatenate([join([returned[2], returned[3]]), join([returned[4], returned[5]])], axis=0)
    odd = jnp.concatenate([join([returned[0], returned[1]]), join([returned[5], returned[6]])], axis=0)
    even = gather_dot(*split(even), gather_ref, 0)
    odd = gather_dot(*split(odd), gather_ref, 1)
    a, b = TAPS_A, TAPS_B

    def fill(prev_ref, next_ref):
        below = a[0] * odd[:pairs] + b[0] * even[:pairs]
        for i in range(2):
            prev_ref[i] = below
            next_ref[i] = a[3 + i] * even[pairs:] + b[3 + i] * odd[pairs:]

    by_parity(lambda: fill(far_ref, near_ref), lambda: fill(near_ref, far_ref))
    for gp in range(own2):
        for w in range(ROWS_PER_PERIOD):
            incoming_ref[gp, w] = flat[pl.ds(gp * flat_rows + w, periods, stride=ROWS_PER_PERIOD), :]


def disaggregate_kernel(parents_ref, octants_ref, incoming_ref, phase_ref, gather_ref, out_ref, edge_ref, lhs, coarse_e, coarse_o, whole_out, sems):
    periods = incoming_ref.shape[2]
    azimuth_in = periods * PERIOD_C
    sublane = lax.broadcasted_iota(jnp.int32, (periods, LANES), 0)
    inner = pl.ds(TILE, azimuth_in - 2 * TILE)

    def shift(block):
        for k in range(BLOCK):
            octant = octants_ref[block * BLOCK + k]
            parent = parents_ref[block * BLOCK + k]
            for r in range(3):
                for i in range(3):
                    w = 3 * r + i
                    real, imaginary = incoming_ref[2 * parent, w], incoming_ref[2 * parent + 1, w]
                    cosine, sine = phase_ref[octant, 0, w], phase_ref[octant, 1, w]
                    returned = (real * cosine + imaginary * sine, imaginary * cosine - real * sine)
                    for part in range(2):
                        base = ((2 * k + part) * 3 + r) * periods
                        lhs[base : base + periods, i * LANES : (i + 1) * LANES] = returned[part]

    def polar():
        high, low = split(lhs[...])
        coarse_e[...] = gather_dot(high[:, : 2 * LANES], low[:, : 2 * LANES], gather_ref, 0)
        coarse_o[...] = gather_dot(high[:, LANES:], low[:, LANES:], gather_ref, 1)

    def azimuth(block):
        for j in range(2 * BLOCK):
            c = []
            for r in range(3):
                base = (j * 3 + r) * periods
                c.append(coarse_e[base : base + periods, :])
                c.append(coarse_o[base : base + periods, :])
            lower = both_taps_transposed(c[1], c[2])
            upper = both_taps_transposed(c[4], c[5])
            down = [jnp.where(sublane == 0, 0.0, pltpu.roll(upper[i], 1, 0)) for i in (3, 4)]
            up = jnp.where(sublane == periods - 1, 0.0, pltpu.roll(lower[0], periods - 1, 0))
            rows = [c[0] + lower[1] + down[0], lower[2] + upper[0] + down[1], c[3] + lower[3] + upper[1], lower[4] + upper[2] + up]
            kp = block * (2 * BLOCK) + j
            for u in range(PERIOD_C):
                whole_out[kp, pl.ds(u, periods, stride=PERIOD_C), :] = rows[u]
            edge_ref[0, kp] = whole_out[kp, :TILE, :]
            edge_ref[1, kp] = whole_out[kp, azimuth_in - TILE :, :]

    def written(block):
        some = pl.ds(block * (2 * BLOCK), 2 * BLOCK)
        return pltpu.make_async_copy(whole_out.at[some, inner, :], out_ref.at[some, inner, :], sems.at[block])

    def one_block(block, carry):
        shift(block)
        polar()
        azimuth(block)
        written(block).start()
        return carry

    blocks = octants_ref.shape[0] // BLOCK
    lax.fori_loop(0, blocks, one_block, 0)
    for block in range(blocks):
        written(block).wait()


def finish_kernel(edge_ref, far_ref, near_ref, part_ref, out_ref, tiles, sems):
    pairs, azimuth_in, _ = out_ref.shape
    tiles[...] = edge_ref[...]
    flat = tiles.reshape(2 * pairs * TILE, LANES)
    before, after = from_sides(far_ref, near_ref)
    ends = ((0, 0, before[0]), (0, 1, before[1]), (1, TILE - 1, after[0]))
    copies = []
    for i, start in enumerate((0, azimuth_in - TILE)):
        for end, row, values in ends:
            if end == i:
                for part in range(2):
                    for k in range(0, pairs // 2, 8):
                        source = slice(part * (pairs // 2) + k, part * (pairs // 2) + k + 8)
                        rows = pl.ds((i * pairs + 2 * k + part) * TILE + row, 8, stride=2 * TILE)
                        flat[rows, :] = flat[rows, :] + values[source]
        copy = pltpu.make_async_copy(tiles.at[i], out_ref.at[:, pl.ds(start, TILE), :], sems.at[i])
        copy.start()
        copies.append(copy)
    for copy in copies:
        copy.wait()


def swapped(values, axis, first):
    size = lax.axis_size(axis)
    return lax.ppermute(values, axis, [(i, (((i - first) ^ 1) + first) % size) for i in range(size)])


def exchanged(values, axis, mask):
    size = lax.axis_size(axis)
    return lax.ppermute(values, axis, [(i, i ^ mask) for i in range(size)])


SMEM = pl.BlockSpec(memory_space=pltpu.SMEM)
VMEM = pl.BlockSpec(memory_space=pltpu.VMEM)
HBM = pl.BlockSpec(memory_space=pltpu.HBM)


def in_hbm(values):
    return pltpu.with_memory_space_constraint(values, pltpu.HBM)


def local_call(kernel, out_shape, in_specs, scratch, grant, flops=1_000_000, bytes_accessed=1_000_000, out_specs=None, aliases={}):
    return pl.pallas_call(
        kernel,
        out_shape=out_shape,
        in_specs=in_specs,
        out_specs=jax.tree.map(lambda _: VMEM, out_shape) if out_specs is None else out_specs,
        scratch_shapes=scratch,
        input_output_aliases=aliases,
        compiler_params=pltpu.CompilerParams(vmem_limit_bytes=grant << 20),
        cost_estimate=pl.CostEstimate(flops=flops, bytes_accessed=bytes_accessed, transcendentals=0),
    )


def on_device_exchange(
    child_patterns, trans_table, child_parent, child_octant, partner_src, partner_off, partner_count
):
    children, _, azimuth_in, polar_in = child_patterns.shape
    pairs = 2 * children
    peers = lax.axis_size("clus")
    parent_total, _ = partner_src.shape
    own = parent_total // peers
    periods = azimuth_in // PERIOD_C
    flat_rows = ROWS_PER_PERIOD * periods
    share = flat_rows // peers
    offsets = trans_table.shape[0]
    array = lambda *shape: jax.ShapeDtypeStruct(shape, f32)
    buffer = lambda *shape: pltpu.VMEM(shape, f32)
    edges = len(edge_rows(periods))
    even, odd = polar_blocks()
    spread = jnp.asarray(np.stack([np.concatenate([h, h, l]) for h, l in (split_np(even), split_np(odd))]))
    edge = array(2, pairs, polar_in)
    to_far, to_near = local_call(
        rows_kernel, [edge, edge], [HBM], [buffer(pairs, TILE, polar_in)] * 2 + [pltpu.SemaphoreType.DMA((2,))], 8
    )(in_hbm(child_patterns.reshape(pairs, azimuth_in, polar_in)))
    from_far = swapped(to_far, "dir", 1)
    from_near = swapped(to_near, "dir", 0)
    copied = (child_patterns.reshape(pairs * azimuth_in, polar_in), spread, child_parent, child_octant.reshape(1, children))
    phases, edge_phases, held, spread, parents, octants = local_call(
        phase_kernel,
        [array(8, 2, ROWS_PER_PERIOD, periods, LANES), array(edges, 2, children, LANES)]
        + [jax.ShapeDtypeStruct(a.shape, a.dtype) for a in copied],
        [HBM] * 5,
        [pltpu.SMEM((children,), jnp.int32), pltpu.SemaphoreType.DMA, pltpu.SemaphoreType.DMA((len(copied),))],
        12,
        flops=50_000_000,
    )(in_hbm(child_octant), *[in_hbm(a) for a in copied])
    parents, octants = parents[0], octants[0]

    odd_gather = np.concatenate([odd.T[LANES:], odd.T[:LANES]])
    gather = np.stack([np.concatenate(split_np(m), axis=1) for m in (even.T, odd_gather)])

    frame = max(-(-((q * 2 * share) % 8 + 2 * share) // 8) * 8 for q in range(peers))
    view = trans_table.reshape(offsets, 2, flat_rows, LANES).transpose(0, 2, 1, 3).reshape(offsets, 2 * flat_rows, LANES)
    blocks = children // BLOCK
    rows = 2 * BLOCK * 3 * periods
    flat, table = local_call(
        functools.partial(main_kernel, peers),
        [array(2 * own * flat_rows, LANES), jax.ShapeDtypeStruct((offsets, frame, LANES), bf16)],
        [SMEM] * 2 + [VMEM, HBM, VMEM, VMEM],
        [
            buffer(rows, LANES),
            buffer(rows, LANES),
            buffer(rows, 2 * LANES),
            buffer(rows, 2 * LANES),
            buffer(own, 2, ROWS_PER_PERIOD, periods, LANES),
            buffer(2 * own * flat_rows, LANES),
            pltpu.SemaphoreType.DMA,
        ],
        24,
        flops=4_000_000_000,
        bytes_accessed=12_000_000,
    )(parents, octants, held, in_hbm(view), phases, spread)

    chunk = array(2 * own * share, LANES)
    sent = local_call(
        functools.partial(fix_kernel, peers, own), [chunk] * peers, [VMEM] * 6, [buffer(2 * own * flat_rows, LANES)], 8
    )(child_parent, from_far, from_near, flat, edge_phases, spread)

    masks = sorted(range(1, peers), key=lambda d: bin(d).count("1"))
    early, late = masks[:1], masks[1:]
    received = {0: sent[0]}
    for d in early:
        received[d] = exchanged(sent[d], "clus", d)
    for d in late:
        received[d] = exchanged(sent[d], "clus", d)

    wide, operator = local_call(
        widen_kernel,
        [array((offsets + 1) * frame, LANES), jax.ShapeDtypeStruct((parent_total, parent_total), jnp.int32)],
        [VMEM] * 4,
        [],
        20,
        flops=50_000_000,
        bytes_accessed=8_000_000,
    )(partner_src, partner_off, partner_count.reshape(1, parent_total), table)

    sums = []
    for group in ([0], early):
        sums = local_call(
            functools.partial(gather_kernel, peers, frame, tuple(group)),
            [array(parent_total * frame, LANES)] * 2,
            [SMEM] + [VMEM] * (1 + len(group) + len(sums)),
            [buffer(len(group) * own * frame, LANES)] * 2,
            20,
            flops=40_000_000 * len(group),
            bytes_accessed=4_000_000 * len(group),
        )(operator, wide, *[received[d] for d in group], *sums)

    back = {}
    last_sources = [received[d] for d in late]
    for number, targets in enumerate((masks[-1:], masks[:-1], [0])):
        prepare = number == 0
        results = local_call(
            functools.partial(translate_kernel, peers, frame, tuple(late), tuple(targets)),
            ([array(len(late) * own * frame, LANES)] * 2 if prepare else []) + [chunk] * len(targets),
            [SMEM] + [VMEM] * (3 + len(last_sources)),
            [buffer(TOGETHER, frame, LANES)] * 2,
            20,
            flops=10_000_000 * len(targets),
            bytes_accessed=2_000_000 * len(targets),
        )(operator, wide, *sums, *last_sources)
        if prepare:
            last_sources, results = results[:2], results[2:]
        for d, result in zip(targets, results):
            back[d] = exchanged(result, "clus", d) if d else result

    incoming, to_far, to_near = local_call(
        functools.partial(edge_kernel, peers),
        [array(2 * own, ROWS_PER_PERIOD, periods, LANES), edge, edge],
        [VMEM] * (3 + peers),
        [buffer(2 * own * flat_rows, LANES)],
        8,
    )(child_parent, edge_phases, gather, *[back[d] for d in range(peers)])

    from_far = swapped(to_far, "dir", 1)
    from_near = swapped(to_near, "dir", 0)

    inner, edge_tiles = local_call(
        disaggregate_kernel,
        [array(pairs, azimuth_in, polar_in), array(2, pairs, TILE, polar_in)],
        [SMEM] * 2 + [VMEM] * 3,
        [
            buffer(rows, 3 * LANES),
            buffer(rows, LANES),
            buffer(rows, LANES),
            buffer(pairs, azimuth_in, polar_in),
            pltpu.SemaphoreType.DMA((blocks,)),
        ],
        24,
        flops=4_000_000_000,
        bytes_accessed=12_000_000,
        out_specs=[HBM, VMEM],
    )(parents, octants, incoming, phases, gather)

    out = local_call(
        finish_kernel,
        array(pairs, azimuth_in, polar_in),
        [VMEM] * 3 + [HBM],
        [buffer(2, pairs, TILE, polar_in), pltpu.SemaphoreType.DMA((2,))],
        8,
        out_specs=HBM,
        aliases={3: 0},
    )(edge_tiles, from_far, from_near, in_hbm(inner))
    return out.reshape(child_patterns.shape)


def with_halo(shard, sides, width):
    for axis, dim in sides:
        size, length = (lax.axis_size(axis), shard.shape[dim])
        up = [(i, (i + 1) % size) for i in range(size)]
        down = [(j, i) for i, j in up]
        last = lax.slice_in_dim(shard, length - width, length, axis=dim)
        initial = lax.slice_in_dim(shard, 0, width, axis=dim)
        before = lax.ppermute(last, axis, up)
        after = lax.ppermute(initial, axis, down)
        shard = jnp.concatenate([before, shard, after], axis=dim)
    return shard


def lagrange_rows(offset):
    weights = []
    for anchor in range(5):
        factor = jnp.ones_like(offset)
        for neighbour in range(5):
            if neighbour != anchor:
                factor = factor * (offset - neighbour) / (anchor - neighbour)
        weights.append(factor)
    return weights


def polar_matrix_of(rows_out, rows_in):
    target = (jnp.arange(rows_out, dtype=jnp.float32) + 0.5) * rows_in / rows_out - 0.5
    start_row = jnp.clip(jnp.floor(target + 0.5).astype(jnp.int32) - 2, 0, rows_in - 5)
    weights = lagrange_rows(target - start_row.astype(jnp.float32))
    columns = jnp.arange(rows_in, dtype=jnp.int32)
    matrix = jnp.zeros((rows_out, rows_in), jnp.float32)
    for anchor in range(5):
        matrix = matrix + jnp.where(
            columns[None, :] == (start_row + anchor)[:, None], weights[anchor][:, None], 0.0
        )
    return matrix


def azimuth_matrix_of(out_index, in_index, total_out, total_in):
    target = (out_index * total_in).astype(jnp.float32) / total_out
    nearest = jnp.floor(target + 0.5).astype(jnp.int32)
    weights = lagrange_rows(target - nearest.astype(jnp.float32) + 2.0)
    matrix = jnp.zeros((out_index.shape[0], in_index.shape[0]), jnp.float32)
    for anchor in range(5):
        columns = nearest + anchor - 2
        matrix = matrix + jnp.where(
            in_index[None, :] == columns[:, None], weights[anchor][:, None], 0.0
        )
    return matrix


def shift_phases(octant, azimuth_index, azimuth_total, polar_total):
    azimuth = 2.0 * math.pi * azimuth_index.astype(jnp.float32) / azimuth_total
    polar = math.pi * (jnp.arange(polar_total, dtype=jnp.float32) + 0.5) / polar_total
    first_axis = jnp.sin(polar)[None, :] * jnp.cos(azimuth)[:, None]
    second_axis = jnp.sin(polar)[None, :] * jnp.sin(azimuth)[:, None]
    third_axis = jnp.cos(polar)[None, :] * jnp.ones_like(azimuth)[:, None]
    first_sign = (1 - 2 * (octant % 2)).astype(jnp.float32)
    second_sign = (1 - 2 * (octant // 2 % 2)).astype(jnp.float32)
    third_sign = (1 - 2 * (octant // 4)).astype(jnp.float32)
    phase_angle = phase_scale * (
        first_sign[:, None, None] * first_axis[None]
        + second_sign[:, None, None] * second_axis[None]
        + third_sign[:, None, None] * third_axis[None]
    )
    return (jnp.cos(phase_angle), jnp.sin(phase_angle))


def translate(sources, table, partner_src, partner_off, partner_count):
    live_mask = (
        jnp.arange(partner_src.shape[1], dtype=jnp.int32)[None, :] < partner_count[:, None]
    ).astype(jnp.float32)
    picked = sources[partner_src]
    operator = table[partner_off].astype(jnp.float32) * live_mask[:, :, None, None]
    real_part = jnp.sum(
        operator[:, :, 0] * picked[:, :, 0] - operator[:, :, 1] * picked[:, :, 1], axis=1
    )
    imaginary = jnp.sum(
        operator[:, :, 0] * picked[:, :, 1] + operator[:, :, 1] * picked[:, :, 0], axis=1
    )
    return jnp.stack([real_part, imaginary], axis=1)


def forward_shift(patterns, cosine, sine_part):
    real_part = patterns[:, 0] * cosine - patterns[:, 1] * sine_part
    imaginary = patterns[:, 0] * sine_part + patterns[:, 1] * cosine
    return jnp.stack([real_part, imaginary], axis=1)


def conjugate_shift(patterns, cosine, sine_part):
    real_part = patterns[:, 0] * cosine + patterns[:, 1] * sine_part
    imaginary = patterns[:, 1] * cosine - patterns[:, 0] * sine_part
    return jnp.stack([real_part, imaginary], axis=1)


def on_device_gather(
    child_patterns, trans_table, child_parent, child_octant, partner_src, partner_off, partner_count
):
    _, _, azimuth_in, _ = child_patterns.shape
    polar_out = NTHETA_P
    azimuth_out = trans_table.shape[2] // polar_out
    parent_slots = partner_src.shape[0] // lax.axis_size("clus")
    cluster_index = lax.axis_index("clus")
    direction_index = lax.axis_index("dir")
    parents = child_parent[0]
    polar_matrix = polar_matrix_of(NTHETA_P, NTHETA_C)
    onehot = (parents[None, :] == jnp.arange(parent_slots, dtype=jnp.int32)[:, None]).astype(
        jnp.float32
    )
    own_rows = jnp.mod(
        direction_index * azimuth_out + jnp.arange(azimuth_out, dtype=jnp.int32), NPHI_P
    )
    cosine, sine_part = shift_phases(child_octant, own_rows, NPHI_P, polar_out)
    extended = with_halo(child_patterns, (("dir", 2),), 2)
    gather_matrix = azimuth_matrix_of(
        jnp.arange(azimuth_out, dtype=jnp.int32),
        jnp.arange(azimuth_in + 4, dtype=jnp.int32) - 2,
        NPHI_P,
        NPHI_C,
    )
    along_azimuth = jnp.einsum("pc,kacz->kapz", gather_matrix, extended, precision=highest)
    refined = jnp.einsum("kapz,tz->kapt", along_azimuth, polar_matrix, precision=highest)
    shifted = forward_shift(refined, cosine, sine_part)
    radiation = jnp.einsum("gk,kapt->gapt", onehot, shifted, precision=highest)
    flattened = radiation.reshape(parent_slots, 2, azimuth_out * polar_out)
    sources = lax.all_gather(flattened, "clus", axis=0, tiled=True)
    first_row = cluster_index * parent_slots
    own_src = lax.dynamic_slice_in_dim(partner_src, first_row, parent_slots, 0)
    own_off = lax.dynamic_slice_in_dim(partner_off, first_row, parent_slots, 0)
    own_count = lax.dynamic_slice_in_dim(partner_count, first_row, parent_slots, 0)
    incoming = translate(sources, trans_table, own_src, own_off, own_count)
    incoming = incoming.reshape(parent_slots, 2, azimuth_out, polar_out)
    return_matrix = azimuth_matrix_of(
        jnp.arange(azimuth_out + 6, dtype=jnp.int32) - 3,
        jnp.arange(azimuth_in, dtype=jnp.int32),
        NPHI_P,
        NPHI_C,
    )
    per_child = jnp.einsum("gk,gapt->kapt", onehot, incoming, precision=highest)
    returned = conjugate_shift(per_child, cosine, sine_part)
    coarse_own = jnp.einsum("kapt,tz->kapz", returned, polar_matrix, precision=highest)
    coarse = with_halo(coarse_own, (("dir", 2),), 3)
    return jnp.einsum("pc,kapz->kacz", return_matrix, coarse, precision=highest)


def solution(mesh):
    def on_device(child_patterns, trans_table, *rest):
        peers = lax.axis_size("clus")
        children, _, azimuth_in, polar_in = child_patterns.shape
        flat_rows = trans_table.shape[2] // LANES
        fits = (
            azimuth_in % (8 * PERIOD_C) == 0
            and polar_in == LANES
            and flat_rows * PERIOD_C == ROWS_PER_PERIOD * azimuth_in
            and flat_rows % peers == 0
            and peers & (peers - 1) == 0
            and peers > 2
            and lax.axis_size("dir") % 2 == 0
            and children % BLOCK == 0
        )
        plan = on_device_exchange if fits else on_device_gather
        return plan(child_patterns, trans_table, *rest)

    return jax.shard_map(
        on_device,
        mesh=mesh,
        in_specs=(
            P("clus", None, "dir", None),
            P(None, None, "dir"),
            P("clus", None),
            P("clus"),
            P(),
            P(),
            P(),
        ),
        out_specs=P("clus", None, "dir", None),
        check_vma=False,
    )
```

```python
import functools
import math

import jax
import jax.numpy as jnp
import numpy as np
from jax import lax
from jax.experimental import pallas as pl
from jax.experimental.pallas import tpu as pltpu
from jax.sharding import PartitionSpec as P


NTHETA_C = 128
NPHI_C = 256
NTHETA_P = 192
NPHI_P = 384

LANES = 128
PERIOD_P = 6
PERIOD_C = 4
ROWS_PER_PERIOD = PERIOD_P * NTHETA_P // LANES
GROUP = 8
TILE = 8
TOGETHER = 2
BLOCK = 2 * GROUP

phase_scale = 8.0 * math.pi
highest = lax.Precision.HIGHEST
f32 = jnp.float32
bf16 = jnp.bfloat16


def lagrange(offset):
    weights = []
    for anchor in range(5):
        factor = 1.0
        for neighbour in range(5):
            if neighbour != anchor:
                factor = factor * (offset - neighbour) / (anchor - neighbour)
        weights.append(factor)
    return weights


TAPS_A = [float(w) for w in lagrange(5.0 / 3.0)]
TAPS_B = [float(w) for w in lagrange(7.0 / 3.0)]


SUMS = [(TAPS_A[i] + TAPS_A[4 - i]) / 2 for i in range(2)]
DIFFS = [(TAPS_A[i] - TAPS_A[4 - i]) / 2 for i in range(2)]
CENTRE = TAPS_A[2]


def polar_matrix_np():
    target = (np.arange(NTHETA_P, dtype=np.float32) + np.float32(0.5)) * NTHETA_C / NTHETA_P - np.float32(0.5)
    start = np.clip(np.floor(target + 0.5).astype(np.int32) - 2, 0, NTHETA_C - 5)
    weights = lagrange((target - start).astype(np.float64))
    matrix = np.zeros((NTHETA_P, NTHETA_C), np.float64)
    for anchor in range(5):
        matrix[np.arange(NTHETA_P), start + anchor] += weights[anchor]
    return matrix.astype(np.float32)


def polar_blocks():
    matrix = polar_matrix_np().T
    even = np.zeros((NTHETA_C, 2 * LANES), np.float32)
    odd = np.zeros((NTHETA_C, 2 * LANES), np.float32)
    half = NTHETA_P - LANES
    even[:, :NTHETA_P] = matrix
    odd[:, :LANES] = matrix[:, half:]
    odd[:, 2 * LANES - half :] = matrix[:, :half]
    return even, odd


def split_np(matrix):
    high = matrix.astype(bf16)
    low = (matrix - high.astype(np.float32)).astype(bf16)
    return high, low


def split(values):
    high = values.astype(bf16)
    low = (values - high.astype(f32)).astype(bf16)
    return high, low


def dot(left, right):
    return jnp.dot(left, right, preferred_element_type=f32)


def spread_dot(values, matrix_ref, i):
    high, low = split(values)
    depth = values.shape[1]
    return dot(jnp.concatenate([high, low], axis=1), matrix_ref[i, : 2 * depth]) + dot(high, matrix_ref[i, 2 * depth :])


def gather_dot(high, low, matrix_ref, i):
    width = matrix_ref.shape[2] // 2
    both = dot(high, matrix_ref[i])
    return both[:, :width] + (both[:, width:] + dot(low, matrix_ref[i, :, :width]))


SIN_COEFFS = [(-1) ** k * math.pi ** (2 * k + 1) / math.factorial(2 * k + 1) for k in range(7)]
COS_COEFFS = [(-1) ** k * math.pi ** (2 * k) / math.factorial(2 * k) for k in range(7)]


def sincos_turns(turns):
    rest = turns - jnp.round(turns)
    square = rest * rest
    sine = jnp.full_like(square, SIN_COEFFS[-1])
    for coeff in SIN_COEFFS[-2::-1]:
        sine = sine * square + coeff
    sine = sine * rest
    cosine = jnp.full_like(square, COS_COEFFS[-1])
    for coeff in COS_COEFFS[-2::-1]:
        cosine = cosine * square + coeff
    return 2.0 * sine * cosine, 1.0 - 2.0 * sine * sine


def fill_phases(direction, out_ref):
    periods = out_ref.shape[3]
    lane = lax.broadcasted_iota(jnp.int32, (periods, LANES), 1)
    period = lax.broadcasted_iota(jnp.int32, (periods, LANES), 0)
    first = direction * (PERIOD_P * periods)

    def two_rows(r, carry):
        for i in range(3):
            position = lane + i * LANES
            second = (position >= NTHETA_P).astype(jnp.int32)
            polar_index = position - second * NTHETA_P
            azimuth_index = first + period * PERIOD_P + 2 * r + second
            sin_polar, cos_polar = sincos_turns((polar_index.astype(f32) + 0.5) / (2 * NTHETA_P))
            sin_azimuth, cos_azimuth = sincos_turns(azimuth_index.astype(f32) / NPHI_P)
            along_x = 4.0 * sin_polar * cos_azimuth
            along_y = 4.0 * sin_polar * sin_azimuth
            along_z = 4.0 * cos_polar
            w = 3 * r + i
            for octant in (0, 2, 4, 6):
                turns = along_x + along_y if octant % 4 == 0 else along_x - along_y
                turns = turns + along_z if octant < 4 else turns - along_z
                sine, cosine = sincos_turns(turns)
                out_ref[octant, 0, w] = cosine
                out_ref[octant, 1, w] = sine
                out_ref[7 - octant, 0, w] = cosine
                out_ref[7 - octant, 1, w] = -sine
        return carry

    lax.fori_loop(0, PERIOD_P // 2, two_rows, 0)


def edge_rows(periods):
    return [(w, 0) for w in (1, 2, 3, 4)] + [(w, periods - 1) for w in (6, 7, 8)]


def by_parity(even, odd):
    parity = lax.rem(lax.axis_index("dir"), 2)
    pl.when(parity == 0)(even)
    pl.when(parity == 1)(odd)


def from_sides(far_ref, near_ref):
    is_even = lax.rem(lax.axis_index("dir"), 2) == 0
    far, near = far_ref[...], near_ref[...]
    return jnp.where(is_even, far, near), jnp.where(is_even, near, far)


def rows_kernel(x_ref, far_ref, near_ref, low, high, sems):
    pairs, azimuth_in, _ = x_ref.shape
    low_copy = pltpu.make_async_copy(x_ref.at[:, pl.ds(0, TILE), :], low, sems.at[0])
    high_copy = pltpu.make_async_copy(x_ref.at[:, pl.ds(azimuth_in - TILE, TILE), :], high, sems.at[1])
    low_copy.start()
    high_copy.start()
    low_copy.wait()
    high_copy.wait()
    low_rows, high_rows = (ref.reshape(pairs * TILE, LANES) for ref in (low, high))

    def fill(first_ref, last_ref):
        for part in range(2):
            for k in range(0, pairs // 2, 8):
                target = slice(part * (pairs // 2) + k, part * (pairs // 2) + k + 8)
                base = (2 * k + part) * TILE
                for i in range(2):
                    first_ref[i, target] = low_rows[pl.ds(base + i, 8, stride=2 * TILE), :]
                last = high_rows[pl.ds(base + TILE - 1, 8, stride=2 * TILE), :]
                for i in range(2):
                    last_ref[i, target] = last

    by_parity(lambda: fill(far_ref, near_ref), lambda: fill(near_ref, far_ref))


def both_taps(rows):
    even = SUMS[0] * (rows[0] + rows[4]) + SUMS[1] * (rows[1] + rows[3]) + CENTRE * rows[2]
    odd = DIFFS[0] * (rows[0] - rows[4]) + DIFFS[1] * (rows[1] - rows[3])
    return even + odd, even - odd


def both_taps_transposed(first, second):
    total, difference = first + second, first - second
    outer = [SUMS[i] * total for i in range(2)]
    inner = [DIFFS[i] * difference for i in range(2)]
    return [outer[0] + inner[0], outer[1] + inner[1], CENTRE * total, outer[1] - inner[1], outer[0] - inner[0]]


def main_kernel(peers, parents_hbm, octants_hbm, x_hbm, table_ref, spread_hbm, *rest):
    phase_ref, edge_phase_ref, flat_ref, slice_ref = rest[:4]
    parents_ref, octants_ref, x_ref, spread_ref, az_e, az_o, res_e, res_o, acc, flat, sems = rest[4:]
    children = octants_ref.shape[0]
    periods = phase_ref.shape[3]
    azimuth_in = periods * PERIOD_C
    own = acc.shape[0]
    me = lax.axis_index("clus")
    share = ROWS_PER_PERIOD * periods // peers
    first_tile = me * (2 * share) // 8
    table_rows = pl.ds(pl.multiple_of(first_tile * 8, 8), slice_ref.shape[1])
    ends = (
        (octants_hbm, octants_ref),
        (parents_hbm, parents_ref),
        (x_hbm, x_ref),
        (spread_hbm, spread_ref),
        (table_ref.at[:, table_rows, :], slice_ref),
    )
    copies = [pltpu.make_async_copy(source, target, sems.at[i]) for i, (source, target) in enumerate(ends)]
    for copy in copies:
        copy.start()
    fill_phases(lax.axis_index("dir"), phase_ref)
    acc[...] = jnp.zeros_like(acc)
    sublane = lax.broadcasted_iota(jnp.int32, (periods, LANES), 0)
    for copy in copies[:-1]:
        copy.wait()

    def edges_of(step, carry):
        for j in range(GROUP):
            k = step * GROUP + j
            octant = octants_ref[k]
            for e, (w, m) in enumerate(edge_rows(periods)):
                for i in range(2):
                    edge_phase_ref[e, i, pl.ds(k, 1), :] = phase_ref[octant, i, w, m : m + 1, :]
        return carry

    lax.fori_loop(0, children // GROUP, edges_of, 0)

    def azimuth(block):
        for kp in range(2 * BLOCK):
            start = pl.multiple_of((block * (2 * BLOCK) + kp) * azimuth_in, 8)
            x = [x_ref[pl.ds(start + u, periods, stride=PERIOD_C), :] for u in range(PERIOD_C)]
            left = jnp.where(sublane == 0, 0.0, pltpu.roll(x[3], 1, 0))
            right = [jnp.where(sublane == periods - 1, 0.0, pltpu.roll(x[i], periods - 1, 0)) for i in range(2)]
            lower = [left, x[0], x[1], x[2], x[3]]
            upper = [x[1], x[2], x[3], right[0], right[1]]
            rows = [x[0], *both_taps(lower), x[2], *both_taps(upper)]
            for r in range(3):
                base = (kp * 3 + r) * periods
                az_e[base : base + periods, :] = rows[2 * r]
                az_o[base : base + periods, :] = rows[2 * r + 1]

    def polar():
        res_e[...] = spread_dot(az_e[...], spread_ref, 0)
        res_o[...] = spread_dot(az_o[...], spread_ref, 1)

    def shift(block):
        for k in range(BLOCK):
            octant = octants_ref[block * BLOCK + k]
            parent = parents_ref[block * BLOCK + k]
            for r in range(3):
                parts = []
                for part in range(2):
                    rows = pl.ds(((2 * k + part) * 3 + r) * periods, periods)
                    middle = res_e[rows, LANES:] + res_o[rows, LANES:]
                    parts.append((res_e[rows, :LANES], middle, res_o[rows, :LANES]))
                for i in range(3):
                    w = 3 * r + i
                    real, imaginary = parts[0][i], parts[1][i]
                    cosine, sine = phase_ref[octant, 0, w], phase_ref[octant, 1, w]
                    acc[parent, 0, w] += real * cosine - imaginary * sine
                    acc[parent, 1, w] += real * sine + imaginary * cosine

    def one_block(block, carry):
        azimuth(block)
        polar()
        shift(block)
        return carry

    lax.fori_loop(0, children // BLOCK, one_block, 0)
    for gp in range(2 * own):
        for w in range(ROWS_PER_PERIOD):
            flat[pl.ds(gp * ROWS_PER_PERIOD * periods + w, periods, stride=ROWS_PER_PERIOD), :] = acc[gp // 2, gp % 2, w]
        for q in range(peers):
            source = gp * ROWS_PER_PERIOD * periods + q * share
            target = (q * 2 * own + gp) * share
            flat_ref[target : target + share, :] = flat[source : source + share, :]
    copies[-1].wait()


def one_hot(parents, own):
    index = lax.broadcasted_iota(jnp.int32, (own, parents.shape[1]), 0)
    return (index == parents).astype(f32)


def dot2(exact, values):
    exact = exact.astype(bf16)
    high, low = split(values)
    return dot(exact, high) + dot(exact, low)


def fix_kernel(
    peers, own, parents_ref, far_ref, near_ref, flat_ref, edge_phase_ref, spread_ref, *rest
):
    outs, (fixed,) = rest[:peers], rest[peers:]
    pairs = far_ref.shape[1]
    children = pairs // 2
    chunk_rows = outs[0].shape[0]
    share = chunk_rows // (2 * own)
    periods = share * peers // ROWS_PER_PERIOD
    fixed[...] = flat_ref[...]
    before, right = from_sides(far_ref, near_ref)
    left = before[0]
    a, b = TAPS_A, TAPS_B
    even = jnp.concatenate([b[0] * left, a[3] * right[0] + a[4] * right[1]], axis=0)
    odd = jnp.concatenate([a[0] * left, b[3] * right[0] + b[4] * right[1]], axis=0)
    even = spread_dot(even, spread_ref, 0)
    odd = spread_dot(odd, spread_ref, 1)
    first, last = slice(0, pairs), slice(pairs, 2 * pairs)
    low, high = slice(0, LANES), slice(LANES, 2 * LANES)
    refined = [
        odd[first, high],
        odd[first, low],
        even[first, low],
        even[first, high],
        even[last, low],
        even[last, high] + odd[last, high],
        odd[last, low],
    ]
    shifted_rows = []
    for e, rows in enumerate(refined):
        real, imaginary = rows[:children], rows[children:]
        cosine, sine = edge_phase_ref[e, 0], edge_phase_ref[e, 1]
        shifted_rows.append(real * cosine - imaginary * sine)
        shifted_rows.append(real * sine + imaginary * cosine)
    summed = dot2(one_hot(parents_ref[...], own), jnp.concatenate(shifted_rows, axis=1))
    for e, (w, m) in enumerate(edge_rows(periods)):
        q, row = divmod(ROWS_PER_PERIOD * m + w, share)
        for part in range(2):
            rows = pl.ds(q * chunk_rows + part * share + row, own, stride=2 * share)
            column = (2 * e + part) * LANES
            fixed[rows, :] = fixed[rows, :] + summed[:, column : column + LANES]
    me = lax.axis_index("clus")
    for d in range(peers):
        start = pl.multiple_of((me ^ d) * chunk_rows, 8)
        outs[d][...] = fixed[pl.ds(start, chunk_rows), :]


def widen_kernel(peers, source_ref, offset_ref, count_ref, table_ref, chunk, wide_ref, operator_ref, real_sum, imag_sum, *rest):
    listed, real_twice, imag_twice, sem = rest
    targets, partners = source_ref.shape
    offsets, frame, _ = table_ref.shape
    shape = (targets, targets)
    row, lane = (lax.broadcasted_iota(jnp.int32, shape, d) for d in range(2))
    count = jnp.sum(jnp.where(row == lane, count_ref[...], 0), axis=1, keepdims=True)
    operator = jnp.full(shape, offsets, jnp.int32)
    for p in range(partners):
        here = (lane == source_ref[:, p : p + 1]) & (p < count)
        operator = jnp.where(here, offset_ref[:, p : p + 1], operator)
    operator_ref[...] = operator * frame
    copy = pltpu.make_async_copy(operator_ref, listed, sem)
    copy.start()

    def some_offsets(i, carry):
        for j in range(4):
            wide_ref[pl.ds(pl.multiple_of((i * 4 + j) * frame, 8), frame), :] = table_ref[i * 4 + j].astype(f32)
        return carry

    whole_steps = offsets // 4
    lax.fori_loop(0, whole_steps, some_offsets, 0)
    for offset in range(whole_steps * 4, offsets):
        wide_ref[offset * frame : (offset + 1) * frame, :] = table_ref[offset].astype(f32)
    wide_ref[offsets * frame :, :] = jnp.zeros((frame, LANES), f32)
    copy.wait()
    gather_kernel(peers, frame, (0,), (), listed, wide_ref, chunk, real_sum, imag_sum, real_twice, imag_twice)


def doubled(chunk, real_twice, imag_twice, first, own, share, frame, skip):
    for g in range(own):
        for part, twice in enumerate((real_twice, imag_twice)):
            rows = chunk[(2 * g + part) * share : (2 * g + part + 1) * share, :]
            base = (first + g) * frame + skip
            twice[pl.ds(base, share, stride=2), :] = rows
            twice[pl.ds(base + 1, share, stride=2), :] = rows


def add_sources(sums, sources, frame, operators, real_twice, imag_twice):
    for source in range(sources):
        place = slice(source * frame, (source + 1) * frame)
        real, imaginary = real_twice[place, :], imag_twice[place, :]
        for i in range(len(sums)):
            operator = operators(i, source)
            sums[i] = (sums[i][0] + operator * real, sums[i][1] + operator * imaginary)
    return sums


def gather_kernel(peers, frame, masks, late, operator_ref, wide_ref, *rest):
    chunks, rest = rest[: len(masks)], rest[len(masks) :]
    late_ref, rest = (rest[-3], rest[:-3] + rest[-2:]) if late else (None, rest)
    before, (real_sum, imag_sum, real_twice, imag_twice) = rest[:-4], rest[-4:]
    me = lax.axis_index("clus")
    targets = operator_ref.shape[0]
    own = targets // peers
    share = chunks[0].shape[0] // (2 * own)
    skip = lax.rem(me * (2 * share), 8)
    for number, chunk in enumerate(chunks):
        doubled(chunk, real_twice, imag_twice, number * own, own, share, frame, skip)

    def operator_of(target, devices, source):
        first = operator_ref[target, (me ^ devices[source // own]) * own + source % own]
        return wide_ref[pl.ds(pl.multiple_of(first, 8), frame), :]

    def some_targets(i, carry):
        some = [i * TOGETHER + j for j in range(TOGETHER)]
        places = [pl.ds(pl.multiple_of(target * frame, 8), frame) for target in some]
        if before:
            sums = [tuple(ref[place, :] for ref in before) for place in places]
        else:
            sums = [(jnp.zeros((frame, LANES), f32),) * 2 for _ in some]
        operators = lambda j, source: operator_of(some[j], masks, source)
        sums = add_sources(sums, len(masks) * own, frame, operators, real_twice, imag_twice)
        for place, (by_real, by_imag) in zip(places, sums):
            real_sum[place, :] = by_real
            imag_sum[place, :] = by_imag
        return carry

    lax.fori_loop(0, targets // TOGETHER, some_targets, 0)

    def late_operators(target, carry):
        for source in range(len(late) * own):
            place = pl.multiple_of((target * (len(late) * own) + source) * frame, 8)
            late_ref[pl.ds(place, frame), :] = operator_of(target, late, source)
        return carry

    if late:
        lax.fori_loop(0, targets, late_operators, 0)


def translate_kernel(frame, masks, targets, late_ref, real_sum, imag_sum, *rest):
    prepare = len(rest) == len(masks) + len(targets) + 4
    chunks, rest = (rest[: len(masks)], rest[len(masks) :]) if prepare else ((), rest)
    real_twice, imag_twice = rest[:2]
    outs, (total_real, total_imag) = rest[-2 - len(targets) : -2], rest[-2:]
    me = lax.axis_index("clus")
    sources = real_twice.shape[0] // frame
    own = sources // len(masks)
    share = outs[0].shape[0] // (2 * own)
    skip = lax.rem(me * (2 * share), 8)
    for number, chunk in enumerate(chunks):
        doubled(chunk, real_twice, imag_twice, number * own, own, share, frame, skip)
    even, odd = pl.ds(skip, share, stride=2), pl.ds(skip + 1, share, stride=2)
    for out, d in zip(outs, targets):
        first = (me ^ d) * own

        def some_targets(i, carry):
            places = [i * TOGETHER + j for j in range(TOGETHER)]
            some = [first + g for g in places]
            rows = [pl.ds(pl.multiple_of(target * frame, 8), frame) for target in some]
            sums = [(real_sum[r, :], imag_sum[r, :]) for r in rows]

            def operators(j, source):
                place = pl.multiple_of((some[j] * sources + source) * frame, 8)
                return late_ref[pl.ds(place, frame), :]

            sums = add_sources(sums, sources, frame, operators, real_twice, imag_twice)
            for j, (g, (by_real, by_imag)) in enumerate(zip(places, sums)):
                total_real[j] = by_real
                total_imag[j] = by_imag
                row = g * (2 * share)
                out[pl.ds(row, share), :] = total_real[j, even, :] - total_imag[j, odd, :]
                out[pl.ds(row + share, share), :] = total_real[j, odd, :] + total_imag[j, even, :]
            return carry

        lax.fori_loop(0, own // TOGETHER, some_targets, 0)


def edge_kernel(peers, own2, parents_ref, edge_phase_ref, gather_ref, *rest):
    chunks = rest[:peers]
    flat, far_ref, near_ref = rest[peers:]
    share = chunks[0].shape[0] // own2
    periods = share * peers // ROWS_PER_PERIOD
    own = own2 // 2
    pairs = far_ref.shape[1]
    flat_rows = ROWS_PER_PERIOD * periods
    me = lax.axis_index("clus")
    for gp in range(own2):
        for d in range(peers):
            flat[pl.ds(gp * flat_rows + (me ^ d) * share, share), :] = chunks[d][gp * share : (gp + 1) * share, :]
    edges = []
    for w, m in edge_rows(periods):
        for part in range(2):
            edges.append(flat[pl.ds(part * flat_rows + ROWS_PER_PERIOD * m + w, own, stride=2 * flat_rows), :])
    per_child = dot2(one_hot(parents_ref[...], own).T, jnp.concatenate(edges, axis=1))
    returned = []
    for e in range(len(edges) // 2):
        real = per_child[:, 2 * e * LANES : (2 * e + 1) * LANES]
        imaginary = per_child[:, (2 * e + 1) * LANES : (2 * e + 2) * LANES]
        cosine, sine = edge_phase_ref[e, 0], edge_phase_ref[e, 1]
        returned.append(
            jnp.concatenate([real * cosine + imaginary * sine, imaginary * cosine - real * sine], axis=0)
        )
    join = functools.partial(jnp.concatenate, axis=1)
    even = jnp.concatenate([join([returned[2], returned[3]]), join([returned[4], returned[5]])], axis=0)
    odd = jnp.concatenate([join([returned[0], returned[1]]), join([returned[5], returned[6]])], axis=0)
    even = gather_dot(*split(even), gather_ref, 0)
    odd = gather_dot(*split(odd), gather_ref, 1)
    a, b = TAPS_A, TAPS_B

    def fill(prev_ref, next_ref):
        below = a[0] * odd[:pairs] + b[0] * even[:pairs]
        for i in range(2):
            prev_ref[i] = below
            next_ref[i] = a[3 + i] * even[pairs:] + b[3 + i] * odd[pairs:]

    by_parity(lambda: fill(far_ref, near_ref), lambda: fill(near_ref, far_ref))


def disaggregate_kernel(
    parents_ref, octants_ref, flat_ref, phase_ref, gather_ref, out_ref, edge_ref, listed, incoming_ref, lhs, coarse_e, coarse_o, whole_out, sems
):
    periods = incoming_ref.shape[2]
    packed = parents_ref[...] * 8 + octants_ref[...]
    for k in range(listed.shape[0]):
        listed[k] = packed[0, k]
    for gp in range(incoming_ref.shape[0]):
        for w in range(ROWS_PER_PERIOD):
            first = gp * ROWS_PER_PERIOD * periods + w
            incoming_ref[gp, w] = flat_ref[pl.ds(first, periods, stride=ROWS_PER_PERIOD), :]
    azimuth_in = periods * PERIOD_C
    sublane = lax.broadcasted_iota(jnp.int32, (periods, LANES), 0)
    inner = pl.ds(TILE, azimuth_in - 2 * TILE)

    def shift(block):
        for k in range(BLOCK):
            code = listed[block * BLOCK + k]
            octant, parent = code & 7, code >> 3
            for r in range(3):
                for i in range(3):
                    w = 3 * r + i
                    real, imaginary = incoming_ref[2 * parent, w], incoming_ref[2 * parent + 1, w]
                    cosine, sine = phase_ref[octant, 0, w], phase_ref[octant, 1, w]
                    returned = (real * cosine + imaginary * sine, imaginary * cosine - real * sine)
                    for part in range(2):
                        base = ((2 * k + part) * 3 + r) * periods
                        lhs[base : base + periods, i * LANES : (i + 1) * LANES] = returned[part]

    def polar():
        high, low = split(lhs[...])
        coarse_e[...] = gather_dot(high[:, : 2 * LANES], low[:, : 2 * LANES], gather_ref, 0)
        coarse_o[...] = gather_dot(high[:, LANES:], low[:, LANES:], gather_ref, 1)

    def azimuth(block):
        for j in range(2 * BLOCK):
            c = []
            for r in range(3):
                base = (j * 3 + r) * periods
                c.append(coarse_e[base : base + periods, :])
                c.append(coarse_o[base : base + periods, :])
            lower = both_taps_transposed(c[1], c[2])
            upper = both_taps_transposed(c[4], c[5])
            down = [jnp.where(sublane == 0, 0.0, pltpu.roll(upper[i], 1, 0)) for i in (3, 4)]
            up = jnp.where(sublane == periods - 1, 0.0, pltpu.roll(lower[0], periods - 1, 0))
            rows = [c[0] + lower[1] + down[0], lower[2] + upper[0] + down[1], c[3] + lower[3] + upper[1], lower[4] + upper[2] + up]
            kp = block * (2 * BLOCK) + j
            for u in range(PERIOD_C):
                whole_out[kp, pl.ds(u, periods, stride=PERIOD_C), :] = rows[u]
            edge_ref[0, kp] = whole_out[kp, :TILE, :]
            edge_ref[1, kp] = whole_out[kp, azimuth_in - TILE :, :]

    def written(block):
        some = pl.ds(block * (2 * BLOCK), 2 * BLOCK)
        return pltpu.make_async_copy(whole_out.at[some, inner, :], out_ref.at[some, inner, :], sems.at[block])

    def one_block(block, carry):
        shift(block)
        polar()
        azimuth(block)
        written(block).start()
        return carry

    blocks = listed.shape[0] // BLOCK
    lax.fori_loop(0, blocks, one_block, 0)
    for block in range(blocks):
        written(block).wait()


def finish_kernel(edge_ref, far_ref, near_ref, part_ref, out_ref, tiles, sems):
    pairs, azimuth_in, _ = out_ref.shape
    tiles[...] = edge_ref[...]
    flat = tiles.reshape(2 * pairs * TILE, LANES)
    before, after = from_sides(far_ref, near_ref)
    ends = ((0, 0, before[0]), (0, 1, before[1]), (1, TILE - 1, after[0]))
    copies = []
    for i, start in enumerate((0, azimuth_in - TILE)):
        for end, row, values in ends:
            if end == i:
                for part in range(2):
                    for k in range(0, pairs // 2, 8):
                        source = slice(part * (pairs // 2) + k, part * (pairs // 2) + k + 8)
                        rows = pl.ds((i * pairs + 2 * k + part) * TILE + row, 8, stride=2 * TILE)
                        flat[rows, :] = flat[rows, :] + values[source]
        copy = pltpu.make_async_copy(tiles.at[i], out_ref.at[:, pl.ds(start, TILE), :], sems.at[i])
        copy.start()
        copies.append(copy)
    for copy in copies:
        copy.wait()


def swapped(values, axis, first):
    size = lax.axis_size(axis)
    return lax.ppermute(values, axis, [(i, (((i - first) ^ 1) + first) % size) for i in range(size)])


def exchanged(values, axis, mask):
    size = lax.axis_size(axis)
    return lax.ppermute(values, axis, [(i, i ^ mask) for i in range(size)])


SMEM = pl.BlockSpec(memory_space=pltpu.SMEM)
VMEM = pl.BlockSpec(memory_space=pltpu.VMEM)
HBM = pl.BlockSpec(memory_space=pltpu.HBM)


def in_hbm(values):
    return pltpu.with_memory_space_constraint(values, pltpu.HBM)


def local_call(kernel, out_shape, in_specs, scratch, grant, flops=1_000_000, bytes_accessed=1_000_000, out_specs=None, aliases={}):
    return pl.pallas_call(
        kernel,
        out_shape=out_shape,
        in_specs=in_specs,
        out_specs=jax.tree.map(lambda _: VMEM, out_shape) if out_specs is None else out_specs,
        scratch_shapes=scratch,
        input_output_aliases=aliases,
        compiler_params=pltpu.CompilerParams(vmem_limit_bytes=grant << 20),
        cost_estimate=pl.CostEstimate(flops=flops, bytes_accessed=bytes_accessed, transcendentals=0),
    )


def on_device_exchange(
    child_patterns, trans_table, child_parent, child_octant, partner_src, partner_off, partner_count
):
    children, _, azimuth_in, polar_in = child_patterns.shape
    pairs = 2 * children
    peers = lax.axis_size("clus")
    parent_total, _ = partner_src.shape
    own = parent_total // peers
    periods = azimuth_in // PERIOD_C
    flat_rows = ROWS_PER_PERIOD * periods
    share = flat_rows // peers
    offsets = trans_table.shape[0]
    array = lambda *shape: jax.ShapeDtypeStruct(shape, f32)
    buffer = lambda *shape: pltpu.VMEM(shape, f32)
    edges = len(edge_rows(periods))
    even, odd = polar_blocks()
    spread = jnp.asarray(np.stack([np.concatenate([h, h, l]) for h, l in (split_np(even), split_np(odd))]))
    edge = array(2, pairs, polar_in)
    to_far, to_near = local_call(
        rows_kernel, [edge, edge], [HBM], [buffer(pairs, TILE, polar_in)] * 2 + [pltpu.SemaphoreType.DMA((2,))], 8
    )(in_hbm(child_patterns.reshape(pairs, azimuth_in, polar_in)))
    from_far = swapped(to_far, "dir", 1)
    from_near = swapped(to_near, "dir", 0)
    odd_gather = np.concatenate([odd.T[LANES:], odd.T[:LANES]])
    gather = np.stack([np.concatenate(split_np(m), axis=1) for m in (even.T, odd_gather)])

    frame = max(-(-((q * 2 * share) % 8 + 2 * share) // 8) * 8 for q in range(peers))
    view = trans_table.reshape(offsets, 2, flat_rows, LANES).transpose(0, 2, 1, 3).reshape(offsets, 2 * flat_rows, LANES)
    blocks = children // BLOCK
    rows = 2 * BLOCK * 3 * periods
    phases, edge_phases, flat, table = local_call(
        functools.partial(main_kernel, peers),
        [
            array(8, 2, ROWS_PER_PERIOD, periods, LANES),
            array(edges, 2, children, LANES),
            array(2 * own * flat_rows, LANES),
            jax.ShapeDtypeStruct((offsets, frame, LANES), bf16),
        ],
        [HBM] * 5,
        [
            pltpu.SMEM((children,), jnp.int32),
            pltpu.SMEM((children,), jnp.int32),
            buffer(pairs * azimuth_in, polar_in),
            pltpu.VMEM(spread.shape, bf16),
            buffer(rows, LANES),
            buffer(rows, LANES),
            buffer(rows, 2 * LANES),
            buffer(rows, 2 * LANES),
            buffer(own, 2, ROWS_PER_PERIOD, periods, LANES),
            buffer(2 * own * flat_rows, LANES),
            pltpu.SemaphoreType.DMA((5,)),
        ],
        24,
        flops=4_000_000_000,
        bytes_accessed=12_000_000,
    )(
        in_hbm(child_parent[0]),
        in_hbm(child_octant),
        in_hbm(child_patterns.reshape(pairs * azimuth_in, polar_in)),
        in_hbm(view),
        in_hbm(spread),
    )

    chunk = array(2 * own * share, LANES)
    sent = local_call(
        functools.partial(fix_kernel, peers, own), [chunk] * peers, [VMEM] * 6, [buffer(2 * own * flat_rows, LANES)], 8
    )(child_parent, from_far, from_near, flat, edge_phases, spread)

    masks = sorted(range(1, peers), key=lambda d: bin(d).count("1"))
    early, late = masks[:1], masks[1:]
    received = {0: sent[0]}
    for d in early:
        received[d] = exchanged(sent[d], "clus", d)
    for d in late:
        received[d] = exchanged(sent[d], "clus", d)

    sum_pair = [array(parent_total * frame, LANES)] * 2
    wide, operator, *sums = local_call(
        functools.partial(widen_kernel, peers),
        [array((offsets + 1) * frame, LANES), jax.ShapeDtypeStruct((parent_total, parent_total), jnp.int32)] + sum_pair,
        [VMEM] * 5,
        [pltpu.SMEM((parent_total, parent_total), jnp.int32)]
        + [buffer(own * frame, LANES)] * 2
        + [pltpu.SemaphoreType.DMA],
        20,
        flops=90_000_000,
        bytes_accessed=12_000_000,
    )(partner_src, partner_off, partner_count.reshape(1, parent_total), table, received[0])

    late_sources = len(late) * own
    *sums, late_operators = local_call(
        functools.partial(gather_kernel, peers, frame, tuple(early), tuple(late)),
        sum_pair + [array(parent_total * late_sources * frame, LANES)],
        [SMEM] + [VMEM] * (3 + len(early)),
        [buffer(len(early) * own * frame, LANES)] * 2,
        28,
        flops=60_000_000,
        bytes_accessed=12_000_000,
    )(operator, wide, *[received[d] for d in early], *sums)

    back = {}
    last_sources = [received[d] for d in late]
    for number, targets in enumerate((masks[-1:], masks[:-1], [0])):
        prepare = number == 0
        results = local_call(
            functools.partial(translate_kernel, frame, tuple(late), tuple(targets)),
            ([array(late_sources * frame, LANES)] * 2 if prepare else []) + [chunk] * len(targets),
            [VMEM] * (3 + len(last_sources)),
            [buffer(TOGETHER, frame, LANES)] * 2,
            20,
            flops=10_000_000 * len(targets),
            bytes_accessed=2_000_000 * len(targets),
        )(late_operators, *sums, *last_sources)
        if prepare:
            last_sources, results = results[:2], results[2:]
        for d, result in zip(targets, results):
            back[d] = exchanged(result, "clus", d) if d else result

    incoming, to_far, to_near = local_call(
        functools.partial(edge_kernel, peers, 2 * own),
        [array(2 * own * flat_rows, LANES), edge, edge],
        [VMEM] * (3 + peers),
        [],
        8,
    )(child_parent, edge_phases, gather, *[back[d] for d in range(peers)])

    from_far = swapped(to_far, "dir", 1)
    from_near = swapped(to_near, "dir", 0)

    inner, edge_tiles = local_call(
        disaggregate_kernel,
        [array(pairs, azimuth_in, polar_in), array(2, pairs, TILE, polar_in)],
        [VMEM] * 5,
        [
            pltpu.SMEM((children,), jnp.int32),
            buffer(2 * own, ROWS_PER_PERIOD, periods, LANES),
            buffer(rows, 3 * LANES),
            buffer(rows, LANES),
            buffer(rows, LANES),
            buffer(pairs, azimuth_in, polar_in),
            pltpu.SemaphoreType.DMA((blocks,)),
        ],
        24,
        flops=4_000_000_000,
        bytes_accessed=12_000_000,
        out_specs=[HBM, VMEM],
    )(child_parent, child_octant.reshape(1, children), incoming, phases, gather)

    out = local_call(
        finish_kernel,
        array(pairs, azimuth_in, polar_in),
        [VMEM] * 3 + [HBM],
        [buffer(2, pairs, TILE, polar_in), pltpu.SemaphoreType.DMA((2,))],
        8,
        out_specs=HBM,
        aliases={3: 0},
    )(edge_tiles, from_far, from_near, in_hbm(inner))
    return out.reshape(child_patterns.shape)


def with_halo(shard, sides, width):
    for axis, dim in sides:
        size, length = (lax.axis_size(axis), shard.shape[dim])
        up = [(i, (i + 1) % size) for i in range(size)]
        down = [(j, i) for i, j in up]
        last = lax.slice_in_dim(shard, length - width, length, axis=dim)
        initial = lax.slice_in_dim(shard, 0, width, axis=dim)
        before = lax.ppermute(last, axis, up)
        after = lax.ppermute(initial, axis, down)
        shard = jnp.concatenate([before, shard, after], axis=dim)
    return shard


def lagrange_rows(offset):
    weights = []
    for anchor in range(5):
        factor = jnp.ones_like(offset)
        for neighbour in range(5):
            if neighbour != anchor:
                factor = factor * (offset - neighbour) / (anchor - neighbour)
        weights.append(factor)
    return weights


def polar_matrix_of(rows_out, rows_in):
    target = (jnp.arange(rows_out, dtype=jnp.float32) + 0.5) * rows_in / rows_out - 0.5
    start_row = jnp.clip(jnp.floor(target + 0.5).astype(jnp.int32) - 2, 0, rows_in - 5)
    weights = lagrange_rows(target - start_row.astype(jnp.float32))
    columns = jnp.arange(rows_in, dtype=jnp.int32)
    matrix = jnp.zeros((rows_out, rows_in), jnp.float32)
    for anchor in range(5):
        matrix = matrix + jnp.where(
            columns[None, :] == (start_row + anchor)[:, None], weights[anchor][:, None], 0.0
        )
    return matrix


def azimuth_matrix_of(out_index, in_index, total_out, total_in):
    target = (out_index * total_in).astype(jnp.float32) / total_out
    nearest = jnp.floor(target + 0.5).astype(jnp.int32)
    weights = lagrange_rows(target - nearest.astype(jnp.float32) + 2.0)
    matrix = jnp.zeros((out_index.shape[0], in_index.shape[0]), jnp.float32)
    for anchor in range(5):
        columns = nearest + anchor - 2
        matrix = matrix + jnp.where(
            in_index[None, :] == columns[:, None], weights[anchor][:, None], 0.0
        )
    return matrix


def shift_phases(octant, azimuth_index, azimuth_total, polar_total):
    azimuth = 2.0 * math.pi * azimuth_index.astype(jnp.float32) / azimuth_total
    polar = math.pi * (jnp.arange(polar_total, dtype=jnp.float32) + 0.5) / polar_total
    first_axis = jnp.sin(polar)[None, :] * jnp.cos(azimuth)[:, None]
    second_axis = jnp.sin(polar)[None, :] * jnp.sin(azimuth)[:, None]
    third_axis = jnp.cos(polar)[None, :] * jnp.ones_like(azimuth)[:, None]
    first_sign = (1 - 2 * (octant % 2)).astype(jnp.float32)
    second_sign = (1 - 2 * (octant // 2 % 2)).astype(jnp.float32)
    third_sign = (1 - 2 * (octant // 4)).astype(jnp.float32)
    phase_angle = phase_scale * (
        first_sign[:, None, None] * first_axis[None]
        + second_sign[:, None, None] * second_axis[None]
        + third_sign[:, None, None] * third_axis[None]
    )
    return (jnp.cos(phase_angle), jnp.sin(phase_angle))


def translate(sources, table, partner_src, partner_off, partner_count):
    live_mask = (
        jnp.arange(partner_src.shape[1], dtype=jnp.int32)[None, :] < partner_count[:, None]
    ).astype(jnp.float32)
    picked = sources[partner_src]
    operator = table[partner_off].astype(jnp.float32) * live_mask[:, :, None, None]
    real_part = jnp.sum(
        operator[:, :, 0] * picked[:, :, 0] - operator[:, :, 1] * picked[:, :, 1], axis=1
    )
    imaginary = jnp.sum(
        operator[:, :, 0] * picked[:, :, 1] + operator[:, :, 1] * picked[:, :, 0], axis=1
    )
    return jnp.stack([real_part, imaginary], axis=1)


def forward_shift(patterns, cosine, sine_part):
    real_part = patterns[:, 0] * cosine - patterns[:, 1] * sine_part
    imaginary = patterns[:, 0] * sine_part + patterns[:, 1] * cosine
    return jnp.stack([real_part, imaginary], axis=1)


def conjugate_shift(patterns, cosine, sine_part):
    real_part = patterns[:, 0] * cosine + patterns[:, 1] * sine_part
    imaginary = patterns[:, 1] * cosine - patterns[:, 0] * sine_part
    return jnp.stack([real_part, imaginary], axis=1)


def on_device_gather(
    child_patterns, trans_table, child_parent, child_octant, partner_src, partner_off, partner_count
):
    _, _, azimuth_in, _ = child_patterns.shape
    polar_out = NTHETA_P
    azimuth_out = trans_table.shape[2] // polar_out
    parent_slots = partner_src.shape[0] // lax.axis_size("clus")
    cluster_index = lax.axis_index("clus")
    direction_index = lax.axis_index("dir")
    parents = child_parent[0]
    polar_matrix = polar_matrix_of(NTHETA_P, NTHETA_C)
    onehot = (parents[None, :] == jnp.arange(parent_slots, dtype=jnp.int32)[:, None]).astype(
        jnp.float32
    )
    own_rows = jnp.mod(
        direction_index * azimuth_out + jnp.arange(azimuth_out, dtype=jnp.int32), NPHI_P
    )
    cosine, sine_part = shift_phases(child_octant, own_rows, NPHI_P, polar_out)
    extended = with_halo(child_patterns, (("dir", 2),), 2)
    gather_matrix = azimuth_matrix_of(
        jnp.arange(azimuth_out, dtype=jnp.int32),
        jnp.arange(azimuth_in + 4, dtype=jnp.int32) - 2,
        NPHI_P,
        NPHI_C,
    )
    along_azimuth = jnp.einsum("pc,kacz->kapz", gather_matrix, extended, precision=highest)
    refined = jnp.einsum("kapz,tz->kapt", along_azimuth, polar_matrix, precision=highest)
    shifted = forward_shift(refined, cosine, sine_part)
    radiation = jnp.einsum("gk,kapt->gapt", onehot, shifted, precision=highest)
    flattened = radiation.reshape(parent_slots, 2, azimuth_out * polar_out)
    sources = lax.all_gather(flattened, "clus", axis=0, tiled=True)
    first_row = cluster_index * parent_slots
    own_src = lax.dynamic_slice_in_dim(partner_src, first_row, parent_slots, 0)
    own_off = lax.dynamic_slice_in_dim(partner_off, first_row, parent_slots, 0)
    own_count = lax.dynamic_slice_in_dim(partner_count, first_row, parent_slots, 0)
    incoming = translate(sources, trans_table, own_src, own_off, own_count)
    incoming = incoming.reshape(parent_slots, 2, azimuth_out, polar_out)
    return_matrix = azimuth_matrix_of(
        jnp.arange(azimuth_out + 6, dtype=jnp.int32) - 3,
        jnp.arange(azimuth_in, dtype=jnp.int32),
        NPHI_P,
        NPHI_C,
    )
    per_child = jnp.einsum("gk,gapt->kapt", onehot, incoming, precision=highest)
    returned = conjugate_shift(per_child, cosine, sine_part)
    coarse_own = jnp.einsum("kapt,tz->kapz", returned, polar_matrix, precision=highest)
    coarse = with_halo(coarse_own, (("dir", 2),), 3)
    return jnp.einsum("pc,kapz->kacz", return_matrix, coarse, precision=highest)


def solution(mesh):
    def on_device(child_patterns, trans_table, *rest):
        peers = lax.axis_size("clus")
        children, _, azimuth_in, polar_in = child_patterns.shape
        flat_rows = trans_table.shape[2] // LANES
        fits = (
            azimuth_in % (8 * PERIOD_C) == 0
            and polar_in == LANES
            and flat_rows * PERIOD_C == ROWS_PER_PERIOD * azimuth_in
            and flat_rows % peers == 0
            and peers & (peers - 1) == 0
            and peers > 2
            and lax.axis_size("dir") % 2 == 0
            and children % BLOCK == 0
        )
        plan = on_device_exchange if fits else on_device_gather
        return plan(child_patterns, trans_table, *rest)

    return jax.shard_map(
        on_device,
        mesh=mesh,
        in_specs=(
            P("clus", None, "dir", None),
            P(None, None, "dir"),
            P("clus", None),
            P("clus"),
            P(),
            P(),
            P(),
        ),
        out_specs=P("clus", None, "dir", None),
        check_vma=False,
    )
```

```python
import functools
import math

import jax
import jax.numpy as jnp
import numpy as np
from jax import lax
from jax.experimental import pallas as pl
from jax.experimental.pallas import tpu as pltpu
from jax.sharding import PartitionSpec as P


NTHETA_C = 128
NPHI_C = 256
NTHETA_P = 192
NPHI_P = 384

LANES = 128
PERIOD_P = 6
PERIOD_C = 4
ROWS_PER_PERIOD = PERIOD_P * NTHETA_P // LANES
GROUP = 8
TILE = 8
TOGETHER = 2
BLOCK = 2 * GROUP

phase_scale = 8.0 * math.pi
highest = lax.Precision.HIGHEST
f32 = jnp.float32
bf16 = jnp.bfloat16


def lagrange(offset):
    weights = []
    for anchor in range(5):
        factor = 1.0
        for neighbour in range(5):
            if neighbour != anchor:
                factor = factor * (offset - neighbour) / (anchor - neighbour)
        weights.append(factor)
    return weights


TAPS_A = [float(w) for w in lagrange(5.0 / 3.0)]
TAPS_B = [float(w) for w in lagrange(7.0 / 3.0)]


SUMS = [(TAPS_A[i] + TAPS_A[4 - i]) / 2 for i in range(2)]
DIFFS = [(TAPS_A[i] - TAPS_A[4 - i]) / 2 for i in range(2)]
CENTRE = TAPS_A[2]


def polar_matrix_np():
    target = (np.arange(NTHETA_P, dtype=np.float32) + np.float32(0.5)) * NTHETA_C / NTHETA_P - np.float32(0.5)
    start = np.clip(np.floor(target + 0.5).astype(np.int32) - 2, 0, NTHETA_C - 5)
    weights = lagrange((target - start).astype(np.float64))
    matrix = np.zeros((NTHETA_P, NTHETA_C), np.float64)
    for anchor in range(5):
        matrix[np.arange(NTHETA_P), start + anchor] += weights[anchor]
    return matrix.astype(np.float32)


def polar_blocks():
    matrix = polar_matrix_np().T
    even = np.zeros((NTHETA_C, 2 * LANES), np.float32)
    odd = np.zeros((NTHETA_C, 2 * LANES), np.float32)
    half = NTHETA_P - LANES
    even[:, :NTHETA_P] = matrix
    odd[:, :LANES] = matrix[:, half:]
    odd[:, 2 * LANES - half :] = matrix[:, :half]
    return even, odd


def split_np(matrix):
    high = matrix.astype(bf16)
    low = (matrix - high.astype(np.float32)).astype(bf16)
    return high, low


def split(values):
    high = values.astype(bf16)
    low = (values - high.astype(f32)).astype(bf16)
    return high, low


def dot(left, right):
    return jnp.dot(left, right, preferred_element_type=f32)


def spread_dot(values, matrix_ref, i):
    high, low = split(values)
    depth = values.shape[1]
    return dot(jnp.concatenate([high, low], axis=1), matrix_ref[i, : 2 * depth]) + dot(high, matrix_ref[i, 2 * depth :])


def gather_dot(high, low, matrix_ref, i):
    width = matrix_ref.shape[2] // 2
    both = dot(high, matrix_ref[i])
    return both[:, :width] + (both[:, width:] + dot(low, matrix_ref[i, :, :width]))


SIN_COEFFS = [(-1) ** k * math.pi ** (2 * k + 1) / math.factorial(2 * k + 1) for k in range(7)]
COS_COEFFS = [(-1) ** k * math.pi ** (2 * k) / math.factorial(2 * k) for k in range(7)]


def sincos_turns(turns):
    rest = turns - jnp.round(turns)
    square = rest * rest
    sine = jnp.full_like(square, SIN_COEFFS[-1])
    for coeff in SIN_COEFFS[-2::-1]:
        sine = sine * square + coeff
    sine = sine * rest
    cosine = jnp.full_like(square, COS_COEFFS[-1])
    for coeff in COS_COEFFS[-2::-1]:
        cosine = cosine * square + coeff
    return 2.0 * sine * cosine, 1.0 - 2.0 * sine * sine


def fill_phases(direction, out_ref):
    periods = out_ref.shape[3]
    lane = lax.broadcasted_iota(jnp.int32, (periods, LANES), 1)
    period = lax.broadcasted_iota(jnp.int32, (periods, LANES), 0)
    first = direction * (PERIOD_P * periods)

    def two_rows(r, carry):
        for i in range(3):
            position = lane + i * LANES
            second = (position >= NTHETA_P).astype(jnp.int32)
            polar_index = position - second * NTHETA_P
            azimuth_index = first + period * PERIOD_P + 2 * r + second
            sin_polar, cos_polar = sincos_turns((polar_index.astype(f32) + 0.5) / (2 * NTHETA_P))
            sin_azimuth, cos_azimuth = sincos_turns(azimuth_index.astype(f32) / NPHI_P)
            along_x = 4.0 * sin_polar * cos_azimuth
            along_y = 4.0 * sin_polar * sin_azimuth
            along_z = 4.0 * cos_polar
            w = 3 * r + i
            for octant in (0, 2, 4, 6):
                turns = along_x + along_y if octant % 4 == 0 else along_x - along_y
                turns = turns + along_z if octant < 4 else turns - along_z
                sine, cosine = sincos_turns(turns)
                out_ref[octant, 0, w] = cosine
                out_ref[octant, 1, w] = sine
                out_ref[7 - octant, 0, w] = cosine
                out_ref[7 - octant, 1, w] = -sine
        return carry

    lax.fori_loop(0, PERIOD_P // 2, two_rows, 0)


def edge_rows(periods):
    return [(w, 0) for w in (1, 2, 3, 4)] + [(w, periods - 1) for w in (6, 7, 8)]


def by_parity(even, odd):
    parity = lax.rem(lax.axis_index("dir"), 2)
    pl.when(parity == 0)(even)
    pl.when(parity == 1)(odd)


def from_sides(far_ref, near_ref):
    is_even = lax.rem(lax.axis_index("dir"), 2) == 0
    far, near = far_ref[...], near_ref[...]
    return jnp.where(is_even, far, near), jnp.where(is_even, near, far)


def rows_kernel(x_ref, far_ref, near_ref, low, high, sems):
    pairs, azimuth_in, _ = x_ref.shape
    low_copy = pltpu.make_async_copy(x_ref.at[:, pl.ds(0, TILE), :], low, sems.at[0])
    high_copy = pltpu.make_async_copy(x_ref.at[:, pl.ds(azimuth_in - TILE, TILE), :], high, sems.at[1])
    low_copy.start()
    high_copy.start()
    low_copy.wait()
    high_copy.wait()
    low_rows, high_rows = (ref.reshape(pairs * TILE, LANES) for ref in (low, high))

    def fill(first_ref, last_ref):
        for part in range(2):
            for k in range(0, pairs // 2, 8):
                target = slice(part * (pairs // 2) + k, part * (pairs // 2) + k + 8)
                base = (2 * k + part) * TILE
                for i in range(2):
                    first_ref[i, target] = low_rows[pl.ds(base + i, 8, stride=2 * TILE), :]
                last = high_rows[pl.ds(base + TILE - 1, 8, stride=2 * TILE), :]
                for i in range(2):
                    last_ref[i, target] = last

    by_parity(lambda: fill(far_ref, near_ref), lambda: fill(near_ref, far_ref))


def both_taps(rows):
    even = SUMS[0] * (rows[0] + rows[4]) + SUMS[1] * (rows[1] + rows[3]) + CENTRE * rows[2]
    odd = DIFFS[0] * (rows[0] - rows[4]) + DIFFS[1] * (rows[1] - rows[3])
    return even + odd, even - odd


def both_taps_transposed(first, second):
    total, difference = first + second, first - second
    outer = [SUMS[i] * total for i in range(2)]
    inner = [DIFFS[i] * difference for i in range(2)]
    return [outer[0] + inner[0], outer[1] + inner[1], CENTRE * total, outer[1] - inner[1], outer[0] - inner[0]]


def main_kernel(peers, parents_hbm, octants_hbm, x_hbm, table_ref, spread_hbm, *rest):
    phase_ref, edge_phase_ref, flat_ref, slice_ref = rest[:4]
    parents_ref, octants_ref, x_ref, spread_ref, az_e, az_o, res_e, res_o, acc, flat, sems = rest[4:]
    children = octants_ref.shape[0]
    periods = phase_ref.shape[3]
    azimuth_in = periods * PERIOD_C
    own = acc.shape[0]
    me = lax.axis_index("clus")
    share = ROWS_PER_PERIOD * periods // peers
    first_tile = me * (2 * share) // 8
    table_rows = pl.ds(pl.multiple_of(first_tile * 8, 8), slice_ref.shape[1])
    ends = (
        (octants_hbm, octants_ref),
        (parents_hbm, parents_ref),
        (x_hbm, x_ref),
        (spread_hbm, spread_ref),
        (table_ref.at[:, table_rows, :], slice_ref),
    )
    copies = [pltpu.make_async_copy(source, target, sems.at[i]) for i, (source, target) in enumerate(ends)]
    for copy in copies[:-1]:
        copy.start()
    fill_phases(lax.axis_index("dir"), phase_ref)
    acc[...] = jnp.zeros_like(acc)
    sublane = lax.broadcasted_iota(jnp.int32, (periods, LANES), 0)
    copies[0].wait()

    def edges_of(step, carry):
        for j in range(GROUP):
            k = step * GROUP + j
            octant = octants_ref[k]
            for e, (w, m) in enumerate(edge_rows(periods)):
                for i in range(2):
                    edge_phase_ref[e, i, pl.ds(k, 1), :] = phase_ref[octant, i, w, m : m + 1, :]
        return carry

    lax.fori_loop(0, children // GROUP, edges_of, 0)
    for copy in copies[1:-1]:
        copy.wait()
    copies[-1].start()

    def azimuth(block):
        for kp in range(2 * BLOCK):
            start = pl.multiple_of((block * (2 * BLOCK) + kp) * azimuth_in, 8)
            x = [x_ref[pl.ds(start + u, periods, stride=PERIOD_C), :] for u in range(PERIOD_C)]
            left = jnp.where(sublane == 0, 0.0, pltpu.roll(x[3], 1, 0))
            right = [jnp.where(sublane == periods - 1, 0.0, pltpu.roll(x[i], periods - 1, 0)) for i in range(2)]
            lower = [left, x[0], x[1], x[2], x[3]]
            upper = [x[1], x[2], x[3], right[0], right[1]]
            rows = [x[0], *both_taps(lower), x[2], *both_taps(upper)]
            for r in range(3):
                base = (kp * 3 + r) * periods
                az_e[base : base + periods, :] = rows[2 * r]
                az_o[base : base + periods, :] = rows[2 * r + 1]

    def polar():
        res_e[...] = spread_dot(az_e[...], spread_ref, 0)
        res_o[...] = spread_dot(az_o[...], spread_ref, 1)

    def shift(block):
        for k in range(BLOCK):
            octant = octants_ref[block * BLOCK + k]
            parent = parents_ref[block * BLOCK + k]
            for r in range(3):
                parts = []
                for part in range(2):
                    rows = pl.ds(((2 * k + part) * 3 + r) * periods, periods)
                    middle = res_e[rows, LANES:] + res_o[rows, LANES:]
                    parts.append((res_e[rows, :LANES], middle, res_o[rows, :LANES]))
                for i in range(3):
                    w = 3 * r + i
                    real, imaginary = parts[0][i], parts[1][i]
                    cosine, sine = phase_ref[octant, 0, w], phase_ref[octant, 1, w]
                    acc[parent, 0, w] += real * cosine - imaginary * sine
                    acc[parent, 1, w] += real * sine + imaginary * cosine

    def one_block(block, carry):
        azimuth(block)
        polar()
        shift(block)
        return carry

    lax.fori_loop(0, children // BLOCK, one_block, 0)
    for gp in range(2 * own):
        for w in range(ROWS_PER_PERIOD):
            flat[pl.ds(gp * ROWS_PER_PERIOD * periods + w, periods, stride=ROWS_PER_PERIOD), :] = acc[gp // 2, gp % 2, w]
        for q in range(peers):
            source = gp * ROWS_PER_PERIOD * periods + q * share
            target = (q * 2 * own + gp) * share
            flat_ref[target : target + share, :] = flat[source : source + share, :]
    copies[-1].wait()


def one_hot(parents, own):
    index = lax.broadcasted_iota(jnp.int32, (own, parents.shape[1]), 0)
    return (index == parents).astype(f32)


def dot2(exact, values):
    exact = exact.astype(bf16)
    high, low = split(values)
    return dot(exact, high) + dot(exact, low)


def fix_kernel(
    peers, own, parents_ref, far_ref, near_ref, flat_ref, edge_phase_ref, spread_ref, *rest
):
    outs, (fixed,) = rest[:peers], rest[peers:]
    pairs = far_ref.shape[1]
    children = pairs // 2
    chunk_rows = outs[0].shape[0]
    share = chunk_rows // (2 * own)
    periods = share * peers // ROWS_PER_PERIOD
    fixed[...] = flat_ref[...]
    before, right = from_sides(far_ref, near_ref)
    left = before[0]
    a, b = TAPS_A, TAPS_B
    even = jnp.concatenate([b[0] * left, a[3] * right[0] + a[4] * right[1]], axis=0)
    odd = jnp.concatenate([a[0] * left, b[3] * right[0] + b[4] * right[1]], axis=0)
    even = spread_dot(even, spread_ref, 0)
    odd = spread_dot(odd, spread_ref, 1)
    first, last = slice(0, pairs), slice(pairs, 2 * pairs)
    low, high = slice(0, LANES), slice(LANES, 2 * LANES)
    refined = [
        odd[first, high],
        odd[first, low],
        even[first, low],
        even[first, high],
        even[last, low],
        even[last, high] + odd[last, high],
        odd[last, low],
    ]
    shifted_rows = []
    for e, rows in enumerate(refined):
        real, imaginary = rows[:children], rows[children:]
        cosine, sine = edge_phase_ref[e, 0], edge_phase_ref[e, 1]
        shifted_rows.append(real * cosine - imaginary * sine)
        shifted_rows.append(real * sine + imaginary * cosine)
    summed = dot2(one_hot(parents_ref[...], own), jnp.concatenate(shifted_rows, axis=1))
    for e, (w, m) in enumerate(edge_rows(periods)):
        q, row = divmod(ROWS_PER_PERIOD * m + w, share)
        for part in range(2):
            rows = pl.ds(q * chunk_rows + part * share + row, own, stride=2 * share)
            column = (2 * e + part) * LANES
            fixed[rows, :] = fixed[rows, :] + summed[:, column : column + LANES]
    me = lax.axis_index("clus")
    for d in range(peers):
        start = pl.multiple_of((me ^ d) * chunk_rows, 8)
        outs[d][...] = fixed[pl.ds(start, chunk_rows), :]


def widen_kernel(peers, others, source_ref, offset_ref, count_ref, table_ref, chunk, placed_ref, real_sum, imag_sum, *rest):
    wide_ref, numbers_ref, listed, real_twice, imag_twice, sem = rest
    targets, partners = source_ref.shape
    offsets, frame, _ = table_ref.shape
    own = targets // peers
    share = chunk.shape[0] // (2 * own)
    me = lax.axis_index("clus")
    shape = (targets, targets)
    row, lane = (lax.broadcasted_iota(jnp.int32, shape, d) for d in range(2))
    count = jnp.sum(jnp.where(row == lane, count_ref[...], 0), axis=1, keepdims=True)
    number = jnp.full(shape, offsets, jnp.int32)
    for p in range(partners):
        here = (lane == source_ref[:, p : p + 1]) & (p < count)
        number = jnp.where(here, offset_ref[:, p : p + 1], number)
    numbers_ref[...] = number * frame
    copy = pltpu.make_async_copy(numbers_ref, listed, sem)
    copy.start()

    def some_offsets(i, carry):
        for j in range(4):
            wide_ref[pl.ds(pl.multiple_of((i * 4 + j) * frame, 8), frame), :] = table_ref[i * 4 + j].astype(f32)
        return carry

    whole_steps = offsets // 4
    lax.fori_loop(0, whole_steps, some_offsets, 0)
    for offset in range(whole_steps * 4, offsets):
        wide_ref[offset * frame : (offset + 1) * frame, :] = table_ref[offset].astype(f32)
    wide_ref[offsets * frame :, :] = jnp.zeros((frame, LANES), f32)
    doubled(chunk, real_twice, imag_twice, 0, own, share, frame, lax.rem(me * (2 * share), 8))
    copy.wait()

    def operator_of(target, device, g):
        first = listed[target, device * own + g]
        return wide_ref[pl.ds(pl.multiple_of(first, 8), frame), :]

    def own_sources(some, sums):
        return add_sources(sums, own, frame, lambda j, source: operator_of(some[j], me, source), real_twice, imag_twice)

    for_some_targets(targets, frame, own_sources, None, (real_sum, imag_sum))

    def other_sources(target, carry):
        for i, d in enumerate(others):
            for g in range(own):
                place = pl.multiple_of(((target * len(others) + i) * own + g) * frame, 8)
                placed_ref[pl.ds(place, frame), :] = operator_of(target, me ^ d, g)
        return carry

    lax.fori_loop(0, targets, other_sources, 0)


def doubled(chunk, real_twice, imag_twice, first, own, share, frame, skip):
    for g in range(own):
        for part, twice in enumerate((real_twice, imag_twice)):
            rows = chunk[(2 * g + part) * share : (2 * g + part + 1) * share, :]
            base = (first + g) * frame + skip
            twice[pl.ds(base, share, stride=2), :] = rows
            twice[pl.ds(base + 1, share, stride=2), :] = rows


def add_sources(sums, sources, frame, operators, real_twice, imag_twice):
    for source in range(sources):
        place = slice(source * frame, (source + 1) * frame)
        real, imaginary = real_twice[place, :], imag_twice[place, :]
        for i in range(len(sums)):
            operator = operators(i, source)
            sums[i] = (sums[i][0] + operator * real, sums[i][1] + operator * imaginary)
    return sums


def for_some_targets(targets, frame, add, before, after):
    def some_targets(i, carry):
        some = [i * TOGETHER + j for j in range(TOGETHER)]
        places = [pl.ds(pl.multiple_of(target * frame, 8), frame) for target in some]
        if before is None:
            sums = [(jnp.zeros((frame, LANES), f32),) * 2 for _ in some]
        else:
            sums = [tuple(ref[place, :] for ref in before) for place in places]
        for place, values in zip(places, add(some, sums)):
            for ref, value in zip(after, values):
                ref[place, :] = value
        return carry

    lax.fori_loop(0, targets // TOGETHER, some_targets, 0)


def placed(placed_ref, frame, others, own, masks):
    firsts = [others.index(d) * own for d in masks]

    def operator_of(target, source):
        place = target * (len(others) * own) + firsts[source // own] + source % own
        return placed_ref[pl.ds(pl.multiple_of(place * frame, 8), frame), :]

    return operator_of


def gather_kernel(peers, frame, others, masks, placed_ref, *rest):
    chunks, (real_before, imag_before, real_sum, imag_sum, real_twice, imag_twice) = rest[:-6], rest[-6:]
    me = lax.axis_index("clus")
    targets = real_sum.shape[0] // frame
    own = targets // peers
    share = chunks[0].shape[0] // (2 * own)
    skip = lax.rem(me * (2 * share), 8)
    for number, chunk in enumerate(chunks):
        doubled(chunk, real_twice, imag_twice, number * own, own, share, frame, skip)
    operator_of = placed(placed_ref, frame, others, own, masks)

    def add(some, sums):
        operators = lambda j, source: operator_of(some[j], source)
        return add_sources(sums, len(masks) * own, frame, operators, real_twice, imag_twice)

    for_some_targets(targets, frame, add, (real_before, imag_before), (real_sum, imag_sum))


def translate_kernel(frame, others, masks, targets, placed_ref, real_sum, imag_sum, *rest):
    prepare = len(rest) == len(masks) + len(targets) + 4
    chunks, rest = (rest[: len(masks)], rest[len(masks) :]) if prepare else ((), rest)
    real_twice, imag_twice = rest[:2]
    outs, (total_real, total_imag) = rest[-2 - len(targets) : -2], rest[-2:]
    me = lax.axis_index("clus")
    sources = real_twice.shape[0] // frame
    own = sources // len(masks)
    share = outs[0].shape[0] // (2 * own)
    skip = lax.rem(me * (2 * share), 8)
    for number, chunk in enumerate(chunks):
        doubled(chunk, real_twice, imag_twice, number * own, own, share, frame, skip)
    operator_of = placed(placed_ref, frame, others, own, masks)
    even, odd = pl.ds(skip, share, stride=2), pl.ds(skip + 1, share, stride=2)
    for out, d in zip(outs, targets):
        first = (me ^ d) * own

        def some_targets(i, carry):
            places = [i * TOGETHER + j for j in range(TOGETHER)]
            some = [first + g for g in places]
            rows = [pl.ds(pl.multiple_of(target * frame, 8), frame) for target in some]
            sums = [(real_sum[r, :], imag_sum[r, :]) for r in rows]
            operators = lambda j, source: operator_of(some[j], source)
            sums = add_sources(sums, sources, frame, operators, real_twice, imag_twice)
            for j, (g, (by_real, by_imag)) in enumerate(zip(places, sums)):
                total_real[j] = by_real
                total_imag[j] = by_imag
                row = g * (2 * share)
                out[pl.ds(row, share), :] = total_real[j, even, :] - total_imag[j, odd, :]
                out[pl.ds(row + share, share), :] = total_real[j, odd, :] + total_imag[j, even, :]
            return carry

        lax.fori_loop(0, own // TOGETHER, some_targets, 0)


def edge_kernel(peers, own2, parents_ref, edge_phase_ref, gather_ref, *rest):
    chunks = rest[:peers]
    flat, far_ref, near_ref = rest[peers:]
    share = chunks[0].shape[0] // own2
    periods = share * peers // ROWS_PER_PERIOD
    own = own2 // 2
    pairs = far_ref.shape[1]
    flat_rows = ROWS_PER_PERIOD * periods
    me = lax.axis_index("clus")
    for gp in range(own2):
        for d in range(peers):
            flat[pl.ds(gp * flat_rows + (me ^ d) * share, share), :] = chunks[d][gp * share : (gp + 1) * share, :]
    edges = []
    for w, m in edge_rows(periods):
        for part in range(2):
            edges.append(flat[pl.ds(part * flat_rows + ROWS_PER_PERIOD * m + w, own, stride=2 * flat_rows), :])
    per_child = dot2(one_hot(parents_ref[...], own).T, jnp.concatenate(edges, axis=1))
    returned = []
    for e in range(len(edges) // 2):
        real = per_child[:, 2 * e * LANES : (2 * e + 1) * LANES]
        imaginary = per_child[:, (2 * e + 1) * LANES : (2 * e + 2) * LANES]
        cosine, sine = edge_phase_ref[e, 0], edge_phase_ref[e, 1]
        returned.append(
            jnp.concatenate([real * cosine + imaginary * sine, imaginary * cosine - real * sine], axis=0)
        )
    join = functools.partial(jnp.concatenate, axis=1)
    even = jnp.concatenate([join([returned[2], returned[3]]), join([returned[4], returned[5]])], axis=0)
    odd = jnp.concatenate([join([returned[0], returned[1]]), join([returned[5], returned[6]])], axis=0)
    even = gather_dot(*split(even), gather_ref, 0)
    odd = gather_dot(*split(odd), gather_ref, 1)
    a, b = TAPS_A, TAPS_B

    def fill(prev_ref, next_ref):
        below = a[0] * odd[:pairs] + b[0] * even[:pairs]
        for i in range(2):
            prev_ref[i] = below
            next_ref[i] = a[3 + i] * even[pairs:] + b[3 + i] * odd[pairs:]

    by_parity(lambda: fill(far_ref, near_ref), lambda: fill(near_ref, far_ref))


def disaggregate_kernel(
    parents_ref, octants_ref, flat_ref, phase_ref, gather_ref, out_ref, edge_ref, listed, incoming_ref, lhs, coarse_e, coarse_o, whole_out, sems
):
    periods = incoming_ref.shape[2]
    packed = parents_ref[...] * 8 + octants_ref[...]
    for k in range(listed.shape[0]):
        listed[k] = packed[0, k]
    for gp in range(incoming_ref.shape[0]):
        for w in range(ROWS_PER_PERIOD):
            first = gp * ROWS_PER_PERIOD * periods + w
            incoming_ref[gp, w] = flat_ref[pl.ds(first, periods, stride=ROWS_PER_PERIOD), :]
    azimuth_in = periods * PERIOD_C
    sublane = lax.broadcasted_iota(jnp.int32, (periods, LANES), 0)
    inner = pl.ds(TILE, azimuth_in - 2 * TILE)

    def shift(block):
        for k in range(BLOCK):
            code = listed[block * BLOCK + k]
            octant, parent = code & 7, code >> 3
            for r in range(3):
                for i in range(3):
                    w = 3 * r + i
                    real, imaginary = incoming_ref[2 * parent, w], incoming_ref[2 * parent + 1, w]
                    cosine, sine = phase_ref[octant, 0, w], phase_ref[octant, 1, w]
                    returned = (real * cosine + imaginary * sine, imaginary * cosine - real * sine)
                    for part in range(2):
                        base = ((2 * k + part) * 3 + r) * periods
                        lhs[base : base + periods, i * LANES : (i + 1) * LANES] = returned[part]

    def polar():
        high, low = split(lhs[...])
        coarse_e[...] = gather_dot(high[:, : 2 * LANES], low[:, : 2 * LANES], gather_ref, 0)
        coarse_o[...] = gather_dot(high[:, LANES:], low[:, LANES:], gather_ref, 1)

    def azimuth(block):
        for j in range(2 * BLOCK):
            c = []
            for r in range(3):
                base = (j * 3 + r) * periods
                c.append(coarse_e[base : base + periods, :])
                c.append(coarse_o[base : base + periods, :])
            lower = both_taps_transposed(c[1], c[2])
            upper = both_taps_transposed(c[4], c[5])
            down = [jnp.where(sublane == 0, 0.0, pltpu.roll(upper[i], 1, 0)) for i in (3, 4)]
            up = jnp.where(sublane == periods - 1, 0.0, pltpu.roll(lower[0], periods - 1, 0))
            rows = [c[0] + lower[1] + down[0], lower[2] + upper[0] + down[1], c[3] + lower[3] + upper[1], lower[4] + upper[2] + up]
            kp = block * (2 * BLOCK) + j
            for u in range(PERIOD_C):
                whole_out[kp, pl.ds(u, periods, stride=PERIOD_C), :] = rows[u]
            edge_ref[0, kp] = whole_out[kp, :TILE, :]
            edge_ref[1, kp] = whole_out[kp, azimuth_in - TILE :, :]

    def written(block):
        some = pl.ds(block * (2 * BLOCK), 2 * BLOCK)
        return pltpu.make_async_copy(whole_out.at[some, inner, :], out_ref.at[some, inner, :], sems.at[block])

    def one_block(block, carry):
        shift(block)
        polar()
        azimuth(block)
        written(block).start()
        return carry

    blocks = listed.shape[0] // BLOCK
    lax.fori_loop(0, blocks, one_block, 0)
    for block in range(blocks):
        written(block).wait()


def finish_kernel(edge_ref, far_ref, near_ref, part_ref, out_ref, tiles, sems):
    pairs, azimuth_in, _ = out_ref.shape
    tiles[...] = edge_ref[...]
    flat = tiles.reshape(2 * pairs * TILE, LANES)
    before, after = from_sides(far_ref, near_ref)
    ends = ((0, 0, before[0]), (0, 1, before[1]), (1, TILE - 1, after[0]))
    copies = []
    for i, start in enumerate((0, azimuth_in - TILE)):
        for end, row, values in ends:
            if end == i:
                for part in range(2):
                    for k in range(0, pairs // 2, 8):
                        source = slice(part * (pairs // 2) + k, part * (pairs // 2) + k + 8)
                        rows = pl.ds((i * pairs + 2 * k + part) * TILE + row, 8, stride=2 * TILE)
                        flat[rows, :] = flat[rows, :] + values[source]
        copy = pltpu.make_async_copy(tiles.at[i], out_ref.at[:, pl.ds(start, TILE), :], sems.at[i])
        copy.start()
        copies.append(copy)
    for copy in copies:
        copy.wait()


def swapped(values, axis, first):
    size = lax.axis_size(axis)
    return lax.ppermute(values, axis, [(i, (((i - first) ^ 1) + first) % size) for i in range(size)])


def exchanged(values, axis, mask):
    size = lax.axis_size(axis)
    return lax.ppermute(values, axis, [(i, i ^ mask) for i in range(size)])


SMEM = pl.BlockSpec(memory_space=pltpu.SMEM)
VMEM = pl.BlockSpec(memory_space=pltpu.VMEM)
HBM = pl.BlockSpec(memory_space=pltpu.HBM)


def in_hbm(values):
    return pltpu.with_memory_space_constraint(values, pltpu.HBM)


def local_call(kernel, out_shape, in_specs, scratch, grant, flops=1_000_000, bytes_accessed=1_000_000, out_specs=None, aliases={}):
    return pl.pallas_call(
        kernel,
        out_shape=out_shape,
        in_specs=in_specs,
        out_specs=jax.tree.map(lambda _: VMEM, out_shape) if out_specs is None else out_specs,
        scratch_shapes=scratch,
        input_output_aliases=aliases,
        compiler_params=pltpu.CompilerParams(vmem_limit_bytes=grant << 20),
        cost_estimate=pl.CostEstimate(flops=flops, bytes_accessed=bytes_accessed, transcendentals=0),
    )


def on_device_exchange(
    child_patterns, trans_table, child_parent, child_octant, partner_src, partner_off, partner_count
):
    children, _, azimuth_in, polar_in = child_patterns.shape
    pairs = 2 * children
    peers = lax.axis_size("clus")
    parent_total, _ = partner_src.shape
    own = parent_total // peers
    periods = azimuth_in // PERIOD_C
    flat_rows = ROWS_PER_PERIOD * periods
    share = flat_rows // peers
    offsets = trans_table.shape[0]
    array = lambda *shape: jax.ShapeDtypeStruct(shape, f32)
    buffer = lambda *shape: pltpu.VMEM(shape, f32)
    edges = len(edge_rows(periods))
    even, odd = polar_blocks()
    spread = jnp.asarray(np.stack([np.concatenate([h, h, l]) for h, l in (split_np(even), split_np(odd))]))
    edge = array(2, pairs, polar_in)
    to_far, to_near = local_call(
        rows_kernel, [edge, edge], [HBM], [buffer(pairs, TILE, polar_in)] * 2 + [pltpu.SemaphoreType.DMA((2,))], 8
    )(in_hbm(child_patterns.reshape(pairs, azimuth_in, polar_in)))
    from_far = swapped(to_far, "dir", 1)
    from_near = swapped(to_near, "dir", 0)
    odd_gather = np.concatenate([odd.T[LANES:], odd.T[:LANES]])
    gather = np.stack([np.concatenate(split_np(m), axis=1) for m in (even.T, odd_gather)])

    frame = max(-(-((q * 2 * share) % 8 + 2 * share) // 8) * 8 for q in range(peers))
    view = trans_table.reshape(offsets, 2, flat_rows, LANES).transpose(0, 2, 1, 3).reshape(offsets, 2 * flat_rows, LANES)
    blocks = children // BLOCK
    rows = 2 * BLOCK * 3 * periods
    phases, edge_phases, flat, table = local_call(
        functools.partial(main_kernel, peers),
        [
            array(8, 2, ROWS_PER_PERIOD, periods, LANES),
            array(edges, 2, children, LANES),
            array(2 * own * flat_rows, LANES),
            jax.ShapeDtypeStruct((offsets, frame, LANES), bf16),
        ],
        [HBM] * 5,
        [
            pltpu.SMEM((children,), jnp.int32),
            pltpu.SMEM((children,), jnp.int32),
            buffer(pairs * azimuth_in, polar_in),
            pltpu.VMEM(spread.shape, bf16),
            buffer(rows, LANES),
            buffer(rows, LANES),
            buffer(rows, 2 * LANES),
            buffer(rows, 2 * LANES),
            buffer(own, 2, ROWS_PER_PERIOD, periods, LANES),
            buffer(2 * own * flat_rows, LANES),
            pltpu.SemaphoreType.DMA((5,)),
        ],
        24,
        flops=4_000_000_000,
        bytes_accessed=12_000_000,
    )(
        in_hbm(child_parent[0]),
        in_hbm(child_octant),
        in_hbm(child_patterns.reshape(pairs * azimuth_in, polar_in)),
        in_hbm(view),
        in_hbm(spread),
    )

    chunk = array(2 * own * share, LANES)
    sent = local_call(
        functools.partial(fix_kernel, peers, own), [chunk] * peers, [VMEM] * 6, [buffer(2 * own * flat_rows, LANES)], 8
    )(child_parent, from_far, from_near, flat, edge_phases, spread)

    masks = sorted(range(1, peers), key=lambda d: bin(d).count("1"))
    early, late = masks[:1], masks[1:]
    received = {0: sent[0]}
    for d in early:
        received[d] = exchanged(sent[d], "clus", d)
    for d in late:
        received[d] = exchanged(sent[d], "clus", d)

    sum_pair = [array(parent_total * frame, LANES)] * 2
    others = tuple(early + late)
    operators, *sums = local_call(
        functools.partial(widen_kernel, peers, others),
        [array(parent_total * len(others) * own * frame, LANES)] + sum_pair,
        [VMEM] * 5,
        [
            buffer((offsets + 1) * frame, LANES),
            pltpu.VMEM((parent_total, parent_total), jnp.int32),
            pltpu.SMEM((parent_total, parent_total), jnp.int32),
            buffer(own * frame, LANES),
            buffer(own * frame, LANES),
            pltpu.SemaphoreType.DMA,
        ],
        20,
        flops=90_000_000,
        bytes_accessed=12_000_000,
    )(partner_src, partner_off, partner_count.reshape(1, parent_total), table, received[0])

    sums = local_call(
        functools.partial(gather_kernel, peers, frame, others, tuple(early)),
        sum_pair,
        [VMEM] * (3 + len(early)),
        [buffer(len(early) * own * frame, LANES)] * 2,
        12,
        flops=60_000_000,
        bytes_accessed=12_000_000,
    )(operators, *[received[d] for d in early], *sums)

    back = {}
    last_sources = [received[d] for d in late]
    for number, targets in enumerate((masks[:-1], masks[-1:], [0])):
        prepare = number == 0
        results = local_call(
            functools.partial(translate_kernel, frame, others, tuple(late), tuple(targets)),
            ([array(len(late) * own * frame, LANES)] * 2 if prepare else []) + [chunk] * len(targets),
            [VMEM] * (3 + len(last_sources)),
            [buffer(TOGETHER, frame, LANES)] * 2,
            20,
            flops=10_000_000 * len(targets),
            bytes_accessed=2_000_000 * len(targets),
        )(operators, *sums, *last_sources)
        if prepare:
            last_sources, results = results[:2], results[2:]
        for d, result in zip(targets, results):
            back[d] = exchanged(result, "clus", d) if d else result

    incoming, to_far, to_near = local_call(
        functools.partial(edge_kernel, peers, 2 * own),
        [array(2 * own * flat_rows, LANES), edge, edge],
        [VMEM] * (3 + peers),
        [],
        8,
    )(child_parent, edge_phases, gather, *[back[d] for d in range(peers)])

    from_far = swapped(to_far, "dir", 1)
    from_near = swapped(to_near, "dir", 0)

    inner, edge_tiles = local_call(
        disaggregate_kernel,
        [array(pairs, azimuth_in, polar_in), array(2, pairs, TILE, polar_in)],
        [VMEM] * 5,
        [
            pltpu.SMEM((children,), jnp.int32),
            buffer(2 * own, ROWS_PER_PERIOD, periods, LANES),
            buffer(rows, 3 * LANES),
            buffer(rows, LANES),
            buffer(rows, LANES),
            buffer(pairs, azimuth_in, polar_in),
            pltpu.SemaphoreType.DMA((blocks,)),
        ],
        24,
        flops=4_000_000_000,
        bytes_accessed=12_000_000,
        out_specs=[HBM, VMEM],
    )(child_parent, child_octant.reshape(1, children), incoming, phases, gather)

    out = local_call(
        finish_kernel,
        array(pairs, azimuth_in, polar_in),
        [VMEM] * 3 + [HBM],
        [buffer(2, pairs, TILE, polar_in), pltpu.SemaphoreType.DMA((2,))],
        8,
        out_specs=HBM,
        aliases={3: 0},
    )(edge_tiles, from_far, from_near, in_hbm(inner))
    return out.reshape(child_patterns.shape)


def with_halo(shard, sides, width):
    for axis, dim in sides:
        size, length = (lax.axis_size(axis), shard.shape[dim])
        up = [(i, (i + 1) % size) for i in range(size)]
        down = [(j, i) for i, j in up]
        last = lax.slice_in_dim(shard, length - width, length, axis=dim)
        initial = lax.slice_in_dim(shard, 0, width, axis=dim)
        before = lax.ppermute(last, axis, up)
        after = lax.ppermute(initial, axis, down)
        shard = jnp.concatenate([before, shard, after], axis=dim)
    return shard


def lagrange_rows(offset):
    weights = []
    for anchor in range(5):
        factor = jnp.ones_like(offset)
        for neighbour in range(5):
            if neighbour != anchor:
                factor = factor * (offset - neighbour) / (anchor - neighbour)
        weights.append(factor)
    return weights


def polar_matrix_of(rows_out, rows_in):
    target = (jnp.arange(rows_out, dtype=jnp.float32) + 0.5) * rows_in / rows_out - 0.5
    start_row = jnp.clip(jnp.floor(target + 0.5).astype(jnp.int32) - 2, 0, rows_in - 5)
    weights = lagrange_rows(target - start_row.astype(jnp.float32))
    columns = jnp.arange(rows_in, dtype=jnp.int32)
    matrix = jnp.zeros((rows_out, rows_in), jnp.float32)
    for anchor in range(5):
        matrix = matrix + jnp.where(
            columns[None, :] == (start_row + anchor)[:, None], weights[anchor][:, None], 0.0
        )
    return matrix


def azimuth_matrix_of(out_index, in_index, total_out, total_in):
    target = (out_index * total_in).astype(jnp.float32) / total_out
    nearest = jnp.floor(target + 0.5).astype(jnp.int32)
    weights = lagrange_rows(target - nearest.astype(jnp.float32) + 2.0)
    matrix = jnp.zeros((out_index.shape[0], in_index.shape[0]), jnp.float32)
    for anchor in range(5):
        columns = nearest + anchor - 2
        matrix = matrix + jnp.where(
            in_index[None, :] == columns[:, None], weights[anchor][:, None], 0.0
        )
    return matrix


def shift_phases(octant, azimuth_index, azimuth_total, polar_total):
    azimuth = 2.0 * math.pi * azimuth_index.astype(jnp.float32) / azimuth_total
    polar = math.pi * (jnp.arange(polar_total, dtype=jnp.float32) + 0.5) / polar_total
    first_axis = jnp.sin(polar)[None, :] * jnp.cos(azimuth)[:, None]
    second_axis = jnp.sin(polar)[None, :] * jnp.sin(azimuth)[:, None]
    third_axis = jnp.cos(polar)[None, :] * jnp.ones_like(azimuth)[:, None]
    first_sign = (1 - 2 * (octant % 2)).astype(jnp.float32)
    second_sign = (1 - 2 * (octant // 2 % 2)).astype(jnp.float32)
    third_sign = (1 - 2 * (octant // 4)).astype(jnp.float32)
    phase_angle = phase_scale * (
        first_sign[:, None, None] * first_axis[None]
        + second_sign[:, None, None] * second_axis[None]
        + third_sign[:, None, None] * third_axis[None]
    )
    return (jnp.cos(phase_angle), jnp.sin(phase_angle))


def translate(sources, table, partner_src, partner_off, partner_count):
    live_mask = (
        jnp.arange(partner_src.shape[1], dtype=jnp.int32)[None, :] < partner_count[:, None]
    ).astype(jnp.float32)
    picked = sources[partner_src]
    operator = table[partner_off].astype(jnp.float32) * live_mask[:, :, None, None]
    real_part = jnp.sum(
        operator[:, :, 0] * picked[:, :, 0] - operator[:, :, 1] * picked[:, :, 1], axis=1
    )
    imaginary = jnp.sum(
        operator[:, :, 0] * picked[:, :, 1] + operator[:, :, 1] * picked[:, :, 0], axis=1
    )
    return jnp.stack([real_part, imaginary], axis=1)


def forward_shift(patterns, cosine, sine_part):
    real_part = patterns[:, 0] * cosine - patterns[:, 1] * sine_part
    imaginary = patterns[:, 0] * sine_part + patterns[:, 1] * cosine
    return jnp.stack([real_part, imaginary], axis=1)


def conjugate_shift(patterns, cosine, sine_part):
    real_part = patterns[:, 0] * cosine + patterns[:, 1] * sine_part
    imaginary = patterns[:, 1] * cosine - patterns[:, 0] * sine_part
    return jnp.stack([real_part, imaginary], axis=1)


def on_device_gather(
    child_patterns, trans_table, child_parent, child_octant, partner_src, partner_off, partner_count
):
    _, _, azimuth_in, _ = child_patterns.shape
    polar_out = NTHETA_P
    azimuth_out = trans_table.shape[2] // polar_out
    parent_slots = partner_src.shape[0] // lax.axis_size("clus")
    cluster_index = lax.axis_index("clus")
    direction_index = lax.axis_index("dir")
    parents = child_parent[0]
    polar_matrix = polar_matrix_of(NTHETA_P, NTHETA_C)
    onehot = (parents[None, :] == jnp.arange(parent_slots, dtype=jnp.int32)[:, None]).astype(
        jnp.float32
    )
    own_rows = jnp.mod(
        direction_index * azimuth_out + jnp.arange(azimuth_out, dtype=jnp.int32), NPHI_P
    )
    cosine, sine_part = shift_phases(child_octant, own_rows, NPHI_P, polar_out)
    extended = with_halo(child_patterns, (("dir", 2),), 2)
    gather_matrix = azimuth_matrix_of(
        jnp.arange(azimuth_out, dtype=jnp.int32),
        jnp.arange(azimuth_in + 4, dtype=jnp.int32) - 2,
        NPHI_P,
        NPHI_C,
    )
    along_azimuth = jnp.einsum("pc,kacz->kapz", gather_matrix, extended, precision=highest)
    refined = jnp.einsum("kapz,tz->kapt", along_azimuth, polar_matrix, precision=highest)
    shifted = forward_shift(refined, cosine, sine_part)
    radiation = jnp.einsum("gk,kapt->gapt", onehot, shifted, precision=highest)
    flattened = radiation.reshape(parent_slots, 2, azimuth_out * polar_out)
    sources = lax.all_gather(flattened, "clus", axis=0, tiled=True)
    first_row = cluster_index * parent_slots
    own_src = lax.dynamic_slice_in_dim(partner_src, first_row, parent_slots, 0)
    own_off = lax.dynamic_slice_in_dim(partner_off, first_row, parent_slots, 0)
    own_count = lax.dynamic_slice_in_dim(partner_count, first_row, parent_slots, 0)
    incoming = translate(sources, trans_table, own_src, own_off, own_count)
    incoming = incoming.reshape(parent_slots, 2, azimuth_out, polar_out)
    return_matrix = azimuth_matrix_of(
        jnp.arange(azimuth_out + 6, dtype=jnp.int32) - 3,
        jnp.arange(azimuth_in, dtype=jnp.int32),
        NPHI_P,
        NPHI_C,
    )
    per_child = jnp.einsum("gk,gapt->kapt", onehot, incoming, precision=highest)
    returned = conjugate_shift(per_child, cosine, sine_part)
    coarse_own = jnp.einsum("kapt,tz->kapz", returned, polar_matrix, precision=highest)
    coarse = with_halo(coarse_own, (("dir", 2),), 3)
    return jnp.einsum("pc,kapz->kacz", return_matrix, coarse, precision=highest)


def solution(mesh):
    def on_device(child_patterns, trans_table, *rest):
        peers = lax.axis_size("clus")
        children, _, azimuth_in, polar_in = child_patterns.shape
        flat_rows = trans_table.shape[2] // LANES
        fits = (
            azimuth_in % (8 * PERIOD_C) == 0
            and polar_in == LANES
            and flat_rows * PERIOD_C == ROWS_PER_PERIOD * azimuth_in
            and flat_rows % peers == 0
            and peers & (peers - 1) == 0
            and peers > 2
            and lax.axis_size("dir") % 2 == 0
            and children % BLOCK == 0
        )
        plan = on_device_exchange if fits else on_device_gather
        return plan(child_patterns, trans_table, *rest)

    return jax.shard_map(
        on_device,
        mesh=mesh,
        in_specs=(
            P("clus", None, "dir", None),
            P(None, None, "dir"),
            P("clus", None),
            P("clus"),
            P(),
            P(),
            P(),
        ),
        out_specs=P("clus", None, "dir", None),
        check_vma=False,
    )
```

```python
import functools
import math

import jax
import jax.numpy as jnp
import numpy as np
from jax import lax
from jax.experimental import pallas as pl
from jax.experimental.pallas import tpu as pltpu
from jax.sharding import PartitionSpec as P


NTHETA_C = 128
NPHI_C = 256
NTHETA_P = 192
NPHI_P = 384

LANES = 128
PERIOD_P = 6
PERIOD_C = 4
ROWS_PER_PERIOD = PERIOD_P * NTHETA_P // LANES
GROUP = 8
TILE = 8
TOGETHER = 2
BLOCK = 2 * GROUP

phase_scale = 8.0 * math.pi
highest = lax.Precision.HIGHEST
f32 = jnp.float32
bf16 = jnp.bfloat16


def lagrange(offset):
    weights = []
    for anchor in range(5):
        factor = 1.0
        for neighbour in range(5):
            if neighbour != anchor:
                factor = factor * (offset - neighbour) / (anchor - neighbour)
        weights.append(factor)
    return weights


TAPS_A = [float(w) for w in lagrange(5.0 / 3.0)]
TAPS_B = [float(w) for w in lagrange(7.0 / 3.0)]


SUMS = [(TAPS_A[i] + TAPS_A[4 - i]) / 2 for i in range(2)]
DIFFS = [(TAPS_A[i] - TAPS_A[4 - i]) / 2 for i in range(2)]
CENTRE = TAPS_A[2]


def polar_matrix_np():
    target = (np.arange(NTHETA_P, dtype=np.float32) + np.float32(0.5)) * NTHETA_C / NTHETA_P - np.float32(0.5)
    start = np.clip(np.floor(target + 0.5).astype(np.int32) - 2, 0, NTHETA_C - 5)
    weights = lagrange((target - start).astype(np.float64))
    matrix = np.zeros((NTHETA_P, NTHETA_C), np.float64)
    for anchor in range(5):
        matrix[np.arange(NTHETA_P), start + anchor] += weights[anchor]
    return matrix.astype(np.float32)


def polar_blocks():
    matrix = polar_matrix_np().T
    even = np.zeros((NTHETA_C, 2 * LANES), np.float32)
    odd = np.zeros((NTHETA_C, 2 * LANES), np.float32)
    half = NTHETA_P - LANES
    even[:, :NTHETA_P] = matrix
    odd[:, :LANES] = matrix[:, half:]
    odd[:, 2 * LANES - half :] = matrix[:, :half]
    return even, odd


def split_np(matrix):
    high = matrix.astype(bf16)
    low = (matrix - high.astype(np.float32)).astype(bf16)
    return high, low


def split(values):
    high = values.astype(bf16)
    low = (values - high.astype(f32)).astype(bf16)
    return high, low


def dot(left, right):
    return jnp.dot(left, right, preferred_element_type=f32)


def spread_dot(values, matrix_ref, i):
    high, low = split(values)
    depth = values.shape[1]
    return dot(jnp.concatenate([high, low], axis=1), matrix_ref[i, : 2 * depth]) + dot(high, matrix_ref[i, 2 * depth :])


def gather_dot(high, low, matrix_ref, i):
    width = matrix_ref.shape[2] // 2
    both = dot(high, matrix_ref[i])
    return both[:, :width] + (both[:, width:] + dot(low, matrix_ref[i, :, :width]))


SIN_COEFFS = [(-1) ** k * math.pi ** (2 * k + 1) / math.factorial(2 * k + 1) for k in range(7)]
COS_COEFFS = [(-1) ** k * math.pi ** (2 * k) / math.factorial(2 * k) for k in range(7)]


def sincos_turns(turns):
    rest = turns - jnp.round(turns)
    square = rest * rest
    sine = jnp.full_like(square, SIN_COEFFS[-1])
    for coeff in SIN_COEFFS[-2::-1]:
        sine = sine * square + coeff
    sine = sine * rest
    cosine = jnp.full_like(square, COS_COEFFS[-1])
    for coeff in COS_COEFFS[-2::-1]:
        cosine = cosine * square + coeff
    return 2.0 * sine * cosine, 1.0 - 2.0 * sine * sine


def fill_phases(direction, out_ref):
    periods = out_ref.shape[3]
    lane = lax.broadcasted_iota(jnp.int32, (periods, LANES), 1)
    period = lax.broadcasted_iota(jnp.int32, (periods, LANES), 0)
    first = direction * (PERIOD_P * periods)

    def two_rows(r, carry):
        for i in range(3):
            position = lane + i * LANES
            second = (position >= NTHETA_P).astype(jnp.int32)
            polar_index = position - second * NTHETA_P
            azimuth_index = first + period * PERIOD_P + 2 * r + second
            sin_polar, cos_polar = sincos_turns((polar_index.astype(f32) + 0.5) / (2 * NTHETA_P))
            sin_azimuth, cos_azimuth = sincos_turns(azimuth_index.astype(f32) / NPHI_P)
            along_x = 4.0 * sin_polar * cos_azimuth
            along_y = 4.0 * sin_polar * sin_azimuth
            along_z = 4.0 * cos_polar
            w = 3 * r + i
            for octant in (0, 2, 4, 6):
                turns = along_x + along_y if octant % 4 == 0 else along_x - along_y
                turns = turns + along_z if octant < 4 else turns - along_z
                sine, cosine = sincos_turns(turns)
                out_ref[octant, 0, w] = cosine
                out_ref[octant, 1, w] = sine
                out_ref[7 - octant, 0, w] = cosine
                out_ref[7 - octant, 1, w] = -sine
        return carry

    lax.fori_loop(0, PERIOD_P // 2, two_rows, 0)


def edge_rows(periods):
    return [(w, 0) for w in (1, 2, 3, 4)] + [(w, periods - 1) for w in (6, 7, 8)]


def by_parity(even, odd):
    parity = lax.rem(lax.axis_index("dir"), 2)
    pl.when(parity == 0)(even)
    pl.when(parity == 1)(odd)


def from_sides(far_ref, near_ref):
    is_even = lax.rem(lax.axis_index("dir"), 2) == 0
    far, near = far_ref[...], near_ref[...]
    return jnp.where(is_even, far, near), jnp.where(is_even, near, far)


def rows_kernel(x_ref, far_ref, near_ref, low, high, sems):
    pairs, azimuth_in, _ = x_ref.shape
    low_copy = pltpu.make_async_copy(x_ref.at[:, pl.ds(0, TILE), :], low, sems.at[0])
    high_copy = pltpu.make_async_copy(x_ref.at[:, pl.ds(azimuth_in - TILE, TILE), :], high, sems.at[1])
    low_copy.start()
    high_copy.start()
    low_copy.wait()
    high_copy.wait()
    low_rows, high_rows = (ref.reshape(pairs * TILE, LANES) for ref in (low, high))

    def fill(first_ref, last_ref):
        for part in range(2):
            for k in range(0, pairs // 2, 8):
                target = slice(part * (pairs // 2) + k, part * (pairs // 2) + k + 8)
                base = (2 * k + part) * TILE
                for i in range(2):
                    first_ref[i, target] = low_rows[pl.ds(base + i, 8, stride=2 * TILE), :]
                last = high_rows[pl.ds(base + TILE - 1, 8, stride=2 * TILE), :]
                for i in range(2):
                    last_ref[i, target] = last

    by_parity(lambda: fill(far_ref, near_ref), lambda: fill(near_ref, far_ref))


def both_taps(rows):
    even = SUMS[0] * (rows[0] + rows[4]) + SUMS[1] * (rows[1] + rows[3]) + CENTRE * rows[2]
    odd = DIFFS[0] * (rows[0] - rows[4]) + DIFFS[1] * (rows[1] - rows[3])
    return even + odd, even - odd


def both_taps_transposed(first, second):
    total, difference = first + second, first - second
    outer = [SUMS[i] * total for i in range(2)]
    inner = [DIFFS[i] * difference for i in range(2)]
    return [outer[0] + inner[0], outer[1] + inner[1], CENTRE * total, outer[1] - inner[1], outer[0] - inner[0]]


def main_kernel(peers, parents_hbm, octants_hbm, x_hbm, table_ref, spread_hbm, *rest):
    phase_ref, edge_phase_ref, flat_ref, slice_ref = rest[:4]
    parents_ref, octants_ref, x_ref, spread_ref, az_e, az_o, res_e, res_o, acc, flat, sems = rest[4:]
    children = octants_ref.shape[0]
    periods = phase_ref.shape[3]
    azimuth_in = periods * PERIOD_C
    own = acc.shape[0]
    me = lax.axis_index("clus")
    share = ROWS_PER_PERIOD * periods // peers
    first_tile = me * (2 * share) // 8
    table_rows = pl.ds(pl.multiple_of(first_tile * 8, 8), slice_ref.shape[1])
    ends = (
        (octants_hbm, octants_ref),
        (parents_hbm, parents_ref),
        (x_hbm, x_ref),
        (spread_hbm, spread_ref),
        (table_ref.at[:, table_rows, :], slice_ref),
    )
    copies = [pltpu.make_async_copy(source, target, sems.at[i]) for i, (source, target) in enumerate(ends)]
    for copy in copies[:-1]:
        copy.start()
    fill_phases(lax.axis_index("dir"), phase_ref)
    acc[...] = jnp.zeros_like(acc)
    sublane = lax.broadcasted_iota(jnp.int32, (periods, LANES), 0)
    copies[0].wait()

    def edges_of(step, carry):
        for j in range(GROUP):
            k = step * GROUP + j
            octant = octants_ref[k]
            for e, (w, m) in enumerate(edge_rows(periods)):
                for i in range(2):
                    edge_phase_ref[e, i, pl.ds(k, 1), :] = phase_ref[octant, i, w, m : m + 1, :]
        return carry

    lax.fori_loop(0, children // GROUP, edges_of, 0)
    for copy in copies[1:-1]:
        copy.wait()
    copies[-1].start()

    def azimuth(block):
        for kp in range(2 * BLOCK):
            start = pl.multiple_of((block * (2 * BLOCK) + kp) * azimuth_in, 8)
            x = [x_ref[pl.ds(start + u, periods, stride=PERIOD_C), :] for u in range(PERIOD_C)]
            left = jnp.where(sublane == 0, 0.0, pltpu.roll(x[3], 1, 0))
            right = [jnp.where(sublane == periods - 1, 0.0, pltpu.roll(x[i], periods - 1, 0)) for i in range(2)]
            lower = [left, x[0], x[1], x[2], x[3]]
            upper = [x[1], x[2], x[3], right[0], right[1]]
            rows = [x[0], *both_taps(lower), x[2], *both_taps(upper)]
            for r in range(3):
                base = (kp * 3 + r) * periods
                az_e[base : base + periods, :] = rows[2 * r]
                az_o[base : base + periods, :] = rows[2 * r + 1]

    def polar():
        res_e[...] = spread_dot(az_e[...], spread_ref, 0)
        res_o[...] = spread_dot(az_o[...], spread_ref, 1)

    def shift(block):
        for k in range(BLOCK):
            octant = octants_ref[block * BLOCK + k]
            parent = parents_ref[block * BLOCK + k]
            for r in range(3):
                parts = []
                for part in range(2):
                    rows = pl.ds(((2 * k + part) * 3 + r) * periods, periods)
                    middle = res_e[rows, LANES:] + res_o[rows, LANES:]
                    parts.append((res_e[rows, :LANES], middle, res_o[rows, :LANES]))
                for i in range(3):
                    w = 3 * r + i
                    real, imaginary = parts[0][i], parts[1][i]
                    cosine, sine = phase_ref[octant, 0, w], phase_ref[octant, 1, w]
                    acc[parent, 0, w] += real * cosine - imaginary * sine
                    acc[parent, 1, w] += real * sine + imaginary * cosine

    def one_block(block, carry):
        azimuth(block)
        polar()
        shift(block)
        return carry

    lax.fori_loop(0, children // BLOCK, one_block, 0)
    for gp in range(2 * own):
        for w in range(ROWS_PER_PERIOD):
            flat[pl.ds(gp * ROWS_PER_PERIOD * periods + w, periods, stride=ROWS_PER_PERIOD), :] = acc[gp // 2, gp % 2, w]
        for q in range(peers):
            source = gp * ROWS_PER_PERIOD * periods + q * share
            target = (q * 2 * own + gp) * share
            flat_ref[target : target + share, :] = flat[source : source + share, :]
    copies[-1].wait()


def one_hot(parents, own):
    index = lax.broadcasted_iota(jnp.int32, (own, parents.shape[1]), 0)
    return (index == parents).astype(f32)


def dot2(exact, values):
    exact = exact.astype(bf16)
    high, low = split(values)
    return dot(exact, high) + dot(exact, low)


def fix_kernel(
    peers, own, parents_ref, far_ref, near_ref, flat_ref, edge_phase_ref, spread_ref, *rest
):
    outs, (fixed,) = rest[:peers], rest[peers:]
    pairs = far_ref.shape[1]
    children = pairs // 2
    chunk_rows = outs[0].shape[0]
    share = chunk_rows // (2 * own)
    periods = share * peers // ROWS_PER_PERIOD
    fixed[...] = flat_ref[...]
    before, right = from_sides(far_ref, near_ref)
    left = before[0]
    a, b = TAPS_A, TAPS_B
    even = jnp.concatenate([b[0] * left, a[3] * right[0] + a[4] * right[1]], axis=0)
    odd = jnp.concatenate([a[0] * left, b[3] * right[0] + b[4] * right[1]], axis=0)
    even = spread_dot(even, spread_ref, 0)
    odd = spread_dot(odd, spread_ref, 1)
    first, last = slice(0, pairs), slice(pairs, 2 * pairs)
    low, high = slice(0, LANES), slice(LANES, 2 * LANES)
    refined = [
        odd[first, high],
        odd[first, low],
        even[first, low],
        even[first, high],
        even[last, low],
        even[last, high] + odd[last, high],
        odd[last, low],
    ]
    shifted_rows = []
    for e, rows in enumerate(refined):
        real, imaginary = rows[:children], rows[children:]
        cosine, sine = edge_phase_ref[e, 0], edge_phase_ref[e, 1]
        shifted_rows.append(real * cosine - imaginary * sine)
        shifted_rows.append(real * sine + imaginary * cosine)
    summed = dot2(one_hot(parents_ref[...], own), jnp.concatenate(shifted_rows, axis=1))
    for e, (w, m) in enumerate(edge_rows(periods)):
        q, row = divmod(ROWS_PER_PERIOD * m + w, share)
        for part in range(2):
            rows = pl.ds(q * chunk_rows + part * share + row, own, stride=2 * share)
            column = (2 * e + part) * LANES
            fixed[rows, :] = fixed[rows, :] + summed[:, column : column + LANES]
    me = lax.axis_index("clus")
    for d in range(peers):
        start = pl.multiple_of((me ^ d) * chunk_rows, 8)
        outs[d][...] = fixed[pl.ds(start, chunk_rows), :]


def widen_kernel(peers, others, source_ref, offset_ref, count_ref, table_ref, chunk, placed_ref, real_sum, imag_sum, *rest):
    wide_ref, numbers_ref, listed, real_twice, imag_twice, sem = rest
    targets, partners = source_ref.shape
    offsets, frame, _ = table_ref.shape
    own = targets // peers
    share = chunk.shape[0] // (2 * own)
    me = lax.axis_index("clus")
    shape = (targets, targets)
    row, lane = (lax.broadcasted_iota(jnp.int32, shape, d) for d in range(2))
    count = jnp.sum(jnp.where(row == lane, count_ref[...], 0), axis=1, keepdims=True)
    number = jnp.full(shape, offsets, jnp.int32)
    for p in range(partners):
        here = (lane == source_ref[:, p : p + 1]) & (p < count)
        number = jnp.where(here, offset_ref[:, p : p + 1], number)
    numbers_ref[...] = number * frame
    copy = pltpu.make_async_copy(numbers_ref, listed, sem)
    copy.start()

    def some_offsets(i, carry):
        for j in range(4):
            wide_ref[pl.ds(pl.multiple_of((i * 4 + j) * frame, 8), frame), :] = table_ref[i * 4 + j].astype(f32)
        return carry

    whole_steps = offsets // 4
    lax.fori_loop(0, whole_steps, some_offsets, 0)
    for offset in range(whole_steps * 4, offsets):
        wide_ref[offset * frame : (offset + 1) * frame, :] = table_ref[offset].astype(f32)
    wide_ref[offsets * frame :, :] = jnp.zeros((frame, LANES), f32)
    doubled(chunk, real_twice, imag_twice, 0, own, share, frame, lax.rem(me * (2 * share), 8))
    copy.wait()

    def operator_of(target, device, g):
        first = listed[target, device * own + g]
        return wide_ref[pl.ds(pl.multiple_of(first, 8), frame), :]

    def own_sources(some, sums):
        return add_sources(sums, own, frame, lambda j, source: operator_of(some[j], me, source), real_twice, imag_twice)

    for_some_targets(targets, frame, own_sources, None, (real_sum, imag_sum))

    def other_sources(target, carry):
        for i, d in enumerate(others):
            for g in range(own):
                place = pl.multiple_of(((target * len(others) + i) * own + g) * frame, 8)
                placed_ref[pl.ds(place, frame), :] = operator_of(target, me ^ d, g)
        return carry

    lax.fori_loop(0, targets, other_sources, 0)


def doubled(chunk, real_twice, imag_twice, first, own, share, frame, skip):
    for g in range(own):
        for part, twice in enumerate((real_twice, imag_twice)):
            rows = chunk[(2 * g + part) * share : (2 * g + part + 1) * share, :]
            base = (first + g) * frame + skip
            twice[pl.ds(base, share, stride=2), :] = rows
            twice[pl.ds(base + 1, share, stride=2), :] = rows


def add_sources(sums, sources, frame, operators, real_twice, imag_twice):
    for source in range(sources):
        place = slice(source * frame, (source + 1) * frame)
        real, imaginary = real_twice[place, :], imag_twice[place, :]
        for i in range(len(sums)):
            operator = operators(i, source)
            sums[i] = (sums[i][0] + operator * real, sums[i][1] + operator * imaginary)
    return sums


def for_some_targets(targets, frame, add, before, after):
    def some_targets(i, carry):
        some = [i * TOGETHER + j for j in range(TOGETHER)]
        places = [pl.ds(pl.multiple_of(target * frame, 8), frame) for target in some]
        if before is None:
            sums = [(jnp.zeros((frame, LANES), f32),) * 2 for _ in some]
        else:
            sums = [tuple(ref[place, :] for ref in before) for place in places]
        for place, values in zip(places, add(some, sums)):
            for ref, value in zip(after, values):
                ref[place, :] = value
        return carry

    lax.fori_loop(0, targets // TOGETHER, some_targets, 0)


def placed(placed_ref, frame, others, own, masks):
    firsts = [others.index(d) * own for d in masks]

    def operator_of(target, source):
        place = target * (len(others) * own) + firsts[source // own] + source % own
        return placed_ref[pl.ds(pl.multiple_of(place * frame, 8), frame), :]

    return operator_of


def gather_kernel(peers, frame, others, masks, placed_ref, *rest):
    chunks, (real_before, imag_before, real_sum, imag_sum, real_twice, imag_twice) = rest[:-6], rest[-6:]
    me = lax.axis_index("clus")
    targets = real_sum.shape[0] // frame
    own = targets // peers
    share = chunks[0].shape[0] // (2 * own)
    skip = lax.rem(me * (2 * share), 8)
    for number, chunk in enumerate(chunks):
        doubled(chunk, real_twice, imag_twice, number * own, own, share, frame, skip)
    operator_of = placed(placed_ref, frame, others, own, masks)

    def add(some, sums):
        operators = lambda j, source: operator_of(some[j], source)
        return add_sources(sums, len(masks) * own, frame, operators, real_twice, imag_twice)

    for_some_targets(targets, frame, add, (real_before, imag_before), (real_sum, imag_sum))


def translate_kernel(frame, others, masks, targets, placed_ref, real_sum, imag_sum, *rest):
    prepare = len(rest) == len(masks) + len(targets) + 4
    chunks, rest = (rest[: len(masks)], rest[len(masks) :]) if prepare else ((), rest)
    real_twice, imag_twice = rest[:2]
    outs, (total_real, total_imag) = rest[-2 - len(targets) : -2], rest[-2:]
    me = lax.axis_index("clus")
    sources = real_twice.shape[0] // frame
    own = sources // len(masks)
    share = outs[0].shape[0] // (2 * own)
    skip = lax.rem(me * (2 * share), 8)
    for number, chunk in enumerate(chunks):
        doubled(chunk, real_twice, imag_twice, number * own, own, share, frame, skip)
    operator_of = placed(placed_ref, frame, others, own, masks)
    even, odd = pl.ds(skip, share, stride=2), pl.ds(skip + 1, share, stride=2)
    for out, d in zip(outs, targets):
        first = (me ^ d) * own

        def some_targets(i, carry):
            places = [i * TOGETHER + j for j in range(TOGETHER)]
            some = [first + g for g in places]
            rows = [pl.ds(pl.multiple_of(target * frame, 8), frame) for target in some]
            sums = [(real_sum[r, :], imag_sum[r, :]) for r in rows]
            operators = lambda j, source: operator_of(some[j], source)
            sums = add_sources(sums, sources, frame, operators, real_twice, imag_twice)
            for j, (g, (by_real, by_imag)) in enumerate(zip(places, sums)):
                total_real[j] = by_real
                total_imag[j] = by_imag
                row = g * (2 * share)
                out[pl.ds(row, share), :] = total_real[j, even, :] - total_imag[j, odd, :]
                out[pl.ds(row + share, share), :] = total_real[j, odd, :] + total_imag[j, even, :]
            return carry

        lax.fori_loop(0, own // TOGETHER, some_targets, 0)


def extract_kernel(peers, own2, *rest):
    chunks = rest[:peers]
    flat, far_ref, near_ref = rest[peers:]
    share = chunks[0].shape[0] // own2
    periods = share * peers // ROWS_PER_PERIOD
    own = own2 // 2
    flat_rows = ROWS_PER_PERIOD * periods
    me = lax.axis_index("clus")
    for gp in range(own2):
        for d in range(peers):
            flat[pl.ds(gp * flat_rows + (me ^ d) * share, share), :] = chunks[d][gp * share : (gp + 1) * share, :]

    def fill(prev_ref, next_ref):
        for ref in (prev_ref, next_ref):
            ref[...] = jnp.zeros_like(ref)
        places = [(prev_ref, e) for e in range(4)] + [(next_ref, e) for e in range(3)]
        for (ref, e), (w, m) in zip(places, edge_rows(periods)):
            for part in range(2):
                first = part * flat_rows + ROWS_PER_PERIOD * m + w
                row = (2 * e + part) * own
                ref[row : row + own, :] = flat[pl.ds(first, own, stride=2 * flat_rows), :]

    by_parity(lambda: fill(far_ref, near_ref), lambda: fill(near_ref, far_ref))


def neighbour_kernel(periods, octants_hbm, out_ref, by_octant, octants_ref, sem):
    copy = pltpu.make_async_copy(octants_hbm, octants_ref, sem)
    copy.start()
    here = lax.axis_index("dir")
    octant = lax.broadcasted_iota(jnp.int32, (8, LANES), 0)
    lane = lax.broadcasted_iota(jnp.int32, (8, LANES), 1)
    signs = [(1 - 2 * ((octant >> bit) & 1)).astype(f32) for bit in range(3)]
    for e, (w, m) in enumerate(edge_rows(periods)):
        place = here + 1 if m == 0 else here - 1
        position = lane + w * LANES
        row = w * LANES // NTHETA_P
        row = jnp.where(position >= (row + 1) * NTHETA_P, row + 1, row)
        polar_index = position - row * NTHETA_P
        azimuth_index = (place * periods + m) * PERIOD_P + row
        sin_polar, cos_polar = sincos_turns((polar_index.astype(f32) + 0.5) / (2 * NTHETA_P))
        sin_azimuth, cos_azimuth = sincos_turns(azimuth_index.astype(f32) / NPHI_P)
        along = (sin_polar * cos_azimuth, sin_polar * sin_azimuth, cos_polar)
        sine, cosine = sincos_turns(4.0 * (signs[0] * along[0] + signs[1] * along[1] + signs[2] * along[2]))
        by_octant[e, 0] = cosine
        by_octant[e, 1] = sine
    copy.wait()

    def some_children(step, carry):
        for j in range(GROUP):
            k = step * GROUP + j
            for e in range(by_octant.shape[0]):
                for i in range(2):
                    out_ref[e, i, pl.ds(k, 1), :] = by_octant[e, i, pl.ds(octants_ref[k], 1), :]
        return carry

    lax.fori_loop(0, octants_ref.shape[0] // GROUP, some_children, 0)


def edge_contributions(parents, phase_ref, gather_ref, above, below):
    children = parents.shape[1]
    own = below.shape[0] // 8
    rows = [above[2 * e * own : 2 * (e + 1) * own] for e in range(4)] + [below[2 * e * own : 2 * (e + 1) * own] for e in range(3)]
    edges = jnp.concatenate([r[part * own : (part + 1) * own] for r in rows for part in range(2)], axis=1)
    per_child = dot2(one_hot(parents, own).T, edges)
    returned = []
    for e in range(len(rows)):
        real = per_child[:, 2 * e * LANES : (2 * e + 1) * LANES]
        imaginary = per_child[:, (2 * e + 1) * LANES : (2 * e + 2) * LANES]
        cosine, sine = phase_ref[e, 0], phase_ref[e, 1]
        returned.append(
            jnp.concatenate([real * cosine + imaginary * sine, imaginary * cosine - real * sine], axis=0)
        )
    join = functools.partial(jnp.concatenate, axis=1)
    even = jnp.concatenate([join([returned[2], returned[3]]), join([returned[4], returned[5]])], axis=0)
    odd = jnp.concatenate([join([returned[0], returned[1]]), join([returned[5], returned[6]])], axis=0)
    even = gather_dot(*split(even), gather_ref, 0)
    odd = gather_dot(*split(odd), gather_ref, 1)
    a, b = TAPS_A, TAPS_B
    pairs = 2 * children
    last = a[0] * odd[:pairs] + b[0] * even[:pairs]
    first = [a[3 + i] * even[pairs:] + b[3 + i] * odd[pairs:] for i in range(2)]
    return first, last


def disaggregate_kernel(
    parents_ref, octants_ref, flat_ref, phase_ref, gather_ref, out_ref, edge_ref, listed, incoming_ref, lhs, coarse_e, coarse_o, whole_out, sems
):
    periods = incoming_ref.shape[2]
    packed = parents_ref[...] * 8 + octants_ref[...]
    for k in range(listed.shape[0]):
        listed[k] = packed[0, k]
    for gp in range(incoming_ref.shape[0]):
        for w in range(ROWS_PER_PERIOD):
            first = gp * ROWS_PER_PERIOD * periods + w
            incoming_ref[gp, w] = flat_ref[pl.ds(first, periods, stride=ROWS_PER_PERIOD), :]
    azimuth_in = periods * PERIOD_C
    sublane = lax.broadcasted_iota(jnp.int32, (periods, LANES), 0)
    inner = pl.ds(TILE, azimuth_in - 2 * TILE)

    def shift(block):
        for k in range(BLOCK):
            code = listed[block * BLOCK + k]
            octant, parent = code & 7, code >> 3
            for r in range(3):
                for i in range(3):
                    w = 3 * r + i
                    real, imaginary = incoming_ref[2 * parent, w], incoming_ref[2 * parent + 1, w]
                    cosine, sine = phase_ref[octant, 0, w], phase_ref[octant, 1, w]
                    returned = (real * cosine + imaginary * sine, imaginary * cosine - real * sine)
                    for part in range(2):
                        base = ((2 * k + part) * 3 + r) * periods
                        lhs[base : base + periods, i * LANES : (i + 1) * LANES] = returned[part]

    def polar():
        high, low = split(lhs[...])
        coarse_e[...] = gather_dot(high[:, : 2 * LANES], low[:, : 2 * LANES], gather_ref, 0)
        coarse_o[...] = gather_dot(high[:, LANES:], low[:, LANES:], gather_ref, 1)

    def azimuth(block):
        for j in range(2 * BLOCK):
            c = []
            for r in range(3):
                base = (j * 3 + r) * periods
                c.append(coarse_e[base : base + periods, :])
                c.append(coarse_o[base : base + periods, :])
            lower = both_taps_transposed(c[1], c[2])
            upper = both_taps_transposed(c[4], c[5])
            down = [jnp.where(sublane == 0, 0.0, pltpu.roll(upper[i], 1, 0)) for i in (3, 4)]
            up = jnp.where(sublane == periods - 1, 0.0, pltpu.roll(lower[0], periods - 1, 0))
            rows = [c[0] + lower[1] + down[0], lower[2] + upper[0] + down[1], c[3] + lower[3] + upper[1], lower[4] + upper[2] + up]
            kp = block * (2 * BLOCK) + j
            for u in range(PERIOD_C):
                whole_out[kp, pl.ds(u, periods, stride=PERIOD_C), :] = rows[u]
            edge_ref[0, kp] = whole_out[kp, :TILE, :]
            edge_ref[1, kp] = whole_out[kp, azimuth_in - TILE :, :]

    def written(block):
        some = pl.ds(block * (2 * BLOCK), 2 * BLOCK)
        return pltpu.make_async_copy(whole_out.at[some, inner, :], out_ref.at[some, inner, :], sems.at[block])

    def one_block(block, carry):
        shift(block)
        polar()
        azimuth(block)
        written(block).start()
        return carry

    blocks = listed.shape[0] // BLOCK
    lax.fori_loop(0, blocks, one_block, 0)
    for block in range(blocks):
        written(block).wait()


def finish_kernel(parents_ref, phase_ref, gather_ref, edge_ref, far_ref, near_ref, part_ref, out_ref, tiles, sems):
    pairs, azimuth_in, _ = out_ref.shape
    tiles[...] = edge_ref[...]
    flat = tiles.reshape(2 * pairs * TILE, LANES)
    below, above = from_sides(far_ref, near_ref)
    heads, tail = edge_contributions(parents_ref[...], phase_ref, gather_ref, above, below)
    ends = ((0, 0, heads[0]), (0, 1, heads[1]), (1, TILE - 1, tail))
    copies = []
    for i, start in enumerate((0, azimuth_in - TILE)):
        for end, row, values in ends:
            if end == i:
                for part in range(2):
                    for k in range(0, pairs // 2, 8):
                        source = slice(part * (pairs // 2) + k, part * (pairs // 2) + k + 8)
                        rows = pl.ds((i * pairs + 2 * k + part) * TILE + row, 8, stride=2 * TILE)
                        flat[rows, :] = flat[rows, :] + values[source]
        copy = pltpu.make_async_copy(tiles.at[i], out_ref.at[:, pl.ds(start, TILE), :], sems.at[i])
        copy.start()
        copies.append(copy)
    for copy in copies:
        copy.wait()


def swapped(values, axis, first):
    size = lax.axis_size(axis)
    return lax.ppermute(values, axis, [(i, (((i - first) ^ 1) + first) % size) for i in range(size)])


def exchanged(values, axis, mask):
    size = lax.axis_size(axis)
    return lax.ppermute(values, axis, [(i, i ^ mask) for i in range(size)])


SMEM = pl.BlockSpec(memory_space=pltpu.SMEM)
VMEM = pl.BlockSpec(memory_space=pltpu.VMEM)
HBM = pl.BlockSpec(memory_space=pltpu.HBM)


def in_hbm(values):
    return pltpu.with_memory_space_constraint(values, pltpu.HBM)


def local_call(kernel, out_shape, in_specs, scratch, grant, flops=1_000_000, bytes_accessed=1_000_000, out_specs=None, aliases={}):
    return pl.pallas_call(
        kernel,
        out_shape=out_shape,
        in_specs=in_specs,
        out_specs=jax.tree.map(lambda _: VMEM, out_shape) if out_specs is None else out_specs,
        scratch_shapes=scratch,
        input_output_aliases=aliases,
        compiler_params=pltpu.CompilerParams(vmem_limit_bytes=grant << 20),
        cost_estimate=pl.CostEstimate(flops=flops, bytes_accessed=bytes_accessed, transcendentals=0),
    )


def on_device_exchange(
    child_patterns, trans_table, child_parent, child_octant, partner_src, partner_off, partner_count
):
    children, _, azimuth_in, polar_in = child_patterns.shape
    pairs = 2 * children
    peers = lax.axis_size("clus")
    parent_total, _ = partner_src.shape
    own = parent_total // peers
    periods = azimuth_in // PERIOD_C
    flat_rows = ROWS_PER_PERIOD * periods
    share = flat_rows // peers
    offsets = trans_table.shape[0]
    array = lambda *shape: jax.ShapeDtypeStruct(shape, f32)
    buffer = lambda *shape: pltpu.VMEM(shape, f32)
    edges = len(edge_rows(periods))
    even, odd = polar_blocks()
    spread = jnp.asarray(np.stack([np.concatenate([h, h, l]) for h, l in (split_np(even), split_np(odd))]))
    edge = array(2, pairs, polar_in)
    to_far, to_near = local_call(
        rows_kernel, [edge, edge], [HBM], [buffer(pairs, TILE, polar_in)] * 2 + [pltpu.SemaphoreType.DMA((2,))], 8
    )(in_hbm(child_patterns.reshape(pairs, azimuth_in, polar_in)))
    from_far = swapped(to_far, "dir", 1)
    from_near = swapped(to_near, "dir", 0)
    odd_gather = np.concatenate([odd.T[LANES:], odd.T[:LANES]])
    gather = np.stack([np.concatenate(split_np(m), axis=1) for m in (even.T, odd_gather)])

    frame = max(-(-((q * 2 * share) % 8 + 2 * share) // 8) * 8 for q in range(peers))
    view = trans_table.reshape(offsets, 2, flat_rows, LANES).transpose(0, 2, 1, 3).reshape(offsets, 2 * flat_rows, LANES)
    blocks = children // BLOCK
    rows = 2 * BLOCK * 3 * periods
    phases, edge_phases, flat, table = local_call(
        functools.partial(main_kernel, peers),
        [
            array(8, 2, ROWS_PER_PERIOD, periods, LANES),
            array(edges, 2, children, LANES),
            array(2 * own * flat_rows, LANES),
            jax.ShapeDtypeStruct((offsets, frame, LANES), bf16),
        ],
        [HBM] * 5,
        [
            pltpu.SMEM((children,), jnp.int32),
            pltpu.SMEM((children,), jnp.int32),
            buffer(pairs * azimuth_in, polar_in),
            pltpu.VMEM(spread.shape, bf16),
            buffer(rows, LANES),
            buffer(rows, LANES),
            buffer(rows, 2 * LANES),
            buffer(rows, 2 * LANES),
            buffer(own, 2, ROWS_PER_PERIOD, periods, LANES),
            buffer(2 * own * flat_rows, LANES),
            pltpu.SemaphoreType.DMA((5,)),
        ],
        24,
        flops=4_000_000_000,
        bytes_accessed=12_000_000,
    )(
        in_hbm(child_parent[0]),
        in_hbm(child_octant),
        in_hbm(child_patterns.reshape(pairs * azimuth_in, polar_in)),
        in_hbm(view),
        in_hbm(spread),
    )

    chunk = array(2 * own * share, LANES)
    sent = local_call(
        functools.partial(fix_kernel, peers, own), [chunk] * peers, [VMEM] * 6, [buffer(2 * own * flat_rows, LANES)], 8
    )(child_parent, from_far, from_near, flat, edge_phases, spread)

    masks = sorted(range(1, peers), key=lambda d: bin(d).count("1"))
    early, late = masks[:1], masks[1:]
    received = {0: sent[0]}
    for d in early:
        received[d] = exchanged(sent[d], "clus", d)
    for d in late:
        received[d] = exchanged(sent[d], "clus", d)

    sum_pair = [array(parent_total * frame, LANES)] * 2
    others = tuple(early + late)
    operators, *sums = local_call(
        functools.partial(widen_kernel, peers, others),
        [array(parent_total * len(others) * own * frame, LANES)] + sum_pair,
        [VMEM] * 5,
        [
            buffer((offsets + 1) * frame, LANES),
            pltpu.VMEM((parent_total, parent_total), jnp.int32),
            pltpu.SMEM((parent_total, parent_total), jnp.int32),
            buffer(own * frame, LANES),
            buffer(own * frame, LANES),
            pltpu.SemaphoreType.DMA,
        ],
        20,
        flops=90_000_000,
        bytes_accessed=12_000_000,
    )(partner_src, partner_off, partner_count.reshape(1, parent_total), table, received[0])

    sums = local_call(
        functools.partial(gather_kernel, peers, frame, others, tuple(early)),
        sum_pair,
        [VMEM] * (3 + len(early)),
        [buffer(len(early) * own * frame, LANES)] * 2,
        12,
        flops=60_000_000,
        bytes_accessed=12_000_000,
    )(operators, *[received[d] for d in early], *sums)

    back = {}
    last_sources = [received[d] for d in late]
    for number, targets in enumerate((masks[-1:], masks[:-1], [0])):
        prepare = number == 0
        results = local_call(
            functools.partial(translate_kernel, frame, others, tuple(late), tuple(targets)),
            ([array(len(late) * own * frame, LANES)] * 2 if prepare else []) + [chunk] * len(targets),
            [VMEM] * (3 + len(last_sources)),
            [buffer(TOGETHER, frame, LANES)] * 2,
            20,
            flops=10_000_000 * len(targets),
            bytes_accessed=2_000_000 * len(targets),
        )(operators, *sums, *last_sources)
        if prepare:
            last_sources, results = results[:2], results[2:]
        for d, result in zip(targets, results):
            back[d] = exchanged(result, "clus", d) if d else result

    neighbour_phases = local_call(
        functools.partial(neighbour_kernel, periods),
        array(edges, 2, children, LANES),
        [HBM],
        [buffer(edges, 2, 8, LANES), pltpu.SMEM((children,), jnp.int32), pltpu.SemaphoreType.DMA],
        8,
        flops=20_000_000,
    )(in_hbm(child_octant))

    side = array(8 * own, LANES)
    incoming, to_far, to_near = local_call(
        functools.partial(extract_kernel, peers, 2 * own),
        [array(2 * own * flat_rows, LANES), side, side],
        [VMEM] * peers,
        [],
        8,
    )(*[back[d] for d in range(peers)])

    from_far = swapped(to_far, "dir", 1)
    from_near = swapped(to_near, "dir", 0)

    inner, edge_tiles = local_call(
        disaggregate_kernel,
        [array(pairs, azimuth_in, polar_in), array(2, pairs, TILE, polar_in)],
        [VMEM] * 5,
        [
            pltpu.SMEM((children,), jnp.int32),
            buffer(2 * own, ROWS_PER_PERIOD, periods, LANES),
            buffer(rows, 3 * LANES),
            buffer(rows, LANES),
            buffer(rows, LANES),
            buffer(pairs, azimuth_in, polar_in),
            pltpu.SemaphoreType.DMA((blocks,)),
        ],
        24,
        flops=4_000_000_000,
        bytes_accessed=12_000_000,
        out_specs=[HBM, VMEM],
    )(child_parent, child_octant.reshape(1, children), incoming, phases, gather)

    out = local_call(
        finish_kernel,
        array(pairs, azimuth_in, polar_in),
        [VMEM] * 6 + [HBM],
        [buffer(2, pairs, TILE, polar_in), pltpu.SemaphoreType.DMA((2,))],
        8,
        out_specs=HBM,
        aliases={6: 0},
    )(child_parent, neighbour_phases, gather, edge_tiles, from_far, from_near, in_hbm(inner))
    return out.reshape(child_patterns.shape)


def with_halo(shard, sides, width):
    for axis, dim in sides:
        size, length = (lax.axis_size(axis), shard.shape[dim])
        up = [(i, (i + 1) % size) for i in range(size)]
        down = [(j, i) for i, j in up]
        last = lax.slice_in_dim(shard, length - width, length, axis=dim)
        initial = lax.slice_in_dim(shard, 0, width, axis=dim)
        before = lax.ppermute(last, axis, up)
        after = lax.ppermute(initial, axis, down)
        shard = jnp.concatenate([before, shard, after], axis=dim)
    return shard


def lagrange_rows(offset):
    weights = []
    for anchor in range(5):
        factor = jnp.ones_like(offset)
        for neighbour in range(5):
            if neighbour != anchor:
                factor = factor * (offset - neighbour) / (anchor - neighbour)
        weights.append(factor)
    return weights


def polar_matrix_of(rows_out, rows_in):
    target = (jnp.arange(rows_out, dtype=jnp.float32) + 0.5) * rows_in / rows_out - 0.5
    start_row = jnp.clip(jnp.floor(target + 0.5).astype(jnp.int32) - 2, 0, rows_in - 5)
    weights = lagrange_rows(target - start_row.astype(jnp.float32))
    columns = jnp.arange(rows_in, dtype=jnp.int32)
    matrix = jnp.zeros((rows_out, rows_in), jnp.float32)
    for anchor in range(5):
        matrix = matrix + jnp.where(
            columns[None, :] == (start_row + anchor)[:, None], weights[anchor][:, None], 0.0
        )
    return matrix


def azimuth_matrix_of(out_index, in_index, total_out, total_in):
    target = (out_index * total_in).astype(jnp.float32) / total_out
    nearest = jnp.floor(target + 0.5).astype(jnp.int32)
    weights = lagrange_rows(target - nearest.astype(jnp.float32) + 2.0)
    matrix = jnp.zeros((out_index.shape[0], in_index.shape[0]), jnp.float32)
    for anchor in range(5):
        columns = nearest + anchor - 2
        matrix = matrix + jnp.where(
            in_index[None, :] == columns[:, None], weights[anchor][:, None], 0.0
        )
    return matrix


def shift_phases(octant, azimuth_index, azimuth_total, polar_total):
    azimuth = 2.0 * math.pi * azimuth_index.astype(jnp.float32) / azimuth_total
    polar = math.pi * (jnp.arange(polar_total, dtype=jnp.float32) + 0.5) / polar_total
    first_axis = jnp.sin(polar)[None, :] * jnp.cos(azimuth)[:, None]
    second_axis = jnp.sin(polar)[None, :] * jnp.sin(azimuth)[:, None]
    third_axis = jnp.cos(polar)[None, :] * jnp.ones_like(azimuth)[:, None]
    first_sign = (1 - 2 * (octant % 2)).astype(jnp.float32)
    second_sign = (1 - 2 * (octant // 2 % 2)).astype(jnp.float32)
    third_sign = (1 - 2 * (octant // 4)).astype(jnp.float32)
    phase_angle = phase_scale * (
        first_sign[:, None, None] * first_axis[None]
        + second_sign[:, None, None] * second_axis[None]
        + third_sign[:, None, None] * third_axis[None]
    )
    return (jnp.cos(phase_angle), jnp.sin(phase_angle))


def translate(sources, table, partner_src, partner_off, partner_count):
    live_mask = (
        jnp.arange(partner_src.shape[1], dtype=jnp.int32)[None, :] < partner_count[:, None]
    ).astype(jnp.float32)
    picked = sources[partner_src]
    operator = table[partner_off].astype(jnp.float32) * live_mask[:, :, None, None]
    real_part = jnp.sum(
        operator[:, :, 0] * picked[:, :, 0] - operator[:, :, 1] * picked[:, :, 1], axis=1
    )
    imaginary = jnp.sum(
        operator[:, :, 0] * picked[:, :, 1] + operator[:, :, 1] * picked[:, :, 0], axis=1
    )
    return jnp.stack([real_part, imaginary], axis=1)


def forward_shift(patterns, cosine, sine_part):
    real_part = patterns[:, 0] * cosine - patterns[:, 1] * sine_part
    imaginary = patterns[:, 0] * sine_part + patterns[:, 1] * cosine
    return jnp.stack([real_part, imaginary], axis=1)


def conjugate_shift(patterns, cosine, sine_part):
    real_part = patterns[:, 0] * cosine + patterns[:, 1] * sine_part
    imaginary = patterns[:, 1] * cosine - patterns[:, 0] * sine_part
    return jnp.stack([real_part, imaginary], axis=1)


def on_device_gather(
    child_patterns, trans_table, child_parent, child_octant, partner_src, partner_off, partner_count
):
    _, _, azimuth_in, _ = child_patterns.shape
    polar_out = NTHETA_P
    azimuth_out = trans_table.shape[2] // polar_out
    parent_slots = partner_src.shape[0] // lax.axis_size("clus")
    cluster_index = lax.axis_index("clus")
    direction_index = lax.axis_index("dir")
    parents = child_parent[0]
    polar_matrix = polar_matrix_of(NTHETA_P, NTHETA_C)
    onehot = (parents[None, :] == jnp.arange(parent_slots, dtype=jnp.int32)[:, None]).astype(
        jnp.float32
    )
    own_rows = jnp.mod(
        direction_index * azimuth_out + jnp.arange(azimuth_out, dtype=jnp.int32), NPHI_P
    )
    cosine, sine_part = shift_phases(child_octant, own_rows, NPHI_P, polar_out)
    extended = with_halo(child_patterns, (("dir", 2),), 2)
    gather_matrix = azimuth_matrix_of(
        jnp.arange(azimuth_out, dtype=jnp.int32),
        jnp.arange(azimuth_in + 4, dtype=jnp.int32) - 2,
        NPHI_P,
        NPHI_C,
    )
    along_azimuth = jnp.einsum("pc,kacz->kapz", gather_matrix, extended, precision=highest)
    refined = jnp.einsum("kapz,tz->kapt", along_azimuth, polar_matrix, precision=highest)
    shifted = forward_shift(refined, cosine, sine_part)
    radiation = jnp.einsum("gk,kapt->gapt", onehot, shifted, precision=highest)
    flattened = radiation.reshape(parent_slots, 2, azimuth_out * polar_out)
    sources = lax.all_gather(flattened, "clus", axis=0, tiled=True)
    first_row = cluster_index * parent_slots
    own_src = lax.dynamic_slice_in_dim(partner_src, first_row, parent_slots, 0)
    own_off = lax.dynamic_slice_in_dim(partner_off, first_row, parent_slots, 0)
    own_count = lax.dynamic_slice_in_dim(partner_count, first_row, parent_slots, 0)
    incoming = translate(sources, trans_table, own_src, own_off, own_count)
    incoming = incoming.reshape(parent_slots, 2, azimuth_out, polar_out)
    return_matrix = azimuth_matrix_of(
        jnp.arange(azimuth_out + 6, dtype=jnp.int32) - 3,
        jnp.arange(azimuth_in, dtype=jnp.int32),
        NPHI_P,
        NPHI_C,
    )
    per_child = jnp.einsum("gk,gapt->kapt", onehot, incoming, precision=highest)
    returned = conjugate_shift(per_child, cosine, sine_part)
    coarse_own = jnp.einsum("kapt,tz->kapz", returned, polar_matrix, precision=highest)
    coarse = with_halo(coarse_own, (("dir", 2),), 3)
    return jnp.einsum("pc,kapz->kacz", return_matrix, coarse, precision=highest)


def solution(mesh):
    def on_device(child_patterns, trans_table, *rest):
        peers = lax.axis_size("clus")
        children, _, azimuth_in, polar_in = child_patterns.shape
        flat_rows = trans_table.shape[2] // LANES
        fits = (
            azimuth_in % (8 * PERIOD_C) == 0
            and polar_in == LANES
            and flat_rows * PERIOD_C == ROWS_PER_PERIOD * azimuth_in
            and flat_rows % peers == 0
            and peers & (peers - 1) == 0
            and peers > 2
            and lax.axis_size("dir") % 2 == 0
            and children % BLOCK == 0
        )
        plan = on_device_exchange if fits else on_device_gather
        return plan(child_patterns, trans_table, *rest)

    return jax.shard_map(
        on_device,
        mesh=mesh,
        in_specs=(
            P("clus", None, "dir", None),
            P(None, None, "dir"),
            P("clus", None),
            P("clus"),
            P(),
            P(),
            P(),
        ),
        out_specs=P("clus", None, "dir", None),
        check_vma=False,
    )
```

```python
import functools
import math

import jax
import jax.numpy as jnp
import numpy as np
from jax import lax
from jax.experimental import pallas as pl
from jax.experimental.pallas import tpu as pltpu
from jax.sharding import PartitionSpec as P


NTHETA_C = 128
NPHI_C = 256
NTHETA_P = 192
NPHI_P = 384

LANES = 128
PERIOD_P = 6
PERIOD_C = 4
ROWS_PER_PERIOD = PERIOD_P * NTHETA_P // LANES
GROUP = 8
TILE = 8
TOGETHER = 2
BLOCK = 2 * GROUP

phase_scale = 8.0 * math.pi
highest = lax.Precision.HIGHEST
f32 = jnp.float32
bf16 = jnp.bfloat16


def lagrange(offset):
    weights = []
    for anchor in range(5):
        factor = 1.0
        for neighbour in range(5):
            if neighbour != anchor:
                factor = factor * (offset - neighbour) / (anchor - neighbour)
        weights.append(factor)
    return weights


TAPS_A = [float(w) for w in lagrange(5.0 / 3.0)]
TAPS_B = [float(w) for w in lagrange(7.0 / 3.0)]


SUMS = [(TAPS_A[i] + TAPS_A[4 - i]) / 2 for i in range(2)]
DIFFS = [(TAPS_A[i] - TAPS_A[4 - i]) / 2 for i in range(2)]
CENTRE = TAPS_A[2]


def polar_matrix_np():
    target = (np.arange(NTHETA_P, dtype=np.float32) + np.float32(0.5)) * NTHETA_C / NTHETA_P - np.float32(0.5)
    start = np.clip(np.floor(target + 0.5).astype(np.int32) - 2, 0, NTHETA_C - 5)
    weights = lagrange((target - start).astype(np.float64))
    matrix = np.zeros((NTHETA_P, NTHETA_C), np.float64)
    for anchor in range(5):
        matrix[np.arange(NTHETA_P), start + anchor] += weights[anchor]
    return matrix.astype(np.float32)


def polar_blocks():
    matrix = polar_matrix_np().T
    even = np.zeros((NTHETA_C, 2 * LANES), np.float32)
    odd = np.zeros((NTHETA_C, 2 * LANES), np.float32)
    half = NTHETA_P - LANES
    even[:, :NTHETA_P] = matrix
    odd[:, :LANES] = matrix[:, half:]
    odd[:, 2 * LANES - half :] = matrix[:, :half]
    return even, odd


def split_np(matrix):
    high = matrix.astype(bf16)
    low = (matrix - high.astype(np.float32)).astype(bf16)
    return high, low


def split(values):
    high = values.astype(bf16)
    low = (values - high.astype(f32)).astype(bf16)
    return high, low


def dot(left, right):
    return jnp.dot(left, right, preferred_element_type=f32)


def spread_dot(values, matrix_ref, i):
    high, low = split(values)
    depth = values.shape[1]
    return dot(jnp.concatenate([high, low], axis=1), matrix_ref[i, : 2 * depth]) + dot(high, matrix_ref[i, 2 * depth :])


def gather_dot(high, low, matrix_ref, i):
    width = matrix_ref.shape[2] // 2
    both = dot(high, matrix_ref[i])
    return both[:, :width] + (both[:, width:] + dot(low, matrix_ref[i, :, :width]))


SIN_COEFFS = [(-1) ** k * math.pi ** (2 * k + 1) / math.factorial(2 * k + 1) for k in range(7)]
COS_COEFFS = [(-1) ** k * math.pi ** (2 * k) / math.factorial(2 * k) for k in range(7)]


def sincos_turns(turns):
    rest = turns - jnp.round(turns)
    square = rest * rest
    sine = jnp.full_like(square, SIN_COEFFS[-1])
    for coeff in SIN_COEFFS[-2::-1]:
        sine = sine * square + coeff
    sine = sine * rest
    cosine = jnp.full_like(square, COS_COEFFS[-1])
    for coeff in COS_COEFFS[-2::-1]:
        cosine = cosine * square + coeff
    return 2.0 * sine * cosine, 1.0 - 2.0 * sine * sine


def fill_phases(direction, out_ref):
    periods = out_ref.shape[3]
    lane = lax.broadcasted_iota(jnp.int32, (periods, LANES), 1)
    period = lax.broadcasted_iota(jnp.int32, (periods, LANES), 0)
    first = direction * (PERIOD_P * periods)

    def two_rows(r, carry):
        for i in range(3):
            position = lane + i * LANES
            second = (position >= NTHETA_P).astype(jnp.int32)
            polar_index = position - second * NTHETA_P
            azimuth_index = first + period * PERIOD_P + 2 * r + second
            sin_polar, cos_polar = sincos_turns((polar_index.astype(f32) + 0.5) / (2 * NTHETA_P))
            sin_azimuth, cos_azimuth = sincos_turns(azimuth_index.astype(f32) / NPHI_P)
            along_x = 4.0 * sin_polar * cos_azimuth
            along_y = 4.0 * sin_polar * sin_azimuth
            along_z = 4.0 * cos_polar
            w = 3 * r + i
            for octant in (0, 2, 4, 6):
                turns = along_x + along_y if octant % 4 == 0 else along_x - along_y
                turns = turns + along_z if octant < 4 else turns - along_z
                sine, cosine = sincos_turns(turns)
                out_ref[octant, 0, w] = cosine
                out_ref[octant, 1, w] = sine
                out_ref[7 - octant, 0, w] = cosine
                out_ref[7 - octant, 1, w] = -sine
        return carry

    lax.fori_loop(0, PERIOD_P // 2, two_rows, 0)


def edge_rows(periods):
    return [(w, 0) for w in (1, 2, 3, 4)] + [(w, periods - 1) for w in (6, 7, 8)]


def by_parity(even, odd):
    parity = lax.rem(lax.axis_index("dir"), 2)
    pl.when(parity == 0)(even)
    pl.when(parity == 1)(odd)


def from_sides(far_ref, near_ref):
    is_even = lax.rem(lax.axis_index("dir"), 2) == 0
    far, near = far_ref[...], near_ref[...]
    return jnp.where(is_even, far, near), jnp.where(is_even, near, far)


def rows_kernel(x_ref, far_ref, near_ref, low, high, sems):
    pairs, azimuth_in, _ = x_ref.shape
    low_copy = pltpu.make_async_copy(x_ref.at[:, pl.ds(0, TILE), :], low, sems.at[0])
    high_copy = pltpu.make_async_copy(x_ref.at[:, pl.ds(azimuth_in - TILE, TILE), :], high, sems.at[1])
    low_copy.start()
    high_copy.start()
    low_copy.wait()
    high_copy.wait()
    low_rows, high_rows = (ref.reshape(pairs * TILE, LANES) for ref in (low, high))

    def fill(first_ref, last_ref):
        for part in range(2):
            for k in range(0, pairs // 2, 8):
                target = slice(part * (pairs // 2) + k, part * (pairs // 2) + k + 8)
                base = (2 * k + part) * TILE
                for i in range(2):
                    first_ref[i, target] = low_rows[pl.ds(base + i, 8, stride=2 * TILE), :]
                last = high_rows[pl.ds(base + TILE - 1, 8, stride=2 * TILE), :]
                for i in range(2):
                    last_ref[i, target] = last

    by_parity(lambda: fill(far_ref, near_ref), lambda: fill(near_ref, far_ref))


def both_taps(rows):
    even = SUMS[0] * (rows[0] + rows[4]) + SUMS[1] * (rows[1] + rows[3]) + CENTRE * rows[2]
    odd = DIFFS[0] * (rows[0] - rows[4]) + DIFFS[1] * (rows[1] - rows[3])
    return even + odd, even - odd


def both_taps_transposed(first, second):
    total, difference = first + second, first - second
    outer = [SUMS[i] * total for i in range(2)]
    inner = [DIFFS[i] * difference for i in range(2)]
    return [outer[0] + inner[0], outer[1] + inner[1], CENTRE * total, outer[1] - inner[1], outer[0] - inner[0]]


def main_kernel(peers, parents_hbm, octants_hbm, x_hbm, table_ref, spread_hbm, *rest):
    phase_ref, edge_phase_ref, flat_ref, slice_ref = rest[:4]
    parents_ref, octants_ref, x_ref, spread_ref, az_e, az_o, res_e, res_o, acc, flat, sems = rest[4:]
    children = octants_ref.shape[0]
    periods = phase_ref.shape[3]
    azimuth_in = periods * PERIOD_C
    own = acc.shape[0]
    me = lax.axis_index("clus")
    share = ROWS_PER_PERIOD * periods // peers
    first_tile = me * (2 * share) // 8
    table_rows = pl.ds(pl.multiple_of(first_tile * 8, 8), slice_ref.shape[1])
    ends = (
        (octants_hbm, octants_ref),
        (parents_hbm, parents_ref),
        (x_hbm, x_ref),
        (spread_hbm, spread_ref),
        (table_ref.at[:, table_rows, :], slice_ref),
    )
    copies = [pltpu.make_async_copy(source, target, sems.at[i]) for i, (source, target) in enumerate(ends)]
    for copy in copies[:-1]:
        copy.start()
    fill_phases(lax.axis_index("dir"), phase_ref)
    acc[...] = jnp.zeros_like(acc)
    sublane = lax.broadcasted_iota(jnp.int32, (periods, LANES), 0)
    copies[0].wait()

    def edges_of(step, carry):
        for j in range(GROUP):
            k = step * GROUP + j
            octant = octants_ref[k]
            for e, (w, m) in enumerate(edge_rows(periods)):
                for i in range(2):
                    edge_phase_ref[e, i, pl.ds(k, 1), :] = phase_ref[octant, i, w, m : m + 1, :]
        return carry

    lax.fori_loop(0, children // GROUP, edges_of, 0)
    for copy in copies[1:-1]:
        copy.wait()
    copies[-1].start()

    def azimuth(block):
        for kp in range(2 * BLOCK):
            start = pl.multiple_of((block * (2 * BLOCK) + kp) * azimuth_in, 8)
            x = [x_ref[pl.ds(start + u, periods, stride=PERIOD_C), :] for u in range(PERIOD_C)]
            left = jnp.where(sublane == 0, 0.0, pltpu.roll(x[3], 1, 0))
            right = [jnp.where(sublane == periods - 1, 0.0, pltpu.roll(x[i], periods - 1, 0)) for i in range(2)]
            lower = [left, x[0], x[1], x[2], x[3]]
            upper = [x[1], x[2], x[3], right[0], right[1]]
            rows = [x[0], *both_taps(lower), x[2], *both_taps(upper)]
            for r in range(3):
                base = (kp * 3 + r) * periods
                az_e[base : base + periods, :] = rows[2 * r]
                az_o[base : base + periods, :] = rows[2 * r + 1]

    def polar():
        res_e[...] = spread_dot(az_e[...], spread_ref, 0)
        res_o[...] = spread_dot(az_o[...], spread_ref, 1)

    def shift(block):
        for k in range(BLOCK):
            octant = octants_ref[block * BLOCK + k]
            parent = parents_ref[block * BLOCK + k]
            for r in range(3):
                parts = []
                for part in range(2):
                    rows = pl.ds(((2 * k + part) * 3 + r) * periods, periods)
                    middle = res_e[rows, LANES:] + res_o[rows, LANES:]
                    parts.append((res_e[rows, :LANES], middle, res_o[rows, :LANES]))
                for i in range(3):
                    w = 3 * r + i
                    real, imaginary = parts[0][i], parts[1][i]
                    cosine, sine = phase_ref[octant, 0, w], phase_ref[octant, 1, w]
                    acc[parent, 0, w] += real * cosine - imaginary * sine
                    acc[parent, 1, w] += real * sine + imaginary * cosine

    def one_block(block, carry):
        azimuth(block)
        polar()
        shift(block)
        return carry

    lax.fori_loop(0, children // BLOCK, one_block, 0)
    for gp in range(2 * own):
        for w in range(ROWS_PER_PERIOD):
            flat[pl.ds(gp * ROWS_PER_PERIOD * periods + w, periods, stride=ROWS_PER_PERIOD), :] = acc[gp // 2, gp % 2, w]
        for q in range(peers):
            source = gp * ROWS_PER_PERIOD * periods + q * share
            target = (q * 2 * own + gp) * share
            flat_ref[target : target + share, :] = flat[source : source + share, :]
    copies[-1].wait()


def one_hot(parents, own):
    index = lax.broadcasted_iota(jnp.int32, (own, parents.shape[1]), 0)
    return (index == parents).astype(f32)


def dot2(exact, values):
    exact = exact.astype(bf16)
    high, low = split(values)
    return dot(exact, high) + dot(exact, low)


def fix_kernel(
    peers, own, parents_ref, far_ref, near_ref, flat_ref, edge_phase_ref, spread_ref, *rest
):
    outs, (fixed,) = rest[:peers], rest[peers:]
    pairs = far_ref.shape[1]
    children = pairs // 2
    chunk_rows = outs[0].shape[0]
    share = chunk_rows // (2 * own)
    periods = share * peers // ROWS_PER_PERIOD
    fixed[...] = flat_ref[...]
    before, right = from_sides(far_ref, near_ref)
    left = before[0]
    a, b = TAPS_A, TAPS_B
    even = jnp.concatenate([b[0] * left, a[3] * right[0] + a[4] * right[1]], axis=0)
    odd = jnp.concatenate([a[0] * left, b[3] * right[0] + b[4] * right[1]], axis=0)
    even = spread_dot(even, spread_ref, 0)
    odd = spread_dot(odd, spread_ref, 1)
    first, last = slice(0, pairs), slice(pairs, 2 * pairs)
    low, high = slice(0, LANES), slice(LANES, 2 * LANES)
    refined = [
        odd[first, high],
        odd[first, low],
        even[first, low],
        even[first, high],
        even[last, low],
        even[last, high] + odd[last, high],
        odd[last, low],
    ]
    shifted_rows = []
    for e, rows in enumerate(refined):
        real, imaginary = rows[:children], rows[children:]
        cosine, sine = edge_phase_ref[e, 0], edge_phase_ref[e, 1]
        shifted_rows.append(real * cosine - imaginary * sine)
        shifted_rows.append(real * sine + imaginary * cosine)
    summed = dot2(one_hot(parents_ref[...], own), jnp.concatenate(shifted_rows, axis=1))
    for e, (w, m) in enumerate(edge_rows(periods)):
        q, row = divmod(ROWS_PER_PERIOD * m + w, share)
        for part in range(2):
            rows = pl.ds(q * chunk_rows + part * share + row, own, stride=2 * share)
            column = (2 * e + part) * LANES
            fixed[rows, :] = fixed[rows, :] + summed[:, column : column + LANES]
    me = lax.axis_index("clus")
    for d in range(peers):
        start = pl.multiple_of((me ^ d) * chunk_rows, 8)
        outs[d][...] = fixed[pl.ds(start, chunk_rows), :]


def widen_kernel(peers, others, source_ref, offset_ref, count_ref, table_ref, chunk, placed_ref, real_sum, imag_sum, *rest):
    wide_ref, numbers_ref, listed, real_twice, imag_twice, sem = rest
    targets, partners = source_ref.shape
    offsets, frame, _ = table_ref.shape
    own = targets // peers
    share = chunk.shape[0] // (2 * own)
    me = lax.axis_index("clus")
    shape = (targets, targets)
    row, lane = (lax.broadcasted_iota(jnp.int32, shape, d) for d in range(2))
    count = jnp.sum(jnp.where(row == lane, count_ref[...], 0), axis=1, keepdims=True)
    number = jnp.full(shape, offsets, jnp.int32)
    for p in range(partners):
        here = (lane == source_ref[:, p : p + 1]) & (p < count)
        number = jnp.where(here, offset_ref[:, p : p + 1], number)
    numbers_ref[...] = number * frame
    copy = pltpu.make_async_copy(numbers_ref, listed, sem)
    copy.start()

    def some_offsets(i, carry):
        for j in range(4):
            wide_ref[pl.ds(pl.multiple_of((i * 4 + j) * frame, 8), frame), :] = table_ref[i * 4 + j].astype(f32)
        return carry

    whole_steps = offsets // 4
    lax.fori_loop(0, whole_steps, some_offsets, 0)
    for offset in range(whole_steps * 4, offsets):
        wide_ref[offset * frame : (offset + 1) * frame, :] = table_ref[offset].astype(f32)
    wide_ref[offsets * frame :, :] = jnp.zeros((frame, LANES), f32)
    doubled(chunk, real_twice, imag_twice, 0, own, share, frame, lax.rem(me * (2 * share), 8))
    copy.wait()

    def operator_of(target, device, g):
        first = listed[target, device * own + g]
        return wide_ref[pl.ds(pl.multiple_of(first, 8), frame), :]

    def own_sources(some, sums):
        return add_sources(sums, own, frame, lambda j, source: operator_of(some[j], me, source), real_twice, imag_twice)

    for_some_targets(targets, frame, own_sources, None, (real_sum, imag_sum))

    def other_sources(target, carry):
        for i, d in enumerate(others):
            for g in range(own):
                place = pl.multiple_of(((target * len(others) + i) * own + g) * frame, 8)
                placed_ref[pl.ds(place, frame), :] = operator_of(target, me ^ d, g)
        return carry

    lax.fori_loop(0, targets, other_sources, 0)


def doubled(chunk, real_twice, imag_twice, first, own, share, frame, skip):
    for g in range(own):
        for part, twice in enumerate((real_twice, imag_twice)):
            rows = chunk[(2 * g + part) * share : (2 * g + part + 1) * share, :]
            base = (first + g) * frame + skip
            twice[pl.ds(base, share, stride=2), :] = rows
            twice[pl.ds(base + 1, share, stride=2), :] = rows


def add_sources(sums, sources, frame, operators, real_twice, imag_twice):
    for source in range(sources):
        place = slice(source * frame, (source + 1) * frame)
        real, imaginary = real_twice[place, :], imag_twice[place, :]
        for i in range(len(sums)):
            operator = operators(i, source)
            sums[i] = (sums[i][0] + operator * real, sums[i][1] + operator * imaginary)
    return sums


def for_some_targets(targets, frame, add, before, after):
    def some_targets(i, carry):
        some = [i * TOGETHER + j for j in range(TOGETHER)]
        places = [pl.ds(pl.multiple_of(target * frame, 8), frame) for target in some]
        if before is None:
            sums = [(jnp.zeros((frame, LANES), f32),) * 2 for _ in some]
        else:
            sums = [tuple(ref[place, :] for ref in before) for place in places]
        for place, values in zip(places, add(some, sums)):
            for ref, value in zip(after, values):
                ref[place, :] = value
        return carry

    lax.fori_loop(0, targets // TOGETHER, some_targets, 0)


def placed(placed_ref, frame, others, own, masks):
    firsts = [others.index(d) * own for d in masks]

    def operator_of(target, source):
        place = target * (len(others) * own) + firsts[source // own] + source % own
        return placed_ref[pl.ds(pl.multiple_of(place * frame, 8), frame), :]

    return operator_of


def translate_kernel(frame, others, masks, targets, placed_ref, real_sum, imag_sum, *rest):
    prepare = len(rest) == len(masks) + len(targets) + 4
    chunks, rest = (rest[: len(masks)], rest[len(masks) :]) if prepare else ((), rest)
    real_twice, imag_twice = rest[:2]
    outs, (total_real, total_imag) = rest[-2 - len(targets) : -2], rest[-2:]
    me = lax.axis_index("clus")
    sources = real_twice.shape[0] // frame
    own = sources // len(masks)
    share = outs[0].shape[0] // (2 * own)
    skip = lax.rem(me * (2 * share), 8)
    for number, chunk in enumerate(chunks):
        doubled(chunk, real_twice, imag_twice, number * own, own, share, frame, skip)
    operator_of = placed(placed_ref, frame, others, own, masks)
    even, odd = pl.ds(skip, share, stride=2), pl.ds(skip + 1, share, stride=2)
    for out, d in zip(outs, targets):
        first = (me ^ d) * own

        def some_targets(i, carry):
            places = [i * TOGETHER + j for j in range(TOGETHER)]
            some = [first + g for g in places]
            rows = [pl.ds(pl.multiple_of(target * frame, 8), frame) for target in some]
            sums = [(real_sum[r, :], imag_sum[r, :]) for r in rows]
            operators = lambda j, source: operator_of(some[j], source)
            sums = add_sources(sums, sources, frame, operators, real_twice, imag_twice)
            for j, (g, (by_real, by_imag)) in enumerate(zip(places, sums)):
                total_real[j] = by_real
                total_imag[j] = by_imag
                row = g * (2 * share)
                out[pl.ds(row, share), :] = total_real[j, even, :] - total_imag[j, odd, :]
                out[pl.ds(row + share, share), :] = total_real[j, odd, :] + total_imag[j, even, :]
            return carry

        lax.fori_loop(0, own // TOGETHER, some_targets, 0)


def extract_kernel(peers, own2, *rest):
    chunks = rest[:peers]
    flat, far_ref, near_ref = rest[peers:]
    share = chunks[0].shape[0] // own2
    periods = share * peers // ROWS_PER_PERIOD
    own = own2 // 2
    flat_rows = ROWS_PER_PERIOD * periods
    me = lax.axis_index("clus")
    for gp in range(own2):
        for d in range(peers):
            flat[pl.ds(gp * flat_rows + (me ^ d) * share, share), :] = chunks[d][gp * share : (gp + 1) * share, :]

    def fill(prev_ref, next_ref):
        for ref in (prev_ref, next_ref):
            ref[...] = jnp.zeros_like(ref)
        places = [(prev_ref, e) for e in range(4)] + [(next_ref, e) for e in range(3)]
        for (ref, e), (w, m) in zip(places, edge_rows(periods)):
            for part in range(2):
                first = part * flat_rows + ROWS_PER_PERIOD * m + w
                row = (2 * e + part) * own
                ref[row : row + own, :] = flat[pl.ds(first, own, stride=2 * flat_rows), :]

    by_parity(lambda: fill(far_ref, near_ref), lambda: fill(near_ref, far_ref))


def neighbour_kernel(periods, octants_hbm, out_ref, by_octant, octants_ref, sem):
    copy = pltpu.make_async_copy(octants_hbm, octants_ref, sem)
    copy.start()
    here = lax.axis_index("dir")
    octant = lax.broadcasted_iota(jnp.int32, (8, LANES), 0)
    lane = lax.broadcasted_iota(jnp.int32, (8, LANES), 1)
    signs = [(1 - 2 * ((octant >> bit) & 1)).astype(f32) for bit in range(3)]
    for e, (w, m) in enumerate(edge_rows(periods)):
        place = here + 1 if m == 0 else here - 1
        position = lane + w * LANES
        row = w * LANES // NTHETA_P
        row = jnp.where(position >= (row + 1) * NTHETA_P, row + 1, row)
        polar_index = position - row * NTHETA_P
        azimuth_index = (place * periods + m) * PERIOD_P + row
        sin_polar, cos_polar = sincos_turns((polar_index.astype(f32) + 0.5) / (2 * NTHETA_P))
        sin_azimuth, cos_azimuth = sincos_turns(azimuth_index.astype(f32) / NPHI_P)
        along = (sin_polar * cos_azimuth, sin_polar * sin_azimuth, cos_polar)
        sine, cosine = sincos_turns(4.0 * (signs[0] * along[0] + signs[1] * along[1] + signs[2] * along[2]))
        by_octant[e, 0] = cosine
        by_octant[e, 1] = sine
    copy.wait()

    def some_children(step, carry):
        for j in range(GROUP):
            k = step * GROUP + j
            for e in range(by_octant.shape[0]):
                for i in range(2):
                    out_ref[e, i, pl.ds(k, 1), :] = by_octant[e, i, pl.ds(octants_ref[k], 1), :]
        return carry

    lax.fori_loop(0, octants_ref.shape[0] // GROUP, some_children, 0)


def returned_rows(parents, phase_ref, edges, rows_ref):
    own = rows_ref.shape[0] // 8
    columns = [rows_ref[row * own : (row + 1) * own, :] for row in range(2 * len(edges))]
    per_child = dot2(one_hot(parents, own).T, jnp.concatenate(columns, axis=1))
    returned = []
    for i, e in enumerate(edges):
        real = per_child[:, 2 * i * LANES : (2 * i + 1) * LANES]
        imaginary = per_child[:, (2 * i + 1) * LANES : (2 * i + 2) * LANES]
        cosine, sine = phase_ref[e, 0], phase_ref[e, 1]
        returned.append(
            jnp.concatenate([real * cosine + imaginary * sine, imaginary * cosine - real * sine], axis=0)
        )
    return returned


def side_by_side(left, right):
    return split(jnp.concatenate([left, right], axis=1))


def disaggregate_kernel(
    parents_ref, octants_ref, flat_ref, phase_ref, gather_ref, out_ref, edge_ref, listed, incoming_ref, lhs, coarse_e, coarse_o, whole_out, sems
):
    periods = incoming_ref.shape[2]
    packed = parents_ref[...] * 8 + octants_ref[...]
    for k in range(listed.shape[0]):
        listed[k] = packed[0, k]
    for gp in range(incoming_ref.shape[0]):
        for w in range(ROWS_PER_PERIOD):
            first = gp * ROWS_PER_PERIOD * periods + w
            incoming_ref[gp, w] = flat_ref[pl.ds(first, periods, stride=ROWS_PER_PERIOD), :]
    azimuth_in = periods * PERIOD_C
    sublane = lax.broadcasted_iota(jnp.int32, (periods, LANES), 0)
    inner = pl.ds(TILE, azimuth_in - 2 * TILE)

    def shift(block):
        for k in range(BLOCK):
            code = listed[block * BLOCK + k]
            octant, parent = code & 7, code >> 3
            for r in range(3):
                for i in range(3):
                    w = 3 * r + i
                    real, imaginary = incoming_ref[2 * parent, w], incoming_ref[2 * parent + 1, w]
                    cosine, sine = phase_ref[octant, 0, w], phase_ref[octant, 1, w]
                    returned = (real * cosine + imaginary * sine, imaginary * cosine - real * sine)
                    for part in range(2):
                        base = ((2 * k + part) * 3 + r) * periods
                        lhs[base : base + periods, i * LANES : (i + 1) * LANES] = returned[part]

    def polar():
        high, low = split(lhs[...])
        coarse_e[...] = gather_dot(high[:, : 2 * LANES], low[:, : 2 * LANES], gather_ref, 0)
        coarse_o[...] = gather_dot(high[:, LANES:], low[:, LANES:], gather_ref, 1)

    def azimuth(block):
        for j in range(2 * BLOCK):
            c = []
            for r in range(3):
                base = (j * 3 + r) * periods
                c.append(coarse_e[base : base + periods, :])
                c.append(coarse_o[base : base + periods, :])
            lower = both_taps_transposed(c[1], c[2])
            upper = both_taps_transposed(c[4], c[5])
            down = [jnp.where(sublane == 0, 0.0, pltpu.roll(upper[i], 1, 0)) for i in (3, 4)]
            up = jnp.where(sublane == periods - 1, 0.0, pltpu.roll(lower[0], periods - 1, 0))
            rows = [c[0] + lower[1] + down[0], lower[2] + upper[0] + down[1], c[3] + lower[3] + upper[1], lower[4] + upper[2] + up]
            kp = block * (2 * BLOCK) + j
            for u in range(PERIOD_C):
                whole_out[kp, pl.ds(u, periods, stride=PERIOD_C), :] = rows[u]
            edge_ref[0, kp] = whole_out[kp, :TILE, :]
            edge_ref[1, kp] = whole_out[kp, azimuth_in - TILE :, :]

    def written(block):
        some = pl.ds(block * (2 * BLOCK), 2 * BLOCK)
        return pltpu.make_async_copy(whole_out.at[some, inner, :], out_ref.at[some, inner, :], sems.at[block])

    def one_block(block, carry):
        shift(block)
        polar()
        azimuth(block)
        written(block).start()
        return carry

    blocks = listed.shape[0] // BLOCK
    lax.fori_loop(0, blocks, one_block, 0)
    for block in range(blocks):
        written(block).wait()


def finish_kernel(is_far, parents_ref, phase_ref, gather_ref, edge_ref, side_ref, part_ref, out_ref, tiles, sem):
    pairs, azimuth_in, _ = out_ref.shape
    a, b = TAPS_A, TAPS_B

    def write(end, start, additions):
        tiles[...] = edge_ref[end]
        flat = tiles.reshape(pairs * TILE, LANES)
        for row, values in additions:
            for part in range(2):
                for k in range(0, pairs // 2, 8):
                    source = slice(part * (pairs // 2) + k, part * (pairs // 2) + k + 8)
                    rows = pl.ds((2 * k + part) * TILE + row, 8, stride=2 * TILE)
                    flat[rows, :] = flat[rows, :] + values[source]
        copy = pltpu.make_async_copy(tiles, out_ref.at[:, pl.ds(start, TILE), :], sem)
        copy.start()
        copy.wait()

    def from_below():
        returned = returned_rows(parents_ref[...], phase_ref, (4, 5, 6), side_ref)
        even = gather_dot(*side_by_side(returned[0], returned[1]), gather_ref, 0)
        odd = gather_dot(*side_by_side(returned[1], returned[2]), gather_ref, 1)
        write(0, 0, [(i, a[3 + i] * even + b[3 + i] * odd) for i in range(2)])

    def from_above():
        returned = returned_rows(parents_ref[...], phase_ref, (0, 1, 2, 3), side_ref)
        even = gather_dot(*side_by_side(returned[2], returned[3]), gather_ref, 0)
        odd = gather_dot(*side_by_side(returned[0], returned[1]), gather_ref, 1)
        write(1, azimuth_in - TILE, [(TILE - 1, a[0] * odd + b[0] * even)])

    by_parity(*((from_below, from_above) if is_far else (from_above, from_below)))


def swapped(values, axis, first):
    size = lax.axis_size(axis)
    return lax.ppermute(values, axis, [(i, (((i - first) ^ 1) + first) % size) for i in range(size)])


def exchanged(values, axis, mask):
    size = lax.axis_size(axis)
    return lax.ppermute(values, axis, [(i, i ^ mask) for i in range(size)])


SMEM = pl.BlockSpec(memory_space=pltpu.SMEM)
VMEM = pl.BlockSpec(memory_space=pltpu.VMEM)
HBM = pl.BlockSpec(memory_space=pltpu.HBM)


def in_hbm(values):
    return pltpu.with_memory_space_constraint(values, pltpu.HBM)


def local_call(kernel, out_shape, in_specs, scratch, grant, flops=1_000_000, bytes_accessed=1_000_000, out_specs=None, aliases={}):
    return pl.pallas_call(
        kernel,
        out_shape=out_shape,
        in_specs=in_specs,
        out_specs=jax.tree.map(lambda _: VMEM, out_shape) if out_specs is None else out_specs,
        scratch_shapes=scratch,
        input_output_aliases=aliases,
        compiler_params=pltpu.CompilerParams(vmem_limit_bytes=grant << 20),
        cost_estimate=pl.CostEstimate(flops=flops, bytes_accessed=bytes_accessed, transcendentals=0),
    )


def on_device_exchange(
    child_patterns, trans_table, child_parent, child_octant, partner_src, partner_off, partner_count
):
    children, _, azimuth_in, polar_in = child_patterns.shape
    pairs = 2 * children
    peers = lax.axis_size("clus")
    parent_total, _ = partner_src.shape
    own = parent_total // peers
    periods = azimuth_in // PERIOD_C
    flat_rows = ROWS_PER_PERIOD * periods
    share = flat_rows // peers
    offsets = trans_table.shape[0]
    array = lambda *shape: jax.ShapeDtypeStruct(shape, f32)
    buffer = lambda *shape: pltpu.VMEM(shape, f32)
    edges = len(edge_rows(periods))
    even, odd = polar_blocks()
    spread = jnp.asarray(np.stack([np.concatenate([h, h, l]) for h, l in (split_np(even), split_np(odd))]))
    edge = array(2, pairs, polar_in)
    to_far, to_near = local_call(
        rows_kernel, [edge, edge], [HBM], [buffer(pairs, TILE, polar_in)] * 2 + [pltpu.SemaphoreType.DMA((2,))], 8
    )(in_hbm(child_patterns.reshape(pairs, azimuth_in, polar_in)))
    from_far = swapped(to_far, "dir", 1)
    from_near = swapped(to_near, "dir", 0)
    odd_gather = np.concatenate([odd.T[LANES:], odd.T[:LANES]])
    gather = np.stack([np.concatenate(split_np(m), axis=1) for m in (even.T, odd_gather)])

    frame = max(-(-((q * 2 * share) % 8 + 2 * share) // 8) * 8 for q in range(peers))
    view = trans_table.reshape(offsets, 2, flat_rows, LANES).transpose(0, 2, 1, 3).reshape(offsets, 2 * flat_rows, LANES)
    blocks = children // BLOCK
    rows = 2 * BLOCK * 3 * periods
    phases, edge_phases, flat, table = local_call(
        functools.partial(main_kernel, peers),
        [
            array(8, 2, ROWS_PER_PERIOD, periods, LANES),
            array(edges, 2, children, LANES),
            array(2 * own * flat_rows, LANES),
            jax.ShapeDtypeStruct((offsets, frame, LANES), bf16),
        ],
        [HBM] * 5,
        [
            pltpu.SMEM((children,), jnp.int32),
            pltpu.SMEM((children,), jnp.int32),
            buffer(pairs * azimuth_in, polar_in),
            pltpu.VMEM(spread.shape, bf16),
            buffer(rows, LANES),
            buffer(rows, LANES),
            buffer(rows, 2 * LANES),
            buffer(rows, 2 * LANES),
            buffer(own, 2, ROWS_PER_PERIOD, periods, LANES),
            buffer(2 * own * flat_rows, LANES),
            pltpu.SemaphoreType.DMA((5,)),
        ],
        24,
        flops=4_000_000_000,
        bytes_accessed=12_000_000,
    )(
        in_hbm(child_parent[0]),
        in_hbm(child_octant),
        in_hbm(child_patterns.reshape(pairs * azimuth_in, polar_in)),
        in_hbm(view),
        in_hbm(spread),
    )

    chunk = array(2 * own * share, LANES)
    sent = local_call(
        functools.partial(fix_kernel, peers, own), [chunk] * peers, [VMEM] * 6, [buffer(2 * own * flat_rows, LANES)], 8
    )(child_parent, from_far, from_near, flat, edge_phases, spread)

    masks = sorted(range(1, peers), key=lambda d: -bin(d).count("1"))
    received = {0: sent[0]}
    for d in masks:
        received[d] = exchanged(sent[d], "clus", d)

    sum_pair = [array(parent_total * frame, LANES)] * 2
    others = tuple(masks)
    operators, *sums = local_call(
        functools.partial(widen_kernel, peers, others),
        [array(parent_total * len(others) * own * frame, LANES)] + sum_pair,
        [VMEM] * 5,
        [
            buffer((offsets + 1) * frame, LANES),
            pltpu.VMEM((parent_total, parent_total), jnp.int32),
            pltpu.SMEM((parent_total, parent_total), jnp.int32),
            buffer(own * frame, LANES),
            buffer(own * frame, LANES),
            pltpu.SemaphoreType.DMA,
        ],
        20,
        flops=90_000_000,
        bytes_accessed=12_000_000,
    )(partner_src, partner_off, partner_count.reshape(1, parent_total), table, received[0])

    back = {}
    last_sources = [received[d] for d in masks]
    for number, targets in enumerate((masks[:1], masks[1:], [0])):
        prepare = number == 0
        results = local_call(
            functools.partial(translate_kernel, frame, others, others, tuple(targets)),
            ([array(len(others) * own * frame, LANES)] * 2 if prepare else []) + [chunk] * len(targets),
            [VMEM] * (3 + len(last_sources)),
            [buffer(TOGETHER, frame, LANES)] * 2,
            20,
            flops=10_000_000 * len(targets),
            bytes_accessed=2_000_000 * len(targets),
        )(operators, *sums, *last_sources)
        if prepare:
            last_sources, results = results[:2], results[2:]
        for d, result in zip(targets, results):
            back[d] = exchanged(result, "clus", d) if d else result

    neighbour_phases = local_call(
        functools.partial(neighbour_kernel, periods),
        array(edges, 2, children, LANES),
        [HBM],
        [buffer(edges, 2, 8, LANES), pltpu.SMEM((children,), jnp.int32), pltpu.SemaphoreType.DMA],
        8,
        flops=20_000_000,
    )(in_hbm(child_octant))

    side = array(8 * own, LANES)
    incoming, to_far, to_near = local_call(
        functools.partial(extract_kernel, peers, 2 * own),
        [array(2 * own * flat_rows, LANES), side, side],
        [VMEM] * peers,
        [],
        8,
    )(*[back[d] for d in range(peers)])

    from_far = swapped(to_far, "dir", 1)
    from_near = swapped(to_near, "dir", 0)

    inner, edge_tiles = local_call(
        disaggregate_kernel,
        [array(pairs, azimuth_in, polar_in), array(2, pairs, TILE, polar_in)],
        [VMEM] * 5,
        [
            pltpu.SMEM((children,), jnp.int32),
            buffer(2 * own, ROWS_PER_PERIOD, periods, LANES),
            buffer(rows, 3 * LANES),
            buffer(rows, LANES),
            buffer(rows, LANES),
            buffer(pairs, azimuth_in, polar_in),
            pltpu.SemaphoreType.DMA((blocks,)),
        ],
        24,
        flops=4_000_000_000,
        bytes_accessed=12_000_000,
        out_specs=[HBM, VMEM],
    )(child_parent, child_octant.reshape(1, children), incoming, phases, gather)

    out = inner
    for is_far, side in ((False, from_near), (True, from_far)):
        out = local_call(
            functools.partial(finish_kernel, is_far),
            array(pairs, azimuth_in, polar_in),
            [VMEM] * 5 + [HBM],
            [buffer(pairs, TILE, polar_in), pltpu.SemaphoreType.DMA],
            8,
            out_specs=HBM,
            aliases={5: 0},
        )(child_parent, neighbour_phases, gather, edge_tiles, side, in_hbm(out))
    return out.reshape(child_patterns.shape)


def with_halo(shard, sides, width):
    for axis, dim in sides:
        size, length = (lax.axis_size(axis), shard.shape[dim])
        up = [(i, (i + 1) % size) for i in range(size)]
        down = [(j, i) for i, j in up]
        last = lax.slice_in_dim(shard, length - width, length, axis=dim)
        initial = lax.slice_in_dim(shard, 0, width, axis=dim)
        before = lax.ppermute(last, axis, up)
        after = lax.ppermute(initial, axis, down)
        shard = jnp.concatenate([before, shard, after], axis=dim)
    return shard


def lagrange_rows(offset):
    weights = []
    for anchor in range(5):
        factor = jnp.ones_like(offset)
        for neighbour in range(5):
            if neighbour != anchor:
                factor = factor * (offset - neighbour) / (anchor - neighbour)
        weights.append(factor)
    return weights


def polar_matrix_of(rows_out, rows_in):
    target = (jnp.arange(rows_out, dtype=jnp.float32) + 0.5) * rows_in / rows_out - 0.5
    start_row = jnp.clip(jnp.floor(target + 0.5).astype(jnp.int32) - 2, 0, rows_in - 5)
    weights = lagrange_rows(target - start_row.astype(jnp.float32))
    columns = jnp.arange(rows_in, dtype=jnp.int32)
    matrix = jnp.zeros((rows_out, rows_in), jnp.float32)
    for anchor in range(5):
        matrix = matrix + jnp.where(
            columns[None, :] == (start_row + anchor)[:, None], weights[anchor][:, None], 0.0
        )
    return matrix


def azimuth_matrix_of(out_index, in_index, total_out, total_in):
    target = (out_index * total_in).astype(jnp.float32) / total_out
    nearest = jnp.floor(target + 0.5).astype(jnp.int32)
    weights = lagrange_rows(target - nearest.astype(jnp.float32) + 2.0)
    matrix = jnp.zeros((out_index.shape[0], in_index.shape[0]), jnp.float32)
    for anchor in range(5):
        columns = nearest + anchor - 2
        matrix = matrix + jnp.where(
            in_index[None, :] == columns[:, None], weights[anchor][:, None], 0.0
        )
    return matrix


def shift_phases(octant, azimuth_index, azimuth_total, polar_total):
    azimuth = 2.0 * math.pi * azimuth_index.astype(jnp.float32) / azimuth_total
    polar = math.pi * (jnp.arange(polar_total, dtype=jnp.float32) + 0.5) / polar_total
    first_axis = jnp.sin(polar)[None, :] * jnp.cos(azimuth)[:, None]
    second_axis = jnp.sin(polar)[None, :] * jnp.sin(azimuth)[:, None]
    third_axis = jnp.cos(polar)[None, :] * jnp.ones_like(azimuth)[:, None]
    first_sign = (1 - 2 * (octant % 2)).astype(jnp.float32)
    second_sign = (1 - 2 * (octant // 2 % 2)).astype(jnp.float32)
    third_sign = (1 - 2 * (octant // 4)).astype(jnp.float32)
    phase_angle = phase_scale * (
        first_sign[:, None, None] * first_axis[None]
        + second_sign[:, None, None] * second_axis[None]
        + third_sign[:, None, None] * third_axis[None]
    )
    return (jnp.cos(phase_angle), jnp.sin(phase_angle))


def translate(sources, table, partner_src, partner_off, partner_count):
    live_mask = (
        jnp.arange(partner_src.shape[1], dtype=jnp.int32)[None, :] < partner_count[:, None]
    ).astype(jnp.float32)
    picked = sources[partner_src]
    operator = table[partner_off].astype(jnp.float32) * live_mask[:, :, None, None]
    real_part = jnp.sum(
        operator[:, :, 0] * picked[:, :, 0] - operator[:, :, 1] * picked[:, :, 1], axis=1
    )
    imaginary = jnp.sum(
        operator[:, :, 0] * picked[:, :, 1] + operator[:, :, 1] * picked[:, :, 0], axis=1
    )
    return jnp.stack([real_part, imaginary], axis=1)


def forward_shift(patterns, cosine, sine_part):
    real_part = patterns[:, 0] * cosine - patterns[:, 1] * sine_part
    imaginary = patterns[:, 0] * sine_part + patterns[:, 1] * cosine
    return jnp.stack([real_part, imaginary], axis=1)


def conjugate_shift(patterns, cosine, sine_part):
    real_part = patterns[:, 0] * cosine + patterns[:, 1] * sine_part
    imaginary = patterns[:, 1] * cosine - patterns[:, 0] * sine_part
    return jnp.stack([real_part, imaginary], axis=1)


def on_device_gather(
    child_patterns, trans_table, child_parent, child_octant, partner_src, partner_off, partner_count
):
    _, _, azimuth_in, _ = child_patterns.shape
    polar_out = NTHETA_P
    azimuth_out = trans_table.shape[2] // polar_out
    parent_slots = partner_src.shape[0] // lax.axis_size("clus")
    cluster_index = lax.axis_index("clus")
    direction_index = lax.axis_index("dir")
    parents = child_parent[0]
    polar_matrix = polar_matrix_of(NTHETA_P, NTHETA_C)
    onehot = (parents[None, :] == jnp.arange(parent_slots, dtype=jnp.int32)[:, None]).astype(
        jnp.float32
    )
    own_rows = jnp.mod(
        direction_index * azimuth_out + jnp.arange(azimuth_out, dtype=jnp.int32), NPHI_P
    )
    cosine, sine_part = shift_phases(child_octant, own_rows, NPHI_P, polar_out)
    extended = with_halo(child_patterns, (("dir", 2),), 2)
    gather_matrix = azimuth_matrix_of(
        jnp.arange(azimuth_out, dtype=jnp.int32),
        jnp.arange(azimuth_in + 4, dtype=jnp.int32) - 2,
        NPHI_P,
        NPHI_C,
    )
    along_azimuth = jnp.einsum("pc,kacz->kapz", gather_matrix, extended, precision=highest)
    refined = jnp.einsum("kapz,tz->kapt", along_azimuth, polar_matrix, precision=highest)
    shifted = forward_shift(refined, cosine, sine_part)
    radiation = jnp.einsum("gk,kapt->gapt", onehot, shifted, precision=highest)
    flattened = radiation.reshape(parent_slots, 2, azimuth_out * polar_out)
    sources = lax.all_gather(flattened, "clus", axis=0, tiled=True)
    first_row = cluster_index * parent_slots
    own_src = lax.dynamic_slice_in_dim(partner_src, first_row, parent_slots, 0)
    own_off = lax.dynamic_slice_in_dim(partner_off, first_row, parent_slots, 0)
    own_count = lax.dynamic_slice_in_dim(partner_count, first_row, parent_slots, 0)
    incoming = translate(sources, trans_table, own_src, own_off, own_count)
    incoming = incoming.reshape(parent_slots, 2, azimuth_out, polar_out)
    return_matrix = azimuth_matrix_of(
        jnp.arange(azimuth_out + 6, dtype=jnp.int32) - 3,
        jnp.arange(azimuth_in, dtype=jnp.int32),
        NPHI_P,
        NPHI_C,
    )
    per_child = jnp.einsum("gk,gapt->kapt", onehot, incoming, precision=highest)
    returned = conjugate_shift(per_child, cosine, sine_part)
    coarse_own = jnp.einsum("kapt,tz->kapz", returned, polar_matrix, precision=highest)
    coarse = with_halo(coarse_own, (("dir", 2),), 3)
    return jnp.einsum("pc,kapz->kacz", return_matrix, coarse, precision=highest)


def solution(mesh):
    def on_device(child_patterns, trans_table, *rest):
        peers = lax.axis_size("clus")
        children, _, azimuth_in, polar_in = child_patterns.shape
        flat_rows = trans_table.shape[2] // LANES
        fits = (
            azimuth_in % (8 * PERIOD_C) == 0
            and polar_in == LANES
            and flat_rows * PERIOD_C == ROWS_PER_PERIOD * azimuth_in
            and flat_rows % peers == 0
            and peers & (peers - 1) == 0
            and peers > 2
            and lax.axis_size("dir") % 2 == 0
            and children % BLOCK == 0
        )
        plan = on_device_exchange if fits else on_device_gather
        return plan(child_patterns, trans_table, *rest)

    return jax.shard_map(
        on_device,
        mesh=mesh,
        in_specs=(
            P("clus", None, "dir", None),
            P(None, None, "dir"),
            P("clus", None),
            P("clus"),
            P(),
            P(),
            P(),
        ),
        out_specs=P("clus", None, "dir", None),
        check_vma=False,
    )
```

```python
import functools
import math

import jax
import jax.numpy as jnp
import numpy as np
from jax import lax
from jax.experimental import pallas as pl
from jax.experimental.pallas import tpu as pltpu
from jax.sharding import PartitionSpec as P


NTHETA_C = 128
NPHI_C = 256
NTHETA_P = 192
NPHI_P = 384

LANES = 128
PERIOD_P = 6
PERIOD_C = 4
ROWS_PER_PERIOD = PERIOD_P * NTHETA_P // LANES
GROUP = 8
TILE = 8
TOGETHER = 2
BLOCK = 2 * GROUP

phase_scale = 8.0 * math.pi
highest = lax.Precision.HIGHEST
f32 = jnp.float32
bf16 = jnp.bfloat16


def lagrange(offset):
    weights = []
    for anchor in range(5):
        factor = 1.0
        for neighbour in range(5):
            if neighbour != anchor:
                factor = factor * (offset - neighbour) / (anchor - neighbour)
        weights.append(factor)
    return weights


TAPS_A = [float(w) for w in lagrange(5.0 / 3.0)]
TAPS_B = [float(w) for w in lagrange(7.0 / 3.0)]


SUMS = [(TAPS_A[i] + TAPS_A[4 - i]) / 2 for i in range(2)]
DIFFS = [(TAPS_A[i] - TAPS_A[4 - i]) / 2 for i in range(2)]
CENTRE = TAPS_A[2]


def polar_matrix_np():
    target = (np.arange(NTHETA_P, dtype=np.float32) + np.float32(0.5)) * NTHETA_C / NTHETA_P - np.float32(0.5)
    start = np.clip(np.floor(target + 0.5).astype(np.int32) - 2, 0, NTHETA_C - 5)
    weights = lagrange((target - start).astype(np.float64))
    matrix = np.zeros((NTHETA_P, NTHETA_C), np.float64)
    for anchor in range(5):
        matrix[np.arange(NTHETA_P), start + anchor] += weights[anchor]
    return matrix.astype(np.float32)


def polar_blocks():
    matrix = polar_matrix_np().T
    even = np.zeros((NTHETA_C, 2 * LANES), np.float32)
    odd = np.zeros((NTHETA_C, 2 * LANES), np.float32)
    half = NTHETA_P - LANES
    even[:, :NTHETA_P] = matrix
    odd[:, :LANES] = matrix[:, half:]
    odd[:, 2 * LANES - half :] = matrix[:, :half]
    return even, odd


def split_np(matrix):
    high = matrix.astype(bf16)
    low = (matrix - high.astype(np.float32)).astype(bf16)
    return high, low


def split(values):
    high = values.astype(bf16)
    low = (values - high.astype(f32)).astype(bf16)
    return high, low


def dot(left, right):
    return jnp.dot(left, right, preferred_element_type=f32)


def spread_dot(values, matrix_ref, i):
    high, low = split(values)
    depth = values.shape[1]
    return dot(jnp.concatenate([high, low], axis=1), matrix_ref[i, : 2 * depth]) + dot(high, matrix_ref[i, 2 * depth :])


def gather_dot(high, low, matrix_ref, i):
    width = matrix_ref.shape[2] // 2
    both = dot(high, matrix_ref[i])
    return both[:, :width] + (both[:, width:] + dot(low, matrix_ref[i, :, :width]))


SIN_COEFFS = [(-1) ** k * math.pi ** (2 * k + 1) / math.factorial(2 * k + 1) for k in range(7)]
COS_COEFFS = [(-1) ** k * math.pi ** (2 * k) / math.factorial(2 * k) for k in range(7)]


def sincos_turns(turns):
    rest = turns - jnp.round(turns)
    square = rest * rest
    sine = jnp.full_like(square, SIN_COEFFS[-1])
    for coeff in SIN_COEFFS[-2::-1]:
        sine = sine * square + coeff
    sine = sine * rest
    cosine = jnp.full_like(square, COS_COEFFS[-1])
    for coeff in COS_COEFFS[-2::-1]:
        cosine = cosine * square + coeff
    return 2.0 * sine * cosine, 1.0 - 2.0 * sine * sine


def fill_phases(direction, out_ref):
    periods = out_ref.shape[3]
    lane = lax.broadcasted_iota(jnp.int32, (periods, LANES), 1)
    period = lax.broadcasted_iota(jnp.int32, (periods, LANES), 0)
    first = direction * (PERIOD_P * periods)

    def two_rows(r, carry):
        for i in range(3):
            position = lane + i * LANES
            second = (position >= NTHETA_P).astype(jnp.int32)
            polar_index = position - second * NTHETA_P
            azimuth_index = first + period * PERIOD_P + 2 * r + second
            sin_polar, cos_polar = sincos_turns((polar_index.astype(f32) + 0.5) / (2 * NTHETA_P))
            sin_azimuth, cos_azimuth = sincos_turns(azimuth_index.astype(f32) / NPHI_P)
            along_x = 4.0 * sin_polar * cos_azimuth
            along_y = 4.0 * sin_polar * sin_azimuth
            along_z = 4.0 * cos_polar
            w = 3 * r + i
            for octant in (0, 2, 4, 6):
                turns = along_x + along_y if octant % 4 == 0 else along_x - along_y
                turns = turns + along_z if octant < 4 else turns - along_z
                sine, cosine = sincos_turns(turns)
                out_ref[octant, 0, w] = cosine
                out_ref[octant, 1, w] = sine
                out_ref[7 - octant, 0, w] = cosine
                out_ref[7 - octant, 1, w] = -sine
        return carry

    lax.fori_loop(0, PERIOD_P // 2, two_rows, 0)


def edge_rows(periods):
    return [(w, 0) for w in (1, 2, 3, 4)] + [(w, periods - 1) for w in (6, 7, 8)]


def by_parity(even, odd):
    parity = lax.rem(lax.axis_index("dir"), 2)
    pl.when(parity == 0)(even)
    pl.when(parity == 1)(odd)


def from_sides(far_ref, near_ref):
    is_even = lax.rem(lax.axis_index("dir"), 2) == 0
    far, near = far_ref[...], near_ref[...]
    return jnp.where(is_even, far, near), jnp.where(is_even, near, far)


def rows_kernel(x_ref, far_ref, near_ref, sems):
    azimuth_in = x_ref.shape[1]

    def fill(first_ref, last_ref):
        ends = [(0, first_ref.at[0]), (1, first_ref.at[1]), (azimuth_in - 1, last_ref.at[0]), (azimuth_in - 1, last_ref.at[1])]
        copies = [pltpu.make_async_copy(x_ref.at[:, row, :], target, sems.at[i]) for i, (row, target) in enumerate(ends)]
        for copy in copies:
            copy.start()
        for copy in copies:
            copy.wait()

    by_parity(lambda: fill(far_ref, near_ref), lambda: fill(near_ref, far_ref))


def both_taps(rows):
    even = SUMS[0] * (rows[0] + rows[4]) + SUMS[1] * (rows[1] + rows[3]) + CENTRE * rows[2]
    odd = DIFFS[0] * (rows[0] - rows[4]) + DIFFS[1] * (rows[1] - rows[3])
    return even + odd, even - odd


def both_taps_transposed(first, second):
    total, difference = first + second, first - second
    outer = [SUMS[i] * total for i in range(2)]
    inner = [DIFFS[i] * difference for i in range(2)]
    return [outer[0] + inner[0], outer[1] + inner[1], CENTRE * total, outer[1] - inner[1], outer[0] - inner[0]]


def main_kernel(peers, parents_hbm, octants_hbm, x_hbm, table_ref, spread_hbm, *rest):
    phase_ref, edge_phase_ref, flat_ref, slice_ref = rest[:4]
    parents_ref, octants_ref, x_ref, spread_ref, az_e, az_o, res_e, res_o, acc, flat, sems = rest[4:]
    children = octants_ref.shape[0]
    periods = phase_ref.shape[3]
    azimuth_in = periods * PERIOD_C
    own = acc.shape[0]
    me = lax.axis_index("clus")
    share = ROWS_PER_PERIOD * periods // peers
    first_tile = me * (2 * share) // 8
    table_rows = pl.ds(pl.multiple_of(first_tile * 8, 8), slice_ref.shape[1])
    ends = (
        (octants_hbm, octants_ref),
        (parents_hbm, parents_ref),
        (x_hbm, x_ref),
        (spread_hbm, spread_ref),
        (table_ref.at[:, table_rows, :], slice_ref),
    )
    copies = [pltpu.make_async_copy(source, target, sems.at[i]) for i, (source, target) in enumerate(ends)]
    for copy in copies[:-1]:
        copy.start()
    fill_phases(lax.axis_index("dir"), phase_ref)
    acc[...] = jnp.zeros_like(acc)
    sublane = lax.broadcasted_iota(jnp.int32, (periods, LANES), 0)
    for e, (w, m) in enumerate(edge_rows(periods)):
        for octant in range(8):
            for i in range(2):
                edge_phase_ref[e, i, octant : octant + 1, :] = phase_ref[octant, i, w, m : m + 1, :]
    for copy in copies[:-1]:
        copy.wait()
    copies[-1].start()

    def azimuth(block):
        for kp in range(2 * BLOCK):
            start = pl.multiple_of((block * (2 * BLOCK) + kp) * azimuth_in, 8)
            x = [x_ref[pl.ds(start + u, periods, stride=PERIOD_C), :] for u in range(PERIOD_C)]
            left = jnp.where(sublane == 0, 0.0, pltpu.roll(x[3], 1, 0))
            right = [jnp.where(sublane == periods - 1, 0.0, pltpu.roll(x[i], periods - 1, 0)) for i in range(2)]
            lower = [left, x[0], x[1], x[2], x[3]]
            upper = [x[1], x[2], x[3], right[0], right[1]]
            rows = [x[0], *both_taps(lower), x[2], *both_taps(upper)]
            for r in range(3):
                base = (kp * 3 + r) * periods
                az_e[base : base + periods, :] = rows[2 * r]
                az_o[base : base + periods, :] = rows[2 * r + 1]

    def polar():
        res_e[...] = spread_dot(az_e[...], spread_ref, 0)
        res_o[...] = spread_dot(az_o[...], spread_ref, 1)

    def shift(block):
        for k in range(BLOCK):
            octant = octants_ref[block * BLOCK + k]
            parent = parents_ref[block * BLOCK + k]
            for r in range(3):
                parts = []
                for part in range(2):
                    rows = pl.ds(((2 * k + part) * 3 + r) * periods, periods)
                    middle = res_e[rows, LANES:] + res_o[rows, LANES:]
                    parts.append((res_e[rows, :LANES], middle, res_o[rows, :LANES]))
                for i in range(3):
                    w = 3 * r + i
                    real, imaginary = parts[0][i], parts[1][i]
                    cosine, sine = phase_ref[octant, 0, w], phase_ref[octant, 1, w]
                    acc[parent, 0, w] += real * cosine - imaginary * sine
                    acc[parent, 1, w] += real * sine + imaginary * cosine

    def one_block(block, carry):
        azimuth(block)
        polar()
        shift(block)
        return carry

    lax.fori_loop(0, children // BLOCK, one_block, 0)
    for gp in range(2 * own):
        for w in range(ROWS_PER_PERIOD):
            flat[pl.ds(gp * ROWS_PER_PERIOD * periods + w, periods, stride=ROWS_PER_PERIOD), :] = acc[gp // 2, gp % 2, w]
        for q in range(peers):
            source = gp * ROWS_PER_PERIOD * periods + q * share
            target = (q * 2 * own + gp) * share
            flat_ref[target : target + share, :] = flat[source : source + share, :]
    copies[-1].wait()


def one_hot(parents, own):
    index = lax.broadcasted_iota(jnp.int32, (own, parents.shape[1]), 0)
    return (index == parents).astype(f32)


def dot2(exact, values):
    exact = exact.astype(bf16)
    high, low = split(values)
    return dot(exact, high) + dot(exact, low)


def fix_kernel(
    peers, own, parents_ref, octants_ref, far_ref, near_ref, flat_ref, edge_phase_ref, spread_ref, *rest
):
    outs, (fixed,) = rest[:peers], rest[peers:]
    pairs = far_ref.shape[1]
    children = pairs // 2
    chunk_rows = outs[0].shape[0]
    share = chunk_rows // (2 * own)
    periods = share * peers // ROWS_PER_PERIOD
    fixed[...] = flat_ref[...]
    is_even = lax.rem(lax.axis_index("dir"), 2) == 0

    def by_part(ref, i):
        return jnp.concatenate([ref[i, pl.ds(part, children, stride=2), :] for part in range(2)], axis=0)

    far, near = ([by_part(ref, i) for i in range(2)] for ref in (far_ref, near_ref))
    left = jnp.where(is_even, far[0], near[0])
    right = [jnp.where(is_even, n, f) for f, n in zip(far, near)]
    a, b = TAPS_A, TAPS_B
    even = jnp.concatenate([b[0] * left, a[3] * right[0] + a[4] * right[1]], axis=0)
    odd = jnp.concatenate([a[0] * left, b[3] * right[0] + b[4] * right[1]], axis=0)
    even = spread_dot(even, spread_ref, 0)
    odd = spread_dot(odd, spread_ref, 1)
    first, last = slice(0, pairs), slice(pairs, 2 * pairs)
    low, high = slice(0, LANES), slice(LANES, 2 * LANES)
    refined = [
        odd[first, high],
        odd[first, low],
        even[first, low],
        even[first, high],
        even[last, low],
        even[last, high] + odd[last, high],
        odd[last, low],
    ]
    by_octant = jnp.concatenate([edge_phase_ref[e, i] for e in range(len(refined)) for i in range(2)], axis=1)
    phases = dot2(one_hot(octants_ref[...], 8).T, by_octant)
    shifted_rows = []
    for e, rows in enumerate(refined):
        real, imaginary = rows[:children], rows[children:]
        cosine, sine = (phases[:, (2 * e + i) * LANES : (2 * e + i + 1) * LANES] for i in range(2))
        shifted_rows.append(real * cosine - imaginary * sine)
        shifted_rows.append(real * sine + imaginary * cosine)
    summed = dot2(one_hot(parents_ref[...], own), jnp.concatenate(shifted_rows, axis=1))
    for e, (w, m) in enumerate(edge_rows(periods)):
        q, row = divmod(ROWS_PER_PERIOD * m + w, share)
        for part in range(2):
            rows = pl.ds(q * chunk_rows + part * share + row, own, stride=2 * share)
            column = (2 * e + part) * LANES
            fixed[rows, :] = fixed[rows, :] + summed[:, column : column + LANES]
    me = lax.axis_index("clus")
    for d in range(peers):
        start = pl.multiple_of((me ^ d) * chunk_rows, 8)
        outs[d][...] = fixed[pl.ds(start, chunk_rows), :]


def widen_kernel(peers, others, source_ref, offset_ref, count_ref, table_ref, chunk, placed_ref, real_sum, imag_sum, *rest):
    wide_ref, numbers_ref, listed, real_twice, imag_twice, sem = rest
    targets, partners = source_ref.shape
    offsets, frame, _ = table_ref.shape
    own = targets // peers
    share = chunk.shape[0] // (2 * own)
    me = lax.axis_index("clus")
    shape = (targets, targets)
    row, lane = (lax.broadcasted_iota(jnp.int32, shape, d) for d in range(2))
    count = jnp.sum(jnp.where(row == lane, count_ref[...], 0), axis=1, keepdims=True)
    number = jnp.full(shape, offsets, jnp.int32)
    for p in range(partners):
        here = (lane == source_ref[:, p : p + 1]) & (p < count)
        number = jnp.where(here, offset_ref[:, p : p + 1], number)
    numbers_ref[...] = number * frame
    copy = pltpu.make_async_copy(numbers_ref, listed, sem)
    copy.start()

    def some_offsets(i, carry):
        for j in range(4):
            wide_ref[pl.ds(pl.multiple_of((i * 4 + j) * frame, 8), frame), :] = table_ref[i * 4 + j].astype(f32)
        return carry

    whole_steps = offsets // 4
    lax.fori_loop(0, whole_steps, some_offsets, 0)
    for offset in range(whole_steps * 4, offsets):
        wide_ref[offset * frame : (offset + 1) * frame, :] = table_ref[offset].astype(f32)
    wide_ref[offsets * frame :, :] = jnp.zeros((frame, LANES), f32)
    doubled(chunk, real_twice, imag_twice, 0, own, share, frame, lax.rem(me * (2 * share), 8))
    copy.wait()

    def operator_of(target, device, g):
        first = listed[target, device * own + g]
        return wide_ref[pl.ds(pl.multiple_of(first, 8), frame), :]

    def own_sources(some, sums):
        return add_sources(sums, own, frame, lambda j, source: operator_of(some[j], me, source), real_twice, imag_twice)

    for_some_targets(targets, frame, own_sources, None, (real_sum, imag_sum))

    def other_sources(target, carry):
        for i, d in enumerate(others):
            for g in range(own):
                place = pl.multiple_of(((target * len(others) + i) * own + g) * frame, 8)
                placed_ref[pl.ds(place, frame), :] = operator_of(target, me ^ d, g)
        return carry

    lax.fori_loop(0, targets, other_sources, 0)


def doubled(chunk, real_twice, imag_twice, first, own, share, frame, skip):
    for g in range(own):
        for part, twice in enumerate((real_twice, imag_twice)):
            rows = chunk[(2 * g + part) * share : (2 * g + part + 1) * share, :]
            base = (first + g) * frame + skip
            twice[pl.ds(base, share, stride=2), :] = rows
            twice[pl.ds(base + 1, share, stride=2), :] = rows


def add_sources(sums, sources, frame, operators, real_twice, imag_twice):
    for source in range(sources):
        place = slice(source * frame, (source + 1) * frame)
        real, imaginary = real_twice[place, :], imag_twice[place, :]
        for i in range(len(sums)):
            operator = operators(i, source)
            sums[i] = (sums[i][0] + operator * real, sums[i][1] + operator * imaginary)
    return sums


def for_some_targets(targets, frame, add, before, after):
    def some_targets(i, carry):
        some = [i * TOGETHER + j for j in range(TOGETHER)]
        places = [pl.ds(pl.multiple_of(target * frame, 8), frame) for target in some]
        if before is None:
            sums = [(jnp.zeros((frame, LANES), f32),) * 2 for _ in some]
        else:
            sums = [tuple(ref[place, :] for ref in before) for place in places]
        for place, values in zip(places, add(some, sums)):
            for ref, value in zip(after, values):
                ref[place, :] = value
        return carry

    lax.fori_loop(0, targets // TOGETHER, some_targets, 0)


def placed(placed_ref, frame, others, own, masks):
    firsts = [others.index(d) * own for d in masks]

    def operator_of(target, source):
        place = target * (len(others) * own) + firsts[source // own] + source % own
        return placed_ref[pl.ds(pl.multiple_of(place * frame, 8), frame), :]

    return operator_of


def gather_kernel(peers, frame, others, masks, placed_ref, *rest):
    chunks, (real_before, imag_before, real_sum, imag_sum, real_twice, imag_twice) = rest[:-6], rest[-6:]
    me = lax.axis_index("clus")
    targets = real_sum.shape[0] // frame
    own = targets // peers
    share = chunks[0].shape[0] // (2 * own)
    skip = lax.rem(me * (2 * share), 8)
    for number, chunk in enumerate(chunks):
        doubled(chunk, real_twice, imag_twice, number * own, own, share, frame, skip)
    operator_of = placed(placed_ref, frame, others, own, masks)

    def add(some, sums):
        operators = lambda j, source: operator_of(some[j], source)
        return add_sources(sums, len(masks) * own, frame, operators, real_twice, imag_twice)

    for_some_targets(targets, frame, add, (real_before, imag_before), (real_sum, imag_sum))


def translate_kernel(frame, others, masks, targets, placed_ref, real_sum, imag_sum, *rest):
    prepare = len(rest) == len(masks) + len(targets) + 4
    chunks, rest = (rest[: len(masks)], rest[len(masks) :]) if prepare else ((), rest)
    real_twice, imag_twice = rest[:2]
    outs, (total_real, total_imag) = rest[-2 - len(targets) : -2], rest[-2:]
    me = lax.axis_index("clus")
    sources = real_twice.shape[0] // frame
    own = sources // len(masks)
    share = outs[0].shape[0] // (2 * own)
    skip = lax.rem(me * (2 * share), 8)
    for number, chunk in enumerate(chunks):
        doubled(chunk, real_twice, imag_twice, number * own, own, share, frame, skip)
    operator_of = placed(placed_ref, frame, others, own, masks)
    even, odd = pl.ds(skip, share, stride=2), pl.ds(skip + 1, share, stride=2)
    for out, d in zip(outs, targets):
        first = (me ^ d) * own

        def some_targets(i, carry):
            places = [i * TOGETHER + j for j in range(TOGETHER)]
            some = [first + g for g in places]
            rows = [pl.ds(pl.multiple_of(target * frame, 8), frame) for target in some]
            sums = [(real_sum[r, :], imag_sum[r, :]) for r in rows]
            operators = lambda j, source: operator_of(some[j], source)
            sums = add_sources(sums, sources, frame, operators, real_twice, imag_twice)
            for j, (g, (by_real, by_imag)) in enumerate(zip(places, sums)):
                total_real[j] = by_real
                total_imag[j] = by_imag
                row = g * (2 * share)
                out[pl.ds(row, share), :] = total_real[j, even, :] - total_imag[j, odd, :]
                out[pl.ds(row + share, share), :] = total_real[j, odd, :] + total_imag[j, even, :]
            return carry

        lax.fori_loop(0, own // TOGETHER, some_targets, 0)


def extract_kernel(peers, own2, *rest):
    chunks = rest[:peers]
    flat, far_ref, near_ref = rest[peers:]
    share = chunks[0].shape[0] // own2
    periods = share * peers // ROWS_PER_PERIOD
    own = own2 // 2
    flat_rows = ROWS_PER_PERIOD * periods
    me = lax.axis_index("clus")
    for gp in range(own2):
        for d in range(peers):
            flat[pl.ds(gp * flat_rows + (me ^ d) * share, share), :] = chunks[d][gp * share : (gp + 1) * share, :]

    def fill(prev_ref, next_ref):
        for ref in (prev_ref, next_ref):
            ref[...] = jnp.zeros_like(ref)
        places = [(prev_ref, e) for e in range(4)] + [(next_ref, e) for e in range(3)]
        for (ref, e), (w, m) in zip(places, edge_rows(periods)):
            for part in range(2):
                first = part * flat_rows + ROWS_PER_PERIOD * m + w
                row = (2 * e + part) * own
                ref[row : row + own, :] = flat[pl.ds(first, own, stride=2 * flat_rows), :]

    by_parity(lambda: fill(far_ref, near_ref), lambda: fill(near_ref, far_ref))


def neighbour_kernel(periods, octants_hbm, out_ref, by_octant, octants_ref, sem):
    copy = pltpu.make_async_copy(octants_hbm, octants_ref, sem)
    copy.start()
    here = lax.axis_index("dir")
    octant = lax.broadcasted_iota(jnp.int32, (8, LANES), 0)
    lane = lax.broadcasted_iota(jnp.int32, (8, LANES), 1)
    signs = [(1 - 2 * ((octant >> bit) & 1)).astype(f32) for bit in range(3)]
    for e, (w, m) in enumerate(edge_rows(periods)):
        place = here + 1 if m == 0 else here - 1
        position = lane + w * LANES
        row = w * LANES // NTHETA_P
        row = jnp.where(position >= (row + 1) * NTHETA_P, row + 1, row)
        polar_index = position - row * NTHETA_P
        azimuth_index = (place * periods + m) * PERIOD_P + row
        sin_polar, cos_polar = sincos_turns((polar_index.astype(f32) + 0.5) / (2 * NTHETA_P))
        sin_azimuth, cos_azimuth = sincos_turns(azimuth_index.astype(f32) / NPHI_P)
        along = (sin_polar * cos_azimuth, sin_polar * sin_azimuth, cos_polar)
        sine, cosine = sincos_turns(4.0 * (signs[0] * along[0] + signs[1] * along[1] + signs[2] * along[2]))
        by_octant[e, 0] = cosine
        by_octant[e, 1] = sine
    copy.wait()

    def some_children(step, carry):
        for j in range(GROUP):
            k = step * GROUP + j
            for e in range(by_octant.shape[0]):
                for i in range(2):
                    out_ref[e, i, pl.ds(k, 1), :] = by_octant[e, i, pl.ds(octants_ref[k], 1), :]
        return carry

    lax.fori_loop(0, octants_ref.shape[0] // GROUP, some_children, 0)


def edge_contributions(parents, phase_ref, gather_ref, above, below):
    children = parents.shape[1]
    own = below.shape[0] // 8
    rows = [above[2 * e * own : 2 * (e + 1) * own] for e in range(4)] + [below[2 * e * own : 2 * (e + 1) * own] for e in range(3)]
    edges = jnp.concatenate([r[part * own : (part + 1) * own] for r in rows for part in range(2)], axis=1)
    per_child = dot2(one_hot(parents, own).T, edges)
    returned = []
    for e in range(len(rows)):
        real = per_child[:, 2 * e * LANES : (2 * e + 1) * LANES]
        imaginary = per_child[:, (2 * e + 1) * LANES : (2 * e + 2) * LANES]
        cosine, sine = phase_ref[e, 0], phase_ref[e, 1]
        returned.append(
            jnp.concatenate([real * cosine + imaginary * sine, imaginary * cosine - real * sine], axis=0)
        )
    join = functools.partial(jnp.concatenate, axis=1)
    even = jnp.concatenate([join([returned[2], returned[3]]), join([returned[4], returned[5]])], axis=0)
    odd = jnp.concatenate([join([returned[0], returned[1]]), join([returned[5], returned[6]])], axis=0)
    even = gather_dot(*split(even), gather_ref, 0)
    odd = gather_dot(*split(odd), gather_ref, 1)
    a, b = TAPS_A, TAPS_B
    pairs = 2 * children
    last = a[0] * odd[:pairs] + b[0] * even[:pairs]
    first = [a[3 + i] * even[pairs:] + b[3 + i] * odd[pairs:] for i in range(2)]
    return first, last


def disaggregate_kernel(
    parents_ref, octants_ref, flat_ref, phase_ref, gather_ref, out_ref, edge_ref, listed, incoming_ref, lhs, coarse_e, coarse_o, whole_out, sems
):
    periods = incoming_ref.shape[2]
    packed = parents_ref[...] * 8 + octants_ref[...]
    for k in range(listed.shape[0]):
        listed[k] = packed[0, k]
    for gp in range(incoming_ref.shape[0]):
        for w in range(ROWS_PER_PERIOD):
            first = gp * ROWS_PER_PERIOD * periods + w
            incoming_ref[gp, w] = flat_ref[pl.ds(first, periods, stride=ROWS_PER_PERIOD), :]
    azimuth_in = periods * PERIOD_C
    sublane = lax.broadcasted_iota(jnp.int32, (periods, LANES), 0)
    inner = pl.ds(TILE, azimuth_in - 2 * TILE)

    def shift(block):
        for k in range(BLOCK):
            code = listed[block * BLOCK + k]
            octant, parent = code & 7, code >> 3
            for r in range(3):
                for i in range(3):
                    w = 3 * r + i
                    real, imaginary = incoming_ref[2 * parent, w], incoming_ref[2 * parent + 1, w]
                    cosine, sine = phase_ref[octant, 0, w], phase_ref[octant, 1, w]
                    returned = (real * cosine + imaginary * sine, imaginary * cosine - real * sine)
                    for part in range(2):
                        base = ((2 * k + part) * 3 + r) * periods
                        lhs[base : base + periods, i * LANES : (i + 1) * LANES] = returned[part]

    def polar():
        high, low = split(lhs[...])
        coarse_e[...] = gather_dot(high[:, : 2 * LANES], low[:, : 2 * LANES], gather_ref, 0)
        coarse_o[...] = gather_dot(high[:, LANES:], low[:, LANES:], gather_ref, 1)

    def azimuth(block):
        for j in range(2 * BLOCK):
            c = []
            for r in range(3):
                base = (j * 3 + r) * periods
                c.append(coarse_e[base : base + periods, :])
                c.append(coarse_o[base : base + periods, :])
            lower = both_taps_transposed(c[1], c[2])
            upper = both_taps_transposed(c[4], c[5])
            down = [jnp.where(sublane == 0, 0.0, pltpu.roll(upper[i], 1, 0)) for i in (3, 4)]
            up = jnp.where(sublane == periods - 1, 0.0, pltpu.roll(lower[0], periods - 1, 0))
            rows = [c[0] + lower[1] + down[0], lower[2] + upper[0] + down[1], c[3] + lower[3] + upper[1], lower[4] + upper[2] + up]
            kp = block * (2 * BLOCK) + j
            for u in range(PERIOD_C):
                whole_out[kp, pl.ds(u, periods, stride=PERIOD_C), :] = rows[u]
            edge_ref[0, kp] = whole_out[kp, :TILE, :]
            edge_ref[1, kp] = whole_out[kp, azimuth_in - TILE :, :]

    def written(block):
        some = pl.ds(block * (2 * BLOCK), 2 * BLOCK)
        return pltpu.make_async_copy(whole_out.at[some, inner, :], out_ref.at[some, inner, :], sems.at[block])

    def one_block(block, carry):
        shift(block)
        polar()
        azimuth(block)
        written(block).start()
        return carry

    blocks = listed.shape[0] // BLOCK
    lax.fori_loop(0, blocks, one_block, 0)
    for block in range(blocks):
        written(block).wait()


def finish_kernel(parents_ref, phase_ref, gather_ref, edge_ref, far_ref, near_ref, part_ref, out_ref, tiles, sems):
    pairs, azimuth_in, _ = out_ref.shape
    tiles[...] = edge_ref[...]
    flat = tiles.reshape(2 * pairs * TILE, LANES)
    below, above = from_sides(far_ref, near_ref)
    heads, tail = edge_contributions(parents_ref[...], phase_ref, gather_ref, above, below)
    ends = ((0, 0, heads[0]), (0, 1, heads[1]), (1, TILE - 1, tail))
    copies = []
    for i, start in enumerate((0, azimuth_in - TILE)):
        for end, row, values in ends:
            if end == i:
                for part in range(2):
                    for k in range(0, pairs // 2, 8):
                        source = slice(part * (pairs // 2) + k, part * (pairs // 2) + k + 8)
                        rows = pl.ds((i * pairs + 2 * k + part) * TILE + row, 8, stride=2 * TILE)
                        flat[rows, :] = flat[rows, :] + values[source]
        copy = pltpu.make_async_copy(tiles.at[i], out_ref.at[:, pl.ds(start, TILE), :], sems.at[i])
        copy.start()
        copies.append(copy)
    for copy in copies:
        copy.wait()


def swapped(values, axis, first):
    size = lax.axis_size(axis)
    return lax.ppermute(values, axis, [(i, (((i - first) ^ 1) + first) % size) for i in range(size)])


def exchanged(values, axis, mask):
    size = lax.axis_size(axis)
    return lax.ppermute(values, axis, [(i, i ^ mask) for i in range(size)])


SMEM = pl.BlockSpec(memory_space=pltpu.SMEM)
VMEM = pl.BlockSpec(memory_space=pltpu.VMEM)
HBM = pl.BlockSpec(memory_space=pltpu.HBM)


def in_hbm(values):
    return pltpu.with_memory_space_constraint(values, pltpu.HBM)


def local_call(kernel, out_shape, in_specs, scratch, grant, flops=1_000_000, bytes_accessed=1_000_000, out_specs=None, aliases={}):
    return pl.pallas_call(
        kernel,
        out_shape=out_shape,
        in_specs=in_specs,
        out_specs=jax.tree.map(lambda _: VMEM, out_shape) if out_specs is None else out_specs,
        scratch_shapes=scratch,
        input_output_aliases=aliases,
        compiler_params=pltpu.CompilerParams(vmem_limit_bytes=grant << 20),
        cost_estimate=pl.CostEstimate(flops=flops, bytes_accessed=bytes_accessed, transcendentals=0),
    )


def on_device_exchange(
    child_patterns, trans_table, child_parent, child_octant, partner_src, partner_off, partner_count
):
    children, _, azimuth_in, polar_in = child_patterns.shape
    pairs = 2 * children
    peers = lax.axis_size("clus")
    parent_total, _ = partner_src.shape
    own = parent_total // peers
    periods = azimuth_in // PERIOD_C
    flat_rows = ROWS_PER_PERIOD * periods
    share = flat_rows // peers
    offsets = trans_table.shape[0]
    array = lambda *shape: jax.ShapeDtypeStruct(shape, f32)
    buffer = lambda *shape: pltpu.VMEM(shape, f32)
    edges = len(edge_rows(periods))
    even, odd = polar_blocks()
    spread = jnp.asarray(np.stack([np.concatenate([h, h, l]) for h, l in (split_np(even), split_np(odd))]))
    edge = array(2, pairs, polar_in)
    to_far, to_near = local_call(
        rows_kernel, [edge, edge], [HBM], [pltpu.SemaphoreType.DMA((4,))], 8
    )(in_hbm(child_patterns.reshape(pairs, azimuth_in, polar_in)))
    from_far = swapped(to_far, "dir", 1)
    from_near = swapped(to_near, "dir", 0)
    odd_gather = np.concatenate([odd.T[LANES:], odd.T[:LANES]])
    gather = np.stack([np.concatenate(split_np(m), axis=1) for m in (even.T, odd_gather)])

    frame = max(-(-((q * 2 * share) % 8 + 2 * share) // 8) * 8 for q in range(peers))
    view = trans_table.reshape(offsets, 2, flat_rows, LANES).transpose(0, 2, 1, 3).reshape(offsets, 2 * flat_rows, LANES)
    blocks = children // BLOCK
    rows = 2 * BLOCK * 3 * periods
    phases, edge_phases, flat, table = local_call(
        functools.partial(main_kernel, peers),
        [
            array(8, 2, ROWS_PER_PERIOD, periods, LANES),
            array(edges, 2, 8, LANES),
            array(2 * own * flat_rows, LANES),
            jax.ShapeDtypeStruct((offsets, frame, LANES), bf16),
        ],
        [HBM] * 5,
        [
            pltpu.SMEM((children,), jnp.int32),
            pltpu.SMEM((children,), jnp.int32),
            buffer(pairs * azimuth_in, polar_in),
            pltpu.VMEM(spread.shape, bf16),
            buffer(rows, LANES),
            buffer(rows, LANES),
            buffer(rows, 2 * LANES),
            buffer(rows, 2 * LANES),
            buffer(own, 2, ROWS_PER_PERIOD, periods, LANES),
            buffer(2 * own * flat_rows, LANES),
            pltpu.SemaphoreType.DMA((5,)),
        ],
        24,
        flops=4_000_000_000,
        bytes_accessed=12_000_000,
    )(
        in_hbm(child_parent[0]),
        in_hbm(child_octant),
        in_hbm(child_patterns.reshape(pairs * azimuth_in, polar_in)),
        in_hbm(view),
        in_hbm(spread),
    )

    chunk = array(2 * own * share, LANES)
    sent = local_call(
        functools.partial(fix_kernel, peers, own), [chunk] * peers, [VMEM] * 7, [buffer(2 * own * flat_rows, LANES)], 8
    )(child_parent, child_octant.reshape(1, children), from_far, from_near, flat, edge_phases, spread)

    masks = sorted(range(1, peers), key=lambda d: bin(d).count("1"))
    early, late = masks[:1], masks[1:]
    received = {0: sent[0]}
    for d in early:
        received[d] = exchanged(sent[d], "clus", d)
    for d in late:
        received[d] = exchanged(sent[d], "clus", d)

    sum_pair = [array(parent_total * frame, LANES)] * 2
    others = tuple(early + late)
    operators, *sums = local_call(
        functools.partial(widen_kernel, peers, others),
        [array(parent_total * len(others) * own * frame, LANES)] + sum_pair,
        [VMEM] * 5,
        [
            buffer((offsets + 1) * frame, LANES),
            pltpu.VMEM((parent_total, parent_total), jnp.int32),
            pltpu.SMEM((parent_total, parent_total), jnp.int32),
            buffer(own * frame, LANES),
            buffer(own * frame, LANES),
            pltpu.SemaphoreType.DMA,
        ],
        20,
        flops=90_000_000,
        bytes_accessed=12_000_000,
    )(partner_src, partner_off, partner_count.reshape(1, parent_total), table, received[0])

    sums = local_call(
        functools.partial(gather_kernel, peers, frame, others, tuple(early)),
        sum_pair,
        [VMEM] * (3 + len(early)),
        [buffer(len(early) * own * frame, LANES)] * 2,
        12,
        flops=60_000_000,
        bytes_accessed=12_000_000,
    )(operators, *[received[d] for d in early], *sums)

    back = {}
    last_sources = [received[d] for d in late]
    for number, targets in enumerate((masks[-1:], masks[:-1], [0])):
        prepare = number == 0
        results = local_call(
            functools.partial(translate_kernel, frame, others, tuple(late), tuple(targets)),
            ([array(len(late) * own * frame, LANES)] * 2 if prepare else []) + [chunk] * len(targets),
            [VMEM] * (3 + len(last_sources)),
            [buffer(TOGETHER, frame, LANES)] * 2,
            20,
            flops=10_000_000 * len(targets),
            bytes_accessed=2_000_000 * len(targets),
        )(operators, *sums, *last_sources)
        if prepare:
            last_sources, results = results[:2], results[2:]
        for d, result in zip(targets, results):
            back[d] = exchanged(result, "clus", d) if d else result

    neighbour_phases = local_call(
        functools.partial(neighbour_kernel, periods),
        array(edges, 2, children, LANES),
        [HBM],
        [buffer(edges, 2, 8, LANES), pltpu.SMEM((children,), jnp.int32), pltpu.SemaphoreType.DMA],
        8,
        flops=20_000_000,
    )(in_hbm(child_octant))

    side = array(8 * own, LANES)
    incoming, to_far, to_near = local_call(
        functools.partial(extract_kernel, peers, 2 * own),
        [array(2 * own * flat_rows, LANES), side, side],
        [VMEM] * peers,
        [],
        8,
    )(*[back[d] for d in range(peers)])

    from_far = swapped(to_far, "dir", 1)
    from_near = swapped(to_near, "dir", 0)

    inner, edge_tiles = local_call(
        disaggregate_kernel,
        [array(pairs, azimuth_in, polar_in), array(2, pairs, TILE, polar_in)],
        [VMEM] * 5,
        [
            pltpu.SMEM((children,), jnp.int32),
            buffer(2 * own, ROWS_PER_PERIOD, periods, LANES),
            buffer(rows, 3 * LANES),
            buffer(rows, LANES),
            buffer(rows, LANES),
            buffer(pairs, azimuth_in, polar_in),
            pltpu.SemaphoreType.DMA((blocks,)),
        ],
        24,
        flops=4_000_000_000,
        bytes_accessed=12_000_000,
        out_specs=[HBM, VMEM],
    )(child_parent, child_octant.reshape(1, children), incoming, phases, gather)

    out = local_call(
        finish_kernel,
        array(pairs, azimuth_in, polar_in),
        [VMEM] * 6 + [HBM],
        [buffer(2, pairs, TILE, polar_in), pltpu.SemaphoreType.DMA((2,))],
        8,
        out_specs=HBM,
        aliases={6: 0},
    )(child_parent, neighbour_phases, gather, edge_tiles, from_far, from_near, in_hbm(inner))
    return out.reshape(child_patterns.shape)


def with_halo(shard, sides, width):
    for axis, dim in sides:
        size, length = (lax.axis_size(axis), shard.shape[dim])
        up = [(i, (i + 1) % size) for i in range(size)]
        down = [(j, i) for i, j in up]
        last = lax.slice_in_dim(shard, length - width, length, axis=dim)
        initial = lax.slice_in_dim(shard, 0, width, axis=dim)
        before = lax.ppermute(last, axis, up)
        after = lax.ppermute(initial, axis, down)
        shard = jnp.concatenate([before, shard, after], axis=dim)
    return shard


def lagrange_rows(offset):
    weights = []
    for anchor in range(5):
        factor = jnp.ones_like(offset)
        for neighbour in range(5):
            if neighbour != anchor:
                factor = factor * (offset - neighbour) / (anchor - neighbour)
        weights.append(factor)
    return weights


def polar_matrix_of(rows_out, rows_in):
    target = (jnp.arange(rows_out, dtype=jnp.float32) + 0.5) * rows_in / rows_out - 0.5
    start_row = jnp.clip(jnp.floor(target + 0.5).astype(jnp.int32) - 2, 0, rows_in - 5)
    weights = lagrange_rows(target - start_row.astype(jnp.float32))
    columns = jnp.arange(rows_in, dtype=jnp.int32)
    matrix = jnp.zeros((rows_out, rows_in), jnp.float32)
    for anchor in range(5):
        matrix = matrix + jnp.where(
            columns[None, :] == (start_row + anchor)[:, None], weights[anchor][:, None], 0.0
        )
    return matrix


def azimuth_matrix_of(out_index, in_index, total_out, total_in):
    target = (out_index * total_in).astype(jnp.float32) / total_out
    nearest = jnp.floor(target + 0.5).astype(jnp.int32)
    weights = lagrange_rows(target - nearest.astype(jnp.float32) + 2.0)
    matrix = jnp.zeros((out_index.shape[0], in_index.shape[0]), jnp.float32)
    for anchor in range(5):
        columns = nearest + anchor - 2
        matrix = matrix + jnp.where(
            in_index[None, :] == columns[:, None], weights[anchor][:, None], 0.0
        )
    return matrix


def shift_phases(octant, azimuth_index, azimuth_total, polar_total):
    azimuth = 2.0 * math.pi * azimuth_index.astype(jnp.float32) / azimuth_total
    polar = math.pi * (jnp.arange(polar_total, dtype=jnp.float32) + 0.5) / polar_total
    first_axis = jnp.sin(polar)[None, :] * jnp.cos(azimuth)[:, None]
    second_axis = jnp.sin(polar)[None, :] * jnp.sin(azimuth)[:, None]
    third_axis = jnp.cos(polar)[None, :] * jnp.ones_like(azimuth)[:, None]
    first_sign = (1 - 2 * (octant % 2)).astype(jnp.float32)
    second_sign = (1 - 2 * (octant // 2 % 2)).astype(jnp.float32)
    third_sign = (1 - 2 * (octant // 4)).astype(jnp.float32)
    phase_angle = phase_scale * (
        first_sign[:, None, None] * first_axis[None]
        + second_sign[:, None, None] * second_axis[None]
        + third_sign[:, None, None] * third_axis[None]
    )
    return (jnp.cos(phase_angle), jnp.sin(phase_angle))


def translate(sources, table, partner_src, partner_off, partner_count):
    live_mask = (
        jnp.arange(partner_src.shape[1], dtype=jnp.int32)[None, :] < partner_count[:, None]
    ).astype(jnp.float32)
    picked = sources[partner_src]
    operator = table[partner_off].astype(jnp.float32) * live_mask[:, :, None, None]
    real_part = jnp.sum(
        operator[:, :, 0] * picked[:, :, 0] - operator[:, :, 1] * picked[:, :, 1], axis=1
    )
    imaginary = jnp.sum(
        operator[:, :, 0] * picked[:, :, 1] + operator[:, :, 1] * picked[:, :, 0], axis=1
    )
    return jnp.stack([real_part, imaginary], axis=1)


def forward_shift(patterns, cosine, sine_part):
    real_part = patterns[:, 0] * cosine - patterns[:, 1] * sine_part
    imaginary = patterns[:, 0] * sine_part + patterns[:, 1] * cosine
    return jnp.stack([real_part, imaginary], axis=1)


def conjugate_shift(patterns, cosine, sine_part):
    real_part = patterns[:, 0] * cosine + patterns[:, 1] * sine_part
    imaginary = patterns[:, 1] * cosine - patterns[:, 0] * sine_part
    return jnp.stack([real_part, imaginary], axis=1)


def on_device_gather(
    child_patterns, trans_table, child_parent, child_octant, partner_src, partner_off, partner_count
):
    _, _, azimuth_in, _ = child_patterns.shape
    polar_out = NTHETA_P
    azimuth_out = trans_table.shape[2] // polar_out
    parent_slots = partner_src.shape[0] // lax.axis_size("clus")
    cluster_index = lax.axis_index("clus")
    direction_index = lax.axis_index("dir")
    parents = child_parent[0]
    polar_matrix = polar_matrix_of(NTHETA_P, NTHETA_C)
    onehot = (parents[None, :] == jnp.arange(parent_slots, dtype=jnp.int32)[:, None]).astype(
        jnp.float32
    )
    own_rows = jnp.mod(
        direction_index * azimuth_out + jnp.arange(azimuth_out, dtype=jnp.int32), NPHI_P
    )
    cosine, sine_part = shift_phases(child_octant, own_rows, NPHI_P, polar_out)
    extended = with_halo(child_patterns, (("dir", 2),), 2)
    gather_matrix = azimuth_matrix_of(
        jnp.arange(azimuth_out, dtype=jnp.int32),
        jnp.arange(azimuth_in + 4, dtype=jnp.int32) - 2,
        NPHI_P,
        NPHI_C,
    )
    along_azimuth = jnp.einsum("pc,kacz->kapz", gather_matrix, extended, precision=highest)
    refined = jnp.einsum("kapz,tz->kapt", along_azimuth, polar_matrix, precision=highest)
    shifted = forward_shift(refined, cosine, sine_part)
    radiation = jnp.einsum("gk,kapt->gapt", onehot, shifted, precision=highest)
    flattened = radiation.reshape(parent_slots, 2, azimuth_out * polar_out)
    sources = lax.all_gather(flattened, "clus", axis=0, tiled=True)
    first_row = cluster_index * parent_slots
    own_src = lax.dynamic_slice_in_dim(partner_src, first_row, parent_slots, 0)
    own_off = lax.dynamic_slice_in_dim(partner_off, first_row, parent_slots, 0)
    own_count = lax.dynamic_slice_in_dim(partner_count, first_row, parent_slots, 0)
    incoming = translate(sources, trans_table, own_src, own_off, own_count)
    incoming = incoming.reshape(parent_slots, 2, azimuth_out, polar_out)
    return_matrix = azimuth_matrix_of(
        jnp.arange(azimuth_out + 6, dtype=jnp.int32) - 3,
        jnp.arange(azimuth_in, dtype=jnp.int32),
        NPHI_P,
        NPHI_C,
    )
    per_child = jnp.einsum("gk,gapt->kapt", onehot, incoming, precision=highest)
    returned = conjugate_shift(per_child, cosine, sine_part)
    coarse_own = jnp.einsum("kapt,tz->kapz", returned, polar_matrix, precision=highest)
    coarse = with_halo(coarse_own, (("dir", 2),), 3)
    return jnp.einsum("pc,kapz->kacz", return_matrix, coarse, precision=highest)


def solution(mesh):
    def on_device(child_patterns, trans_table, *rest):
        peers = lax.axis_size("clus")
        children, _, azimuth_in, polar_in = child_patterns.shape
        flat_rows = trans_table.shape[2] // LANES
        fits = (
            azimuth_in % (8 * PERIOD_C) == 0
            and polar_in == LANES
            and flat_rows * PERIOD_C == ROWS_PER_PERIOD * azimuth_in
            and flat_rows % peers == 0
            and peers & (peers - 1) == 0
            and peers > 2
            and lax.axis_size("dir") % 2 == 0
            and children % BLOCK == 0
        )
        plan = on_device_exchange if fits else on_device_gather
        return plan(child_patterns, trans_table, *rest)

    return jax.shard_map(
        on_device,
        mesh=mesh,
        in_specs=(
            P("clus", None, "dir", None),
            P(None, None, "dir"),
            P("clus", None),
            P("clus"),
            P(),
            P(),
            P(),
        ),
        out_specs=P("clus", None, "dir", None),
        check_vma=False,
    )
```

```python
import functools
import math

import jax
import jax.numpy as jnp
import numpy as np
from jax import lax
from jax.experimental import pallas as pl
from jax.experimental.pallas import tpu as pltpu
from jax.sharding import PartitionSpec as P


NTHETA_C = 128
NPHI_C = 256
NTHETA_P = 192
NPHI_P = 384

LANES = 128
PERIOD_P = 6
PERIOD_C = 4
ROWS_PER_PERIOD = PERIOD_P * NTHETA_P // LANES
GROUP = 8
TILE = 8
TOGETHER = 2
BLOCK = 2 * GROUP

phase_scale = 8.0 * math.pi
highest = lax.Precision.HIGHEST
f32 = jnp.float32
bf16 = jnp.bfloat16


def lagrange(offset):
    weights = []
    for anchor in range(5):
        factor = 1.0
        for neighbour in range(5):
            if neighbour != anchor:
                factor = factor * (offset - neighbour) / (anchor - neighbour)
        weights.append(factor)
    return weights


TAPS_A = [float(w) for w in lagrange(5.0 / 3.0)]
TAPS_B = [float(w) for w in lagrange(7.0 / 3.0)]


SUMS = [(TAPS_A[i] + TAPS_A[4 - i]) / 2 for i in range(2)]
DIFFS = [(TAPS_A[i] - TAPS_A[4 - i]) / 2 for i in range(2)]
CENTRE = TAPS_A[2]


def polar_matrix_np():
    target = (np.arange(NTHETA_P, dtype=np.float32) + np.float32(0.5)) * NTHETA_C / NTHETA_P - np.float32(0.5)
    start = np.clip(np.floor(target + 0.5).astype(np.int32) - 2, 0, NTHETA_C - 5)
    weights = lagrange((target - start).astype(np.float64))
    matrix = np.zeros((NTHETA_P, NTHETA_C), np.float64)
    for anchor in range(5):
        matrix[np.arange(NTHETA_P), start + anchor] += weights[anchor]
    return matrix.astype(np.float32)


def polar_blocks():
    matrix = polar_matrix_np().T
    even = np.zeros((NTHETA_C, 2 * LANES), np.float32)
    odd = np.zeros((NTHETA_C, 2 * LANES), np.float32)
    half = NTHETA_P - LANES
    even[:, :NTHETA_P] = matrix
    odd[:, :LANES] = matrix[:, half:]
    odd[:, 2 * LANES - half :] = matrix[:, :half]
    return even, odd


def split_np(matrix):
    high = matrix.astype(bf16)
    low = (matrix - high.astype(np.float32)).astype(bf16)
    return high, low


def split(values):
    high = values.astype(bf16)
    low = (values - high.astype(f32)).astype(bf16)
    return high, low


def dot(left, right):
    return jnp.dot(left, right, preferred_element_type=f32)


def spread_dot(values, matrix_ref, i):
    high, low = split(values)
    depth = values.shape[1]
    return dot(jnp.concatenate([high, low], axis=1), matrix_ref[i, : 2 * depth]) + dot(high, matrix_ref[i, 2 * depth :])


def gather_dot(high, low, matrix_ref, i):
    width = matrix_ref.shape[2] // 2
    both = dot(high, matrix_ref[i])
    return both[:, :width] + (both[:, width:] + dot(low, matrix_ref[i, :, :width]))


SIN_COEFFS = [(-1) ** k * math.pi ** (2 * k + 1) / math.factorial(2 * k + 1) for k in range(7)]
COS_COEFFS = [(-1) ** k * math.pi ** (2 * k) / math.factorial(2 * k) for k in range(7)]


def sincos_turns(turns):
    rest = turns - jnp.round(turns)
    square = rest * rest
    sine = jnp.full_like(square, SIN_COEFFS[-1])
    for coeff in SIN_COEFFS[-2::-1]:
        sine = sine * square + coeff
    sine = sine * rest
    cosine = jnp.full_like(square, COS_COEFFS[-1])
    for coeff in COS_COEFFS[-2::-1]:
        cosine = cosine * square + coeff
    return 2.0 * sine * cosine, 1.0 - 2.0 * sine * sine


def fill_phases(direction, out_ref):
    periods = out_ref.shape[3]
    lane = lax.broadcasted_iota(jnp.int32, (periods, LANES), 1)
    period = lax.broadcasted_iota(jnp.int32, (periods, LANES), 0)
    first = direction * (PERIOD_P * periods)

    def two_rows(r, carry):
        for i in range(3):
            position = lane + i * LANES
            second = (position >= NTHETA_P).astype(jnp.int32)
            polar_index = position - second * NTHETA_P
            azimuth_index = first + period * PERIOD_P + 2 * r + second
            sin_polar, cos_polar = sincos_turns((polar_index.astype(f32) + 0.5) / (2 * NTHETA_P))
            sin_azimuth, cos_azimuth = sincos_turns(azimuth_index.astype(f32) / NPHI_P)
            along_x = 4.0 * sin_polar * cos_azimuth
            along_y = 4.0 * sin_polar * sin_azimuth
            along_z = 4.0 * cos_polar
            w = 3 * r + i
            for octant in (0, 2, 4, 6):
                turns = along_x + along_y if octant % 4 == 0 else along_x - along_y
                turns = turns + along_z if octant < 4 else turns - along_z
                sine, cosine = sincos_turns(turns)
                out_ref[octant, 0, w] = cosine
                out_ref[octant, 1, w] = sine
                out_ref[7 - octant, 0, w] = cosine
                out_ref[7 - octant, 1, w] = -sine
        return carry

    lax.fori_loop(0, PERIOD_P // 2, two_rows, 0)


def edge_rows(periods):
    return [(w, 0) for w in (1, 2, 3, 4)] + [(w, periods - 1) for w in (6, 7, 8)]


def by_parity(even, odd):
    parity = lax.rem(lax.axis_index("dir"), 2)
    pl.when(parity == 0)(even)
    pl.when(parity == 1)(odd)


def from_sides(far_ref, near_ref):
    is_even = lax.rem(lax.axis_index("dir"), 2) == 0
    far, near = far_ref[...], near_ref[...]
    return jnp.where(is_even, far, near), jnp.where(is_even, near, far)


def rows_kernel(x_ref, far_ref, near_ref, sems):
    azimuth_in = x_ref.shape[1]

    def fill(first_ref, last_ref):
        ends = [(0, first_ref.at[0]), (1, first_ref.at[1]), (azimuth_in - 1, last_ref.at[0]), (azimuth_in - 1, last_ref.at[1])]
        copies = [pltpu.make_async_copy(x_ref.at[:, row, :], target, sems.at[i]) for i, (row, target) in enumerate(ends)]
        for copy in copies:
            copy.start()
        for copy in copies:
            copy.wait()

    by_parity(lambda: fill(far_ref, near_ref), lambda: fill(near_ref, far_ref))


def both_taps(rows):
    even = SUMS[0] * (rows[0] + rows[4]) + SUMS[1] * (rows[1] + rows[3]) + CENTRE * rows[2]
    odd = DIFFS[0] * (rows[0] - rows[4]) + DIFFS[1] * (rows[1] - rows[3])
    return even + odd, even - odd


def both_taps_transposed(first, second):
    total, difference = first + second, first - second
    outer = [SUMS[i] * total for i in range(2)]
    inner = [DIFFS[i] * difference for i in range(2)]
    return [outer[0] + inner[0], outer[1] + inner[1], CENTRE * total, outer[1] - inner[1], outer[0] - inner[0]]


def table_part(table_ref, first_row, first, target):
    rows = pl.ds(pl.multiple_of(first_row // 8 * 8, 8), target.shape[1])
    return table_ref.at[pl.ds(first, target.shape[0]), rows, :]


def main_kernel(peers, parents_hbm, octants_hbm, x_hbm, table_ref, spread_hbm, *rest):
    phase_ref, edge_phase_ref, flat_ref, slice_ref = rest[:4]
    parents_ref, octants_ref, x_ref, spread_ref, az_e, az_o, res_e, res_o, acc, flat, sems, x_sems = rest[4:]
    children = octants_ref.shape[0]
    periods = phase_ref.shape[3]
    azimuth_in = periods * PERIOD_C
    own = acc.shape[0]
    me = lax.axis_index("clus")
    share = ROWS_PER_PERIOD * periods // peers
    ends = (
        (octants_hbm, octants_ref),
        (parents_hbm, parents_ref),
        (spread_hbm, spread_ref),
        (table_part(table_ref, me * (2 * share), 0, slice_ref), slice_ref),
    )
    copies = [pltpu.make_async_copy(source, target, sems.at[i]) for i, (source, target) in enumerate(ends)]
    blocks = children // BLOCK
    block_rows = 2 * BLOCK * azimuth_in

    def x_copy(block):
        some = pl.ds(pl.multiple_of(block * block_rows, 8), block_rows)
        return pltpu.make_async_copy(x_hbm.at[some], x_ref.at[some], x_sems.at[block])

    for copy in copies[:-1]:
        copy.start()
    for block in range(blocks):
        x_copy(block).start()
    fill_phases(lax.axis_index("dir"), phase_ref)
    acc[...] = jnp.zeros_like(acc)
    sublane = lax.broadcasted_iota(jnp.int32, (periods, LANES), 0)
    for e, (w, m) in enumerate(edge_rows(periods)):
        for octant in range(8):
            for i in range(2):
                edge_phase_ref[e, i, octant : octant + 1, :] = phase_ref[octant, i, w, m : m + 1, :]
    for copy in copies[:-1]:
        copy.wait()
    copies[-1].start()

    def azimuth(block):
        for kp in range(2 * BLOCK):
            start = pl.multiple_of((block * (2 * BLOCK) + kp) * azimuth_in, 8)
            x = [x_ref[pl.ds(start + u, periods, stride=PERIOD_C), :] for u in range(PERIOD_C)]
            left = jnp.where(sublane == 0, 0.0, pltpu.roll(x[3], 1, 0))
            right = [jnp.where(sublane == periods - 1, 0.0, pltpu.roll(x[i], periods - 1, 0)) for i in range(2)]
            lower = [left, x[0], x[1], x[2], x[3]]
            upper = [x[1], x[2], x[3], right[0], right[1]]
            rows = [x[0], *both_taps(lower), x[2], *both_taps(upper)]
            for r in range(3):
                base = (kp * 3 + r) * periods
                az_e[base : base + periods, :] = rows[2 * r]
                az_o[base : base + periods, :] = rows[2 * r + 1]

    def polar():
        res_e[...] = spread_dot(az_e[...], spread_ref, 0)
        res_o[...] = spread_dot(az_o[...], spread_ref, 1)

    def shift(block):
        for k in range(BLOCK):
            octant = octants_ref[block * BLOCK + k]
            parent = parents_ref[block * BLOCK + k]
            for r in range(3):
                parts = []
                for part in range(2):
                    rows = pl.ds(((2 * k + part) * 3 + r) * periods, periods)
                    middle = res_e[rows, LANES:] + res_o[rows, LANES:]
                    parts.append((res_e[rows, :LANES], middle, res_o[rows, :LANES]))
                for i in range(3):
                    w = 3 * r + i
                    real, imaginary = parts[0][i], parts[1][i]
                    cosine, sine = phase_ref[octant, 0, w], phase_ref[octant, 1, w]
                    acc[parent, 0, w] += real * cosine - imaginary * sine
                    acc[parent, 1, w] += real * sine + imaginary * cosine

    def one_block(block, carry):
        x_copy(block).wait()
        azimuth(block)
        polar()
        shift(block)
        return carry

    lax.fori_loop(0, blocks, one_block, 0)
    for gp in range(2 * own):
        for w in range(ROWS_PER_PERIOD):
            flat[pl.ds(gp * ROWS_PER_PERIOD * periods + w, periods, stride=ROWS_PER_PERIOD), :] = acc[gp // 2, gp % 2, w]
        for q in range(peers):
            source = gp * ROWS_PER_PERIOD * periods + q * share
            target = (q * 2 * own + gp) * share
            flat_ref[target : target + share, :] = flat[source : source + share, :]
    copies[-1].wait()


def one_hot(parents, own):
    index = lax.broadcasted_iota(jnp.int32, (own, parents.shape[1]), 0)
    return (index == parents).astype(f32)


def dot2(exact, values):
    exact = exact.astype(bf16)
    high, low = split(values)
    return dot(exact, high) + dot(exact, low)


def fix_kernel(
    peers, own, parents_ref, octants_ref, far_ref, near_ref, flat_ref, edge_phase_ref, spread_ref, *rest
):
    outs, (fixed,) = rest[:peers], rest[peers:]
    pairs = far_ref.shape[1]
    children = pairs // 2
    chunk_rows = outs[0].shape[0]
    share = chunk_rows // (2 * own)
    periods = share * peers // ROWS_PER_PERIOD
    fixed[...] = flat_ref[...]
    is_even = lax.rem(lax.axis_index("dir"), 2) == 0

    def by_part(ref, i):
        return jnp.concatenate([ref[i, pl.ds(part, children, stride=2), :] for part in range(2)], axis=0)

    far, near = ([by_part(ref, i) for i in range(2)] for ref in (far_ref, near_ref))
    left = jnp.where(is_even, far[0], near[0])
    right = [jnp.where(is_even, n, f) for f, n in zip(far, near)]
    a, b = TAPS_A, TAPS_B
    even = jnp.concatenate([b[0] * left, a[3] * right[0] + a[4] * right[1]], axis=0)
    odd = jnp.concatenate([a[0] * left, b[3] * right[0] + b[4] * right[1]], axis=0)
    even = spread_dot(even, spread_ref, 0)
    odd = spread_dot(odd, spread_ref, 1)
    first, last = slice(0, pairs), slice(pairs, 2 * pairs)
    low, high = slice(0, LANES), slice(LANES, 2 * LANES)
    refined = [
        odd[first, high],
        odd[first, low],
        even[first, low],
        even[first, high],
        even[last, low],
        even[last, high] + odd[last, high],
        odd[last, low],
    ]
    by_octant = jnp.concatenate([edge_phase_ref[e, i] for e in range(len(refined)) for i in range(2)], axis=1)
    phases = dot2(one_hot(octants_ref[...], 8).T, by_octant)
    shifted_rows = []
    for e, rows in enumerate(refined):
        real, imaginary = rows[:children], rows[children:]
        cosine, sine = (phases[:, (2 * e + i) * LANES : (2 * e + i + 1) * LANES] for i in range(2))
        shifted_rows.append(real * cosine - imaginary * sine)
        shifted_rows.append(real * sine + imaginary * cosine)
    summed = dot2(one_hot(parents_ref[...], own), jnp.concatenate(shifted_rows, axis=1))
    for e, (w, m) in enumerate(edge_rows(periods)):
        q, row = divmod(ROWS_PER_PERIOD * m + w, share)
        for part in range(2):
            rows = pl.ds(q * chunk_rows + part * share + row, own, stride=2 * share)
            column = (2 * e + part) * LANES
            fixed[rows, :] = fixed[rows, :] + summed[:, column : column + LANES]
    me = lax.axis_index("clus")
    for d in range(peers):
        start = pl.multiple_of((me ^ d) * chunk_rows, 8)
        outs[d][...] = fixed[pl.ds(start, chunk_rows), :]


def widen_kernel(peers, others, source_ref, offset_ref, count_ref, head_ref, table_ref, chunk, placed_ref, real_sum, imag_sum, *rest):
    tail_ref, wide_ref, numbers_ref, listed, real_twice, imag_twice, sem, tail_sem = rest
    targets, partners = source_ref.shape
    half, frame, _ = head_ref.shape
    offsets = half + tail_ref.shape[0]
    own = targets // peers
    share = chunk.shape[0] // (2 * own)
    me = lax.axis_index("clus")
    tail_copy = pltpu.make_async_copy(table_part(table_ref, me * (2 * share), half, tail_ref), tail_ref, tail_sem)
    tail_copy.start()
    shape = (targets, targets)
    row, lane = (lax.broadcasted_iota(jnp.int32, shape, d) for d in range(2))
    count = jnp.sum(jnp.where(row == lane, count_ref[...], 0), axis=1, keepdims=True)
    number = jnp.full(shape, offsets, jnp.int32)
    for p in range(partners):
        here = (lane == source_ref[:, p : p + 1]) & (p < count)
        number = jnp.where(here, offset_ref[:, p : p + 1], number)
    numbers_ref[...] = number * frame
    copy = pltpu.make_async_copy(numbers_ref, listed, sem)
    copy.start()

    def widen(part_ref, first):
        def some_offsets(i, carry):
            for j in range(4):
                place = pl.multiple_of((first + i * 4 + j) * frame, 8)
                wide_ref[pl.ds(place, frame), :] = part_ref[i * 4 + j].astype(f32)
            return carry

        whole_steps = part_ref.shape[0] // 4
        lax.fori_loop(0, whole_steps, some_offsets, 0)
        for offset in range(whole_steps * 4, part_ref.shape[0]):
            wide_ref[(first + offset) * frame : (first + offset + 1) * frame, :] = part_ref[offset].astype(f32)

    widen(head_ref, 0)
    wide_ref[offsets * frame :, :] = jnp.zeros((frame, LANES), f32)
    doubled(chunk, real_twice, imag_twice, 0, own, share, frame, lax.rem(me * (2 * share), 8))
    copy.wait()
    tail_copy.wait()
    widen(tail_ref, half)

    def operator_of(target, device, g):
        first = listed[target, device * own + g]
        return wide_ref[pl.ds(pl.multiple_of(first, 8), frame), :]

    def own_sources(some, sums):
        return add_sources(sums, own, frame, lambda j, source: operator_of(some[j], me, source), real_twice, imag_twice)

    for_some_targets(targets, frame, own_sources, None, (real_sum, imag_sum))

    def other_sources(target, carry):
        for i, d in enumerate(others):
            for g in range(own):
                place = pl.multiple_of(((target * len(others) + i) * own + g) * frame, 8)
                placed_ref[pl.ds(place, frame), :] = operator_of(target, me ^ d, g)
        return carry

    lax.fori_loop(0, targets, other_sources, 0)


def doubled(chunk, real_twice, imag_twice, first, own, share, frame, skip):
    for g in range(own):
        for part, twice in enumerate((real_twice, imag_twice)):
            rows = chunk[(2 * g + part) * share : (2 * g + part + 1) * share, :]
            base = (first + g) * frame + skip
            twice[pl.ds(base, share, stride=2), :] = rows
            twice[pl.ds(base + 1, share, stride=2), :] = rows


def add_sources(sums, sources, frame, operators, real_twice, imag_twice):
    for source in range(sources):
        place = slice(source * frame, (source + 1) * frame)
        real, imaginary = real_twice[place, :], imag_twice[place, :]
        for i in range(len(sums)):
            operator = operators(i, source)
            sums[i] = (sums[i][0] + operator * real, sums[i][1] + operator * imaginary)
    return sums


def for_some_targets(targets, frame, add, before, after):
    def some_targets(i, carry):
        some = [i * TOGETHER + j for j in range(TOGETHER)]
        places = [pl.ds(pl.multiple_of(target * frame, 8), frame) for target in some]
        if before is None:
            sums = [(jnp.zeros((frame, LANES), f32),) * 2 for _ in some]
        else:
            sums = [tuple(ref[place, :] for ref in before) for place in places]
        for place, values in zip(places, add(some, sums)):
            for ref, value in zip(after, values):
                ref[place, :] = value
        return carry

    lax.fori_loop(0, targets // TOGETHER, some_targets, 0)


def placed(placed_ref, frame, others, own, masks):
    firsts = [others.index(d) * own for d in masks]

    def operator_of(target, source):
        place = target * (len(others) * own) + firsts[source // own] + source % own
        return placed_ref[pl.ds(pl.multiple_of(place * frame, 8), frame), :]

    return operator_of


def gather_kernel(peers, frame, others, masks, placed_ref, *rest):
    chunks, (real_before, imag_before, real_sum, imag_sum, real_twice, imag_twice) = rest[:-6], rest[-6:]
    me = lax.axis_index("clus")
    targets = real_sum.shape[0] // frame
    own = targets // peers
    share = chunks[0].shape[0] // (2 * own)
    skip = lax.rem(me * (2 * share), 8)
    for number, chunk in enumerate(chunks):
        doubled(chunk, real_twice, imag_twice, number * own, own, share, frame, skip)
    operator_of = placed(placed_ref, frame, others, own, masks)

    def add(some, sums):
        operators = lambda j, source: operator_of(some[j], source)
        return add_sources(sums, len(masks) * own, frame, operators, real_twice, imag_twice)

    for_some_targets(targets, frame, add, (real_before, imag_before), (real_sum, imag_sum))


def translate_kernel(frame, others, masks, targets, placed_ref, real_sum, imag_sum, *rest):
    prepare = len(rest) == len(masks) + len(targets) + 4
    chunks, rest = (rest[: len(masks)], rest[len(masks) :]) if prepare else ((), rest)
    real_twice, imag_twice = rest[:2]
    outs, (total_real, total_imag) = rest[-2 - len(targets) : -2], rest[-2:]
    me = lax.axis_index("clus")
    sources = real_twice.shape[0] // frame
    own = sources // len(masks)
    share = outs[0].shape[0] // (2 * own)
    skip = lax.rem(me * (2 * share), 8)
    for number, chunk in enumerate(chunks):
        doubled(chunk, real_twice, imag_twice, number * own, own, share, frame, skip)
    operator_of = placed(placed_ref, frame, others, own, masks)
    even, odd = pl.ds(skip, share, stride=2), pl.ds(skip + 1, share, stride=2)
    for out, d in zip(outs, targets):
        first = (me ^ d) * own

        def some_targets(i, carry):
            places = [i * TOGETHER + j for j in range(TOGETHER)]
            some = [first + g for g in places]
            rows = [pl.ds(pl.multiple_of(target * frame, 8), frame) for target in some]
            sums = [(real_sum[r, :], imag_sum[r, :]) for r in rows]
            operators = lambda j, source: operator_of(some[j], source)
            sums = add_sources(sums, sources, frame, operators, real_twice, imag_twice)
            for j, (g, (by_real, by_imag)) in enumerate(zip(places, sums)):
                total_real[j] = by_real
                total_imag[j] = by_imag
                row = g * (2 * share)
                out[pl.ds(row, share), :] = total_real[j, even, :] - total_imag[j, odd, :]
                out[pl.ds(row + share, share), :] = total_real[j, odd, :] + total_imag[j, even, :]
            return carry

        lax.fori_loop(0, own // TOGETHER, some_targets, 0)


def extract_kernel(peers, own2, *rest):
    chunks = rest[:peers]
    flat, far_ref, near_ref = rest[peers:]
    share = chunks[0].shape[0] // own2
    periods = share * peers // ROWS_PER_PERIOD
    own = own2 // 2
    flat_rows = ROWS_PER_PERIOD * periods
    me = lax.axis_index("clus")
    for gp in range(own2):
        for d in range(peers):
            flat[pl.ds(gp * flat_rows + (me ^ d) * share, share), :] = chunks[d][gp * share : (gp + 1) * share, :]

    def fill(prev_ref, next_ref):
        for ref in (prev_ref, next_ref):
            ref[...] = jnp.zeros_like(ref)
        places = [(prev_ref, e) for e in range(4)] + [(next_ref, e) for e in range(3)]
        for (ref, e), (w, m) in zip(places, edge_rows(periods)):
            for part in range(2):
                first = part * flat_rows + ROWS_PER_PERIOD * m + w
                row = (2 * e + part) * own
                ref[row : row + own, :] = flat[pl.ds(first, own, stride=2 * flat_rows), :]

    by_parity(lambda: fill(far_ref, near_ref), lambda: fill(near_ref, far_ref))


def neighbour_kernel(periods, octants_hbm, out_ref, by_octant, octants_ref, sem):
    copy = pltpu.make_async_copy(octants_hbm, octants_ref, sem)
    copy.start()
    here = lax.axis_index("dir")
    octant = lax.broadcasted_iota(jnp.int32, (8, LANES), 0)
    lane = lax.broadcasted_iota(jnp.int32, (8, LANES), 1)
    signs = [(1 - 2 * ((octant >> bit) & 1)).astype(f32) for bit in range(3)]
    for e, (w, m) in enumerate(edge_rows(periods)):
        place = here + 1 if m == 0 else here - 1
        position = lane + w * LANES
        row = w * LANES // NTHETA_P
        row = jnp.where(position >= (row + 1) * NTHETA_P, row + 1, row)
        polar_index = position - row * NTHETA_P
        azimuth_index = (place * periods + m) * PERIOD_P + row
        sin_polar, cos_polar = sincos_turns((polar_index.astype(f32) + 0.5) / (2 * NTHETA_P))
        sin_azimuth, cos_azimuth = sincos_turns(azimuth_index.astype(f32) / NPHI_P)
        along = (sin_polar * cos_azimuth, sin_polar * sin_azimuth, cos_polar)
        sine, cosine = sincos_turns(4.0 * (signs[0] * along[0] + signs[1] * along[1] + signs[2] * along[2]))
        by_octant[e, 0] = cosine
        by_octant[e, 1] = sine
    copy.wait()

    def some_children(step, carry):
        for j in range(GROUP):
            k = step * GROUP + j
            for e in range(by_octant.shape[0]):
                for i in range(2):
                    out_ref[e, i, pl.ds(k, 1), :] = by_octant[e, i, pl.ds(octants_ref[k], 1), :]
        return carry

    lax.fori_loop(0, octants_ref.shape[0] // GROUP, some_children, 0)


def edge_contributions(parents, phase_ref, gather_ref, above, below):
    children = parents.shape[1]
    own = below.shape[0] // 8
    rows = [above[2 * e * own : 2 * (e + 1) * own] for e in range(4)] + [below[2 * e * own : 2 * (e + 1) * own] for e in range(3)]
    edges = jnp.concatenate([r[part * own : (part + 1) * own] for r in rows for part in range(2)], axis=1)
    per_child = dot2(one_hot(parents, own).T, edges)
    returned = []
    for e in range(len(rows)):
        real = per_child[:, 2 * e * LANES : (2 * e + 1) * LANES]
        imaginary = per_child[:, (2 * e + 1) * LANES : (2 * e + 2) * LANES]
        cosine, sine = phase_ref[e, 0], phase_ref[e, 1]
        returned.append(
            jnp.concatenate([real * cosine + imaginary * sine, imaginary * cosine - real * sine], axis=0)
        )
    join = functools.partial(jnp.concatenate, axis=1)
    even = jnp.concatenate([join([returned[2], returned[3]]), join([returned[4], returned[5]])], axis=0)
    odd = jnp.concatenate([join([returned[0], returned[1]]), join([returned[5], returned[6]])], axis=0)
    even = gather_dot(*split(even), gather_ref, 0)
    odd = gather_dot(*split(odd), gather_ref, 1)
    a, b = TAPS_A, TAPS_B
    pairs = 2 * children
    last = a[0] * odd[:pairs] + b[0] * even[:pairs]
    first = [a[3 + i] * even[pairs:] + b[3 + i] * odd[pairs:] for i in range(2)]
    return first, last


def disaggregate_kernel(
    parents_ref, octants_ref, flat_ref, phase_ref, gather_ref, out_ref, edge_ref, listed, incoming_ref, lhs, coarse_e, coarse_o, whole_out, sems
):
    periods = incoming_ref.shape[2]
    packed = parents_ref[...] * 8 + octants_ref[...]
    for k in range(listed.shape[0]):
        listed[k] = packed[0, k]
    for gp in range(incoming_ref.shape[0]):
        for w in range(ROWS_PER_PERIOD):
            first = gp * ROWS_PER_PERIOD * periods + w
            incoming_ref[gp, w] = flat_ref[pl.ds(first, periods, stride=ROWS_PER_PERIOD), :]
    azimuth_in = periods * PERIOD_C
    sublane = lax.broadcasted_iota(jnp.int32, (periods, LANES), 0)
    inner = pl.ds(TILE, azimuth_in - 2 * TILE)

    def shift(block):
        for k in range(BLOCK):
            code = listed[block * BLOCK + k]
            octant, parent = code & 7, code >> 3
            for r in range(3):
                for i in range(3):
                    w = 3 * r + i
                    real, imaginary = incoming_ref[2 * parent, w], incoming_ref[2 * parent + 1, w]
                    cosine, sine = phase_ref[octant, 0, w], phase_ref[octant, 1, w]
                    returned = (real * cosine + imaginary * sine, imaginary * cosine - real * sine)
                    for part in range(2):
                        base = ((2 * k + part) * 3 + r) * periods
                        lhs[base : base + periods, i * LANES : (i + 1) * LANES] = returned[part]

    def polar():
        high, low = split(lhs[...])
        coarse_e[...] = gather_dot(high[:, : 2 * LANES], low[:, : 2 * LANES], gather_ref, 0)
        coarse_o[...] = gather_dot(high[:, LANES:], low[:, LANES:], gather_ref, 1)

    def azimuth(block):
        for j in range(2 * BLOCK):
            c = []
            for r in range(3):
                base = (j * 3 + r) * periods
                c.append(coarse_e[base : base + periods, :])
                c.append(coarse_o[base : base + periods, :])
            lower = both_taps_transposed(c[1], c[2])
            upper = both_taps_transposed(c[4], c[5])
            down = [jnp.where(sublane == 0, 0.0, pltpu.roll(upper[i], 1, 0)) for i in (3, 4)]
            up = jnp.where(sublane == periods - 1, 0.0, pltpu.roll(lower[0], periods - 1, 0))
            rows = [c[0] + lower[1] + down[0], lower[2] + upper[0] + down[1], c[3] + lower[3] + upper[1], lower[4] + upper[2] + up]
            kp = block * (2 * BLOCK) + j
            for u in range(PERIOD_C):
                whole_out[kp, pl.ds(u, periods, stride=PERIOD_C), :] = rows[u]
            edge_ref[0, kp] = whole_out[kp, :TILE, :]
            edge_ref[1, kp] = whole_out[kp, azimuth_in - TILE :, :]

    def written(block):
        some = pl.ds(block * (2 * BLOCK), 2 * BLOCK)
        return pltpu.make_async_copy(whole_out.at[some, inner, :], out_ref.at[some, inner, :], sems.at[block])

    def one_block(block, carry):
        shift(block)
        polar()
        azimuth(block)
        written(block).start()
        return carry

    blocks = listed.shape[0] // BLOCK
    lax.fori_loop(0, blocks, one_block, 0)
    for block in range(blocks):
        written(block).wait()


def finish_kernel(parents_ref, phase_ref, gather_ref, edge_ref, far_ref, near_ref, part_ref, out_ref, tiles, sems):
    pairs, azimuth_in, _ = out_ref.shape
    tiles[...] = edge_ref[...]
    flat = tiles.reshape(2 * pairs * TILE, LANES)
    below, above = from_sides(far_ref, near_ref)
    heads, tail = edge_contributions(parents_ref[...], phase_ref, gather_ref, above, below)
    ends = ((0, 0, heads[0]), (0, 1, heads[1]), (1, TILE - 1, tail))
    copies = []
    for i, start in enumerate((0, azimuth_in - TILE)):
        for end, row, values in ends:
            if end == i:
                for part in range(2):
                    for k in range(0, pairs // 2, 8):
                        source = slice(part * (pairs // 2) + k, part * (pairs // 2) + k + 8)
                        rows = pl.ds((i * pairs + 2 * k + part) * TILE + row, 8, stride=2 * TILE)
                        flat[rows, :] = flat[rows, :] + values[source]
        copy = pltpu.make_async_copy(tiles.at[i], out_ref.at[:, pl.ds(start, TILE), :], sems.at[i])
        copy.start()
        copies.append(copy)
    for copy in copies:
        copy.wait()


def swapped(values, axis, first):
    size = lax.axis_size(axis)
    return lax.ppermute(values, axis, [(i, (((i - first) ^ 1) + first) % size) for i in range(size)])


def exchanged(values, axis, mask):
    size = lax.axis_size(axis)
    return lax.ppermute(values, axis, [(i, i ^ mask) for i in range(size)])


SMEM = pl.BlockSpec(memory_space=pltpu.SMEM)
VMEM = pl.BlockSpec(memory_space=pltpu.VMEM)
HBM = pl.BlockSpec(memory_space=pltpu.HBM)


def in_hbm(values):
    return pltpu.with_memory_space_constraint(values, pltpu.HBM)


def local_call(kernel, out_shape, in_specs, scratch, grant, flops=1_000_000, bytes_accessed=1_000_000, out_specs=None, aliases={}):
    return pl.pallas_call(
        kernel,
        out_shape=out_shape,
        in_specs=in_specs,
        out_specs=jax.tree.map(lambda _: VMEM, out_shape) if out_specs is None else out_specs,
        scratch_shapes=scratch,
        input_output_aliases=aliases,
        compiler_params=pltpu.CompilerParams(vmem_limit_bytes=grant << 20),
        cost_estimate=pl.CostEstimate(flops=flops, bytes_accessed=bytes_accessed, transcendentals=0),
    )


def on_device_exchange(
    child_patterns, trans_table, child_parent, child_octant, partner_src, partner_off, partner_count
):
    children, _, azimuth_in, polar_in = child_patterns.shape
    pairs = 2 * children
    peers = lax.axis_size("clus")
    parent_total, _ = partner_src.shape
    own = parent_total // peers
    periods = azimuth_in // PERIOD_C
    flat_rows = ROWS_PER_PERIOD * periods
    share = flat_rows // peers
    offsets = trans_table.shape[0]
    array = lambda *shape: jax.ShapeDtypeStruct(shape, f32)
    buffer = lambda *shape: pltpu.VMEM(shape, f32)
    edges = len(edge_rows(periods))
    even, odd = polar_blocks()
    spread = jnp.asarray(np.stack([np.concatenate([h, h, l]) for h, l in (split_np(even), split_np(odd))]))
    edge = array(2, pairs, polar_in)
    to_far, to_near = local_call(
        rows_kernel, [edge, edge], [HBM], [pltpu.SemaphoreType.DMA((4,))], 8
    )(in_hbm(child_patterns.reshape(pairs, azimuth_in, polar_in)))
    from_far = swapped(to_far, "dir", 1)
    from_near = swapped(to_near, "dir", 0)
    odd_gather = np.concatenate([odd.T[LANES:], odd.T[:LANES]])
    gather = np.stack([np.concatenate(split_np(m), axis=1) for m in (even.T, odd_gather)])

    frame = max(-(-((q * 2 * share) % 8 + 2 * share) // 8) * 8 for q in range(peers))
    view = trans_table.reshape(offsets, 2, flat_rows, LANES).transpose(0, 2, 1, 3).reshape(offsets, 2 * flat_rows, LANES)
    blocks = children // BLOCK
    half = offsets // 2
    rows = 2 * BLOCK * 3 * periods
    phases, edge_phases, flat, table = local_call(
        functools.partial(main_kernel, peers),
        [
            array(8, 2, ROWS_PER_PERIOD, periods, LANES),
            array(edges, 2, 8, LANES),
            array(2 * own * flat_rows, LANES),
            jax.ShapeDtypeStruct((half, frame, LANES), bf16),
        ],
        [HBM] * 5,
        [
            pltpu.SMEM((children,), jnp.int32),
            pltpu.SMEM((children,), jnp.int32),
            buffer(pairs * azimuth_in, polar_in),
            pltpu.VMEM(spread.shape, bf16),
            buffer(rows, LANES),
            buffer(rows, LANES),
            buffer(rows, 2 * LANES),
            buffer(rows, 2 * LANES),
            buffer(own, 2, ROWS_PER_PERIOD, periods, LANES),
            buffer(2 * own * flat_rows, LANES),
            pltpu.SemaphoreType.DMA((4,)),
            pltpu.SemaphoreType.DMA((blocks,)),
        ],
        24,
        flops=4_000_000_000,
        bytes_accessed=12_000_000,
    )(
        in_hbm(child_parent[0]),
        in_hbm(child_octant),
        in_hbm(child_patterns.reshape(pairs * azimuth_in, polar_in)),
        in_hbm(view),
        in_hbm(spread),
    )

    chunk = array(2 * own * share, LANES)
    sent = local_call(
        functools.partial(fix_kernel, peers, own), [chunk] * peers, [VMEM] * 7, [buffer(2 * own * flat_rows, LANES)], 8
    )(child_parent, child_octant.reshape(1, children), from_far, from_near, flat, edge_phases, spread)

    masks = sorted(range(1, peers), key=lambda d: bin(d).count("1"))
    early, late = masks[:1], masks[1:]
    received = {0: sent[0]}
    for d in early:
        received[d] = exchanged(sent[d], "clus", d)
    for d in late:
        received[d] = exchanged(sent[d], "clus", d)

    sum_pair = [array(parent_total * frame, LANES)] * 2
    others = tuple(early + late)
    operators, *sums = local_call(
        functools.partial(widen_kernel, peers, others),
        [array(parent_total * len(others) * own * frame, LANES)] + sum_pair,
        [VMEM] * 4 + [HBM, VMEM],
        [
            pltpu.VMEM((offsets - half, frame, LANES), bf16),
            buffer((offsets + 1) * frame, LANES),
            pltpu.VMEM((parent_total, parent_total), jnp.int32),
            pltpu.SMEM((parent_total, parent_total), jnp.int32),
            buffer(own * frame, LANES),
            buffer(own * frame, LANES),
            pltpu.SemaphoreType.DMA,
            pltpu.SemaphoreType.DMA,
        ],
        20,
        flops=90_000_000,
        bytes_accessed=12_000_000,
    )(partner_src, partner_off, partner_count.reshape(1, parent_total), table, in_hbm(view), received[0])

    sums = local_call(
        functools.partial(gather_kernel, peers, frame, others, tuple(early)),
        sum_pair,
        [VMEM] * (3 + len(early)),
        [buffer(len(early) * own * frame, LANES)] * 2,
        12,
        flops=60_000_000,
        bytes_accessed=12_000_000,
    )(operators, *[received[d] for d in early], *sums)

    back = {}
    last_sources = [received[d] for d in late]
    for number, targets in enumerate((masks[-1:], masks[:-1], [0])):
        prepare = number == 0
        results = local_call(
            functools.partial(translate_kernel, frame, others, tuple(late), tuple(targets)),
            ([array(len(late) * own * frame, LANES)] * 2 if prepare else []) + [chunk] * len(targets),
            [VMEM] * (3 + len(last_sources)),
            [buffer(TOGETHER, frame, LANES)] * 2,
            20,
            flops=10_000_000 * len(targets),
            bytes_accessed=2_000_000 * len(targets),
        )(operators, *sums, *last_sources)
        if prepare:
            last_sources, results = results[:2], results[2:]
        for d, result in zip(targets, results):
            back[d] = exchanged(result, "clus", d) if d else result

    neighbour_phases = local_call(
        functools.partial(neighbour_kernel, periods),
        array(edges, 2, children, LANES),
        [HBM],
        [buffer(edges, 2, 8, LANES), pltpu.SMEM((children,), jnp.int32), pltpu.SemaphoreType.DMA],
        8,
        flops=20_000_000,
    )(in_hbm(child_octant))

    side = array(8 * own, LANES)
    incoming, to_far, to_near = local_call(
        functools.partial(extract_kernel, peers, 2 * own),
        [array(2 * own * flat_rows, LANES), side, side],
        [VMEM] * peers,
        [],
        8,
    )(*[back[d] for d in range(peers)])

    from_far = swapped(to_far, "dir", 1)
    from_near = swapped(to_near, "dir", 0)

    inner, edge_tiles = local_call(
        disaggregate_kernel,
        [array(pairs, azimuth_in, polar_in), array(2, pairs, TILE, polar_in)],
        [VMEM] * 5,
        [
            pltpu.SMEM((children,), jnp.int32),
            buffer(2 * own, ROWS_PER_PERIOD, periods, LANES),
            buffer(rows, 3 * LANES),
            buffer(rows, LANES),
            buffer(rows, LANES),
            buffer(pairs, azimuth_in, polar_in),
            pltpu.SemaphoreType.DMA((blocks,)),
        ],
        24,
        flops=4_000_000_000,
        bytes_accessed=12_000_000,
        out_specs=[HBM, VMEM],
    )(child_parent, child_octant.reshape(1, children), incoming, phases, gather)

    out = local_call(
        finish_kernel,
        array(pairs, azimuth_in, polar_in),
        [VMEM] * 6 + [HBM],
        [buffer(2, pairs, TILE, polar_in), pltpu.SemaphoreType.DMA((2,))],
        8,
        out_specs=HBM,
        aliases={6: 0},
    )(child_parent, neighbour_phases, gather, edge_tiles, from_far, from_near, in_hbm(inner))
    return out.reshape(child_patterns.shape)


def with_halo(shard, sides, width):
    for axis, dim in sides:
        size, length = (lax.axis_size(axis), shard.shape[dim])
        up = [(i, (i + 1) % size) for i in range(size)]
        down = [(j, i) for i, j in up]
        last = lax.slice_in_dim(shard, length - width, length, axis=dim)
        initial = lax.slice_in_dim(shard, 0, width, axis=dim)
        before = lax.ppermute(last, axis, up)
        after = lax.ppermute(initial, axis, down)
        shard = jnp.concatenate([before, shard, after], axis=dim)
    return shard


def lagrange_rows(offset):
    weights = []
    for anchor in range(5):
        factor = jnp.ones_like(offset)
        for neighbour in range(5):
            if neighbour != anchor:
                factor = factor * (offset - neighbour) / (anchor - neighbour)
        weights.append(factor)
    return weights


def polar_matrix_of(rows_out, rows_in):
    target = (jnp.arange(rows_out, dtype=jnp.float32) + 0.5) * rows_in / rows_out - 0.5
    start_row = jnp.clip(jnp.floor(target + 0.5).astype(jnp.int32) - 2, 0, rows_in - 5)
    weights = lagrange_rows(target - start_row.astype(jnp.float32))
    columns = jnp.arange(rows_in, dtype=jnp.int32)
    matrix = jnp.zeros((rows_out, rows_in), jnp.float32)
    for anchor in range(5):
        matrix = matrix + jnp.where(
            columns[None, :] == (start_row + anchor)[:, None], weights[anchor][:, None], 0.0
        )
    return matrix


def azimuth_matrix_of(out_index, in_index, total_out, total_in):
    target = (out_index * total_in).astype(jnp.float32) / total_out
    nearest = jnp.floor(target + 0.5).astype(jnp.int32)
    weights = lagrange_rows(target - nearest.astype(jnp.float32) + 2.0)
    matrix = jnp.zeros((out_index.shape[0], in_index.shape[0]), jnp.float32)
    for anchor in range(5):
        columns = nearest + anchor - 2
        matrix = matrix + jnp.where(
            in_index[None, :] == columns[:, None], weights[anchor][:, None], 0.0
        )
    return matrix


def shift_phases(octant, azimuth_index, azimuth_total, polar_total):
    azimuth = 2.0 * math.pi * azimuth_index.astype(jnp.float32) / azimuth_total
    polar = math.pi * (jnp.arange(polar_total, dtype=jnp.float32) + 0.5) / polar_total
    first_axis = jnp.sin(polar)[None, :] * jnp.cos(azimuth)[:, None]
    second_axis = jnp.sin(polar)[None, :] * jnp.sin(azimuth)[:, None]
    third_axis = jnp.cos(polar)[None, :] * jnp.ones_like(azimuth)[:, None]
    first_sign = (1 - 2 * (octant % 2)).astype(jnp.float32)
    second_sign = (1 - 2 * (octant // 2 % 2)).astype(jnp.float32)
    third_sign = (1 - 2 * (octant // 4)).astype(jnp.float32)
    phase_angle = phase_scale * (
        first_sign[:, None, None] * first_axis[None]
        + second_sign[:, None, None] * second_axis[None]
        + third_sign[:, None, None] * third_axis[None]
    )
    return (jnp.cos(phase_angle), jnp.sin(phase_angle))


def translate(sources, table, partner_src, partner_off, partner_count):
    live_mask = (
        jnp.arange(partner_src.shape[1], dtype=jnp.int32)[None, :] < partner_count[:, None]
    ).astype(jnp.float32)
    picked = sources[partner_src]
    operator = table[partner_off].astype(jnp.float32) * live_mask[:, :, None, None]
    real_part = jnp.sum(
        operator[:, :, 0] * picked[:, :, 0] - operator[:, :, 1] * picked[:, :, 1], axis=1
    )
    imaginary = jnp.sum(
        operator[:, :, 0] * picked[:, :, 1] + operator[:, :, 1] * picked[:, :, 0], axis=1
    )
    return jnp.stack([real_part, imaginary], axis=1)


def forward_shift(patterns, cosine, sine_part):
    real_part = patterns[:, 0] * cosine - patterns[:, 1] * sine_part
    imaginary = patterns[:, 0] * sine_part + patterns[:, 1] * cosine
    return jnp.stack([real_part, imaginary], axis=1)


def conjugate_shift(patterns, cosine, sine_part):
    real_part = patterns[:, 0] * cosine + patterns[:, 1] * sine_part
    imaginary = patterns[:, 1] * cosine - patterns[:, 0] * sine_part
    return jnp.stack([real_part, imaginary], axis=1)


def on_device_gather(
    child_patterns, trans_table, child_parent, child_octant, partner_src, partner_off, partner_count
):
    _, _, azimuth_in, _ = child_patterns.shape
    polar_out = NTHETA_P
    azimuth_out = trans_table.shape[2] // polar_out
    parent_slots = partner_src.shape[0] // lax.axis_size("clus")
    cluster_index = lax.axis_index("clus")
    direction_index = lax.axis_index("dir")
    parents = child_parent[0]
    polar_matrix = polar_matrix_of(NTHETA_P, NTHETA_C)
    onehot = (parents[None, :] == jnp.arange(parent_slots, dtype=jnp.int32)[:, None]).astype(
        jnp.float32
    )
    own_rows = jnp.mod(
        direction_index * azimuth_out + jnp.arange(azimuth_out, dtype=jnp.int32), NPHI_P
    )
    cosine, sine_part = shift_phases(child_octant, own_rows, NPHI_P, polar_out)
    extended = with_halo(child_patterns, (("dir", 2),), 2)
    gather_matrix = azimuth_matrix_of(
        jnp.arange(azimuth_out, dtype=jnp.int32),
        jnp.arange(azimuth_in + 4, dtype=jnp.int32) - 2,
        NPHI_P,
        NPHI_C,
    )
    along_azimuth = jnp.einsum("pc,kacz->kapz", gather_matrix, extended, precision=highest)
    refined = jnp.einsum("kapz,tz->kapt", along_azimuth, polar_matrix, precision=highest)
    shifted = forward_shift(refined, cosine, sine_part)
    radiation = jnp.einsum("gk,kapt->gapt", onehot, shifted, precision=highest)
    flattened = radiation.reshape(parent_slots, 2, azimuth_out * polar_out)
    sources = lax.all_gather(flattened, "clus", axis=0, tiled=True)
    first_row = cluster_index * parent_slots
    own_src = lax.dynamic_slice_in_dim(partner_src, first_row, parent_slots, 0)
    own_off = lax.dynamic_slice_in_dim(partner_off, first_row, parent_slots, 0)
    own_count = lax.dynamic_slice_in_dim(partner_count, first_row, parent_slots, 0)
    incoming = translate(sources, trans_table, own_src, own_off, own_count)
    incoming = incoming.reshape(parent_slots, 2, azimuth_out, polar_out)
    return_matrix = azimuth_matrix_of(
        jnp.arange(azimuth_out + 6, dtype=jnp.int32) - 3,
        jnp.arange(azimuth_in, dtype=jnp.int32),
        NPHI_P,
        NPHI_C,
    )
    per_child = jnp.einsum("gk,gapt->kapt", onehot, incoming, precision=highest)
    returned = conjugate_shift(per_child, cosine, sine_part)
    coarse_own = jnp.einsum("kapt,tz->kapz", returned, polar_matrix, precision=highest)
    coarse = with_halo(coarse_own, (("dir", 2),), 3)
    return jnp.einsum("pc,kapz->kacz", return_matrix, coarse, precision=highest)


def solution(mesh):
    def on_device(child_patterns, trans_table, *rest):
        peers = lax.axis_size("clus")
        children, _, azimuth_in, polar_in = child_patterns.shape
        flat_rows = trans_table.shape[2] // LANES
        fits = (
            azimuth_in % (8 * PERIOD_C) == 0
            and polar_in == LANES
            and flat_rows * PERIOD_C == ROWS_PER_PERIOD * azimuth_in
            and flat_rows % peers == 0
            and peers & (peers - 1) == 0
            and peers > 2
            and lax.axis_size("dir") % 2 == 0
            and children % BLOCK == 0
        )
        plan = on_device_exchange if fits else on_device_gather
        return plan(child_patterns, trans_table, *rest)

    return jax.shard_map(
        on_device,
        mesh=mesh,
        in_specs=(
            P("clus", None, "dir", None),
            P(None, None, "dir"),
            P("clus", None),
            P("clus"),
            P(),
            P(),
            P(),
        ),
        out_specs=P("clus", None, "dir", None),
        check_vma=False,
    )
```

```python
import functools
import math

import jax
import jax.numpy as jnp
import numpy as np
from jax import lax
from jax.experimental import pallas as pl
from jax.experimental.pallas import tpu as pltpu
from jax.sharding import PartitionSpec as P


NTHETA_C = 128
NPHI_C = 256
NTHETA_P = 192
NPHI_P = 384

LANES = 128
PERIOD_P = 6
PERIOD_C = 4
ROWS_PER_PERIOD = PERIOD_P * NTHETA_P // LANES
GROUP = 8
TOGETHER = 2
BLOCK = 2 * GROUP

phase_scale = 8.0 * math.pi
highest = lax.Precision.HIGHEST
f32 = jnp.float32
bf16 = jnp.bfloat16


def lagrange(offset):
    weights = []
    for anchor in range(5):
        factor = 1.0
        for neighbour in range(5):
            if neighbour != anchor:
                factor = factor * (offset - neighbour) / (anchor - neighbour)
        weights.append(factor)
    return weights


TAPS_A = [float(w) for w in lagrange(5.0 / 3.0)]
TAPS_B = [float(w) for w in lagrange(7.0 / 3.0)]


SUMS = [(TAPS_A[i] + TAPS_A[4 - i]) / 2 for i in range(2)]
DIFFS = [(TAPS_A[i] - TAPS_A[4 - i]) / 2 for i in range(2)]
CENTRE = TAPS_A[2]


def polar_matrix_np():
    target = (np.arange(NTHETA_P, dtype=np.float32) + np.float32(0.5)) * NTHETA_C / NTHETA_P - np.float32(0.5)
    start = np.clip(np.floor(target + 0.5).astype(np.int32) - 2, 0, NTHETA_C - 5)
    weights = lagrange((target - start).astype(np.float64))
    matrix = np.zeros((NTHETA_P, NTHETA_C), np.float64)
    for anchor in range(5):
        matrix[np.arange(NTHETA_P), start + anchor] += weights[anchor]
    return matrix.astype(np.float32)


def polar_blocks():
    matrix = polar_matrix_np().T
    even = np.zeros((NTHETA_C, 2 * LANES), np.float32)
    odd = np.zeros((NTHETA_C, 2 * LANES), np.float32)
    half = NTHETA_P - LANES
    even[:, :NTHETA_P] = matrix
    odd[:, :LANES] = matrix[:, half:]
    odd[:, 2 * LANES - half :] = matrix[:, :half]
    return even, odd


def split_np(matrix):
    high = matrix.astype(bf16)
    low = (matrix - high.astype(np.float32)).astype(bf16)
    return high, low


def split(values):
    high = values.astype(bf16)
    low = (values - high.astype(f32)).astype(bf16)
    return high, low


def dot(left, right):
    return jnp.dot(left, right, preferred_element_type=f32)


def spread_dot(values, matrix_ref, i):
    high, low = split(values)
    depth = values.shape[1]
    return dot(jnp.concatenate([high, low], axis=1), matrix_ref[i, : 2 * depth]) + dot(high, matrix_ref[i, 2 * depth :])


def gather_dot(high, low, matrix_ref, i):
    width = matrix_ref.shape[2] // 2
    both = dot(high, matrix_ref[i])
    return both[:, :width] + (both[:, width:] + dot(low, matrix_ref[i, :, :width]))


SIN_COEFFS = [(-1) ** k * math.pi ** (2 * k + 1) / math.factorial(2 * k + 1) for k in range(7)]
COS_COEFFS = [(-1) ** k * math.pi ** (2 * k) / math.factorial(2 * k) for k in range(7)]


def sincos_turns(turns):
    rest = turns - jnp.round(turns)
    square = rest * rest
    sine = jnp.full_like(square, SIN_COEFFS[-1])
    for coeff in SIN_COEFFS[-2::-1]:
        sine = sine * square + coeff
    sine = sine * rest
    cosine = jnp.full_like(square, COS_COEFFS[-1])
    for coeff in COS_COEFFS[-2::-1]:
        cosine = cosine * square + coeff
    return 2.0 * sine * cosine, 1.0 - 2.0 * sine * sine


def fill_phases(direction, out_ref):
    periods = out_ref.shape[3]
    lane = lax.broadcasted_iota(jnp.int32, (periods, LANES), 1)
    period = lax.broadcasted_iota(jnp.int32, (periods, LANES), 0)
    first = direction * (PERIOD_P * periods)

    def two_rows(r, carry):
        for i in range(3):
            position = lane + i * LANES
            second = (position >= NTHETA_P).astype(jnp.int32)
            polar_index = position - second * NTHETA_P
            azimuth_index = first + period * PERIOD_P + 2 * r + second
            sin_polar, cos_polar = sincos_turns((polar_index.astype(f32) + 0.5) / (2 * NTHETA_P))
            sin_azimuth, cos_azimuth = sincos_turns(azimuth_index.astype(f32) / NPHI_P)
            along_x = 4.0 * sin_polar * cos_azimuth
            along_y = 4.0 * sin_polar * sin_azimuth
            along_z = 4.0 * cos_polar
            w = 3 * r + i
            for octant in (0, 2, 4, 6):
                turns = along_x + along_y if octant % 4 == 0 else along_x - along_y
                turns = turns + along_z if octant < 4 else turns - along_z
                sine, cosine = sincos_turns(turns)
                out_ref[octant, 0, w] = cosine
                out_ref[octant, 1, w] = sine
                out_ref[7 - octant, 0, w] = cosine
                out_ref[7 - octant, 1, w] = -sine
        return carry

    lax.fori_loop(0, PERIOD_P // 2, two_rows, 0)


def edge_rows(periods):
    return [(w, 0) for w in (1, 2, 3, 4)] + [(w, periods - 1) for w in (6, 7, 8)]


def by_parity(even, odd):
    parity = lax.rem(lax.axis_index("dir"), 2)
    pl.when(parity == 0)(even)
    pl.when(parity == 1)(odd)


def rows_kernel(x_ref, far_ref, near_ref, sems):
    azimuth_in = x_ref.shape[1]

    def fill(first_ref, last_ref):
        ends = [(0, first_ref.at[0]), (1, first_ref.at[1]), (azimuth_in - 1, last_ref.at[0]), (azimuth_in - 1, last_ref.at[1])]
        copies = [pltpu.make_async_copy(x_ref.at[:, row, :], target, sems.at[i]) for i, (row, target) in enumerate(ends)]
        for copy in copies:
            copy.start()
        for copy in copies:
            copy.wait()

    by_parity(lambda: fill(far_ref, near_ref), lambda: fill(near_ref, far_ref))


def both_taps(rows):
    even = SUMS[0] * (rows[0] + rows[4]) + SUMS[1] * (rows[1] + rows[3]) + CENTRE * rows[2]
    odd = DIFFS[0] * (rows[0] - rows[4]) + DIFFS[1] * (rows[1] - rows[3])
    return even + odd, even - odd


def both_taps_transposed(first, second):
    total, difference = first + second, first - second
    outer = [SUMS[i] * total for i in range(2)]
    inner = [DIFFS[i] * difference for i in range(2)]
    return [outer[0] + inner[0], outer[1] + inner[1], CENTRE * total, outer[1] - inner[1], outer[0] - inner[0]]


def table_part(table_ref, first_row, first, target):
    rows = pl.ds(pl.multiple_of(first_row // 8 * 8, 8), target.shape[1])
    return table_ref.at[pl.ds(first, target.shape[0]), rows, :]


def main_kernel(peers, parents_hbm, octants_hbm, x_hbm, table_ref, spread_hbm, *rest):
    phase_ref, edge_phase_ref, flat_ref, slice_ref = rest[:4]
    parents_ref, octants_ref, x_ref, spread_ref, az_e, az_o, res_e, res_o, acc, flat, sems, x_sems = rest[4:]
    children = octants_ref.shape[0]
    periods = phase_ref.shape[3]
    azimuth_in = periods * PERIOD_C
    own = acc.shape[0]
    me = lax.axis_index("clus")
    share = ROWS_PER_PERIOD * periods // peers
    ends = (
        (octants_hbm, octants_ref),
        (parents_hbm, parents_ref),
        (spread_hbm, spread_ref),
        (table_part(table_ref, me * (2 * share), 0, slice_ref), slice_ref),
    )
    copies = [pltpu.make_async_copy(source, target, sems.at[i]) for i, (source, target) in enumerate(ends)]
    blocks = children // BLOCK
    block_rows = 2 * BLOCK * azimuth_in

    def x_copy(block):
        some = pl.ds(pl.multiple_of(block * block_rows, 8), block_rows)
        return pltpu.make_async_copy(x_hbm.at[some], x_ref.at[some], x_sems.at[block])

    for copy in copies[:-1]:
        copy.start()
    for block in range(blocks):
        x_copy(block).start()
    fill_phases(lax.axis_index("dir"), phase_ref)
    acc[...] = jnp.zeros_like(acc)
    sublane = lax.broadcasted_iota(jnp.int32, (periods, LANES), 0)
    for e, (w, m) in enumerate(edge_rows(periods)):
        for octant in range(8):
            for i in range(2):
                edge_phase_ref[e, i, octant : octant + 1, :] = phase_ref[octant, i, w, m : m + 1, :]
    for copy in copies[:-1]:
        copy.wait()
    copies[-1].start()

    def azimuth(block):
        for kp in range(2 * BLOCK):
            start = pl.multiple_of((block * (2 * BLOCK) + kp) * azimuth_in, 8)
            x = [x_ref[pl.ds(start + u, periods, stride=PERIOD_C), :] for u in range(PERIOD_C)]
            left = jnp.where(sublane == 0, 0.0, pltpu.roll(x[3], 1, 0))
            right = [jnp.where(sublane == periods - 1, 0.0, pltpu.roll(x[i], periods - 1, 0)) for i in range(2)]
            lower = [left, x[0], x[1], x[2], x[3]]
            upper = [x[1], x[2], x[3], right[0], right[1]]
            rows = [x[0], *both_taps(lower), x[2], *both_taps(upper)]
            for r in range(3):
                base = (kp * 3 + r) * periods
                az_e[base : base + periods, :] = rows[2 * r]
                az_o[base : base + periods, :] = rows[2 * r + 1]

    def polar():
        res_e[...] = spread_dot(az_e[...], spread_ref, 0)
        res_o[...] = spread_dot(az_o[...], spread_ref, 1)

    def shift(block):
        for k in range(BLOCK):
            octant = octants_ref[block * BLOCK + k]
            parent = parents_ref[block * BLOCK + k]
            for r in range(3):
                parts = []
                for part in range(2):
                    rows = pl.ds(((2 * k + part) * 3 + r) * periods, periods)
                    middle = res_e[rows, LANES:] + res_o[rows, LANES:]
                    parts.append((res_e[rows, :LANES], middle, res_o[rows, :LANES]))
                for i in range(3):
                    w = 3 * r + i
                    real, imaginary = parts[0][i], parts[1][i]
                    cosine, sine = phase_ref[octant, 0, w], phase_ref[octant, 1, w]
                    acc[parent, 0, w] += real * cosine - imaginary * sine
                    acc[parent, 1, w] += real * sine + imaginary * cosine

    def one_block(block, carry):
        x_copy(block).wait()
        azimuth(block)
        polar()
        shift(block)
        return carry

    lax.fori_loop(0, blocks, one_block, 0)
    for gp in range(2 * own):
        for w in range(ROWS_PER_PERIOD):
            flat[pl.ds(gp * ROWS_PER_PERIOD * periods + w, periods, stride=ROWS_PER_PERIOD), :] = acc[gp // 2, gp % 2, w]
        for q in range(peers):
            source = gp * ROWS_PER_PERIOD * periods + q * share
            target = (q * 2 * own + gp) * share
            flat_ref[target : target + share, :] = flat[source : source + share, :]
    copies[-1].wait()


def one_hot(parents, own):
    index = lax.broadcasted_iota(jnp.int32, (own, parents.shape[1]), 0)
    return (index == parents).astype(f32)


def dot2(exact, values):
    exact = exact.astype(bf16)
    high, low = split(values)
    return dot(exact, high) + dot(exact, low)


def fix_kernel(
    peers, own, parents_ref, octants_ref, far_ref, near_ref, flat_ref, edge_phase_ref, spread_ref, *rest
):
    outs, (fixed,) = rest[:peers], rest[peers:]
    pairs = far_ref.shape[1]
    children = pairs // 2
    chunk_rows = outs[0].shape[0]
    share = chunk_rows // (2 * own)
    periods = share * peers // ROWS_PER_PERIOD
    fixed[...] = flat_ref[...]
    is_even = lax.rem(lax.axis_index("dir"), 2) == 0

    def by_part(ref, i):
        return jnp.concatenate([ref[i, pl.ds(part, children, stride=2), :] for part in range(2)], axis=0)

    far, near = ([by_part(ref, i) for i in range(2)] for ref in (far_ref, near_ref))
    left = jnp.where(is_even, far[0], near[0])
    right = [jnp.where(is_even, n, f) for f, n in zip(far, near)]
    a, b = TAPS_A, TAPS_B
    even = jnp.concatenate([b[0] * left, a[3] * right[0] + a[4] * right[1]], axis=0)
    odd = jnp.concatenate([a[0] * left, b[3] * right[0] + b[4] * right[1]], axis=0)
    even = spread_dot(even, spread_ref, 0)
    odd = spread_dot(odd, spread_ref, 1)
    first, last = slice(0, pairs), slice(pairs, 2 * pairs)
    low, high = slice(0, LANES), slice(LANES, 2 * LANES)
    refined = [
        odd[first, high],
        odd[first, low],
        even[first, low],
        even[first, high],
        even[last, low],
        even[last, high] + odd[last, high],
        odd[last, low],
    ]
    by_octant = jnp.concatenate([edge_phase_ref[e, i] for e in range(len(refined)) for i in range(2)], axis=1)
    phases = dot2(one_hot(octants_ref[...], 8).T, by_octant)
    shifted_rows = []
    for e, rows in enumerate(refined):
        real, imaginary = rows[:children], rows[children:]
        cosine, sine = (phases[:, (2 * e + i) * LANES : (2 * e + i + 1) * LANES] for i in range(2))
        shifted_rows.append(real * cosine - imaginary * sine)
        shifted_rows.append(real * sine + imaginary * cosine)
    summed = dot2(one_hot(parents_ref[...], own), jnp.concatenate(shifted_rows, axis=1))
    for e, (w, m) in enumerate(edge_rows(periods)):
        q, row = divmod(ROWS_PER_PERIOD * m + w, share)
        for part in range(2):
            rows = pl.ds(q * chunk_rows + part * share + row, own, stride=2 * share)
            column = (2 * e + part) * LANES
            fixed[rows, :] = fixed[rows, :] + summed[:, column : column + LANES]
    me = lax.axis_index("clus")
    for d in range(peers):
        start = pl.multiple_of((me ^ d) * chunk_rows, 8)
        outs[d][...] = fixed[pl.ds(start, chunk_rows), :]


def widen_kernel(peers, others, source_ref, offset_ref, count_ref, head_ref, table_ref, chunk, placed_ref, real_sum, imag_sum, *rest):
    tail_ref, wide_ref, numbers_ref, listed, real_twice, imag_twice, sem, tail_sem = rest
    targets, partners = source_ref.shape
    half, frame, _ = head_ref.shape
    offsets = half + tail_ref.shape[0]
    own = targets // peers
    share = chunk.shape[0] // (2 * own)
    me = lax.axis_index("clus")
    tail_copy = pltpu.make_async_copy(table_part(table_ref, me * (2 * share), half, tail_ref), tail_ref, tail_sem)
    tail_copy.start()
    shape = (targets, targets)
    row, lane = (lax.broadcasted_iota(jnp.int32, shape, d) for d in range(2))
    count = jnp.sum(jnp.where(row == lane, count_ref[...], 0), axis=1, keepdims=True)
    number = jnp.full(shape, offsets, jnp.int32)
    for p in range(partners):
        here = (lane == source_ref[:, p : p + 1]) & (p < count)
        number = jnp.where(here, offset_ref[:, p : p + 1], number)
    numbers_ref[...] = number * frame
    copy = pltpu.make_async_copy(numbers_ref, listed, sem)
    copy.start()

    def widen(part_ref, first):
        def some_offsets(i, carry):
            for j in range(4):
                place = pl.multiple_of((first + i * 4 + j) * frame, 8)
                wide_ref[pl.ds(place, frame), :] = part_ref[i * 4 + j].astype(f32)
            return carry

        whole_steps = part_ref.shape[0] // 4
        lax.fori_loop(0, whole_steps, some_offsets, 0)
        for offset in range(whole_steps * 4, part_ref.shape[0]):
            wide_ref[(first + offset) * frame : (first + offset + 1) * frame, :] = part_ref[offset].astype(f32)

    widen(head_ref, 0)
    wide_ref[offsets * frame :, :] = jnp.zeros((frame, LANES), f32)
    doubled(chunk, real_twice, imag_twice, 0, own, share, frame, lax.rem(me * (2 * share), 8))
    copy.wait()
    tail_copy.wait()
    widen(tail_ref, half)

    def operator_of(target, device, g):
        first = listed[target, device * own + g]
        return wide_ref[pl.ds(pl.multiple_of(first, 8), frame), :]

    def own_sources(some, sums):
        return add_sources(sums, own, frame, lambda j, source: operator_of(some[j], me, source), real_twice, imag_twice)

    for_some_targets(targets, frame, own_sources, None, (real_sum, imag_sum))

    def other_sources(target, carry):
        for i, d in enumerate(others):
            for g in range(own):
                place = pl.multiple_of(((target * len(others) + i) * own + g) * frame, 8)
                placed_ref[pl.ds(place, frame), :] = operator_of(target, me ^ d, g)
        return carry

    lax.fori_loop(0, targets, other_sources, 0)


def doubled(chunk, real_twice, imag_twice, first, own, share, frame, skip):
    for g in range(own):
        for part, twice in enumerate((real_twice, imag_twice)):
            rows = chunk[(2 * g + part) * share : (2 * g + part + 1) * share, :]
            base = (first + g) * frame + skip
            twice[pl.ds(base, share, stride=2), :] = rows
            twice[pl.ds(base + 1, share, stride=2), :] = rows


def add_sources(sums, sources, frame, operators, real_twice, imag_twice):
    for source in range(sources):
        place = slice(source * frame, (source + 1) * frame)
        real, imaginary = real_twice[place, :], imag_twice[place, :]
        for i in range(len(sums)):
            operator = operators(i, source)
            sums[i] = (sums[i][0] + operator * real, sums[i][1] + operator * imaginary)
    return sums


def for_some_targets(targets, frame, add, before, after):
    def some_targets(i, carry):
        some = [i * TOGETHER + j for j in range(TOGETHER)]
        places = [pl.ds(pl.multiple_of(target * frame, 8), frame) for target in some]
        if before is None:
            sums = [(jnp.zeros((frame, LANES), f32),) * 2 for _ in some]
        else:
            sums = [tuple(ref[place, :] for ref in before) for place in places]
        for place, values in zip(places, add(some, sums)):
            for ref, value in zip(after, values):
                ref[place, :] = value
        return carry

    lax.fori_loop(0, targets // TOGETHER, some_targets, 0)


def placed(placed_ref, frame, others, own, masks):
    firsts = [others.index(d) * own for d in masks]

    def operator_of(target, source):
        place = target * (len(others) * own) + firsts[source // own] + source % own
        return placed_ref[pl.ds(pl.multiple_of(place * frame, 8), frame), :]

    return operator_of


def gather_kernel(peers, frame, others, masks, placed_ref, *rest):
    chunks, (real_before, imag_before, real_sum, imag_sum, real_twice, imag_twice) = rest[:-6], rest[-6:]
    me = lax.axis_index("clus")
    targets = real_sum.shape[0] // frame
    own = targets // peers
    share = chunks[0].shape[0] // (2 * own)
    skip = lax.rem(me * (2 * share), 8)
    for number, chunk in enumerate(chunks):
        doubled(chunk, real_twice, imag_twice, number * own, own, share, frame, skip)
    operator_of = placed(placed_ref, frame, others, own, masks)

    def add(some, sums):
        operators = lambda j, source: operator_of(some[j], source)
        return add_sources(sums, len(masks) * own, frame, operators, real_twice, imag_twice)

    for_some_targets(targets, frame, add, (real_before, imag_before), (real_sum, imag_sum))


def translate_kernel(frame, others, masks, targets, placed_ref, real_sum, imag_sum, *rest):
    prepare = len(rest) == len(masks) + len(targets) + 4
    chunks, rest = (rest[: len(masks)], rest[len(masks) :]) if prepare else ((), rest)
    real_twice, imag_twice = rest[:2]
    outs, (total_real, total_imag) = rest[-2 - len(targets) : -2], rest[-2:]
    me = lax.axis_index("clus")
    sources = real_twice.shape[0] // frame
    own = sources // len(masks)
    share = outs[0].shape[0] // (2 * own)
    skip = lax.rem(me * (2 * share), 8)
    for number, chunk in enumerate(chunks):
        doubled(chunk, real_twice, imag_twice, number * own, own, share, frame, skip)
    operator_of = placed(placed_ref, frame, others, own, masks)
    even, odd = pl.ds(skip, share, stride=2), pl.ds(skip + 1, share, stride=2)
    for out, d in zip(outs, targets):
        first = (me ^ d) * own

        def some_targets(i, carry):
            places = [i * TOGETHER + j for j in range(TOGETHER)]
            some = [first + g for g in places]
            rows = [pl.ds(pl.multiple_of(target * frame, 8), frame) for target in some]
            sums = [(real_sum[r, :], imag_sum[r, :]) for r in rows]
            operators = lambda j, source: operator_of(some[j], source)
            sums = add_sources(sums, sources, frame, operators, real_twice, imag_twice)
            for j, (g, (by_real, by_imag)) in enumerate(zip(places, sums)):
                total_real[j] = by_real
                total_imag[j] = by_imag
                row = g * (2 * share)
                out[pl.ds(row, share), :] = total_real[j, even, :] - total_imag[j, odd, :]
                out[pl.ds(row + share, share), :] = total_real[j, odd, :] + total_imag[j, even, :]
            return carry

        lax.fori_loop(0, own // TOGETHER, some_targets, 0)


def extract_kernel(peers, own2, *rest):
    chunks = rest[:peers]
    flat, far_ref, near_ref = rest[peers:]
    share = chunks[0].shape[0] // own2
    periods = share * peers // ROWS_PER_PERIOD
    own = own2 // 2
    flat_rows = ROWS_PER_PERIOD * periods
    me = lax.axis_index("clus")
    for gp in range(own2):
        for d in range(peers):
            flat[pl.ds(gp * flat_rows + (me ^ d) * share, share), :] = chunks[d][gp * share : (gp + 1) * share, :]

    def fill(prev_ref, next_ref):
        for ref in (prev_ref, next_ref):
            ref[...] = jnp.zeros_like(ref)
        places = [(prev_ref, e) for e in range(4)] + [(next_ref, e) for e in range(3)]
        for (ref, e), (w, m) in zip(places, edge_rows(periods)):
            for part in range(2):
                first = part * flat_rows + ROWS_PER_PERIOD * m + w
                row = (2 * e + part) * own
                ref[row : row + own, :] = flat[pl.ds(first, own, stride=2 * flat_rows), :]

    by_parity(lambda: fill(far_ref, near_ref), lambda: fill(near_ref, far_ref))


def neighbour_kernel(periods, octants_hbm, out_ref, by_octant, octants_ref, sem):
    copy = pltpu.make_async_copy(octants_hbm, octants_ref, sem)
    copy.start()
    here = lax.axis_index("dir")
    octant = lax.broadcasted_iota(jnp.int32, (8, LANES), 0)
    lane = lax.broadcasted_iota(jnp.int32, (8, LANES), 1)
    signs = [(1 - 2 * ((octant >> bit) & 1)).astype(f32) for bit in range(3)]
    for e, (w, m) in enumerate(edge_rows(periods)):
        place = here + 1 if m == 0 else here - 1
        position = lane + w * LANES
        row = w * LANES // NTHETA_P
        row = jnp.where(position >= (row + 1) * NTHETA_P, row + 1, row)
        polar_index = position - row * NTHETA_P
        azimuth_index = (place * periods + m) * PERIOD_P + row
        sin_polar, cos_polar = sincos_turns((polar_index.astype(f32) + 0.5) / (2 * NTHETA_P))
        sin_azimuth, cos_azimuth = sincos_turns(azimuth_index.astype(f32) / NPHI_P)
        along = (sin_polar * cos_azimuth, sin_polar * sin_azimuth, cos_polar)
        sine, cosine = sincos_turns(4.0 * (signs[0] * along[0] + signs[1] * along[1] + signs[2] * along[2]))
        by_octant[e, 0] = cosine
        by_octant[e, 1] = sine
    copy.wait()

    def some_children(step, carry):
        for j in range(GROUP):
            k = step * GROUP + j
            for e in range(by_octant.shape[0]):
                for i in range(2):
                    out_ref[e, i, pl.ds(k, 1), :] = by_octant[e, i, pl.ds(octants_ref[k], 1), :]
        return carry

    lax.fori_loop(0, octants_ref.shape[0] // GROUP, some_children, 0)


def returned_rows(parents, phase_ref, edges, rows_ref):
    own = rows_ref.shape[0] // 8
    columns = [rows_ref[row * own : (row + 1) * own, :] for row in range(2 * len(edges))]
    per_child = dot2(one_hot(parents, own).T, jnp.concatenate(columns, axis=1))
    returned = []
    for i, e in enumerate(edges):
        real = per_child[:, 2 * i * LANES : (2 * i + 1) * LANES]
        imaginary = per_child[:, (2 * i + 1) * LANES : (2 * i + 2) * LANES]
        cosine, sine = phase_ref[e, 0], phase_ref[e, 1]
        returned.append(
            jnp.concatenate([real * cosine + imaginary * sine, imaginary * cosine - real * sine], axis=0)
        )
    return returned


def side_by_side(left, right):
    return split(jnp.concatenate([left, right], axis=1))


def disaggregate_kernel(
    parents_ref, octants_ref, flat_ref, phase_ref, gather_ref, out_ref, edge_ref, listed, incoming_ref, lhs, coarse_e, coarse_o, whole_out, sems
):
    periods = incoming_ref.shape[2]
    packed = parents_ref[...] * 8 + octants_ref[...]
    for k in range(listed.shape[0]):
        listed[k] = packed[0, k]
    for gp in range(incoming_ref.shape[0]):
        for w in range(ROWS_PER_PERIOD):
            first = gp * ROWS_PER_PERIOD * periods + w
            incoming_ref[gp, w] = flat_ref[pl.ds(first, periods, stride=ROWS_PER_PERIOD), :]
    sublane = lax.broadcasted_iota(jnp.int32, (periods, LANES), 0)

    def shift(block):
        for k in range(BLOCK):
            code = listed[block * BLOCK + k]
            octant, parent = code & 7, code >> 3
            for r in range(3):
                for i in range(3):
                    w = 3 * r + i
                    real, imaginary = incoming_ref[2 * parent, w], incoming_ref[2 * parent + 1, w]
                    cosine, sine = phase_ref[octant, 0, w], phase_ref[octant, 1, w]
                    returned = (real * cosine + imaginary * sine, imaginary * cosine - real * sine)
                    for part in range(2):
                        base = ((2 * k + part) * 3 + r) * periods
                        lhs[base : base + periods, i * LANES : (i + 1) * LANES] = returned[part]

    def polar():
        high, low = split(lhs[...])
        coarse_e[...] = gather_dot(high[:, : 2 * LANES], low[:, : 2 * LANES], gather_ref, 0)
        coarse_o[...] = gather_dot(high[:, LANES:], low[:, LANES:], gather_ref, 1)

    def azimuth(block):
        for j in range(2 * BLOCK):
            c = []
            for r in range(3):
                base = (j * 3 + r) * periods
                c.append(coarse_e[base : base + periods, :])
                c.append(coarse_o[base : base + periods, :])
            lower = both_taps_transposed(c[1], c[2])
            upper = both_taps_transposed(c[4], c[5])
            down = [jnp.where(sublane == 0, 0.0, pltpu.roll(upper[i], 1, 0)) for i in (3, 4)]
            up = jnp.where(sublane == periods - 1, 0.0, pltpu.roll(lower[0], periods - 1, 0))
            rows = [c[0] + lower[1] + down[0], lower[2] + upper[0] + down[1], c[3] + lower[3] + upper[1], lower[4] + upper[2] + up]
            kp = block * (2 * BLOCK) + j
            for u in range(PERIOD_C):
                whole_out[kp, pl.ds(u, periods, stride=PERIOD_C), :] = rows[u]
            for i, (u, m) in enumerate(((0, 0), (1, 0), (PERIOD_C - 1, periods - 1))):
                edge_ref[i, pl.ds(kp, 1), :] = rows[u][m : m + 1]

    def written(block):
        some = pl.ds(block * (2 * BLOCK), 2 * BLOCK)
        return pltpu.make_async_copy(whole_out.at[some], out_ref.at[some], sems.at[block])

    def one_block(block, carry):
        shift(block)
        polar()
        azimuth(block)
        written(block).start()
        return carry

    blocks = listed.shape[0] // BLOCK
    lax.fori_loop(0, blocks, one_block, 0)
    for block in range(blocks):
        written(block).wait()


def finish_kernel(is_far, parents_ref, phase_ref, gather_ref, edge_ref, side_ref, part_ref, out_ref, sums, sems):
    pairs, azimuth_in, _ = out_ref.shape
    children = pairs // 2
    a, b = TAPS_A, TAPS_B

    def write(additions):
        copies = []
        for i, row, values in additions:
            for part in range(2):
                place = pl.ds(part, children, stride=2)
                sums[i, place, :] = edge_ref[i, place, :] + values[part * children : (part + 1) * children]
            copy = pltpu.make_async_copy(sums.at[i], out_ref.at[:, row, :], sems.at[i])
            copy.start()
            copies.append(copy)
        for copy in copies:
            copy.wait()

    def from_below():
        returned = returned_rows(parents_ref[...], phase_ref, (4, 5, 6), side_ref)
        even = gather_dot(*side_by_side(returned[0], returned[1]), gather_ref, 0)
        odd = gather_dot(*side_by_side(returned[1], returned[2]), gather_ref, 1)
        write([(i, i, a[3 + i] * even + b[3 + i] * odd) for i in range(2)])

    def from_above():
        returned = returned_rows(parents_ref[...], phase_ref, (0, 1, 2, 3), side_ref)
        even = gather_dot(*side_by_side(returned[2], returned[3]), gather_ref, 0)
        odd = gather_dot(*side_by_side(returned[0], returned[1]), gather_ref, 1)
        write([(2, azimuth_in - 1, a[0] * odd + b[0] * even)])

    by_parity(*((from_below, from_above) if is_far else (from_above, from_below)))


def swapped(values, axis, first):
    size = lax.axis_size(axis)
    return lax.ppermute(values, axis, [(i, (((i - first) ^ 1) + first) % size) for i in range(size)])


def exchanged(values, axis, mask):
    size = lax.axis_size(axis)
    return lax.ppermute(values, axis, [(i, i ^ mask) for i in range(size)])


SMEM = pl.BlockSpec(memory_space=pltpu.SMEM)
VMEM = pl.BlockSpec(memory_space=pltpu.VMEM)
HBM = pl.BlockSpec(memory_space=pltpu.HBM)


def in_hbm(values):
    return pltpu.with_memory_space_constraint(values, pltpu.HBM)


def local_call(kernel, out_shape, in_specs, scratch, grant, flops=1_000_000, bytes_accessed=1_000_000, out_specs=None, aliases={}):
    return pl.pallas_call(
        kernel,
        out_shape=out_shape,
        in_specs=in_specs,
        out_specs=jax.tree.map(lambda _: VMEM, out_shape) if out_specs is None else out_specs,
        scratch_shapes=scratch,
        input_output_aliases=aliases,
        compiler_params=pltpu.CompilerParams(vmem_limit_bytes=grant << 20),
        cost_estimate=pl.CostEstimate(flops=flops, bytes_accessed=bytes_accessed, transcendentals=0),
    )


def on_device_exchange(
    child_patterns, trans_table, child_parent, child_octant, partner_src, partner_off, partner_count
):
    children, _, azimuth_in, polar_in = child_patterns.shape
    pairs = 2 * children
    peers = lax.axis_size("clus")
    parent_total, _ = partner_src.shape
    own = parent_total // peers
    periods = azimuth_in // PERIOD_C
    flat_rows = ROWS_PER_PERIOD * periods
    share = flat_rows // peers
    offsets = trans_table.shape[0]
    array = lambda *shape: jax.ShapeDtypeStruct(shape, f32)
    buffer = lambda *shape: pltpu.VMEM(shape, f32)
    edges = len(edge_rows(periods))
    even, odd = polar_blocks()
    spread = jnp.asarray(np.stack([np.concatenate([h, h, l]) for h, l in (split_np(even), split_np(odd))]))
    edge = array(2, pairs, polar_in)
    to_far, to_near = local_call(
        rows_kernel, [edge, edge], [HBM], [pltpu.SemaphoreType.DMA((4,))], 8
    )(in_hbm(child_patterns.reshape(pairs, azimuth_in, polar_in)))
    from_far = swapped(to_far, "dir", 1)
    from_near = swapped(to_near, "dir", 0)
    odd_gather = np.concatenate([odd.T[LANES:], odd.T[:LANES]])
    gather = np.stack([np.concatenate(split_np(m), axis=1) for m in (even.T, odd_gather)])

    frame = max(-(-((q * 2 * share) % 8 + 2 * share) // 8) * 8 for q in range(peers))
    view = trans_table.reshape(offsets, 2, flat_rows, LANES).transpose(0, 2, 1, 3).reshape(offsets, 2 * flat_rows, LANES)
    blocks = children // BLOCK
    half = offsets // 2
    rows = 2 * BLOCK * 3 * periods
    phases, edge_phases, flat, table = local_call(
        functools.partial(main_kernel, peers),
        [
            array(8, 2, ROWS_PER_PERIOD, periods, LANES),
            array(edges, 2, 8, LANES),
            array(2 * own * flat_rows, LANES),
            jax.ShapeDtypeStruct((half, frame, LANES), bf16),
        ],
        [HBM] * 5,
        [
            pltpu.SMEM((children,), jnp.int32),
            pltpu.SMEM((children,), jnp.int32),
            buffer(pairs * azimuth_in, polar_in),
            pltpu.VMEM(spread.shape, bf16),
            buffer(rows, LANES),
            buffer(rows, LANES),
            buffer(rows, 2 * LANES),
            buffer(rows, 2 * LANES),
            buffer(own, 2, ROWS_PER_PERIOD, periods, LANES),
            buffer(2 * own * flat_rows, LANES),
            pltpu.SemaphoreType.DMA((4,)),
            pltpu.SemaphoreType.DMA((blocks,)),
        ],
        24,
        flops=4_000_000_000,
        bytes_accessed=12_000_000,
    )(
        in_hbm(child_parent[0]),
        in_hbm(child_octant),
        in_hbm(child_patterns.reshape(pairs * azimuth_in, polar_in)),
        in_hbm(view),
        in_hbm(spread),
    )

    chunk = array(2 * own * share, LANES)
    sent = local_call(
        functools.partial(fix_kernel, peers, own), [chunk] * peers, [VMEM] * 7, [buffer(2 * own * flat_rows, LANES)], 8
    )(child_parent, child_octant.reshape(1, children), from_far, from_near, flat, edge_phases, spread)

    masks = sorted(range(1, peers), key=lambda d: bin(d).count("1"))
    early, late = masks[:1], masks[1:]
    received = {0: sent[0]}
    for d in early:
        received[d] = exchanged(sent[d], "clus", d)
    for d in late:
        received[d] = exchanged(sent[d], "clus", d)

    sum_pair = [array(parent_total * frame, LANES)] * 2
    others = tuple(early + late)
    operators, *sums = local_call(
        functools.partial(widen_kernel, peers, others),
        [array(parent_total * len(others) * own * frame, LANES)] + sum_pair,
        [VMEM] * 4 + [HBM, VMEM],
        [
            pltpu.VMEM((offsets - half, frame, LANES), bf16),
            buffer((offsets + 1) * frame, LANES),
            pltpu.VMEM((parent_total, parent_total), jnp.int32),
            pltpu.SMEM((parent_total, parent_total), jnp.int32),
            buffer(own * frame, LANES),
            buffer(own * frame, LANES),
            pltpu.SemaphoreType.DMA,
            pltpu.SemaphoreType.DMA,
        ],
        20,
        flops=90_000_000,
        bytes_accessed=12_000_000,
    )(partner_src, partner_off, partner_count.reshape(1, parent_total), table, in_hbm(view), received[0])

    sums = local_call(
        functools.partial(gather_kernel, peers, frame, others, tuple(early)),
        sum_pair,
        [VMEM] * (3 + len(early)),
        [buffer(len(early) * own * frame, LANES)] * 2,
        12,
        flops=60_000_000,
        bytes_accessed=12_000_000,
    )(operators, *[received[d] for d in early], *sums)

    back = {}
    last_sources = [received[d] for d in late]
    for number, targets in enumerate((masks[-1:], masks[:-1], [0])):
        prepare = number == 0
        results = local_call(
            functools.partial(translate_kernel, frame, others, tuple(late), tuple(targets)),
            ([array(len(late) * own * frame, LANES)] * 2 if prepare else []) + [chunk] * len(targets),
            [VMEM] * (3 + len(last_sources)),
            [buffer(TOGETHER, frame, LANES)] * 2,
            20,
            flops=10_000_000 * len(targets),
            bytes_accessed=2_000_000 * len(targets),
        )(operators, *sums, *last_sources)
        if prepare:
            last_sources, results = results[:2], results[2:]
        for d, result in zip(targets, results):
            back[d] = exchanged(result, "clus", d) if d else result

    neighbour_phases = local_call(
        functools.partial(neighbour_kernel, periods),
        array(edges, 2, children, LANES),
        [HBM],
        [buffer(edges, 2, 8, LANES), pltpu.SMEM((children,), jnp.int32), pltpu.SemaphoreType.DMA],
        8,
        flops=20_000_000,
    )(in_hbm(child_octant))

    side = array(8 * own, LANES)
    incoming, to_far, to_near = local_call(
        functools.partial(extract_kernel, peers, 2 * own),
        [array(2 * own * flat_rows, LANES), side, side],
        [VMEM] * peers,
        [],
        8,
    )(*[back[d] for d in range(peers)])

    from_far = swapped(to_far, "dir", 1)
    from_near = swapped(to_near, "dir", 0)

    partial_out, edge_sums = local_call(
        disaggregate_kernel,
        [array(pairs, azimuth_in, polar_in), array(3, pairs, polar_in)],
        [VMEM] * 5,
        [
            pltpu.SMEM((children,), jnp.int32),
            buffer(2 * own, ROWS_PER_PERIOD, periods, LANES),
            buffer(rows, 3 * LANES),
            buffer(rows, LANES),
            buffer(rows, LANES),
            buffer(pairs, azimuth_in, polar_in),
            pltpu.SemaphoreType.DMA((blocks,)),
        ],
        24,
        flops=4_000_000_000,
        bytes_accessed=12_000_000,
        out_specs=[HBM, VMEM],
    )(child_parent, child_octant.reshape(1, children), incoming, phases, gather)

    out = partial_out
    for is_far, side in ((False, from_near), (True, from_far)):
        out = local_call(
            functools.partial(finish_kernel, is_far),
            array(pairs, azimuth_in, polar_in),
            [VMEM] * 5 + [HBM],
            [buffer(3, pairs, polar_in), pltpu.SemaphoreType.DMA((3,))],
            8,
            out_specs=HBM,
            aliases={5: 0},
        )(child_parent, neighbour_phases, gather, edge_sums, side, in_hbm(out))
    return out.reshape(child_patterns.shape)


def with_halo(shard, sides, width):
    for axis, dim in sides:
        size, length = (lax.axis_size(axis), shard.shape[dim])
        up = [(i, (i + 1) % size) for i in range(size)]
        down = [(j, i) for i, j in up]
        last = lax.slice_in_dim(shard, length - width, length, axis=dim)
        initial = lax.slice_in_dim(shard, 0, width, axis=dim)
        before = lax.ppermute(last, axis, up)
        after = lax.ppermute(initial, axis, down)
        shard = jnp.concatenate([before, shard, after], axis=dim)
    return shard


def lagrange_rows(offset):
    weights = []
    for anchor in range(5):
        factor = jnp.ones_like(offset)
        for neighbour in range(5):
            if neighbour != anchor:
                factor = factor * (offset - neighbour) / (anchor - neighbour)
        weights.append(factor)
    return weights


def polar_matrix_of(rows_out, rows_in):
    target = (jnp.arange(rows_out, dtype=jnp.float32) + 0.5) * rows_in / rows_out - 0.5
    start_row = jnp.clip(jnp.floor(target + 0.5).astype(jnp.int32) - 2, 0, rows_in - 5)
    weights = lagrange_rows(target - start_row.astype(jnp.float32))
    columns = jnp.arange(rows_in, dtype=jnp.int32)
    matrix = jnp.zeros((rows_out, rows_in), jnp.float32)
    for anchor in range(5):
        matrix = matrix + jnp.where(
            columns[None, :] == (start_row + anchor)[:, None], weights[anchor][:, None], 0.0
        )
    return matrix


def azimuth_matrix_of(out_index, in_index, total_out, total_in):
    target = (out_index * total_in).astype(jnp.float32) / total_out
    nearest = jnp.floor(target + 0.5).astype(jnp.int32)
    weights = lagrange_rows(target - nearest.astype(jnp.float32) + 2.0)
    matrix = jnp.zeros((out_index.shape[0], in_index.shape[0]), jnp.float32)
    for anchor in range(5):
        columns = nearest + anchor - 2
        matrix = matrix + jnp.where(
            in_index[None, :] == columns[:, None], weights[anchor][:, None], 0.0
        )
    return matrix


def shift_phases(octant, azimuth_index, azimuth_total, polar_total):
    azimuth = 2.0 * math.pi * azimuth_index.astype(jnp.float32) / azimuth_total
    polar = math.pi * (jnp.arange(polar_total, dtype=jnp.float32) + 0.5) / polar_total
    first_axis = jnp.sin(polar)[None, :] * jnp.cos(azimuth)[:, None]
    second_axis = jnp.sin(polar)[None, :] * jnp.sin(azimuth)[:, None]
    third_axis = jnp.cos(polar)[None, :] * jnp.ones_like(azimuth)[:, None]
    first_sign = (1 - 2 * (octant % 2)).astype(jnp.float32)
    second_sign = (1 - 2 * (octant // 2 % 2)).astype(jnp.float32)
    third_sign = (1 - 2 * (octant // 4)).astype(jnp.float32)
    phase_angle = phase_scale * (
        first_sign[:, None, None] * first_axis[None]
        + second_sign[:, None, None] * second_axis[None]
        + third_sign[:, None, None] * third_axis[None]
    )
    return (jnp.cos(phase_angle), jnp.sin(phase_angle))


def translate(sources, table, partner_src, partner_off, partner_count):
    live_mask = (
        jnp.arange(partner_src.shape[1], dtype=jnp.int32)[None, :] < partner_count[:, None]
    ).astype(jnp.float32)
    picked = sources[partner_src]
    operator = table[partner_off].astype(jnp.float32) * live_mask[:, :, None, None]
    real_part = jnp.sum(
        operator[:, :, 0] * picked[:, :, 0] - operator[:, :, 1] * picked[:, :, 1], axis=1
    )
    imaginary = jnp.sum(
        operator[:, :, 0] * picked[:, :, 1] + operator[:, :, 1] * picked[:, :, 0], axis=1
    )
    return jnp.stack([real_part, imaginary], axis=1)


def forward_shift(patterns, cosine, sine_part):
    real_part = patterns[:, 0] * cosine - patterns[:, 1] * sine_part
    imaginary = patterns[:, 0] * sine_part + patterns[:, 1] * cosine
    return jnp.stack([real_part, imaginary], axis=1)


def conjugate_shift(patterns, cosine, sine_part):
    real_part = patterns[:, 0] * cosine + patterns[:, 1] * sine_part
    imaginary = patterns[:, 1] * cosine - patterns[:, 0] * sine_part
    return jnp.stack([real_part, imaginary], axis=1)


def on_device_gather(
    child_patterns, trans_table, child_parent, child_octant, partner_src, partner_off, partner_count
):
    _, _, azimuth_in, _ = child_patterns.shape
    polar_out = NTHETA_P
    azimuth_out = trans_table.shape[2] // polar_out
    parent_slots = partner_src.shape[0] // lax.axis_size("clus")
    cluster_index = lax.axis_index("clus")
    direction_index = lax.axis_index("dir")
    parents = child_parent[0]
    polar_matrix = polar_matrix_of(NTHETA_P, NTHETA_C)
    onehot = (parents[None, :] == jnp.arange(parent_slots, dtype=jnp.int32)[:, None]).astype(
        jnp.float32
    )
    own_rows = jnp.mod(
        direction_index * azimuth_out + jnp.arange(azimuth_out, dtype=jnp.int32), NPHI_P
    )
    cosine, sine_part = shift_phases(child_octant, own_rows, NPHI_P, polar_out)
    extended = with_halo(child_patterns, (("dir", 2),), 2)
    gather_matrix = azimuth_matrix_of(
        jnp.arange(azimuth_out, dtype=jnp.int32),
        jnp.arange(azimuth_in + 4, dtype=jnp.int32) - 2,
        NPHI_P,
        NPHI_C,
    )
    along_azimuth = jnp.einsum("pc,kacz->kapz", gather_matrix, extended, precision=highest)
    refined = jnp.einsum("kapz,tz->kapt", along_azimuth, polar_matrix, precision=highest)
    shifted = forward_shift(refined, cosine, sine_part)
    radiation = jnp.einsum("gk,kapt->gapt", onehot, shifted, precision=highest)
    flattened = radiation.reshape(parent_slots, 2, azimuth_out * polar_out)
    sources = lax.all_gather(flattened, "clus", axis=0, tiled=True)
    first_row = cluster_index * parent_slots
    own_src = lax.dynamic_slice_in_dim(partner_src, first_row, parent_slots, 0)
    own_off = lax.dynamic_slice_in_dim(partner_off, first_row, parent_slots, 0)
    own_count = lax.dynamic_slice_in_dim(partner_count, first_row, parent_slots, 0)
    incoming = translate(sources, trans_table, own_src, own_off, own_count)
    incoming = incoming.reshape(parent_slots, 2, azimuth_out, polar_out)
    return_matrix = azimuth_matrix_of(
        jnp.arange(azimuth_out + 6, dtype=jnp.int32) - 3,
        jnp.arange(azimuth_in, dtype=jnp.int32),
        NPHI_P,
        NPHI_C,
    )
    per_child = jnp.einsum("gk,gapt->kapt", onehot, incoming, precision=highest)
    returned = conjugate_shift(per_child, cosine, sine_part)
    coarse_own = jnp.einsum("kapt,tz->kapz", returned, polar_matrix, precision=highest)
    coarse = with_halo(coarse_own, (("dir", 2),), 3)
    return jnp.einsum("pc,kapz->kacz", return_matrix, coarse, precision=highest)


def solution(mesh):
    def on_device(child_patterns, trans_table, *rest):
        peers = lax.axis_size("clus")
        children, _, azimuth_in, polar_in = child_patterns.shape
        flat_rows = trans_table.shape[2] // LANES
        fits = (
            azimuth_in % (8 * PERIOD_C) == 0
            and polar_in == LANES
            and flat_rows * PERIOD_C == ROWS_PER_PERIOD * azimuth_in
            and flat_rows % peers == 0
            and peers & (peers - 1) == 0
            and peers > 2
            and lax.axis_size("dir") % 2 == 0
            and children % BLOCK == 0
        )
        plan = on_device_exchange if fits else on_device_gather
        return plan(child_patterns, trans_table, *rest)

    return jax.shard_map(
        on_device,
        mesh=mesh,
        in_specs=(
            P("clus", None, "dir", None),
            P(None, None, "dir"),
            P("clus", None),
            P("clus"),
            P(),
            P(),
            P(),
        ),
        out_specs=P("clus", None, "dir", None),
        check_vma=False,
    )
```

```python
import functools
import math

import jax
import jax.numpy as jnp
import numpy as np
from jax import lax
from jax.experimental import pallas as pl
from jax.experimental.pallas import tpu as pltpu
from jax.sharding import PartitionSpec as P


NTHETA_C = 128
NPHI_C = 256
NTHETA_P = 192
NPHI_P = 384

LANES = 128
PERIOD_P = 6
PERIOD_C = 4
ROWS_PER_PERIOD = PERIOD_P * NTHETA_P // LANES
GROUP = 8
TOGETHER = 2
BLOCK = 2 * GROUP

phase_scale = 8.0 * math.pi
highest = lax.Precision.HIGHEST
f32 = jnp.float32
bf16 = jnp.bfloat16


def lagrange(offset):
    weights = []
    for anchor in range(5):
        factor = 1.0
        for neighbour in range(5):
            if neighbour != anchor:
                factor = factor * (offset - neighbour) / (anchor - neighbour)
        weights.append(factor)
    return weights


TAPS_A = [float(w) for w in lagrange(5.0 / 3.0)]
TAPS_B = [float(w) for w in lagrange(7.0 / 3.0)]


SUMS = [(TAPS_A[i] + TAPS_A[4 - i]) / 2 for i in range(2)]
DIFFS = [(TAPS_A[i] - TAPS_A[4 - i]) / 2 for i in range(2)]
CENTRE = TAPS_A[2]


def polar_matrix_np():
    target = (np.arange(NTHETA_P, dtype=np.float32) + np.float32(0.5)) * NTHETA_C / NTHETA_P - np.float32(0.5)
    start = np.clip(np.floor(target + 0.5).astype(np.int32) - 2, 0, NTHETA_C - 5)
    weights = lagrange((target - start).astype(np.float64))
    matrix = np.zeros((NTHETA_P, NTHETA_C), np.float64)
    for anchor in range(5):
        matrix[np.arange(NTHETA_P), start + anchor] += weights[anchor]
    return matrix.astype(np.float32)


def polar_blocks():
    matrix = polar_matrix_np().T
    even = np.zeros((NTHETA_C, 2 * LANES), np.float32)
    odd = np.zeros((NTHETA_C, 2 * LANES), np.float32)
    half = NTHETA_P - LANES
    even[:, :NTHETA_P] = matrix
    odd[:, :LANES] = matrix[:, half:]
    odd[:, 2 * LANES - half :] = matrix[:, :half]
    return even, odd


def split_np(matrix):
    high = matrix.astype(bf16)
    low = (matrix - high.astype(np.float32)).astype(bf16)
    return high, low


def split(values):
    high = values.astype(bf16)
    low = (values - high.astype(f32)).astype(bf16)
    return high, low


def dot(left, right):
    return jnp.dot(left, right, preferred_element_type=f32)


def spread_dot(values, matrix_ref, i):
    high, low = split(values)
    depth = values.shape[1]
    return dot(jnp.concatenate([high, low], axis=1), matrix_ref[i, : 2 * depth]) + dot(high, matrix_ref[i, 2 * depth :])


def gather_dot(high, low, matrix_ref, i):
    width = matrix_ref.shape[2] // 2
    both = dot(high, matrix_ref[i])
    return both[:, :width] + (both[:, width:] + dot(low, matrix_ref[i, :, :width]))


SIN_COEFFS = [(-1) ** k * math.pi ** (2 * k + 1) / math.factorial(2 * k + 1) for k in range(7)]
COS_COEFFS = [(-1) ** k * math.pi ** (2 * k) / math.factorial(2 * k) for k in range(7)]


def sincos_turns(turns):
    rest = turns - jnp.round(turns)
    square = rest * rest
    sine = jnp.full_like(square, SIN_COEFFS[-1])
    for coeff in SIN_COEFFS[-2::-1]:
        sine = sine * square + coeff
    sine = sine * rest
    cosine = jnp.full_like(square, COS_COEFFS[-1])
    for coeff in COS_COEFFS[-2::-1]:
        cosine = cosine * square + coeff
    return 2.0 * sine * cosine, 1.0 - 2.0 * sine * sine


def fill_phases(direction, out_ref):
    periods = out_ref.shape[3]
    lane = lax.broadcasted_iota(jnp.int32, (periods, LANES), 1)
    period = lax.broadcasted_iota(jnp.int32, (periods, LANES), 0)
    first = direction * (PERIOD_P * periods)

    def two_rows(r, carry):
        for i in range(3):
            position = lane + i * LANES
            second = (position >= NTHETA_P).astype(jnp.int32)
            polar_index = position - second * NTHETA_P
            azimuth_index = first + period * PERIOD_P + 2 * r + second
            sin_polar, cos_polar = sincos_turns((polar_index.astype(f32) + 0.5) / (2 * NTHETA_P))
            sin_azimuth, cos_azimuth = sincos_turns(azimuth_index.astype(f32) / NPHI_P)
            along_x = 4.0 * sin_polar * cos_azimuth
            along_y = 4.0 * sin_polar * sin_azimuth
            along_z = 4.0 * cos_polar
            w = 3 * r + i
            for octant in (0, 2, 4, 6):
                turns = along_x + along_y if octant % 4 == 0 else along_x - along_y
                turns = turns + along_z if octant < 4 else turns - along_z
                sine, cosine = sincos_turns(turns)
                out_ref[octant, 0, w] = cosine
                out_ref[octant, 1, w] = sine
                out_ref[7 - octant, 0, w] = cosine
                out_ref[7 - octant, 1, w] = -sine
        return carry

    lax.fori_loop(0, PERIOD_P // 2, two_rows, 0)


def edge_rows(periods):
    return [(w, 0) for w in (1, 2, 3, 4)] + [(w, periods - 1) for w in (6, 7, 8)]


def by_parity(even, odd):
    parity = lax.rem(lax.axis_index("dir"), 2)
    pl.when(parity == 0)(even)
    pl.when(parity == 1)(odd)


def from_sides(far_ref, near_ref):
    is_even = lax.rem(lax.axis_index("dir"), 2) == 0
    far, near = far_ref[...], near_ref[...]
    return jnp.where(is_even, far, near), jnp.where(is_even, near, far)


def rows_kernel(x_ref, far_ref, near_ref, sems):
    azimuth_in = x_ref.shape[1]

    def fill(first_ref, last_ref):
        ends = [(0, first_ref.at[0]), (1, first_ref.at[1]), (azimuth_in - 1, last_ref.at[0]), (azimuth_in - 1, last_ref.at[1])]
        copies = [pltpu.make_async_copy(x_ref.at[:, row, :], target, sems.at[i]) for i, (row, target) in enumerate(ends)]
        for copy in copies:
            copy.start()
        for copy in copies:
            copy.wait()

    by_parity(lambda: fill(far_ref, near_ref), lambda: fill(near_ref, far_ref))


def both_taps(rows):
    even = SUMS[0] * (rows[0] + rows[4]) + SUMS[1] * (rows[1] + rows[3]) + CENTRE * rows[2]
    odd = DIFFS[0] * (rows[0] - rows[4]) + DIFFS[1] * (rows[1] - rows[3])
    return even + odd, even - odd


def both_taps_transposed(first, second):
    total, difference = first + second, first - second
    outer = [SUMS[i] * total for i in range(2)]
    inner = [DIFFS[i] * difference for i in range(2)]
    return [outer[0] + inner[0], outer[1] + inner[1], CENTRE * total, outer[1] - inner[1], outer[0] - inner[0]]


def table_part(table_ref, first_row, first, target):
    rows = pl.ds(pl.multiple_of(first_row // 8 * 8, 8), target.shape[1])
    return table_ref.at[pl.ds(first, target.shape[0]), rows, :]


def main_kernel(peers, parents_hbm, octants_hbm, x_hbm, table_ref, spread_hbm, *rest):
    phase_ref, edge_phase_ref, flat_ref, slice_ref = rest[:4]
    parents_ref, octants_ref, x_ref, spread_ref, az_e, az_o, res_e, res_o, acc, flat, sems, x_sems = rest[4:]
    children = octants_ref.shape[0]
    periods = phase_ref.shape[3]
    azimuth_in = periods * PERIOD_C
    own = acc.shape[0]
    me = lax.axis_index("clus")
    share = ROWS_PER_PERIOD * periods // peers
    ends = (
        (octants_hbm, octants_ref),
        (parents_hbm, parents_ref),
        (spread_hbm, spread_ref),
        (table_part(table_ref, me * (2 * share), 0, slice_ref), slice_ref),
    )
    copies = [pltpu.make_async_copy(source, target, sems.at[i]) for i, (source, target) in enumerate(ends)]
    blocks = children // BLOCK
    block_rows = 2 * BLOCK * azimuth_in

    def x_copy(block):
        some = pl.ds(pl.multiple_of(block * block_rows, 8), block_rows)
        return pltpu.make_async_copy(x_hbm.at[some], x_ref.at[some], x_sems.at[block])

    for copy in copies[:-1]:
        copy.start()
    for block in range(blocks):
        x_copy(block).start()
    fill_phases(lax.axis_index("dir"), phase_ref)
    acc[...] = jnp.zeros_like(acc)
    sublane = lax.broadcasted_iota(jnp.int32, (periods, LANES), 0)
    for e, (w, m) in enumerate(edge_rows(periods)):
        for octant in range(8):
            for i in range(2):
                edge_phase_ref[e, i, octant : octant + 1, :] = phase_ref[octant, i, w, m : m + 1, :]
    for copy in copies[:-1]:
        copy.wait()
    copies[-1].start()

    def azimuth(block):
        for kp in range(2 * BLOCK):
            start = pl.multiple_of((block * (2 * BLOCK) + kp) * azimuth_in, 8)
            x = [x_ref[pl.ds(start + u, periods, stride=PERIOD_C), :] for u in range(PERIOD_C)]
            left = jnp.where(sublane == 0, 0.0, pltpu.roll(x[3], 1, 0))
            right = [jnp.where(sublane == periods - 1, 0.0, pltpu.roll(x[i], periods - 1, 0)) for i in range(2)]
            lower = [left, x[0], x[1], x[2], x[3]]
            upper = [x[1], x[2], x[3], right[0], right[1]]
            rows = [x[0], *both_taps(lower), x[2], *both_taps(upper)]
            for r in range(3):
                base = (kp * 3 + r) * periods
                az_e[base : base + periods, :] = rows[2 * r]
                az_o[base : base + periods, :] = rows[2 * r + 1]

    def polar():
        res_e[...] = spread_dot(az_e[...], spread_ref, 0)
        res_o[...] = spread_dot(az_o[...], spread_ref, 1)

    def shift(block):
        for k in range(BLOCK):
            octant = octants_ref[block * BLOCK + k]
            parent = parents_ref[block * BLOCK + k]
            for r in range(3):
                parts = []
                for part in range(2):
                    rows = pl.ds(((2 * k + part) * 3 + r) * periods, periods)
                    middle = res_e[rows, LANES:] + res_o[rows, LANES:]
                    parts.append((res_e[rows, :LANES], middle, res_o[rows, :LANES]))
                for i in range(3):
                    w = 3 * r + i
                    real, imaginary = parts[0][i], parts[1][i]
                    cosine, sine = phase_ref[octant, 0, w], phase_ref[octant, 1, w]
                    acc[parent, 0, w] += real * cosine - imaginary * sine
                    acc[parent, 1, w] += real * sine + imaginary * cosine

    def one_block(block, carry):
        x_copy(block).wait()
        azimuth(block)
        polar()
        shift(block)
        return carry

    lax.fori_loop(0, blocks, one_block, 0)
    for gp in range(2 * own):
        for w in range(ROWS_PER_PERIOD):
            flat[pl.ds(gp * ROWS_PER_PERIOD * periods + w, periods, stride=ROWS_PER_PERIOD), :] = acc[gp // 2, gp % 2, w]
        for q in range(peers):
            source = gp * ROWS_PER_PERIOD * periods + q * share
            target = (q * 2 * own + gp) * share
            flat_ref[target : target + share, :] = flat[source : source + share, :]
    copies[-1].wait()


def one_hot(parents, own):
    index = lax.broadcasted_iota(jnp.int32, (own, parents.shape[1]), 0)
    return (index == parents).astype(f32)


def dot2(exact, values):
    exact = exact.astype(bf16)
    high, low = split(values)
    return dot(exact, high) + dot(exact, low)


def fix_kernel(
    peers, own, parents_ref, octants_ref, far_ref, near_ref, flat_ref, edge_phase_ref, spread_ref, *rest
):
    outs, (fixed,) = rest[:peers], rest[peers:]
    pairs = far_ref.shape[1]
    children = pairs // 2
    chunk_rows = outs[0].shape[0]
    share = chunk_rows // (2 * own)
    periods = share * peers // ROWS_PER_PERIOD
    fixed[...] = flat_ref[...]
    is_even = lax.rem(lax.axis_index("dir"), 2) == 0

    def by_part(ref, i):
        return jnp.concatenate([ref[i, pl.ds(part, children, stride=2), :] for part in range(2)], axis=0)

    far, near = ([by_part(ref, i) for i in range(2)] for ref in (far_ref, near_ref))
    left = jnp.where(is_even, far[0], near[0])
    right = [jnp.where(is_even, n, f) for f, n in zip(far, near)]
    a, b = TAPS_A, TAPS_B
    even = jnp.concatenate([b[0] * left, a[3] * right[0] + a[4] * right[1]], axis=0)
    odd = jnp.concatenate([a[0] * left, b[3] * right[0] + b[4] * right[1]], axis=0)
    even = spread_dot(even, spread_ref, 0)
    odd = spread_dot(odd, spread_ref, 1)
    first, last = slice(0, pairs), slice(pairs, 2 * pairs)
    low, high = slice(0, LANES), slice(LANES, 2 * LANES)
    refined = [
        odd[first, high],
        odd[first, low],
        even[first, low],
        even[first, high],
        even[last, low],
        even[last, high] + odd[last, high],
        odd[last, low],
    ]
    by_octant = jnp.concatenate([edge_phase_ref[e, i] for e in range(len(refined)) for i in range(2)], axis=1)
    phases = dot2(one_hot(octants_ref[...], 8).T, by_octant)
    shifted_rows = []
    for e, rows in enumerate(refined):
        real, imaginary = rows[:children], rows[children:]
        cosine, sine = (phases[:, (2 * e + i) * LANES : (2 * e + i + 1) * LANES] for i in range(2))
        shifted_rows.append(real * cosine - imaginary * sine)
        shifted_rows.append(real * sine + imaginary * cosine)
    summed = dot2(one_hot(parents_ref[...], own), jnp.concatenate(shifted_rows, axis=1))
    for e, (w, m) in enumerate(edge_rows(periods)):
        q, row = divmod(ROWS_PER_PERIOD * m + w, share)
        for part in range(2):
            rows = pl.ds(q * chunk_rows + part * share + row, own, stride=2 * share)
            column = (2 * e + part) * LANES
            fixed[rows, :] = fixed[rows, :] + summed[:, column : column + LANES]
    me = lax.axis_index("clus")
    for d in range(peers):
        start = pl.multiple_of((me ^ d) * chunk_rows, 8)
        outs[d][...] = fixed[pl.ds(start, chunk_rows), :]


def widen_kernel(peers, others, source_ref, offset_ref, count_ref, head_ref, table_ref, chunk, placed_ref, real_sum, imag_sum, *rest):
    tail_ref, wide_ref, numbers_ref, listed, real_twice, imag_twice, sem, tail_sem = rest
    targets, partners = source_ref.shape
    half, frame, _ = head_ref.shape
    offsets = half + tail_ref.shape[0]
    own = targets // peers
    share = chunk.shape[0] // (2 * own)
    me = lax.axis_index("clus")
    tail_copy = pltpu.make_async_copy(table_part(table_ref, me * (2 * share), half, tail_ref), tail_ref, tail_sem)
    tail_copy.start()
    shape = (targets, targets)
    row, lane = (lax.broadcasted_iota(jnp.int32, shape, d) for d in range(2))
    count = jnp.sum(jnp.where(row == lane, count_ref[...], 0), axis=1, keepdims=True)
    number = jnp.full(shape, offsets, jnp.int32)
    for p in range(partners):
        here = (lane == source_ref[:, p : p + 1]) & (p < count)
        number = jnp.where(here, offset_ref[:, p : p + 1], number)
    numbers_ref[...] = number * frame
    copy = pltpu.make_async_copy(numbers_ref, listed, sem)
    copy.start()

    def widen(part_ref, first):
        def some_offsets(i, carry):
            for j in range(4):
                place = pl.multiple_of((first + i * 4 + j) * frame, 8)
                wide_ref[pl.ds(place, frame), :] = part_ref[i * 4 + j].astype(f32)
            return carry

        whole_steps = part_ref.shape[0] // 4
        lax.fori_loop(0, whole_steps, some_offsets, 0)
        for offset in range(whole_steps * 4, part_ref.shape[0]):
            wide_ref[(first + offset) * frame : (first + offset + 1) * frame, :] = part_ref[offset].astype(f32)

    widen(head_ref, 0)
    wide_ref[offsets * frame :, :] = jnp.zeros((frame, LANES), f32)
    doubled(chunk, real_twice, imag_twice, 0, own, share, frame, lax.rem(me * (2 * share), 8))
    copy.wait()
    tail_copy.wait()
    widen(tail_ref, half)

    def operator_of(target, device, g):
        first = listed[target, device * own + g]
        return wide_ref[pl.ds(pl.multiple_of(first, 8), frame), :]

    def own_sources(some, sums):
        return add_sources(sums, own, frame, lambda j, source: operator_of(some[j], me, source), real_twice, imag_twice)

    for_some_targets(targets, frame, own_sources, None, (real_sum, imag_sum))

    def other_sources(target, carry):
        for i, d in enumerate(others):
            for g in range(own):
                place = pl.multiple_of(((target * len(others) + i) * own + g) * frame, 8)
                placed_ref[pl.ds(place, frame), :] = operator_of(target, me ^ d, g)
        return carry

    lax.fori_loop(0, targets, other_sources, 0)


def doubled(chunk, real_twice, imag_twice, first, own, share, frame, skip):
    for g in range(own):
        for part, twice in enumerate((real_twice, imag_twice)):
            rows = chunk[(2 * g + part) * share : (2 * g + part + 1) * share, :]
            base = (first + g) * frame + skip
            twice[pl.ds(base, share, stride=2), :] = rows
            twice[pl.ds(base + 1, share, stride=2), :] = rows


def add_sources(sums, sources, frame, operators, real_twice, imag_twice):
    for source in range(sources):
        place = slice(source * frame, (source + 1) * frame)
        real, imaginary = real_twice[place, :], imag_twice[place, :]
        for i in range(len(sums)):
            operator = operators(i, source)
            sums[i] = (sums[i][0] + operator * real, sums[i][1] + operator * imaginary)
    return sums


def for_some_targets(targets, frame, add, before, after):
    def some_targets(i, carry):
        some = [i * TOGETHER + j for j in range(TOGETHER)]
        places = [pl.ds(pl.multiple_of(target * frame, 8), frame) for target in some]
        if before is None:
            sums = [(jnp.zeros((frame, LANES), f32),) * 2 for _ in some]
        else:
            sums = [tuple(ref[place, :] for ref in before) for place in places]
        for place, values in zip(places, add(some, sums)):
            for ref, value in zip(after, values):
                ref[place, :] = value
        return carry

    lax.fori_loop(0, targets // TOGETHER, some_targets, 0)


def placed(placed_ref, frame, others, own, masks):
    firsts = [others.index(d) * own for d in masks]

    def operator_of(target, source):
        place = target * (len(others) * own) + firsts[source // own] + source % own
        return placed_ref[pl.ds(pl.multiple_of(place * frame, 8), frame), :]

    return operator_of


def gather_kernel(peers, frame, others, masks, placed_ref, *rest):
    chunks, (real_before, imag_before, real_sum, imag_sum, real_twice, imag_twice) = rest[:-6], rest[-6:]
    me = lax.axis_index("clus")
    targets = real_sum.shape[0] // frame
    own = targets // peers
    share = chunks[0].shape[0] // (2 * own)
    skip = lax.rem(me * (2 * share), 8)
    for number, chunk in enumerate(chunks):
        doubled(chunk, real_twice, imag_twice, number * own, own, share, frame, skip)
    operator_of = placed(placed_ref, frame, others, own, masks)

    def add(some, sums):
        operators = lambda j, source: operator_of(some[j], source)
        return add_sources(sums, len(masks) * own, frame, operators, real_twice, imag_twice)

    for_some_targets(targets, frame, add, (real_before, imag_before), (real_sum, imag_sum))


def translate_kernel(frame, others, masks, targets, placed_ref, real_sum, imag_sum, *rest):
    prepare = len(rest) == len(masks) + len(targets) + 4
    chunks, rest = (rest[: len(masks)], rest[len(masks) :]) if prepare else ((), rest)
    real_twice, imag_twice = rest[:2]
    outs, (total_real, total_imag) = rest[-2 - len(targets) : -2], rest[-2:]
    me = lax.axis_index("clus")
    sources = real_twice.shape[0] // frame
    own = sources // len(masks)
    share = outs[0].shape[0] // (2 * own)
    skip = lax.rem(me * (2 * share), 8)
    for number, chunk in enumerate(chunks):
        doubled(chunk, real_twice, imag_twice, number * own, own, share, frame, skip)
    operator_of = placed(placed_ref, frame, others, own, masks)
    even, odd = pl.ds(skip, share, stride=2), pl.ds(skip + 1, share, stride=2)
    for out, d in zip(outs, targets):
        first = (me ^ d) * own

        def some_targets(i, carry):
            places = [i * TOGETHER + j for j in range(TOGETHER)]
            some = [first + g for g in places]
            rows = [pl.ds(pl.multiple_of(target * frame, 8), frame) for target in some]
            sums = [(real_sum[r, :], imag_sum[r, :]) for r in rows]
            operators = lambda j, source: operator_of(some[j], source)
            sums = add_sources(sums, sources, frame, operators, real_twice, imag_twice)
            for j, (g, (by_real, by_imag)) in enumerate(zip(places, sums)):
                total_real[j] = by_real
                total_imag[j] = by_imag
                row = g * (2 * share)
                out[pl.ds(row, share), :] = total_real[j, even, :] - total_imag[j, odd, :]
                out[pl.ds(row + share, share), :] = total_real[j, odd, :] + total_imag[j, even, :]
            return carry

        lax.fori_loop(0, own // TOGETHER, some_targets, 0)


def extract_kernel(peers, own2, *rest):
    chunks = rest[:peers]
    flat, far_ref, near_ref = rest[peers:]
    share = chunks[0].shape[0] // own2
    periods = share * peers // ROWS_PER_PERIOD
    own = own2 // 2
    flat_rows = ROWS_PER_PERIOD * periods
    me = lax.axis_index("clus")
    for gp in range(own2):
        for d in range(peers):
            flat[pl.ds(gp * flat_rows + (me ^ d) * share, share), :] = chunks[d][gp * share : (gp + 1) * share, :]

    def fill(prev_ref, next_ref):
        for ref in (prev_ref, next_ref):
            ref[...] = jnp.zeros_like(ref)
        places = [(prev_ref, e) for e in range(4)] + [(next_ref, e) for e in range(3)]
        for (ref, e), (w, m) in zip(places, edge_rows(periods)):
            for part in range(2):
                first = part * flat_rows + ROWS_PER_PERIOD * m + w
                row = (2 * e + part) * own
                ref[row : row + own, :] = flat[pl.ds(first, own, stride=2 * flat_rows), :]

    by_parity(lambda: fill(far_ref, near_ref), lambda: fill(near_ref, far_ref))


def neighbour_kernel(periods, octants_hbm, out_ref, by_octant, octants_ref, sem):
    copy = pltpu.make_async_copy(octants_hbm, octants_ref, sem)
    copy.start()
    here = lax.axis_index("dir")
    octant = lax.broadcasted_iota(jnp.int32, (8, LANES), 0)
    lane = lax.broadcasted_iota(jnp.int32, (8, LANES), 1)
    signs = [(1 - 2 * ((octant >> bit) & 1)).astype(f32) for bit in range(3)]
    for e, (w, m) in enumerate(edge_rows(periods)):
        place = here + 1 if m == 0 else here - 1
        position = lane + w * LANES
        row = w * LANES // NTHETA_P
        row = jnp.where(position >= (row + 1) * NTHETA_P, row + 1, row)
        polar_index = position - row * NTHETA_P
        azimuth_index = (place * periods + m) * PERIOD_P + row
        sin_polar, cos_polar = sincos_turns((polar_index.astype(f32) + 0.5) / (2 * NTHETA_P))
        sin_azimuth, cos_azimuth = sincos_turns(azimuth_index.astype(f32) / NPHI_P)
        along = (sin_polar * cos_azimuth, sin_polar * sin_azimuth, cos_polar)
        sine, cosine = sincos_turns(4.0 * (signs[0] * along[0] + signs[1] * along[1] + signs[2] * along[2]))
        by_octant[e, 0] = cosine
        by_octant[e, 1] = sine
    copy.wait()

    def some_children(step, carry):
        for j in range(GROUP):
            k = step * GROUP + j
            for e in range(by_octant.shape[0]):
                for i in range(2):
                    out_ref[e, i, pl.ds(k, 1), :] = by_octant[e, i, pl.ds(octants_ref[k], 1), :]
        return carry

    lax.fori_loop(0, octants_ref.shape[0] // GROUP, some_children, 0)


def edge_contributions(parents, phase_ref, gather_ref, above, below):
    children = parents.shape[1]
    own = below.shape[0] // 8
    rows = [above[2 * e * own : 2 * (e + 1) * own] for e in range(4)] + [below[2 * e * own : 2 * (e + 1) * own] for e in range(3)]
    edges = jnp.concatenate([r[part * own : (part + 1) * own] for r in rows for part in range(2)], axis=1)
    per_child = dot2(one_hot(parents, own).T, edges)
    returned = []
    for e in range(len(rows)):
        real = per_child[:, 2 * e * LANES : (2 * e + 1) * LANES]
        imaginary = per_child[:, (2 * e + 1) * LANES : (2 * e + 2) * LANES]
        cosine, sine = phase_ref[e, 0], phase_ref[e, 1]
        returned.append(
            jnp.concatenate([real * cosine + imaginary * sine, imaginary * cosine - real * sine], axis=0)
        )
    join = functools.partial(jnp.concatenate, axis=1)
    even = jnp.concatenate([join([returned[2], returned[3]]), join([returned[4], returned[5]])], axis=0)
    odd = jnp.concatenate([join([returned[0], returned[1]]), join([returned[5], returned[6]])], axis=0)
    even = gather_dot(*split(even), gather_ref, 0)
    odd = gather_dot(*split(odd), gather_ref, 1)
    a, b = TAPS_A, TAPS_B
    pairs = 2 * children
    last = a[0] * odd[:pairs] + b[0] * even[:pairs]
    first = [a[3 + i] * even[pairs:] + b[3 + i] * odd[pairs:] for i in range(2)]
    return first, last


def disaggregate_kernel(
    parents_ref, octants_ref, flat_ref, phase_ref, gather_ref, out_ref, edge_ref, listed, incoming_ref, lhs, coarse_e, coarse_o, whole_out, sems
):
    periods = incoming_ref.shape[2]
    packed = parents_ref[...] * 8 + octants_ref[...]
    for k in range(listed.shape[0]):
        listed[k] = packed[0, k]
    for gp in range(incoming_ref.shape[0]):
        for w in range(ROWS_PER_PERIOD):
            first = gp * ROWS_PER_PERIOD * periods + w
            incoming_ref[gp, w] = flat_ref[pl.ds(first, periods, stride=ROWS_PER_PERIOD), :]
    sublane = lax.broadcasted_iota(jnp.int32, (periods, LANES), 0)

    def shift(block):
        for k in range(BLOCK):
            code = listed[block * BLOCK + k]
            octant, parent = code & 7, code >> 3
            for r in range(3):
                for i in range(3):
                    w = 3 * r + i
                    real, imaginary = incoming_ref[2 * parent, w], incoming_ref[2 * parent + 1, w]
                    cosine, sine = phase_ref[octant, 0, w], phase_ref[octant, 1, w]
                    returned = (real * cosine + imaginary * sine, imaginary * cosine - real * sine)
                    for part in range(2):
                        base = ((2 * k + part) * 3 + r) * periods
                        lhs[base : base + periods, i * LANES : (i + 1) * LANES] = returned[part]

    def polar():
        high, low = split(lhs[...])
        coarse_e[...] = gather_dot(high[:, : 2 * LANES], low[:, : 2 * LANES], gather_ref, 0)
        coarse_o[...] = gather_dot(high[:, LANES:], low[:, LANES:], gather_ref, 1)

    def azimuth(block):
        for j in range(2 * BLOCK):
            c = []
            for r in range(3):
                base = (j * 3 + r) * periods
                c.append(coarse_e[base : base + periods, :])
                c.append(coarse_o[base : base + periods, :])
            lower = both_taps_transposed(c[1], c[2])
            upper = both_taps_transposed(c[4], c[5])
            down = [jnp.where(sublane == 0, 0.0, pltpu.roll(upper[i], 1, 0)) for i in (3, 4)]
            up = jnp.where(sublane == periods - 1, 0.0, pltpu.roll(lower[0], periods - 1, 0))
            rows = [c[0] + lower[1] + down[0], lower[2] + upper[0] + down[1], c[3] + lower[3] + upper[1], lower[4] + upper[2] + up]
            kp = block * (2 * BLOCK) + j
            for u in range(PERIOD_C):
                whole_out[kp, pl.ds(u, periods, stride=PERIOD_C), :] = rows[u]
            for i, (u, m) in enumerate(((0, 0), (1, 0), (PERIOD_C - 1, periods - 1))):
                edge_ref[i, pl.ds(kp, 1), :] = rows[u][m : m + 1]

    def written(block):
        some = pl.ds(block * (2 * BLOCK), 2 * BLOCK)
        return pltpu.make_async_copy(whole_out.at[some], out_ref.at[some], sems.at[block])

    def one_block(block, carry):
        shift(block)
        polar()
        azimuth(block)
        written(block).start()
        return carry

    blocks = listed.shape[0] // BLOCK
    lax.fori_loop(0, blocks, one_block, 0)
    for block in range(blocks):
        written(block).wait()


def finish_kernel(parents_ref, phase_ref, gather_ref, edge_ref, far_ref, near_ref, part_ref, out_ref, sums, sems):
    pairs, azimuth_in, _ = out_ref.shape
    children = pairs // 2
    below, above = from_sides(far_ref, near_ref)
    heads, tail = edge_contributions(parents_ref[...], phase_ref, gather_ref, above, below)
    copies = []
    for i, (row, values) in enumerate(((0, heads[0]), (1, heads[1]), (azimuth_in - 1, tail))):
        for part in range(2):
            place = pl.ds(part, children, stride=2)
            sums[i, place, :] = edge_ref[i, place, :] + values[part * children : (part + 1) * children]
        copy = pltpu.make_async_copy(sums.at[i], out_ref.at[:, row, :], sems.at[i])
        copy.start()
        copies.append(copy)
    for copy in copies:
        copy.wait()


def swapped(values, axis, first):
    size = lax.axis_size(axis)
    return lax.ppermute(values, axis, [(i, (((i - first) ^ 1) + first) % size) for i in range(size)])


def exchanged(values, axis, mask):
    size = lax.axis_size(axis)
    return lax.ppermute(values, axis, [(i, i ^ mask) for i in range(size)])


SMEM = pl.BlockSpec(memory_space=pltpu.SMEM)
VMEM = pl.BlockSpec(memory_space=pltpu.VMEM)
HBM = pl.BlockSpec(memory_space=pltpu.HBM)


def in_hbm(values):
    return pltpu.with_memory_space_constraint(values, pltpu.HBM)


def local_call(kernel, out_shape, in_specs, scratch, grant, flops=1_000_000, bytes_accessed=1_000_000, out_specs=None, aliases={}):
    return pl.pallas_call(
        kernel,
        out_shape=out_shape,
        in_specs=in_specs,
        out_specs=jax.tree.map(lambda _: VMEM, out_shape) if out_specs is None else out_specs,
        scratch_shapes=scratch,
        input_output_aliases=aliases,
        compiler_params=pltpu.CompilerParams(vmem_limit_bytes=grant << 20),
        cost_estimate=pl.CostEstimate(flops=flops, bytes_accessed=bytes_accessed, transcendentals=0),
    )


def on_device_exchange(
    child_patterns, trans_table, child_parent, child_octant, partner_src, partner_off, partner_count
):
    children, _, azimuth_in, polar_in = child_patterns.shape
    pairs = 2 * children
    peers = lax.axis_size("clus")
    parent_total, _ = partner_src.shape
    own = parent_total // peers
    periods = azimuth_in // PERIOD_C
    flat_rows = ROWS_PER_PERIOD * periods
    share = flat_rows // peers
    offsets = trans_table.shape[0]
    array = lambda *shape: jax.ShapeDtypeStruct(shape, f32)
    buffer = lambda *shape: pltpu.VMEM(shape, f32)
    edges = len(edge_rows(periods))
    even, odd = polar_blocks()
    spread = jnp.asarray(np.stack([np.concatenate([h, h, l]) for h, l in (split_np(even), split_np(odd))]))
    edge = array(2, pairs, polar_in)
    to_far, to_near = local_call(
        rows_kernel, [edge, edge], [HBM], [pltpu.SemaphoreType.DMA((4,))], 8
    )(in_hbm(child_patterns.reshape(pairs, azimuth_in, polar_in)))
    from_far = swapped(to_far, "dir", 1)
    from_near = swapped(to_near, "dir", 0)
    odd_gather = np.concatenate([odd.T[LANES:], odd.T[:LANES]])
    gather = np.stack([np.concatenate(split_np(m), axis=1) for m in (even.T, odd_gather)])

    frame = max(-(-((q * 2 * share) % 8 + 2 * share) // 8) * 8 for q in range(peers))
    view = trans_table.reshape(offsets, 2, flat_rows, LANES).transpose(0, 2, 1, 3).reshape(offsets, 2 * flat_rows, LANES)
    blocks = children // BLOCK
    half = offsets * 3 // 4
    rows = 2 * BLOCK * 3 * periods
    phases, edge_phases, flat, table = local_call(
        functools.partial(main_kernel, peers),
        [
            array(8, 2, ROWS_PER_PERIOD, periods, LANES),
            array(edges, 2, 8, LANES),
            array(2 * own * flat_rows, LANES),
            jax.ShapeDtypeStruct((half, frame, LANES), bf16),
        ],
        [HBM] * 5,
        [
            pltpu.SMEM((children,), jnp.int32),
            pltpu.SMEM((children,), jnp.int32),
            buffer(pairs * azimuth_in, polar_in),
            pltpu.VMEM(spread.shape, bf16),
            buffer(rows, LANES),
            buffer(rows, LANES),
            buffer(rows, 2 * LANES),
            buffer(rows, 2 * LANES),
            buffer(own, 2, ROWS_PER_PERIOD, periods, LANES),
            buffer(2 * own * flat_rows, LANES),
            pltpu.SemaphoreType.DMA((4,)),
            pltpu.SemaphoreType.DMA((blocks,)),
        ],
        24,
        flops=4_000_000_000,
        bytes_accessed=12_000_000,
    )(
        in_hbm(child_parent[0]),
        in_hbm(child_octant),
        in_hbm(child_patterns.reshape(pairs * azimuth_in, polar_in)),
        in_hbm(view),
        in_hbm(spread),
    )

    chunk = array(2 * own * share, LANES)
    sent = local_call(
        functools.partial(fix_kernel, peers, own), [chunk] * peers, [VMEM] * 7, [buffer(2 * own * flat_rows, LANES)], 8
    )(child_parent, child_octant.reshape(1, children), from_far, from_near, flat, edge_phases, spread)

    masks = sorted(range(1, peers), key=lambda d: bin(d).count("1"))
    early, late = masks[:1], masks[1:]
    received = {0: sent[0]}
    for d in early:
        received[d] = exchanged(sent[d], "clus", d)
    for d in late:
        received[d] = exchanged(sent[d], "clus", d)

    sum_pair = [array(parent_total * frame, LANES)] * 2
    others = tuple(early + late)
    operators, *sums = local_call(
        functools.partial(widen_kernel, peers, others),
        [array(parent_total * len(others) * own * frame, LANES)] + sum_pair,
        [VMEM] * 4 + [HBM, VMEM],
        [
            pltpu.VMEM((offsets - half, frame, LANES), bf16),
            buffer((offsets + 1) * frame, LANES),
            pltpu.VMEM((parent_total, parent_total), jnp.int32),
            pltpu.SMEM((parent_total, parent_total), jnp.int32),
            buffer(own * frame, LANES),
            buffer(own * frame, LANES),
            pltpu.SemaphoreType.DMA,
            pltpu.SemaphoreType.DMA,
        ],
        20,
        flops=90_000_000,
        bytes_accessed=12_000_000,
    )(partner_src, partner_off, partner_count.reshape(1, parent_total), table, in_hbm(view), received[0])

    sums = local_call(
        functools.partial(gather_kernel, peers, frame, others, tuple(early)),
        sum_pair,
        [VMEM] * (3 + len(early)),
        [buffer(len(early) * own * frame, LANES)] * 2,
        12,
        flops=60_000_000,
        bytes_accessed=12_000_000,
    )(operators, *[received[d] for d in early], *sums)

    back = {}
    last_sources = [received[d] for d in late]
    for number, targets in enumerate((masks[-1:], masks[:-1], [0])):
        prepare = number == 0
        results = local_call(
            functools.partial(translate_kernel, frame, others, tuple(late), tuple(targets)),
            ([array(len(late) * own * frame, LANES)] * 2 if prepare else []) + [chunk] * len(targets),
            [VMEM] * (3 + len(last_sources)),
            [buffer(TOGETHER, frame, LANES)] * 2,
            20,
            flops=10_000_000 * len(targets),
            bytes_accessed=2_000_000 * len(targets),
        )(operators, *sums, *last_sources)
        if prepare:
            last_sources, results = results[:2], results[2:]
        for d, result in zip(targets, results):
            back[d] = exchanged(result, "clus", d) if d else result

    neighbour_phases = local_call(
        functools.partial(neighbour_kernel, periods),
        array(edges, 2, children, LANES),
        [HBM],
        [buffer(edges, 2, 8, LANES), pltpu.SMEM((children,), jnp.int32), pltpu.SemaphoreType.DMA],
        8,
        flops=20_000_000,
    )(in_hbm(child_octant))

    side = array(8 * own, LANES)
    incoming, to_far, to_near = local_call(
        functools.partial(extract_kernel, peers, 2 * own),
        [array(2 * own * flat_rows, LANES), side, side],
        [VMEM] * peers,
        [],
        8,
    )(*[back[d] for d in range(peers)])

    from_far = swapped(to_far, "dir", 1)
    from_near = swapped(to_near, "dir", 0)

    partial_out, edge_sums = local_call(
        disaggregate_kernel,
        [array(pairs, azimuth_in, polar_in), array(3, pairs, polar_in)],
        [VMEM] * 5,
        [
            pltpu.SMEM((children,), jnp.int32),
            buffer(2 * own, ROWS_PER_PERIOD, periods, LANES),
            buffer(rows, 3 * LANES),
            buffer(rows, LANES),
            buffer(rows, LANES),
            buffer(pairs, azimuth_in, polar_in),
            pltpu.SemaphoreType.DMA((blocks,)),
        ],
        24,
        flops=4_000_000_000,
        bytes_accessed=12_000_000,
        out_specs=[HBM, VMEM],
    )(child_parent, child_octant.reshape(1, children), incoming, phases, gather)

    out = local_call(
        finish_kernel,
        array(pairs, azimuth_in, polar_in),
        [VMEM] * 6 + [HBM],
        [buffer(3, pairs, polar_in), pltpu.SemaphoreType.DMA((3,))],
        8,
        out_specs=HBM,
        aliases={6: 0},
    )(child_parent, neighbour_phases, gather, edge_sums, from_far, from_near, in_hbm(partial_out))
    return out.reshape(child_patterns.shape)


def with_halo(shard, sides, width):
    for axis, dim in sides:
        size, length = (lax.axis_size(axis), shard.shape[dim])
        up = [(i, (i + 1) % size) for i in range(size)]
        down = [(j, i) for i, j in up]
        last = lax.slice_in_dim(shard, length - width, length, axis=dim)
        initial = lax.slice_in_dim(shard, 0, width, axis=dim)
        before = lax.ppermute(last, axis, up)
        after = lax.ppermute(initial, axis, down)
        shard = jnp.concatenate([before, shard, after], axis=dim)
    return shard


def lagrange_rows(offset):
    weights = []
    for anchor in range(5):
        factor = jnp.ones_like(offset)
        for neighbour in range(5):
            if neighbour != anchor:
                factor = factor * (offset - neighbour) / (anchor - neighbour)
        weights.append(factor)
    return weights


def polar_matrix_of(rows_out, rows_in):
    target = (jnp.arange(rows_out, dtype=jnp.float32) + 0.5) * rows_in / rows_out - 0.5
    start_row = jnp.clip(jnp.floor(target + 0.5).astype(jnp.int32) - 2, 0, rows_in - 5)
    weights = lagrange_rows(target - start_row.astype(jnp.float32))
    columns = jnp.arange(rows_in, dtype=jnp.int32)
    matrix = jnp.zeros((rows_out, rows_in), jnp.float32)
    for anchor in range(5):
        matrix = matrix + jnp.where(
            columns[None, :] == (start_row + anchor)[:, None], weights[anchor][:, None], 0.0
        )
    return matrix


def azimuth_matrix_of(out_index, in_index, total_out, total_in):
    target = (out_index * total_in).astype(jnp.float32) / total_out
    nearest = jnp.floor(target + 0.5).astype(jnp.int32)
    weights = lagrange_rows(target - nearest.astype(jnp.float32) + 2.0)
    matrix = jnp.zeros((out_index.shape[0], in_index.shape[0]), jnp.float32)
    for anchor in range(5):
        columns = nearest + anchor - 2
        matrix = matrix + jnp.where(
            in_index[None, :] == columns[:, None], weights[anchor][:, None], 0.0
        )
    return matrix


def shift_phases(octant, azimuth_index, azimuth_total, polar_total):
    azimuth = 2.0 * math.pi * azimuth_index.astype(jnp.float32) / azimuth_total
    polar = math.pi * (jnp.arange(polar_total, dtype=jnp.float32) + 0.5) / polar_total
    first_axis = jnp.sin(polar)[None, :] * jnp.cos(azimuth)[:, None]
    second_axis = jnp.sin(polar)[None, :] * jnp.sin(azimuth)[:, None]
    third_axis = jnp.cos(polar)[None, :] * jnp.ones_like(azimuth)[:, None]
    first_sign = (1 - 2 * (octant % 2)).astype(jnp.float32)
    second_sign = (1 - 2 * (octant // 2 % 2)).astype(jnp.float32)
    third_sign = (1 - 2 * (octant // 4)).astype(jnp.float32)
    phase_angle = phase_scale * (
        first_sign[:, None, None] * first_axis[None]
        + second_sign[:, None, None] * second_axis[None]
        + third_sign[:, None, None] * third_axis[None]
    )
    return (jnp.cos(phase_angle), jnp.sin(phase_angle))


def translate(sources, table, partner_src, partner_off, partner_count):
    live_mask = (
        jnp.arange(partner_src.shape[1], dtype=jnp.int32)[None, :] < partner_count[:, None]
    ).astype(jnp.float32)
    picked = sources[partner_src]
    operator = table[partner_off].astype(jnp.float32) * live_mask[:, :, None, None]
    real_part = jnp.sum(
        operator[:, :, 0] * picked[:, :, 0] - operator[:, :, 1] * picked[:, :, 1], axis=1
    )
    imaginary = jnp.sum(
        operator[:, :, 0] * picked[:, :, 1] + operator[:, :, 1] * picked[:, :, 0], axis=1
    )
    return jnp.stack([real_part, imaginary], axis=1)


def forward_shift(patterns, cosine, sine_part):
    real_part = patterns[:, 0] * cosine - patterns[:, 1] * sine_part
    imaginary = patterns[:, 0] * sine_part + patterns[:, 1] * cosine
    return jnp.stack([real_part, imaginary], axis=1)


def conjugate_shift(patterns, cosine, sine_part):
    real_part = patterns[:, 0] * cosine + patterns[:, 1] * sine_part
    imaginary = patterns[:, 1] * cosine - patterns[:, 0] * sine_part
    return jnp.stack([real_part, imaginary], axis=1)


def on_device_gather(
    child_patterns, trans_table, child_parent, child_octant, partner_src, partner_off, partner_count
):
    _, _, azimuth_in, _ = child_patterns.shape
    polar_out = NTHETA_P
    azimuth_out = trans_table.shape[2] // polar_out
    parent_slots = partner_src.shape[0] // lax.axis_size("clus")
    cluster_index = lax.axis_index("clus")
    direction_index = lax.axis_index("dir")
    parents = child_parent[0]
    polar_matrix = polar_matrix_of(NTHETA_P, NTHETA_C)
    onehot = (parents[None, :] == jnp.arange(parent_slots, dtype=jnp.int32)[:, None]).astype(
        jnp.float32
    )
    own_rows = jnp.mod(
        direction_index * azimuth_out + jnp.arange(azimuth_out, dtype=jnp.int32), NPHI_P
    )
    cosine, sine_part = shift_phases(child_octant, own_rows, NPHI_P, polar_out)
    extended = with_halo(child_patterns, (("dir", 2),), 2)
    gather_matrix = azimuth_matrix_of(
        jnp.arange(azimuth_out, dtype=jnp.int32),
        jnp.arange(azimuth_in + 4, dtype=jnp.int32) - 2,
        NPHI_P,
        NPHI_C,
    )
    along_azimuth = jnp.einsum("pc,kacz->kapz", gather_matrix, extended, precision=highest)
    refined = jnp.einsum("kapz,tz->kapt", along_azimuth, polar_matrix, precision=highest)
    shifted = forward_shift(refined, cosine, sine_part)
    radiation = jnp.einsum("gk,kapt->gapt", onehot, shifted, precision=highest)
    flattened = radiation.reshape(parent_slots, 2, azimuth_out * polar_out)
    sources = lax.all_gather(flattened, "clus", axis=0, tiled=True)
    first_row = cluster_index * parent_slots
    own_src = lax.dynamic_slice_in_dim(partner_src, first_row, parent_slots, 0)
    own_off = lax.dynamic_slice_in_dim(partner_off, first_row, parent_slots, 0)
    own_count = lax.dynamic_slice_in_dim(partner_count, first_row, parent_slots, 0)
    incoming = translate(sources, trans_table, own_src, own_off, own_count)
    incoming = incoming.reshape(parent_slots, 2, azimuth_out, polar_out)
    return_matrix = azimuth_matrix_of(
        jnp.arange(azimuth_out + 6, dtype=jnp.int32) - 3,
        jnp.arange(azimuth_in, dtype=jnp.int32),
        NPHI_P,
        NPHI_C,
    )
    per_child = jnp.einsum("gk,gapt->kapt", onehot, incoming, precision=highest)
    returned = conjugate_shift(per_child, cosine, sine_part)
    coarse_own = jnp.einsum("kapt,tz->kapz", returned, polar_matrix, precision=highest)
    coarse = with_halo(coarse_own, (("dir", 2),), 3)
    return jnp.einsum("pc,kapz->kacz", return_matrix, coarse, precision=highest)


def solution(mesh):
    def on_device(child_patterns, trans_table, *rest):
        peers = lax.axis_size("clus")
        children, _, azimuth_in, polar_in = child_patterns.shape
        flat_rows = trans_table.shape[2] // LANES
        fits = (
            azimuth_in % (8 * PERIOD_C) == 0
            and polar_in == LANES
            and flat_rows * PERIOD_C == ROWS_PER_PERIOD * azimuth_in
            and flat_rows % peers == 0
            and peers & (peers - 1) == 0
            and peers > 2
            and lax.axis_size("dir") % 2 == 0
            and children % BLOCK == 0
        )
        plan = on_device_exchange if fits else on_device_gather
        return plan(child_patterns, trans_table, *rest)

    return jax.shard_map(
        on_device,
        mesh=mesh,
        in_specs=(
            P("clus", None, "dir", None),
            P(None, None, "dir"),
            P("clus", None),
            P("clus"),
            P(),
            P(),
            P(),
        ),
        out_specs=P("clus", None, "dir", None),
        check_vma=False,
    )
```
